32 devices in a mesh: fsdp: 32 (over z, y, x, core).
Axes of the slice: x: 2, y: 2, z: 4, core: 2. Of those that a mesh axis runs over, the one named last changes fastest.
Arguments:
- x_global: bfloat16 [128, 197, 768], P('fsdp'), may hold values from -6 to 6
- x_local: bfloat16 [320, 37, 768], P('fsdp'), may hold values from -6 to 6
- cot_global: bfloat16 [128, 197, 768], P('fsdp'), may hold values from -6 to 6
- cot_local: bfloat16 [320, 37, 768], P('fsdp'), may hold values from -6 to 6
- global_count: int32 [32], P('fsdp'), may hold values from 1 to 4, as said below
- local_count: int32 [32], P('fsdp'), may hold values from 0 to 10, as said below
- index_global: int32 [197, 197], replicated, may hold values from 0 to 731, as said below
- index_local: int32 [37, 37], replicated, may hold values from 732 to 855, as said below
- ln1_gain: bfloat16 [768], P('fsdp'), may hold values from 0.5 to 1.5
- ln1_bias: bfloat16 [768], P('fsdp'), may hold values from -1 to 1
- qkv_weight: bfloat16 [768, 2304], P('fsdp'), may hold values from -0.21875 to 0.21875
- q_bias: bfloat16 [768], P('fsdp'), may hold values from -1.5 to 1.5
- v_bias: bfloat16 [768], P('fsdp'), may hold values from -1.5 to 1.5
- proj_weight: bfloat16 [768, 768], P('fsdp'), may hold values from -0.625 to 0.625
- proj_bias: bfloat16 [768], P('fsdp'), may hold values from -1 to 1
- gamma1: bfloat16 [768], P('fsdp'), may hold values from 0.29882812 to 1.5
- bias_table: bfloat16 [896, 12], P('fsdp'), may hold values from -3 to 3
- ln2_gain: bfloat16 [768], P('fsdp'), may hold values from 0.5 to 1.5
- ln2_bias: bfloat16 [768], P('fsdp'), may hold values from -1 to 1
- fc1_weight: bfloat16 [768, 3072], P('fsdp'), may hold values from -0.21875 to 0.21875
- fc1_bias: bfloat16 [3072], P('fsdp'), may hold values from -1.5 to 1.5
- fc2_weight: bfloat16 [3072, 768], P('fsdp'), may hold values from -0.109375 to 0.109375
- fc2_bias: bfloat16 [768], P('fsdp'), may hold values from -1 to 1
- gamma2: bfloat16 [768], P('fsdp'), may hold values from 0.29882812 to 1.5
Outputs:
- out_global: bfloat16 [128, 197, 768], P('fsdp')
- out_local: bfloat16 [320, 37, 768], P('fsdp')
- grad_x_global: bfloat16 [128, 197, 768], P('fsdp')
- grad_x_local: bfloat16 [320, 37, 768], P('fsdp')
- grad_ln1_gain: float32 [768], P('fsdp')
- grad_ln1_bias: float32 [768], P('fsdp')
- grad_qkv_weight: float32 [768, 2304], P('fsdp')
- grad_q_bias: float32 [768], P('fsdp')
- grad_v_bias: float32 [768], P('fsdp')
- grad_proj_weight: float32 [768, 768], P('fsdp')
- grad_proj_bias: float32 [768], P('fsdp')
- grad_gamma1: float32 [768], P('fsdp')
- grad_bias_table: float32 [896, 12], P('fsdp')
- grad_ln2_gain: float32 [768], P('fsdp')
- grad_ln2_bias: float32 [768], P('fsdp')
- grad_fc1_weight: float32 [768, 3072], P('fsdp')
- grad_fc1_bias: float32 [3072], P('fsdp')
- grad_fc2_weight: float32 [3072, 768], P('fsdp')
- grad_fc2_bias: float32 [768], P('fsdp')
- grad_gamma2: float32 [768], P('fsdp')
The draws below stay inside these ranges and needn't reach their ends.
Inputs may be any that keep to these rules, and one draw needn't show every extreme that they name: Each index of fsdp holds 4 global crop slots of which the first global_count are used; some index uses all of them. Each index of fsdp holds 10 local crop slots of which the first local_count are used; some index uses all of them. `index_global`: a relabeling of the relative position index of a 14 x 14 patch grid with a class token: entries of two patch pairs agree when their offsets agree, with rows of their own for class to patch, patch to class and class to class; every value of the range occurs. `index_local`: likewise for the 6 x 6 grid, in rows of the table after those of the global grid; every value of the range occurs.
All inputs are finite; a program needn't handle non-finite values.
Results may differ from the reference program's by a relative error of at most 0.012.
Values may be sent and summed in bfloat16 or wider, within the bound.
A program may use at most 192 MiB of HBM per device.

```python
import math
import jax
import jax.numpy as jnp
from jax import lax

D = 768
HEADS = 12
FF = 3072
GRID_G = 14
GRID_L = 6
TABLE_ROWS = 896
GLOB_SLOTS = 4
LOC_SLOTS = 10
SEQ_G = 197
SEQ_L = 37
GLOB_CROPS = 128
LOC_CROPS = 320
N_FSDP = 32


def used_slots(key, lowest, slots):
    pick_key, full_key = jax.random.split(key)
    counts = jax.random.randint(pick_key, (N_FSDP,), lowest, slots + 1)
    busiest = jax.random.randint(full_key, (), 0, N_FSDP)
    return jnp.where(jnp.arange(N_FSDP) == busiest, slots, counts).astype(jnp.int32)


def relative_index(key, grid, offset):
    cells = grid * grid
    span = 2 * grid - 1
    order = jnp.arange(cells, dtype=jnp.int32)
    row_of = order // grid
    col_of = order % grid
    offsets = (row_of[:, None] - row_of[None, :] + grid - 1) * span + (col_of[:, None] - col_of[None, :] + grid - 1)
    first = span * span
    filled = jnp.full((cells + 1, cells + 1), first + 2, jnp.int32)
    filled = filled.at[1:, 1:].set(offsets.astype(jnp.int32))
    filled = filled.at[0, 1:].set(first)
    filled = filled.at[1:, 0].set(first + 1)
    labels = jax.random.permutation(key, first + 3).astype(jnp.int32)
    return (labels[filled] + offset).astype(jnp.int32)


def draw_global_count(key, part):
    return used_slots(key, 1, GLOB_SLOTS)


def draw_local_count(key, part):
    return used_slots(key, 0, LOC_SLOTS)


def draw_index_global(key, part):
    return relative_index(key, GRID_G, 0)


def draw_index_local(key, part):
    return relative_index(key, GRID_L, (2 * GRID_G - 1) ** 2 + 3)


def steps_of(key, dims, cuts, smallest, top_value):
    gain, own = 1.0, jax.random.fold_in(key, 6)
    for position, shards_of in cuts:
        draws = jnp.exp(jax.random.uniform(jax.random.fold_in(own, position), (shards_of,), jnp.float32, smallest / len(cuts), top_value / len(cuts)))
        gain = gain * jnp.repeat(draws, dims[position] // shards_of).reshape([-1 if axis == position else 1 for axis in range(len(dims))])
    return gain


def centred(key, shape, width, reach, shards=(), kind=jnp.bfloat16):
    entries = width * jax.random.normal(key, shape, jnp.float32)
    if shards:
        entries = entries * steps_of(key, shape, shards, -0.22, 0.18)
    return jnp.clip(entries, -reach, reach).astype(kind)


def setup_inputs(seed: int = 0) -> dict:
    arg_keys = jax.random.split(jax.random.key(seed), 25)
    return {
        "x_global": centred(arg_keys[0], (GLOB_CROPS, SEQ_G, D), 1.0, 6.0, ((0, 32),)),
        "x_local": centred(arg_keys[1], (LOC_CROPS, SEQ_L, D), 1.0, 6.0, ((0, 32),)),
        "cot_global": centred(arg_keys[2], (GLOB_CROPS, SEQ_G, D), 1.0, 6.0, ((0, 32),)),
        "cot_local": centred(arg_keys[3], (LOC_CROPS, SEQ_L, D), 1.0, 6.0, ((0, 32),)),
        "global_count": draw_global_count(jax.random.fold_in(arg_keys[24], 71), 0),
        "local_count": draw_local_count(jax.random.fold_in(arg_keys[24], 71), 0),
        "index_global": draw_index_global(jax.random.fold_in(arg_keys[24], 71), 0),
        "index_local": draw_index_local(jax.random.fold_in(arg_keys[24], 71), 0),
        "ln1_gain": jnp.clip(1.0 + 0.1 * jax.random.normal(arg_keys[8], (D,), jnp.float32), 0.5, 1.5).astype(jnp.bfloat16),
        "ln1_bias": centred(arg_keys[9], (D,), 0.2, 1.0, ((0, 32),)),
        "qkv_weight": centred(arg_keys[10], (D, 3 * D), D ** -0.5, 0.21875, ((0, 32),)),
        "q_bias": centred(arg_keys[11], (D,), 0.3, 1.5, ((0, 32),)),
        "v_bias": centred(arg_keys[12], (D,), 0.3, 1.5, ((0, 32),)),
        "proj_weight": centred(arg_keys[13], (D, D), (D // 8) ** -0.5, 0.625, ((0, 32),)),
        "proj_bias": centred(arg_keys[14], (D,), 0.2, 1.0, ((0, 32),)),
        "gamma1": jnp.clip(jnp.exp(math.log(1.5) - 1.6133518 * jax.random.uniform(arg_keys[15], (D,), jnp.float32) ** steps_of(arg_keys[15], (D,), ((0, 32),), -0.2, 0.2)), 0.29882812, 1.5).astype(jnp.bfloat16),
        "bias_table": centred(arg_keys[16], (TABLE_ROWS, HEADS), 0.5, 3.0, ((0, 32),)),
        "ln2_gain": jnp.clip(1.0 + 0.1 * jax.random.normal(arg_keys[17], (D,), jnp.float32), 0.5, 1.5).astype(jnp.bfloat16),
        "ln2_bias": centred(arg_keys[18], (D,), 0.2, 1.0, ((0, 32),)),
        "fc1_weight": centred(arg_keys[19], (D, FF), D ** -0.5, 0.21875, ((0, 32),)),
        "fc1_bias": centred(arg_keys[20], (FF,), 0.3, 1.5, ((0, 32),)),
        "fc2_weight": centred(arg_keys[21], (FF, D), FF ** -0.5, 0.109375, ((0, 32),)),
        "fc2_bias": centred(arg_keys[22], (D,), 0.2, 1.0, ((0, 32),)),
        "gamma2": jnp.clip(jnp.exp(math.log(1.5) - 1.6133518 * jax.random.uniform(arg_keys[23], (D,), jnp.float32) ** steps_of(arg_keys[23], (D,), ((0, 32),), -0.2, 0.2)), 0.29882812, 1.5).astype(jnp.bfloat16),
    }


EPSILON = 1e-06
HIGHEST = lax.Precision.HIGHEST

@jax.custom_vjp
def low(v):
    return lax.optimization_barrier(v.astype(jnp.bfloat16)).astype(jnp.float32)

@jax.custom_vjp
def low_back(v):
    return v

def low_keep(v):
    return (low(v), None)

def low_pass(kept, grad):
    return (grad,)

def back_keep(v):
    return (v, None)

def back_low(kept, grad):
    return (low(grad),)
low.defvjp(low_keep, low_pass)
low_back.defvjp(back_keep, back_low)

def layer_norm(values, norm_gain, norm_shift):
    average = lax.optimization_barrier(jnp.mean(values, axis=-1, keepdims=True))
    centered = values - average
    variance = lax.optimization_barrier(jnp.mean(centered * centered, axis=-1, keepdims=True))
    return centered * lax.rsqrt(variance + EPSILON) * norm_gain + norm_shift

def project(values, weight):
    return jnp.einsum('csd,de->cse', values, weight, precision=HIGHEST)

def attend(qkv_rows, position_bias):
    crop_count, length, triple = qkv_rows.shape
    features = triple // 3
    head_count = position_bias.shape[0]
    per_head = features // head_count
    pieces = qkv_rows.reshape(crop_count, length, 3, head_count, per_head)
    scores = jnp.einsum('cqhe,ckhe->chqk', pieces[:, :, 0], pieces[:, :, 1], precision=HIGHEST)
    scores = low_back(scores * per_head ** (-0.5) + position_bias[None])
    weights = low(jax.nn.softmax(scores, axis=-1))
    mixed_rows = jnp.einsum('chqk,ckhe->cqhe', weights, pieces[:, :, 2], precision=HIGHEST)
    return low(low_back(mixed_rows.reshape(crop_count, length, features)))

def branch_pair(params, inputs, index_rows):
    ln1_gain, ln1_bias, qkv_weight, q_bias, v_bias, proj_weight, proj_bias, gamma1, bias_table, ln2_gain, ln2_bias, fc1_weight, fc1_bias, fc2_weight, fc2_bias, gamma2 = params
    position_bias = jnp.transpose(bias_table[index_rows], (2, 0, 1))
    normed = low(layer_norm(inputs, ln1_gain, ln1_bias))
    zero_part = jnp.zeros_like(q_bias)
    qkv_rows = low(low_back(project(normed, qkv_weight) + jnp.concatenate([q_bias, zero_part, v_bias])))
    attn_out = low_back(project(attend(qkv_rows, position_bias), proj_weight) + proj_bias)
    residual = inputs + gamma1 * attn_out
    normed_two = low(layer_norm(residual, ln2_gain, ln2_bias))
    hidden = low_back(project(normed_two, fc1_weight) + fc1_bias)
    active = low(jax.nn.gelu(hidden, approximate=False))
    branch = low_back(project(active, fc2_weight) + fc2_bias)
    return residual + gamma2 * branch

def reference(x_global, x_local, cot_global, cot_local, global_count, local_count, index_global, index_local, ln1_gain, ln1_bias, qkv_weight, q_bias, v_bias, proj_weight, proj_bias, gamma1, bias_table, ln2_gain, ln2_bias, fc1_weight, fc1_bias, fc2_weight, fc2_bias, gamma2):
    params = tuple((weight.astype(jnp.float32) for weight in (ln1_gain, ln1_bias, qkv_weight, q_bias, v_bias, proj_weight, proj_bias, gamma1, bias_table, ln2_gain, ln2_bias, fc1_weight, fc1_bias, fc2_weight, fc2_bias, gamma2)))
    glob_mask = (jnp.arange(GLOB_SLOTS, dtype=jnp.int32)[None, :] < global_count[:, None]).astype(jnp.float32)
    loc_mask = (jnp.arange(LOC_SLOTS, dtype=jnp.int32)[None, :] < local_count[:, None]).astype(jnp.float32)
    glob_in = x_global.astype(jnp.float32).reshape(N_FSDP, GLOB_SLOTS, SEQ_G, D)
    loc_in = x_local.astype(jnp.float32).reshape(N_FSDP, LOC_SLOTS, SEQ_L, D)
    glob_cot = cot_global.astype(jnp.float32).reshape(N_FSDP, GLOB_SLOTS, SEQ_G, D) * glob_mask[:, :, None, None]
    loc_cot = cot_local.astype(jnp.float32).reshape(N_FSDP, LOC_SLOTS, SEQ_L, D) * loc_mask[:, :, None, None]

    def device_step(summed, device_item):
        glob_rows, loc_rows, glob_back, loc_back, glob_keep, loc_keep = device_item

        def layer_run(weights_in, glob_part, loc_part):
            return (branch_pair(weights_in, glob_part, index_global), branch_pair(weights_in, loc_part, index_local))
        (glob_out, loc_out), pullback = jax.vjp(layer_run, params, glob_rows, loc_rows)
        grad_params, grad_glob, grad_loc = pullback((glob_back, loc_back))
        summed = jax.tree.map(jnp.add, summed, grad_params)
        glob_out = (glob_out * glob_keep[:, None, None]).astype(jnp.bfloat16)
        loc_out = (loc_out * loc_keep[:, None, None]).astype(jnp.bfloat16)
        return (summed, (glob_out, loc_out, grad_glob.astype(jnp.bfloat16), grad_loc.astype(jnp.bfloat16)))
    initial = tuple((jnp.zeros_like(weight) for weight in params))
    summed, (glob_out, loc_out, grad_glob, grad_loc) = lax.scan(device_step, initial, (glob_in, loc_in, glob_cot, loc_cot, glob_mask, loc_mask))
    return (glob_out.reshape(N_FSDP * GLOB_SLOTS, SEQ_G, D), loc_out.reshape(N_FSDP * LOC_SLOTS, SEQ_L, D), grad_glob.reshape(N_FSDP * GLOB_SLOTS, SEQ_G, D), grad_loc.reshape(N_FSDP * LOC_SLOTS, SEQ_L, D), summed[0], summed[1], summed[2], summed[3], summed[4], summed[5], summed[6], summed[7], summed[8], summed[9], summed[10], summed[11], summed[12], summed[13], summed[14], summed[15])
```

```python
import functools
import jax
import jax.numpy as jnp
from jax import lax
from jax.experimental import pallas as pl
from jax.experimental.pallas import tpu as pltpu
from jax.sharding import PartitionSpec as P


MESH = pl.DeviceIdType.MESH
LINE = 4
GRID = (LINE, 2, 2, 2)


def place():
    me = lax.axis_index("fsdp")
    return (me // 8, (me // 4) % 2, (me // 2) % 2, me % 2)


def device_at(z, y, x, c):
    return (((z * 2 + y) * 2 + x) * 2 + c,)


def greet():
    z, y, x, c = place()
    barrier = pltpu.get_barrier_semaphore()
    for peer in (device_at(z, y, x, 1 - c), device_at(z, y, 1 - x, c), device_at(z, 1 - y, x, c)):
        pl.semaphore_signal(barrier, inc=1, device_id=peer, device_id_type=MESH)

    @pl.when(z > 0)
    def _():
        pl.semaphore_signal(barrier, inc=1, device_id=device_at(z - 1, y, x, c), device_id_type=MESH)

    @pl.when(z < LINE - 1)
    def _():
        pl.semaphore_signal(barrier, inc=1, device_id=device_at(z + 1, y, x, c), device_id_type=MESH)

    @pl.when((z > 0) & (z < LINE - 1))
    def _():
        pl.semaphore_wait(barrier, 5)

    @pl.when((z == 0) | (z == LINE - 1))
    def _():
        pl.semaphore_wait(barrier, 4)


def remote(src, dst, send, recv, peer):
    return pltpu.make_async_remote_copy(
        src_ref=src, dst_ref=dst, send_sem=send, recv_sem=recv, device_id=peer, device_id_type=MESH
    )


class Gather:
    STAGES = 7
    SEMS = 16

    def __init__(self, own, full, send, recv, local):
        self.own, self.full, self.send, self.recv, self.local = own, full, send, recv, local
        self.z, self.y, self.x, self.c = place()
        cols = own.shape[-1] // 2
        self.halves = (pl.ds(0, cols), pl.ds(cols, cols))

    def line_copy(self, step, up):
        z, y, x, c = self.z, self.y, self.x, self.c
        held = z - step if up else z + step
        slot = self.full.at[held, y, x, c]
        src = self.own if step == 0 else slot
        peer = device_at(z + 1 if up else z - 1, y, x, c)
        k = step if up else 3 + step
        return remote(src, slot, self.send.at[k], self.recv.at[k], peer)

    def line_send(self, step):
        z = self.z

        @pl.when((z - step >= 0) & (z < LINE - 1))
        def _():
            self.line_copy(step, True).start()

        @pl.when((z + step <= LINE - 1) & (z > 0))
        def _():
            self.line_copy(step, False).start()

    def line_wait(self, step):
        z = self.z

        @pl.when(z - step >= 1)
        def _():
            self.line_copy(step, True).wait_recv()

        @pl.when(z + step <= LINE - 2)
        def _():
            self.line_copy(step, False).wait_recv()

    def cross(self, k, part, half, flip_y):
        z, y, x, c = self.z, self.y, self.x, self.c
        peer = device_at(z, 1 - y, x, c) if flip_y else device_at(z, y, 1 - x, c)
        ref = self.full.at[part + (slice(None), self.halves[half])]
        return remote(ref, ref, self.send.at[k], self.recv.at[k], peer)

    def pair(self, k, part, half=None):
        z, y, x, c = self.z, self.y, self.x, self.c
        ref = self.full.at[part]
        if half is not None:
            ref = self.full.at[part + (slice(None), self.halves[half])]
        return remote(ref, ref, self.send.at[k], self.recv.at[k], device_at(z, y, x, 1 - c))

    def copy(self, name):
        y, x, c = self.y, self.x, self.c
        every = slice(None)
        return {
            "xa": lambda: self.cross(6, (every, y, x, c), 0, False),
            "yb": lambda: self.cross(7, (every, y, x, c), 1, True),
            "ya": lambda: self.cross(8, (every, y, every, c), 0, True),
            "xb": lambda: self.cross(9, (every, every, x, c), 1, False),
            "c0": lambda: self.pair(10, (every, y, x, c)),
            "c1": lambda: self.pair(11, (every, y, 1 - x, c), 0),
            "c2": lambda: self.pair(12, (every, 1 - y, x, c), 1),
            "c3": lambda: self.pair(13, (every, 1 - y, every, c), 0),
            "c4": lambda: self.pair(14, (every, every, 1 - x, c), 1),
        }[name]()

    def stage(self, s):
        z, y, x, c = self.z, self.y, self.x, self.c
        mine = lambda: pltpu.make_async_copy(self.own, self.full.at[z, y, x, c], self.local)
        if s == 0:
            mine().start()
            self.line_send(0)
        elif s <= 3:
            self.line_wait(s - 1)
            if s < 3:
                self.line_send(s)
            else:
                mine().wait()
                for name in ("xa", "yb", "c0"):
                    self.copy(name).start()
        elif s == 4:
            self.copy("xa").wait_recv()
            self.copy("ya").start()
            self.copy("yb").wait_recv()
            self.copy("xb").start()
            self.copy("c1").start()
            self.copy("c2").start()
        elif s == 5:
            self.copy("ya").wait_recv()
            self.copy("c3").start()
            self.copy("xb").wait_recv()
            self.copy("c4").start()
        else:
            for name in ("c0", "c1", "c2", "c3", "c4"):
                self.copy(name).wait_recv()

    def drain(self):
        z = self.z
        for step in range(LINE - 1):
            @pl.when((z - step >= 0) & (z < LINE - 1))
            def _():
                self.line_copy(step, True).wait_send()

            @pl.when((z + step <= LINE - 1) & (z > 0))
            def _():
                self.line_copy(step, False).wait_send()

        for name in ("xa", "yb", "ya", "xb", "c0", "c1", "c2", "c3", "c4"):
            self.copy(name).wait_send()


def wavefront(count, stages, lag):
    order = [(s + lag * t, t, s) for t in range(count) for s in range(stages)]
    return [(t, s) for _, t, s in sorted(order)]


GATHER_LAG = 1.5


def gather_kernel(count, *refs):
    own, full = refs[:count], refs[count : 2 * count]
    send, recv, local = refs[2 * count :]
    greet()
    flows = [Gather(own[t], full[t], send.at[t], recv.at[t], local.at[t]) for t in range(count)]
    for t, s in wavefront(count, Gather.STAGES, GATHER_LAG):
        flows[t].stage(s)
    for flow in flows:
        flow.drain()


def gather_all(shards):
    count = len(shards)
    return pl.pallas_call(
        functools.partial(gather_kernel, count),
        out_shape=[jax.ShapeDtypeStruct(GRID + s.shape, s.dtype) for s in shards],
        in_specs=[pl.BlockSpec(memory_space=pltpu.VMEM)] * count,
        out_specs=[pl.BlockSpec(memory_space=pl.ANY)] * count,
        scratch_shapes=[
            pltpu.SemaphoreType.DMA((count, Gather.SEMS)),
            pltpu.SemaphoreType.DMA((count, Gather.SEMS)),
            pltpu.SemaphoreType.DMA((count,)),
        ],
        compiler_params=pltpu.CompilerParams(collective_id=0, has_side_effects=True),
        name="gather_all",
    )(*shards)


class Scatter:
    STAGES = 8
    SEMS = 16

    def __init__(self, terms, out, bufs, send, recv, local):
        self.terms, self.out = terms, out
        self.own, self.pairbuf, self.buf1a, self.buf1b, self.buf2a, self.buf2b, self.up, self.down = bufs
        self.send, self.recv, self.local = send, recv, local
        self.z, self.y, self.x, self.c = place()
        cols = terms.shape[-1] // 2
        self.halves = (pl.ds(0, cols), pl.ds(cols, cols))

    @staticmethod
    def scratch(shape, dtype):
        rows, cols = shape
        half = cols // 2
        return [
            pltpu.VMEM((LINE, 2, 2, rows, cols), dtype),
            pltpu.VMEM((LINE, 2, 2, rows, cols), dtype),
            pltpu.VMEM((LINE, 2, rows, half), dtype),
            pltpu.VMEM((LINE, 2, rows, half), dtype),
            pltpu.VMEM((LINE, rows, half), dtype),
            pltpu.VMEM((LINE, rows, half), dtype),
            pltpu.VMEM((LINE, rows, cols), dtype),
            pltpu.VMEM((LINE, rows, cols), dtype),
        ]

    def load(self):
        every = slice(None)
        return pltpu.make_async_copy(self.terms.at[every, every, every, self.c], self.own, self.local)

    def copy(self, name):
        z, y, x, c = self.z, self.y, self.x, self.c
        every = slice(None)
        a, b = self.halves
        over_y, over_x = device_at(z, 1 - y, x, c), device_at(z, y, 1 - x, c)
        sem = lambda k: (self.send.at[k], self.recv.at[k])
        return {
            "pair": lambda: remote(self.terms.at[every, every, every, 1 - c], self.pairbuf, *sem(0), device_at(z, y, x, 1 - c)),
            "1a": lambda: remote(self.own.at[every, 1 - y, every, every, a], self.buf1a, *sem(1), over_y),
            "1b": lambda: remote(self.own.at[every, every, 1 - x, every, b], self.buf1b, *sem(2), over_x),
            "2a": lambda: remote(self.own.at[every, y, 1 - x, every, a], self.buf2a, *sem(3), over_x),
            "2b": lambda: remote(self.own.at[every, 1 - y, x, every, b], self.buf2b, *sem(4), over_y),
        }[name]()

    def line_copy(self, target, up):
        z, y, x, c = self.z, self.y, self.x, self.c
        buf = self.up if up else self.down
        k = 5 + target if up else 9 + target
        peer = device_at(z + 1 if up else z - 1, y, x, c)
        return remote(self.own.at[target, y, x], buf.at[target], self.send.at[k], self.recv.at[k], peer)

    def stage(self, s):
        z, y, x, c = self.z, self.y, self.x, self.c
        own = self.own
        a, b = self.halves
        if s == 0:
            self.load().start()
            self.copy("pair").start()
        elif s == 1:
            self.load().wait()
            self.copy("pair").wait_recv()

            @pl.loop(0, LINE)
            def _(i):
                for j in range(2):
                    for k in range(2):
                        own[i, j, k] = own[i, j, k] + self.pairbuf[i, j, k]

            self.copy("1a").start()
            self.copy("1b").start()
        elif s == 2:
            self.copy("1a").wait_recv()
            self.copy("1b").wait_recv()

            @pl.loop(0, LINE)
            def _(i):
                for k in range(2):
                    own[i, y, k, :, a] = own[i, y, k, :, a] + self.buf1a[i, k]
                    own[i, k, x, :, b] = own[i, k, x, :, b] + self.buf1b[i, k]

            self.copy("2a").start()
            self.copy("2b").start()
        elif s == 3:
            self.copy("2a").wait_recv()
            self.copy("2b").wait_recv()

            @pl.loop(0, LINE)
            def _(i):
                own[i, y, x, :, a] = own[i, y, x, :, a] + self.buf2a[i]
                own[i, y, x, :, b] = own[i, y, x, :, b] + self.buf2b[i]

        elif s <= 6:
            for target, up in ((LINE - 1 - (s - 4), True), (s - 4, False)):
                @pl.when((z < target) if up else (z > target))
                def _():
                    @pl.when((z > 0) if up else (z < LINE - 1))
                    def _():
                        self.line_copy(target, up).wait_recv()
                        buf = self.up if up else self.down
                        own[target, y, x] = own[target, y, x] + buf[target]

                    self.line_copy(target, up).start()

        else:
            for target in range(LINE):
                @pl.when((z == target) & (z > 0))
                def _():
                    self.line_copy(target, True).wait_recv()

                @pl.when((z == target) & (z < LINE - 1))
                def _():
                    self.line_copy(target, False).wait_recv()

            self.out[...] = own[z, y, x].astype(jnp.float32)

            @pl.when(z > 0)
            def _():
                self.out[...] = self.out[...] + self.up[z].astype(jnp.float32)

            @pl.when(z < LINE - 1)
            def _():
                self.out[...] = self.out[...] + self.down[z].astype(jnp.float32)

    def drain(self):
        z = self.z
        for name in ("pair", "1a", "1b", "2a", "2b"):
            self.copy(name).wait_send()
        for target in range(LINE):
            @pl.when(z < target)
            def _():
                self.line_copy(target, True).wait_send()

            @pl.when(z > target)
            def _():
                self.line_copy(target, False).wait_send()


SCATTER_LAG = 1.5


def scatter_kernel(count, *refs):
    terms, outs = refs[:count], refs[count : 2 * count]
    bufs = refs[2 * count : 10 * count]
    send, recv, local = refs[10 * count :]
    greet()
    flows = [
        Scatter(terms[t], outs[t], bufs[8 * t : 8 * t + 8], send.at[t], recv.at[t], local.at[t]) for t in range(count)
    ]
    for t, s in wavefront(count, Scatter.STAGES, SCATTER_LAG):
        flows[t].stage(s)
    for flow in flows:
        flow.drain()


def scatter_all(terms):
    count = len(terms)
    shapes = [t.shape[4:] for t in terms]
    scratch = []
    for t, s in zip(terms, shapes):
        scratch += Scatter.scratch(s, t.dtype)
    return pl.pallas_call(
        functools.partial(scatter_kernel, count),
        out_shape=[jax.ShapeDtypeStruct(s, jnp.float32) for s in shapes],
        in_specs=[pl.BlockSpec(memory_space=pl.ANY)] * count,
        out_specs=[pl.BlockSpec(memory_space=pltpu.VMEM)] * count,
        scratch_shapes=scratch
        + [
            pltpu.SemaphoreType.DMA((count, Scatter.SEMS)),
            pltpu.SemaphoreType.DMA((count, Scatter.SEMS)),
            pltpu.SemaphoreType.DMA((count,)),
        ],
        compiler_params=pltpu.CompilerParams(
            collective_id=1, has_side_effects=True, vmem_limit_bytes=56 * 1024 * 1024
        ),
        name="scatter_all",
    )(*terms)


PACK_ROWS, PACK_LANES = 16, 128


def pack_small(vectors, hidden_shift, table):
    lanes = lambda v: jnp.pad(v.astype(jnp.float32), ((0, 0), (0, PACK_LANES - v.shape[1])))
    rows = jnp.concatenate([lanes(jnp.stack(vectors)), lanes(hidden_shift[None]), lanes(table.reshape(3, -1))])
    rows = jnp.pad(rows, ((0, PACK_ROWS - rows.shape[0]), (0, 0)))
    return jnp.concatenate([rows[:8], rows[8:]], axis=1)


def unpack_small(block, count, hidden, table_shape):
    rows = jnp.concatenate([block[:, :, :PACK_LANES], block[:, :, PACK_LANES:]], axis=1)
    devices = rows.shape[0]
    vectors = jnp.transpose(rows[:, :10, :count], (1, 0, 2)).reshape(10, devices * count)
    table = rows[:, 11:14, : table_shape[0] * table_shape[1] // 3].reshape(devices * table_shape[0], table_shape[1])
    return (vectors, rows[:, 10, :hidden].reshape(devices * hidden), table)


def gather_params(devices, vectors, hidden_shift, table, weights):
    if devices != 32:
        whole = lambda v: lax.all_gather(v, "fsdp", axis=0, tiled=True)
        return (
            [as_float(whole(v)) for v in vectors], as_float(whole(hidden_shift)), as_float(whole(table)),
            [whole(w) for w in weights],
        )
    small, *full = gather_all([pack_small(vectors, hidden_shift, table)] + list(weights))
    stacked, hidden_full, table_full = unpack_small(
        small.reshape((devices,) + small.shape[4:]), vectors[0].shape[0], hidden_shift.shape[0], table.shape
    )
    full = [f.reshape((devices * f.shape[4], f.shape[5])) for f in full]
    return ([stacked[k] for k in range(10)], hidden_full, table_full, full)


def scatter_grads(devices, vectors, hidden_shift, table, weights):
    if devices != 32:
        share = lambda v: lax.psum_scatter(as_float(v), "fsdp", scatter_dimension=0, tiled=True)
        return ([share(v) for v in vectors], share(hidden_shift), share(table), [share(w) for w in weights])
    rows = jnp.transpose(jnp.stack(vectors).reshape(10, devices, -1), (1, 0, 2))
    lanes = lambda v: jnp.pad(v, ((0, 0), (0, 0), (0, PACK_LANES - v.shape[2])))
    rows = jnp.concatenate(
        [lanes(rows), lanes(hidden_shift.reshape(devices, 1, -1)), lanes(table.reshape(devices, 3, -1))], axis=1
    )
    rows = jnp.pad(rows, ((0, 0), (0, PACK_ROWS - rows.shape[1]), (0, 0)))
    block = jnp.concatenate([rows[:, :8], rows[:, 8:]], axis=2)
    terms = [block.reshape(GRID + block.shape[1:])] + [
        w.astype(jnp.bfloat16).reshape(GRID + (w.shape[0] // devices, w.shape[1])) for w in weights
    ]
    small, *shares = scatter_all(terms)
    sums, hidden_sum, table_sum = unpack_small(
        small[None], vectors[0].shape[0] // devices, hidden_shift.shape[0] // devices,
        (table.shape[0] // devices, table.shape[1]),
    )
    return ([sums[k] for k in range(10)], hidden_sum, table_sum, shares)

EPSILON = 1e-06
CONTRACT_ROWS = (((0,), (0,)), ((), ()))
CONTRACT_COLS = (((1,), (1,)), ((), ()))


def layer_norm(values, norm_gain, norm_shift):
    average = jnp.mean(values, axis=-1, keepdims=True)
    centered = values - average
    variance = jnp.mean(centered * centered, axis=-1, keepdims=True)
    return centered * lax.rsqrt(variance + EPSILON) * norm_gain + norm_shift


def gelu_exact(values):
    return jax.nn.gelu(values, approximate=False)


def as_float(values):
    return values.astype(jnp.float32)


def table_blocking(table_count):
    block_rows = 128
    first_rows = jnp.arange(table_count // block_rows, dtype=jnp.int32) * block_rows
    return (block_rows, first_rows)


def table_bias(index_rows, table_low):
    length = index_rows.shape[0]
    table_count, head_count = table_low.shape
    block_rows, first_rows = table_blocking(table_count)
    flat_index = index_rows.reshape(-1)
    table_blocks = table_low.reshape(table_count // block_rows, block_rows, head_count)

    def add_block(summed, scan_item):
        first_row, table_piece = scan_item
        table_ids = first_row + jnp.arange(block_rows, dtype=jnp.int32)
        picker = (flat_index[:, None] == table_ids[None, :]).astype(jnp.bfloat16)
        return (summed + jnp.dot(picker, table_piece, preferred_element_type=jnp.float32), None)

    initial = jnp.zeros((flat_index.shape[0], head_count), jnp.float32)
    summed, unused = lax.scan(add_block, initial, (first_rows, table_blocks))
    return jnp.transpose(summed.reshape(length, length, head_count), (2, 0, 1))


def table_grad(index_rows, grad_scores, table_count):
    crop_count, head_count = (grad_scores.shape[0], grad_scores.shape[1])
    block_rows, first_rows = table_blocking(table_count)
    flat_index = index_rows.reshape(-1)
    grad_flat = grad_scores.reshape(crop_count, head_count, -1)

    def one_block(first_row):
        table_ids = first_row + jnp.arange(block_rows, dtype=jnp.int32)
        picker = (flat_index[:, None] == table_ids[None, :]).astype(jnp.bfloat16)
        return jnp.einsum("chn,nr->rh", grad_flat, picker, preferred_element_type=jnp.float32)

    return lax.map(one_block, first_rows).reshape(table_count, head_count)


def split_heads(qkv_low, head_count):
    crop_count, length, triple = qkv_low.shape
    per_head = triple // (3 * head_count)
    pieces = qkv_low.reshape(crop_count, length, 3, head_count, per_head)
    return (pieces[:, :, 0], pieces[:, :, 1], pieces[:, :, 2], per_head ** (-0.5))


def attend_scores(queries, keyset, factor, position_bias):
    scores = jnp.einsum("cqhe,ckhe->chqk", queries, keyset, preferred_element_type=jnp.float32)
    return scores * factor + position_bias[None]


def attend_forward(qkv_low, position_bias):
    queries, keyset, valueset, factor = split_heads(qkv_low, position_bias.shape[0])
    scores = attend_scores(queries, keyset, factor, position_bias)
    highest_score = jnp.max(scores, axis=-1, keepdims=True)
    log_total = (
        jnp.log(jnp.sum(jnp.exp(scores - highest_score), axis=-1, keepdims=True)) + highest_score
    )
    weights = jnp.exp(scores - log_total).astype(jnp.bfloat16)
    mixed_rows = jnp.einsum(
        "chqk,ckhe->cqhe", weights, valueset, preferred_element_type=jnp.float32
    )
    crop_count, length = (qkv_low.shape[0], qkv_low.shape[1])
    return (mixed_rows.reshape(crop_count * length, -1).astype(jnp.bfloat16), log_total)


def attend_backward(qkv_low, position_bias, log_total, grad_mixed):
    queries, keyset, valueset, factor = split_heads(qkv_low, position_bias.shape[0])
    crop_count, length, triple = qkv_low.shape
    grad_heads = grad_mixed.reshape(queries.shape)
    scores = attend_scores(queries, keyset, factor, position_bias)
    weights = jnp.exp(scores - log_total)
    grad_values = jnp.einsum(
        "chqk,cqhe->ckhe",
        weights.astype(jnp.bfloat16),
        grad_heads,
        preferred_element_type=jnp.float32,
    )
    grad_weights = jnp.einsum(
        "cqhe,ckhe->chqk", grad_heads, valueset, preferred_element_type=jnp.float32
    )
    inner_sum = jnp.sum(grad_weights * weights, axis=-1, keepdims=True)
    grad_scores = (weights * (grad_weights - inner_sum)).astype(jnp.bfloat16)
    grad_queries = (
        jnp.einsum("chqk,ckhe->cqhe", grad_scores, keyset, preferred_element_type=jnp.float32)
        * factor
    )
    grad_keys = (
        jnp.einsum("chqk,cqhe->ckhe", grad_scores, queries, preferred_element_type=jnp.float32)
        * factor
    )
    grad_qkv = jnp.stack([grad_queries, grad_keys, grad_values], axis=2).astype(jnp.bfloat16)
    return (grad_qkv.reshape(crop_count * length, triple), grad_scores)


def make_qkv(normed_low, qkv_full, qbias_full, vbias_full):
    query_shift = as_float(qbias_full)
    shift_row = jnp.concatenate([query_shift, jnp.zeros_like(query_shift), as_float(vbias_full)])
    return (jnp.dot(normed_low, qkv_full, preferred_element_type=jnp.float32) + shift_row).astype(
        jnp.bfloat16
    )


def mlp_forward(residual, mlp_parts):
    norm_gain, norm_shift, fc1_full, fc1_shift, fc2_full, fc2_shift, scale_two = mlp_parts
    normed_two, norm_pull = jax.vjp(layer_norm, residual, as_float(norm_gain), as_float(norm_shift))
    normed_low = normed_two.astype(jnp.bfloat16)
    hidden = jnp.dot(normed_low, fc1_full, preferred_element_type=jnp.float32) + as_float(fc1_shift)
    active, gelu_pull = jax.vjp(gelu_exact, hidden)
    active_low = active.astype(jnp.bfloat16)
    branch = jnp.dot(active_low, fc2_full, preferred_element_type=jnp.float32) + as_float(fc2_shift)
    return (normed_low, norm_pull, active_low, gelu_pull, branch)


def per_device(
    x_global,
    x_local,
    cot_global,
    cot_local,
    global_count,
    local_count,
    index_global,
    index_local,
    ln1_gain,
    ln1_bias,
    qkv_weight,
    q_bias,
    v_bias,
    proj_weight,
    proj_bias,
    gamma1,
    bias_table,
    ln2_gain,
    ln2_bias,
    fc1_weight,
    fc1_bias,
    fc2_weight,
    fc2_bias,
    gamma2,
):
    glob_slots, glob_len, features = x_global.shape
    loc_slots, loc_len = (x_local.shape[0], x_local.shape[1])
    glob_rows = glob_slots * glob_len
    devices = lax.axis_size("fsdp")
    small_full, hidden_full, table_full, weights_full = gather_params(
        devices,
        [ln1_gain, ln1_bias, q_bias, v_bias, proj_bias, gamma1, ln2_gain, ln2_bias, fc2_bias, gamma2],
        fc1_bias,
        bias_table,
        [qkv_weight, proj_weight, fc1_weight, fc2_weight],
    )
    (
        norm1_gain, norm1_shift, qbias_full, vbias_full, pbias_full, scale1_full, norm2_gain, norm2_shift,
        fc2_shift_full, scale2_full,
    ) = small_full
    qkv_full, proj_full, fc1_full, fc2_full = weights_full
    table_full = table_full.astype(jnp.bfloat16)
    mlp_full = (norm2_gain, norm2_shift, fc1_full, hidden_full, fc2_full, fc2_shift_full, scale2_full)
    glob_keep = (jnp.arange(glob_slots, dtype=jnp.int32) < global_count[0]).astype(jnp.float32)
    loc_keep = (jnp.arange(loc_slots, dtype=jnp.int32) < local_count[0]).astype(jnp.float32)
    row_keep = jnp.concatenate([jnp.repeat(glob_keep, glob_len), jnp.repeat(loc_keep, loc_len)])[
        :, None
    ]
    inputs = jnp.concatenate(
        [x_global.reshape(glob_rows, features), x_local.reshape(-1, features)]
    ).astype(jnp.float32)
    bias_glob = table_bias(index_global, table_full)
    bias_loc = table_bias(index_local, table_full)
    normed_low = layer_norm(inputs, as_float(norm1_gain), as_float(norm1_shift)).astype(
        jnp.bfloat16
    )
    qkv_low = make_qkv(normed_low, qkv_full, qbias_full, vbias_full)
    mixed_glob, lse_glob = attend_forward(
        qkv_low[:glob_rows].reshape(glob_slots, glob_len, -1), bias_glob
    )
    mixed_loc, lse_loc = attend_forward(
        qkv_low[glob_rows:].reshape(loc_slots, loc_len, -1), bias_loc
    )
    mixed_low = jnp.concatenate([mixed_glob, mixed_loc])
    attn_out = jnp.dot(mixed_low, proj_full, preferred_element_type=jnp.float32) + as_float(
        pbias_full
    )
    residual = inputs + as_float(scale1_full) * attn_out
    normed_unused, pull_unused, active_unused, gelu_unused, branch = mlp_forward(residual, mlp_full)
    outputs = ((residual + as_float(mlp_full[6]) * branch) * row_keep).astype(jnp.bfloat16)
    grad_out = (
        jnp.concatenate(
            [cot_global.reshape(glob_rows, features), cot_local.reshape(-1, features)]
        ).astype(jnp.float32)
        * row_keep
    )
    mlp_back = mlp_full
    normed_again, norm_again_pull, active_again, gelu_pull, branch_again = mlp_forward(
        residual, mlp_back
    )
    grad_scale_two = jnp.sum(grad_out * branch_again, axis=0)
    grad_branch = (as_float(mlp_back[6]) * grad_out).astype(jnp.bfloat16)
    grad_fc2_shift = jnp.sum(grad_branch, axis=0, dtype=jnp.float32)
    grad_fc2_full = lax.dot_general(
        active_again, grad_branch, CONTRACT_ROWS, preferred_element_type=jnp.float32
    )
    grad_active = lax.dot_general(
        grad_branch, mlp_back[4], CONTRACT_COLS, preferred_element_type=jnp.float32
    )
    grad_hidden = gelu_pull(grad_active)[0].astype(jnp.bfloat16)
    grad_fc1_shift = jnp.sum(grad_hidden, axis=0, dtype=jnp.float32)
    grad_fc1_full = lax.dot_general(
        normed_again, grad_hidden, CONTRACT_ROWS, preferred_element_type=jnp.float32
    )
    grad_normed_two = lax.dot_general(
        grad_hidden, mlp_back[2], CONTRACT_COLS, preferred_element_type=jnp.float32
    )
    grad_through_two, grad_norm2_gain, grad_norm2_shift = norm_again_pull(grad_normed_two)
    grad_residual = grad_out + grad_through_two
    back_gain, back_shift, back_qkv, back_qbias, back_vbias, back_proj, back_scale = (
        norm1_gain, norm1_shift, qkv_full, qbias_full, vbias_full, proj_full, scale1_full,
    )
    grad_scale_one = jnp.sum(grad_residual * attn_out, axis=0)
    grad_attn = (as_float(back_scale) * grad_residual).astype(jnp.bfloat16)
    grad_proj_shift = jnp.sum(grad_attn, axis=0, dtype=jnp.float32)
    grad_proj_full = lax.dot_general(
        mixed_low, grad_attn, CONTRACT_ROWS, preferred_element_type=jnp.float32
    )
    grad_mixed = lax.dot_general(
        grad_attn, back_proj, CONTRACT_COLS, preferred_element_type=jnp.float32
    ).astype(jnp.bfloat16)
    normed_first, norm_one_pull = jax.vjp(
        layer_norm, inputs, as_float(back_gain), as_float(back_shift)
    )
    normed_first_low = normed_first.astype(jnp.bfloat16)
    qkv_again = make_qkv(normed_first_low, back_qkv, back_qbias, back_vbias)
    grad_qkv_glob, scores_grad_glob = attend_backward(
        qkv_again[:glob_rows].reshape(glob_slots, glob_len, -1),
        bias_glob,
        lse_glob,
        grad_mixed[:glob_rows],
    )
    grad_qkv_loc, scores_grad_loc = attend_backward(
        qkv_again[glob_rows:].reshape(loc_slots, loc_len, -1),
        bias_loc,
        lse_loc,
        grad_mixed[glob_rows:],
    )
    grad_qkv = jnp.concatenate([grad_qkv_glob, grad_qkv_loc])
    grad_qbias = jnp.sum(grad_qkv[:, :features], axis=0, dtype=jnp.float32)
    grad_vbias = jnp.sum(grad_qkv[:, 2 * features :], axis=0, dtype=jnp.float32)
    grad_qkv_full = lax.dot_general(
        normed_first_low, grad_qkv, CONTRACT_ROWS, preferred_element_type=jnp.float32
    )
    grad_normed_one = lax.dot_general(
        grad_qkv, back_qkv, CONTRACT_COLS, preferred_element_type=jnp.float32
    )
    grad_through_one, grad_norm1_gain, grad_norm1_shift = norm_one_pull(grad_normed_one)
    grad_inputs = (grad_residual + grad_through_one).astype(jnp.bfloat16)
    table_count = table_full.shape[0]
    grad_table = table_grad(index_global, scores_grad_glob, table_count) + table_grad(
        index_local, scores_grad_loc, table_count
    )
    sums, hidden_sum, table_sum, shares = scatter_grads(
        devices,
        [
            grad_norm1_gain, grad_norm1_shift, grad_qbias, grad_vbias, grad_proj_shift, grad_scale_one,
            grad_norm2_gain, grad_norm2_shift, grad_fc2_shift, grad_scale_two,
        ],
        grad_fc1_shift,
        grad_table,
        [grad_qkv_full, grad_proj_full, grad_fc1_full, grad_fc2_full],
    )
    return (
        outputs[:glob_rows].reshape(x_global.shape),
        outputs[glob_rows:].reshape(x_local.shape),
        grad_inputs[:glob_rows].reshape(x_global.shape),
        grad_inputs[glob_rows:].reshape(x_local.shape),
        sums[0],
        sums[1],
        shares[0],
        sums[2],
        sums[3],
        shares[1],
        sums[4],
        sums[5],
        table_sum,
        sums[6],
        sums[7],
        shares[2],
        hidden_sum,
        shares[3],
        sums[8],
        sums[9],
    )


def solution(mesh):
    placed = (
        P("fsdp", None, None),
        P("fsdp", None, None),
        P("fsdp", None, None),
        P("fsdp", None, None),
        P("fsdp"),
        P("fsdp"),
        P(),
        P(),
        P("fsdp"),
        P("fsdp"),
        P("fsdp", None),
        P("fsdp"),
        P("fsdp"),
        P("fsdp", None),
        P("fsdp"),
        P("fsdp"),
        P("fsdp", None),
        P("fsdp"),
        P("fsdp"),
        P("fsdp", None),
        P("fsdp"),
        P("fsdp", None),
        P("fsdp"),
        P("fsdp"),
    )
    return jax.shard_map(
        per_device,
        mesh=mesh,
        in_specs=placed,
        out_specs=(
            P("fsdp", None, None),
            P("fsdp", None, None),
            P("fsdp", None, None),
            P("fsdp", None, None),
            P("fsdp"),
            P("fsdp"),
            P("fsdp", None),
            P("fsdp"),
            P("fsdp"),
            P("fsdp", None),
            P("fsdp"),
            P("fsdp"),
            P("fsdp", None),
            P("fsdp"),
            P("fsdp"),
            P("fsdp", None),
            P("fsdp"),
            P("fsdp", None),
            P("fsdp"),
            P("fsdp"),
        ),
        check_vma=False,
    )
```

```python
import functools
import math

import jax
import jax.numpy as jnp
from jax import lax
from jax.experimental import pallas as pl
from jax.experimental.pallas import tpu as pltpu
from jax.sharding import PartitionSpec as P

EPSILON = 1e-06
NEG = -1e30
ROWS_IN = (((0,), (0,)), ((), ()))
COLS_IN = (((1,), (1,)), ((), ()))
BIG = 60 * 1024 * 1024


def as_float(values):
    return values.astype(jnp.float32)


def dot(a, b):
    return jnp.dot(a, b, preferred_element_type=jnp.float32)


def dot_tn(a, b):
    return lax.dot_general(a, b, ROWS_IN, preferred_element_type=jnp.float32)


def dot_nt(a, b):
    return lax.dot_general(a, b, COLS_IN, preferred_element_type=jnp.float32)


def round_up(value, unit):
    return (value + unit - 1) // unit * unit


def unit_rows(values):
    average = jnp.mean(values, axis=-1, keepdims=True)
    centered = values - average
    spread = lax.rsqrt(jnp.mean(centered * centered, axis=-1, keepdims=True) + EPSILON)
    return (centered * spread, spread)


def unit_back(grad, unit, spread):
    return spread * (
        grad - jnp.mean(grad, axis=-1, keepdims=True) - unit * jnp.mean(grad * unit, axis=-1, keepdims=True)
    )


def column_sum(values):
    return jnp.sum(values, axis=0, keepdims=True)


V_LN1G, V_LN1B, V_QB, V_VB, V_PB, V_G1, V_LN2G, V_LN2B, V_FB, V_G2 = range(10)


def mlp_kernel(
    steps, blocks, resid_ref, cot_ref, keep_ref, vec_ref, w1_ref, b1_ref, w2_ref,
    out_ref, gres_ref, gw1_ref, gw2_ref, gb1_ref, small_ref,
    normed, gbranch, branch, gnorm, active, ghidden,
):
    step = pl.program_id(0)
    rows, features = resid_ref.shape
    size = rows // blocks
    vec = lambda k: vec_ref[pl.ds(k, 1), :]

    @pl.when(step == 0)
    def _():
        @pl.loop(0, blocks)
        def _(i):
            part = pl.ds(pl.multiple_of(i * size, size), size)
            unit, _ = unit_rows(resid_ref[part, :])
            normed[part, :] = (unit * vec(V_LN2G) + vec(V_LN2B)).astype(jnp.bfloat16)
            grad = as_float(cot_ref[part, :]) * keep_ref[part, :]
            gbranch[part, :] = (vec(V_G2) * grad).astype(jnp.bfloat16)

    w1, w2 = w1_ref[...], w2_ref[...]
    hidden_sum = jnp.zeros_like(b1_ref)

    def block(i, hidden_sum):
        part = pl.ds(pl.multiple_of(i * size, size), size)
        hidden = dot(normed[part, :], w1) + b1_ref[...]
        phi = 0.5 * lax.erf(hidden * (0.5**0.5)) + 0.5
        low = (hidden * phi).astype(jnp.bfloat16)
        active[part, :] = low
        slope = phi + hidden * (jnp.exp(hidden * hidden * -0.5) * 0.3989422804014327)
        add = dot(low, w2)
        grad = dot_nt(gbranch[part, :], w2) * slope
        glow = grad.astype(jnp.bfloat16)
        ghidden[part, :] = glow
        gadd = dot_nt(glow, w1)

        @pl.when(step == 0)
        def _():
            branch[part, :] = add
            gnorm[part, :] = gadd

        @pl.when(step > 0)
        def _():
            branch[part, :] = branch[part, :] + add
            gnorm[part, :] = gnorm[part, :] + gadd

        return hidden_sum + column_sum(as_float(glow))

    gb1_ref[...] = lax.fori_loop(0, blocks, block, jnp.zeros(gb1_ref.shape, jnp.float32))
    gw2_ref[...] = dot_tn(active[...], gbranch[...]).astype(gw2_ref.dtype)
    gw1_ref[...] = dot_tn(normed[...], ghidden[...]).astype(gw1_ref.dtype)

    @pl.when(step == steps - 1)
    def _():
        zero = jnp.zeros((1, features), jnp.float32)

        def block(i, sums):
            part = pl.ds(pl.multiple_of(i * size, size), size)
            keep = keep_ref[part, :]
            resid = resid_ref[part, :]
            full = branch[part, :] + vec(V_FB)
            out_ref[part, :] = ((resid + vec(V_G2) * full) * keep).astype(out_ref.dtype)
            grad = as_float(cot_ref[part, :]) * keep
            unit, spread = unit_rows(resid)
            gn = gnorm[part, :]
            gres_ref[part, :] = grad + unit_back(gn * vec(V_LN2G), unit, spread)
            return (
                sums[0] + column_sum(gn * unit),
                sums[1] + column_sum(gn),
                sums[2] + column_sum(as_float(gbranch[part, :])),
                sums[3] + column_sum(grad * full),
            )

        sums = lax.fori_loop(0, blocks, block, (zero,) * 4)
        small_ref[...] = jnp.zeros_like(small_ref)
        for k in range(4):
            small_ref[pl.ds(k, 1), :] = sums[k]


def mlp_both(resid, cot, keep, vectors, w1, b1, w2, out_dtype, grad_dtype):
    rows, features = resid.shape
    hidden = w1.shape[1]
    chunk = 512
    steps = hidden // chunk
    whole = lambda shape: pl.BlockSpec(shape, lambda j: (0,) * len(shape), pipeline_mode=pl.Buffered(1))
    return pl.pallas_call(
        functools.partial(mlp_kernel, steps, 6),
        grid=(steps,),
        out_shape=[
            jax.ShapeDtypeStruct((rows, features), out_dtype),
            jax.ShapeDtypeStruct((rows, features), jnp.float32),
            jax.ShapeDtypeStruct((features, hidden), grad_dtype),
            jax.ShapeDtypeStruct((hidden, features), grad_dtype),
            jax.ShapeDtypeStruct((1, hidden), jnp.float32),
            jax.ShapeDtypeStruct((8, features), jnp.float32),
        ],
        in_specs=[
            whole((rows, features)),
            whole((rows, features)),
            whole((rows, 1)),
            whole(vectors.shape),
            pl.BlockSpec((features, chunk), lambda j: (0, j)),
            pl.BlockSpec((1, chunk), lambda j: (0, j)),
            pl.BlockSpec((chunk, features), lambda j: (j, 0)),
        ],
        out_specs=[
            whole((rows, features)),
            whole((rows, features)),
            pl.BlockSpec((features, chunk), lambda j: (0, j)),
            pl.BlockSpec((chunk, features), lambda j: (j, 0)),
            pl.BlockSpec((1, chunk), lambda j: (0, j)),
            whole((8, features)),
        ],
        scratch_shapes=[
            pltpu.VMEM((rows, features), jnp.bfloat16),
            pltpu.VMEM((rows, features), jnp.bfloat16),
            pltpu.VMEM((rows, features), jnp.float32),
            pltpu.VMEM((rows, features), jnp.float32),
            pltpu.VMEM((rows, chunk), jnp.bfloat16),
            pltpu.VMEM((rows, chunk), jnp.bfloat16),
        ],
        compiler_params=pltpu.CompilerParams(vmem_limit_bytes=BIG),
        name="mlp_both",
    )(resid, cot, keep, vectors, w1, b1, w2)


def expand_kernel(grids, table_ref, *refs):
    count = len(grids)
    for n, (side, seq, copies, slot) in enumerate(grids):
        index_ref, bias_ref = refs[n], refs[count + n]
        low_ref, high_ref, first_ref = refs[2 * count + 3 * n : 2 * count + 3 * n + 3]
        heads, cells, lanes = bias_ref.shape[0], side * side, bias_ref.shape[2]
        tables = lax.broadcasted_iota(jnp.int32, (table_ref.shape[1], lanes), 0)

        def pick(row):
            picked = index_ref[pl.ds(row, 1), :] == tables
            return dot(table_ref[...], picked.astype(jnp.bfloat16))

        def one(c, carry):
            low_ref[:, pl.ds(c, 1), :] = pick(1 + c)[:heads].reshape(heads, 1, lanes)
            high_ref[:, pl.ds(c, 1), :] = pick(1 + (side - 1) * side + c)[:heads].reshape(heads, 1, lanes)
            return carry

        lax.fori_loop(0, side, one, 0)
        first_ref[...] = pick(0)[:heads].reshape(heads, 1, lanes)
        lane = lax.broadcasted_iota(jnp.int32, (side, lanes), 1)
        lane_one = lax.broadcasted_iota(jnp.int32, (1, lanes), 1)

        def spread(values, at):
            if copies > 1:
                if at * slot:
                    values = pltpu.roll(values, at * slot, 1)
            where = lax.broadcasted_iota(jnp.int32, values.shape, 1) - at * slot
            return jnp.where((where >= 0) & (where < seq), values, NEG)

        def head(h, carry):
            bias_ref[h] = jnp.full(bias_ref.shape[1:], NEG, jnp.float32)
            low, high, first = low_ref[h], high_ref[h], first_ref[h]
            for at in range(copies):
                bias_ref[h, pl.ds(at * slot, 1), :] = spread(first, at)
            for r in range(side):
                from_high = pltpu.roll(high, (lanes - side * (side - 1 - r)) % lanes, 1)
                from_low = pltpu.roll(low, side * r, 1) if r else low
                rows = jnp.where(lane - 1 < side * (r + 1), from_high, from_low)
                rows = jnp.where(lane == 0, low, rows)
                for at in range(copies):
                    bias_ref[h, pl.ds(at * slot + 1 + side * r, side), :] = spread(rows, at)
            return carry

        lax.fori_loop(0, heads, head, 0)


def expand_bias(table, indices, grids, heads, seq):
    lanes = round_up(seq, 128)
    padded = [
        jnp.pad(i, ((0, 0), (0, lanes - i.shape[1])), constant_values=-1) for i in indices
    ]
    scratch = []
    for side, _, _, _ in grids:
        scratch += [
            pltpu.VMEM((heads, side, lanes), jnp.float32),
            pltpu.VMEM((heads, side, lanes), jnp.float32),
            pltpu.VMEM((heads, 1, lanes), jnp.float32),
        ]
    return pl.pallas_call(
        functools.partial(expand_kernel, grids),
        out_shape=[jax.ShapeDtypeStruct((heads, seq, lanes), jnp.float32)] * len(grids),
        scratch_shapes=scratch,
        compiler_params=pltpu.CompilerParams(vmem_limit_bytes=BIG),
        name="expand_bias",
    )(table, *padded)


def collect_kernel(grids, *refs):
    count = len(grids)
    grad_ref = refs[2 * count]
    table_rows = grad_ref.shape[1]
    total = jnp.zeros(grad_ref.shape, jnp.float32)
    for n, (side, seq, copies, slot) in enumerate(grids):
        index_ref, sums_ref = refs[n], refs[count + n]
        low_ref, high_ref, first_ref = refs[2 * count + 1 + 3 * n : 2 * count + 4 + 3 * n]
        heads, lanes = sums_ref.shape[0], sums_ref.shape[2]
        lane = lax.broadcasted_iota(jnp.int32, (side, lanes), 1)
        lane_one = lax.broadcasted_iota(jnp.int32, (1, lanes), 1)

        def gathered(h, start, size):
            rows = None
            where = lax.broadcasted_iota(jnp.int32, (size, lanes), 1)
            for at in range(copies):
                piece = sums_ref[h, pl.ds(at * slot + start, size), :]
                if at:
                    piece = pltpu.roll(piece, lanes - at * slot, 1)
                rows = piece if rows is None else rows + piece
            return jnp.where(where < seq, rows, 0.0) if copies > 1 else rows

        def head(h, carry):
            low = jnp.zeros((side, lanes), jnp.float32)
            high = jnp.zeros((side, lanes), jnp.float32)
            for r in range(side):
                rows = gathered(h, 1 + side * r, side)
                is_high = (lane >= 1) & (lane - 1 < side * (r + 1))
                low_part = jnp.where((lane >= 1) & (lane - 1 >= side * (r + 1)), rows, 0.0)
                if r:
                    low_part = pltpu.roll(low_part, (lanes - side * r) % lanes, 1)
                low = low + low_part + jnp.where(lane == 0, rows, 0.0)
                high_part = jnp.where(is_high, rows, 0.0)
                shift = side * (side - 1 - r)
                high = high + (pltpu.roll(high_part, shift, 1) if shift else high_part)
            low_ref[h], high_ref[h] = low, high
            first_ref[h] = gathered(h, 0, 1)
            return carry

        lax.fori_loop(0, heads, head, 0)
        tables = lax.broadcasted_iota(jnp.int32, (table_rows, lanes), 0)

        def place_sum(row, values):
            picked = (index_ref[pl.ds(row, 1), :] == tables).astype(jnp.bfloat16)
            top = values.astype(jnp.bfloat16)
            rest = values - as_float(top)
            middle = rest.astype(jnp.bfloat16)
            last = (rest - as_float(middle)).astype(jnp.bfloat16)
            return dot_nt(top, picked) + dot_nt(middle, picked) + dot_nt(last, picked)

        def one(c, total):
            low = low_ref[:, pl.ds(c, 1), :].reshape(heads, lanes)
            high = high_ref[:, pl.ds(c, 1), :].reshape(heads, lanes)
            return total + place_sum(1 + c, low) + place_sum(1 + (side - 1) * side + c, high)

        total = lax.fori_loop(0, side, one, total)
        total = total + place_sum(0, first_ref[...].reshape(heads, lanes))
    grad_ref[...] = total


def collect_bias(sums, indices, grids, table_rows):
    heads, _, lanes = sums[0].shape
    padded = [
        jnp.pad(i, ((0, 0), (0, lanes - i.shape[1])), constant_values=-1) for i in indices
    ]
    scratch = []
    for side, _, _, _ in grids:
        scratch += [
            pltpu.VMEM((heads, side, lanes), jnp.float32),
            pltpu.VMEM((heads, side, lanes), jnp.float32),
            pltpu.VMEM((heads, 1, lanes), jnp.float32),
        ]
    return pl.pallas_call(
        functools.partial(collect_kernel, grids),
        out_shape=jax.ShapeDtypeStruct((heads, table_rows), jnp.float32),
        scratch_shapes=scratch,
        compiler_params=pltpu.CompilerParams(vmem_limit_bytes=BIG),
        name="collect_bias",
    )(*padded, *sums)


def head_lanes(shape, width):
    return lax.broadcasted_iota(jnp.int32, shape, 1) < width


def stack_heads(pair, width):
    first = head_lanes(pair.shape, width)
    zero = jnp.zeros_like(pair)
    return jnp.concatenate([jnp.where(first, pair, zero), jnp.where(first, zero, pair)], axis=0)


def merge_heads(stacked, width):
    rows = stacked.shape[0] // 2
    top, low = stacked[:rows], stacked[rows:]
    return jnp.where(head_lanes(top.shape, width), top, low)


def attend_kernel(
    glob, heads, x_ref, wqkv_ref, wproj_ref, vec_ref, bias_ref,
    normed_ref, qkv_ref, probs_ref, mixed_ref, attn_ref, resid_ref,
):
    seq, features = x_ref.shape
    width = features // heads
    vec = lambda k: vec_ref[pl.ds(k, 1), :]
    inputs = as_float(x_ref[...])
    unit, _ = unit_rows(inputs)
    normed = (unit * vec(V_LN1G) + vec(V_LN1B)).astype(jnp.bfloat16)
    normed_ref[...] = normed
    qkv_ref[:, pl.ds(0, features)] = (dot(normed, wqkv_ref[:, pl.ds(0, features)]) + vec(V_QB)).astype(jnp.bfloat16)
    qkv_ref[:, pl.ds(features, features)] = dot(normed, wqkv_ref[:, pl.ds(features, features)]).astype(jnp.bfloat16)
    qkv_ref[:, pl.ds(2 * features, features)] = (
        dot(normed, wqkv_ref[:, pl.ds(2 * features, features)]) + vec(V_VB)
    ).astype(jnp.bfloat16)

    for pair in range(heads // 2):
        at = 2 * width * pair
        queries = stack_heads(qkv_ref[:, pl.ds(at, 2 * width)], width)
        keys = qkv_ref[:, pl.ds(features + at, 2 * width)]
        values = qkv_ref[:, pl.ds(2 * features + at, 2 * width)]
        bias = bias_ref[0, pl.ds(2 * pair, 2), :, pl.ds(0, seq)].reshape(2 * seq, seq)
        scores = dot_nt(queries, keys) * (width**-0.5) + bias
        weights = jnp.exp(scores - jnp.max(scores, axis=-1, keepdims=True))
        probs = (weights * (1.0 / jnp.sum(weights, axis=-1, keepdims=True))).astype(jnp.bfloat16)
        probs_ref[0, pair] = probs
        mixed_ref[:, pl.ds(at, 2 * width)] = merge_heads(dot(probs, values), width).astype(jnp.bfloat16)

    attn = dot(mixed_ref[...], wproj_ref[...]) + vec(V_PB)
    attn_ref[...] = attn
    resid_ref[...] = inputs + vec(V_G1) * attn


def attend_forward(x, wqkv, wproj, vectors, bias, packs, glob, heads):
    rows, features = x.shape
    seq = rows // packs
    whole = lambda shape: pl.BlockSpec(shape, lambda p: (0,) * len(shape), pipeline_mode=pl.Buffered(1))
    by_rows = lambda cols: pl.BlockSpec((seq, cols), lambda p: (p, 0))
    return pl.pallas_call(
        functools.partial(attend_kernel, glob, heads),
        grid=(packs,),
        out_shape=[
            jax.ShapeDtypeStruct((rows, features), jnp.bfloat16),
            jax.ShapeDtypeStruct((rows, 3 * features), jnp.bfloat16),
            jax.ShapeDtypeStruct((packs, heads // 2, 2 * seq, seq), jnp.bfloat16),
            jax.ShapeDtypeStruct((rows, features), jnp.bfloat16),
            jax.ShapeDtypeStruct((rows, features), jnp.float32),
            jax.ShapeDtypeStruct((rows, features), jnp.float32),
        ],
        in_specs=[
            by_rows(features),
            whole(wqkv.shape),
            whole(wproj.shape),
            whole(vectors.shape),
            pl.BlockSpec((1,) + bias.shape[1:], lambda p: (jnp.where(p < glob, 0, 1), 0, 0, 0)),
        ],
        out_specs=[
            by_rows(features),
            by_rows(3 * features),
            pl.BlockSpec((1, heads // 2, 2 * seq, seq), lambda p: (p, 0, 0, 0)),
            by_rows(features),
            by_rows(features),
            by_rows(features),
        ],
        compiler_params=pltpu.CompilerParams(vmem_limit_bytes=BIG),
        name="attend_forward",
    )(x, wqkv, wproj, vectors, bias)


def attend_back_kernel(
    packs, glob, heads, chunk, x_ref, normed_ref, qkv_ref, probs_ref, mixed_ref, attn_ref, gres_ref, wqkv_ref, wproj_ref, vec_ref,
    gx_ref, gwqkv_ref, gwproj_ref, bsum_ref, small_ref, gqb_ref,
    normed_all, mixed_all, gattn_all, gqkv_all,
):
    step = pl.program_id(0)
    seq, features = x_ref.shape
    width = features // heads
    vec = lambda k: vec_ref[pl.ds(k, 1), :]
    rows = packs * seq

    @pl.when(step == 0)
    def _():
        small_ref[...] = jnp.zeros_like(small_ref)
        gqb_ref[...] = jnp.zeros_like(gqb_ref)

    @pl.when((step == 0) | (step == glob))
    def _():
        bsum_ref[...] = jnp.zeros_like(bsum_ref)

    @pl.when(step < packs)
    def _():
        part = pl.ds(pl.multiple_of(step * seq, seq), seq)
        gres = gres_ref[...]
        gattn = (vec(V_G1) * gres).astype(jnp.bfloat16)
        gattn_all[part, :] = gattn
        mixed_all[part, :] = mixed_ref[...]
        normed_all[part, :] = normed_ref[...]
        small_ref[pl.ds(2, 1), :] += column_sum(as_float(gattn))
        small_ref[pl.ds(3, 1), :] += column_sum(gres * attn_ref[...])
        gmixed = dot_nt(gattn, wproj_ref[...]).astype(jnp.bfloat16)
        scale = width**-0.5
        for pair in range(heads // 2):
            at = 2 * width * pair
            queries = stack_heads(qkv_ref[:, pl.ds(at, 2 * width)], width)
            keys = qkv_ref[:, pl.ds(features + at, 2 * width)]
            values = qkv_ref[:, pl.ds(2 * features + at, 2 * width)]
            grads = stack_heads(gmixed[:, at : at + 2 * width], width)
            mixed = as_float(mixed_ref[:, pl.ds(at, 2 * width)])
            probs = probs_ref[0, pair]
            twice = jnp.concatenate([mixed, mixed], axis=0)
            inner = jnp.sum(as_float(grads) * twice, axis=-1, keepdims=True)
            gscores = as_float(probs) * (dot_nt(grads, values) - inner)
            bsum_ref[0, pl.ds(2 * pair, 2), :, pl.ds(0, seq)] += gscores.reshape(2, seq, seq)
            low = gscores.astype(jnp.bfloat16)
            gqkv_all[part, pl.ds(at, 2 * width)] = (merge_heads(dot(low, keys), width) * scale).astype(jnp.bfloat16)
            gqkv_all[part, pl.ds(features + at, 2 * width)] = (dot_tn(low, queries) * scale).astype(jnp.bfloat16)
            gqkv_all[part, pl.ds(2 * features + at, 2 * width)] = dot_tn(probs, grads).astype(jnp.bfloat16)
        gqkv = gqkv_all[part, :]
        gqb_ref[...] += column_sum(as_float(gqkv))
        gnorm = dot_nt(gqkv, wqkv_ref[...])
        unit, spread = unit_rows(as_float(x_ref[...]))
        small_ref[pl.ds(0, 1), :] += column_sum(gnorm * unit)
        small_ref[pl.ds(1, 1), :] += column_sum(gnorm)
        gx_ref[...] = (gres + unit_back(gnorm * vec(V_LN1G), unit, spread)).astype(gx_ref.dtype)

    @pl.when(step >= packs)
    def _():
        j = step - packs
        wide = 3 * features // chunk

        @pl.when(j < wide)
        def _():
            gwqkv_ref[...] = dot_tn(normed_all[...], gqkv_all[:, pl.ds(pl.multiple_of(j * chunk, chunk), chunk)]).astype(gwqkv_ref.dtype)

        @pl.when(j >= wide)
        def _():
            gwproj_ref[...] = dot_tn(mixed_all[...], gattn_all[:, pl.ds(pl.multiple_of((j - wide) * chunk, chunk), chunk)]).astype(gwproj_ref.dtype)


def attend_backward(x, normed, qkv, probs, mixed, attn, gres, wqkv, wproj, vectors, packs, glob, heads, out_dtype, grad_dtype, lanes):
    rows, features = x.shape
    seq = rows // packs
    chunk = 256
    wide, narrow = 3 * features // chunk, features // chunk
    whole = lambda shape: pl.BlockSpec(shape, lambda s: (0,) * len(shape), pipeline_mode=pl.Buffered(1))
    pack = lambda s: jnp.minimum(s, packs - 1)
    by_rows = lambda cols: pl.BlockSpec((seq, cols), lambda s: (pack(s), 0))
    return pl.pallas_call(
        functools.partial(attend_back_kernel, packs, glob, heads, chunk),
        grid=(packs + wide + narrow,),
        out_shape=[
            jax.ShapeDtypeStruct((rows, features), out_dtype),
            jax.ShapeDtypeStruct((features, 3 * features), grad_dtype),
            jax.ShapeDtypeStruct((features, features), grad_dtype),
            jax.ShapeDtypeStruct((2, heads, seq, lanes), jnp.float32),
            jax.ShapeDtypeStruct((8, features), jnp.float32),
            jax.ShapeDtypeStruct((1, 3 * features), jnp.float32),
        ],
        in_specs=[
            by_rows(features),
            by_rows(features),
            by_rows(3 * features),
            pl.BlockSpec((1, heads // 2, 2 * seq, seq), lambda s: (pack(s), 0, 0, 0)),
            by_rows(features),
            by_rows(features),
            by_rows(features),
            whole(wqkv.shape),
            whole(wproj.shape),
            whole(vectors.shape),
        ],
        out_specs=[
            by_rows(features),
            pl.BlockSpec((features, chunk), lambda s: (0, jnp.clip(s - packs, 0, wide - 1))),
            pl.BlockSpec((features, chunk), lambda s: (0, jnp.clip(s - packs - wide, 0, narrow - 1))),
            pl.BlockSpec((1, heads, seq, lanes), lambda s: (jnp.where(s < glob, 0, 1), 0, 0, 0)),
            whole((8, features)),
            whole((1, 3 * features)),
        ],
        scratch_shapes=[
            pltpu.VMEM((rows, features), jnp.bfloat16),
            pltpu.VMEM((rows, features), jnp.bfloat16),
            pltpu.VMEM((rows, features), jnp.bfloat16),
            pltpu.VMEM((rows, 3 * features), jnp.bfloat16),
        ],
        compiler_params=pltpu.CompilerParams(vmem_limit_bytes=BIG),
        name="attend_backward",
    )(x, normed, qkv, probs, mixed, attn, gres, wqkv, wproj, vectors)


MESH = pl.DeviceIdType.MESH
LINE = 4
GRID = (LINE, 2, 2, 2)


def place():
    me = lax.axis_index("fsdp")
    return (me // 8, (me // 4) % 2, (me // 2) % 2, me % 2)


def device_at(z, y, x, c):
    return (((z * 2 + y) * 2 + x) * 2 + c,)


def greet():
    z, y, x, c = place()
    barrier = pltpu.get_barrier_semaphore()
    for peer in (device_at(z, y, x, 1 - c), device_at(z, y, 1 - x, c), device_at(z, 1 - y, x, c)):
        pl.semaphore_signal(barrier, inc=1, device_id=peer, device_id_type=MESH)

    @pl.when(z > 0)
    def _():
        pl.semaphore_signal(barrier, inc=1, device_id=device_at(z - 1, y, x, c), device_id_type=MESH)

    @pl.when(z < LINE - 1)
    def _():
        pl.semaphore_signal(barrier, inc=1, device_id=device_at(z + 1, y, x, c), device_id_type=MESH)

    @pl.when((z > 0) & (z < LINE - 1))
    def _():
        pl.semaphore_wait(barrier, 5)

    @pl.when((z == 0) | (z == LINE - 1))
    def _():
        pl.semaphore_wait(barrier, 4)


def remote(src, dst, send, recv, peer):
    return pltpu.make_async_remote_copy(
        src_ref=src, dst_ref=dst, send_sem=send, recv_sem=recv, device_id=peer, device_id_type=MESH
    )


class Gather:
    STAGES = 7
    SEMS = 16

    def __init__(self, own, full, send, recv, local):
        self.own, self.full, self.send, self.recv, self.local = own, full, send, recv, local
        self.z, self.y, self.x, self.c = place()
        cols = own.shape[-1] // 2
        self.halves = (pl.ds(0, cols), pl.ds(cols, cols))

    def line_copy(self, step, up):
        z, y, x, c = self.z, self.y, self.x, self.c
        held = z - step if up else z + step
        slot = self.full.at[held, y, x, c]
        src = self.own if step == 0 else slot
        peer = device_at(z + 1 if up else z - 1, y, x, c)
        k = step if up else 3 + step
        return remote(src, slot, self.send.at[k], self.recv.at[k], peer)

    def line_send(self, step):
        z = self.z

        @pl.when((z - step >= 0) & (z < LINE - 1))
        def _():
            self.line_copy(step, True).start()

        @pl.when((z + step <= LINE - 1) & (z > 0))
        def _():
            self.line_copy(step, False).start()

    def line_wait(self, step):
        z = self.z

        @pl.when(z - step >= 1)
        def _():
            self.line_copy(step, True).wait_recv()

        @pl.when(z + step <= LINE - 2)
        def _():
            self.line_copy(step, False).wait_recv()

    def cross(self, k, part, half, flip_y):
        z, y, x, c = self.z, self.y, self.x, self.c
        peer = device_at(z, 1 - y, x, c) if flip_y else device_at(z, y, 1 - x, c)
        ref = self.full.at[part + (slice(None), self.halves[half])]
        return remote(ref, ref, self.send.at[k], self.recv.at[k], peer)

    def pair(self, k, part, half=None):
        z, y, x, c = self.z, self.y, self.x, self.c
        ref = self.full.at[part]
        if half is not None:
            ref = self.full.at[part + (slice(None), self.halves[half])]
        return remote(ref, ref, self.send.at[k], self.recv.at[k], device_at(z, y, x, 1 - c))

    def copy(self, name):
        y, x, c = self.y, self.x, self.c
        every = slice(None)
        return {
            "xa": lambda: self.cross(6, (every, y, x, c), 0, False),
            "yb": lambda: self.cross(7, (every, y, x, c), 1, True),
            "ya": lambda: self.cross(8, (every, y, every, c), 0, True),
            "xb": lambda: self.cross(9, (every, every, x, c), 1, False),
            "c0": lambda: self.pair(10, (every, y, x, c)),
            "c1": lambda: self.pair(11, (every, y, 1 - x, c), 0),
            "c2": lambda: self.pair(12, (every, 1 - y, x, c), 1),
            "c3": lambda: self.pair(13, (every, 1 - y, every, c), 0),
            "c4": lambda: self.pair(14, (every, every, 1 - x, c), 1),
        }[name]()

    def stage(self, s):
        z, y, x, c = self.z, self.y, self.x, self.c
        mine = lambda: pltpu.make_async_copy(self.own, self.full.at[z, y, x, c], self.local)
        if s == 0:
            mine().start()
            self.line_send(0)
        elif s <= 3:
            self.line_wait(s - 1)
            if s < 3:
                self.line_send(s)
            else:
                mine().wait()
                for name in ("xa", "yb", "c0"):
                    self.copy(name).start()
        elif s == 4:
            self.copy("xa").wait_recv()
            self.copy("ya").start()
            self.copy("yb").wait_recv()
            self.copy("xb").start()
            self.copy("c1").start()
            self.copy("c2").start()
        elif s == 5:
            self.copy("ya").wait_recv()
            self.copy("c3").start()
            self.copy("xb").wait_recv()
            self.copy("c4").start()
        else:
            for name in ("c0", "c1", "c2", "c3", "c4"):
                self.copy(name).wait_recv()

    def drain(self):
        z = self.z
        for step in range(LINE - 1):
            @pl.when((z - step >= 0) & (z < LINE - 1))
            def _():
                self.line_copy(step, True).wait_send()

            @pl.when((z + step <= LINE - 1) & (z > 0))
            def _():
                self.line_copy(step, False).wait_send()

        for name in ("xa", "yb", "ya", "xb", "c0", "c1", "c2", "c3", "c4"):
            self.copy(name).wait_send()


def wavefront(count, stages, lag):
    order = [(s + lag * t, t, s) for t in range(count) for s in range(stages)]
    return [(t, s) for _, t, s in sorted(order)]


GATHER_LAG = 1.5


def gather_kernel(count, *refs):
    own, full = refs[:count], refs[count : 2 * count]
    send, recv, local = refs[2 * count :]
    greet()
    flows = [Gather(own[t], full[t], send.at[t], recv.at[t], local.at[t]) for t in range(count)]
    for t, s in wavefront(count, Gather.STAGES, GATHER_LAG):
        flows[t].stage(s)
    for flow in flows:
        flow.drain()


def gather_all(shards):
    count = len(shards)
    return pl.pallas_call(
        functools.partial(gather_kernel, count),
        out_shape=[jax.ShapeDtypeStruct(GRID + s.shape, s.dtype) for s in shards],
        in_specs=[pl.BlockSpec(memory_space=pltpu.VMEM)] * count,
        out_specs=[pl.BlockSpec(memory_space=pl.ANY)] * count,
        scratch_shapes=[
            pltpu.SemaphoreType.DMA((count, Gather.SEMS)),
            pltpu.SemaphoreType.DMA((count, Gather.SEMS)),
            pltpu.SemaphoreType.DMA((count,)),
        ],
        compiler_params=pltpu.CompilerParams(collective_id=0, has_side_effects=True),
        name="gather_all",
    )(*shards)


class Scatter:
    STAGES = 8
    SEMS = 16

    def __init__(self, terms, out, bufs, send, recv, local):
        self.terms, self.out = terms, out
        self.own, self.pairbuf, self.buf1a, self.buf1b, self.buf2a, self.buf2b, self.up, self.down = bufs
        self.send, self.recv, self.local = send, recv, local
        self.z, self.y, self.x, self.c = place()
        cols = terms.shape[-1] // 2
        self.halves = (pl.ds(0, cols), pl.ds(cols, cols))

    @staticmethod
    def scratch(shape, dtype):
        rows, cols = shape
        half = cols // 2
        return [
            pltpu.VMEM((LINE, 2, 2, rows, cols), dtype),
            pltpu.VMEM((LINE, 2, 2, rows, cols), dtype),
            pltpu.VMEM((LINE, 2, rows, half), dtype),
            pltpu.VMEM((LINE, 2, rows, half), dtype),
            pltpu.VMEM((LINE, rows, half), dtype),
            pltpu.VMEM((LINE, rows, half), dtype),
            pltpu.VMEM((LINE, rows, cols), dtype),
            pltpu.VMEM((LINE, rows, cols), dtype),
        ]

    def load(self):
        every = slice(None)
        return pltpu.make_async_copy(self.terms.at[every, every, every, self.c], self.own, self.local)

    def copy(self, name):
        z, y, x, c = self.z, self.y, self.x, self.c
        every = slice(None)
        a, b = self.halves
        over_y, over_x = device_at(z, 1 - y, x, c), device_at(z, y, 1 - x, c)
        sem = lambda k: (self.send.at[k], self.recv.at[k])
        return {
            "pair": lambda: remote(self.terms.at[every, every, every, 1 - c], self.pairbuf, *sem(0), device_at(z, y, x, 1 - c)),
            "1a": lambda: remote(self.own.at[every, 1 - y, every, every, a], self.buf1a, *sem(1), over_y),
            "1b": lambda: remote(self.own.at[every, every, 1 - x, every, b], self.buf1b, *sem(2), over_x),
            "2a": lambda: remote(self.own.at[every, y, 1 - x, every, a], self.buf2a, *sem(3), over_x),
            "2b": lambda: remote(self.own.at[every, 1 - y, x, every, b], self.buf2b, *sem(4), over_y),
        }[name]()

    def line_copy(self, target, up):
        z, y, x, c = self.z, self.y, self.x, self.c
        buf = self.up if up else self.down
        k = 5 + target if up else 9 + target
        peer = device_at(z + 1 if up else z - 1, y, x, c)
        return remote(self.own.at[target, y, x], buf.at[target], self.send.at[k], self.recv.at[k], peer)

    def stage(self, s):
        z, y, x, c = self.z, self.y, self.x, self.c
        own = self.own
        a, b = self.halves
        if s == 0:
            self.load().start()
            self.copy("pair").start()
        elif s == 1:
            self.load().wait()
            self.copy("pair").wait_recv()

            @pl.loop(0, LINE)
            def _(i):
                for j in range(2):
                    for k in range(2):
                        own[i, j, k] = own[i, j, k] + self.pairbuf[i, j, k]

            self.copy("1a").start()
            self.copy("1b").start()
        elif s == 2:
            self.copy("1a").wait_recv()
            self.copy("1b").wait_recv()

            @pl.loop(0, LINE)
            def _(i):
                for k in range(2):
                    own[i, y, k, :, a] = own[i, y, k, :, a] + self.buf1a[i, k]
                    own[i, k, x, :, b] = own[i, k, x, :, b] + self.buf1b[i, k]

            self.copy("2a").start()
            self.copy("2b").start()
        elif s == 3:
            self.copy("2a").wait_recv()
            self.copy("2b").wait_recv()

            @pl.loop(0, LINE)
            def _(i):
                own[i, y, x, :, a] = own[i, y, x, :, a] + self.buf2a[i]
                own[i, y, x, :, b] = own[i, y, x, :, b] + self.buf2b[i]

        elif s <= 6:
            for target, up in ((LINE - 1 - (s - 4), True), (s - 4, False)):
                @pl.when((z < target) if up else (z > target))
                def _():
                    @pl.when((z > 0) if up else (z < LINE - 1))
                    def _():
                        self.line_copy(target, up).wait_recv()
                        buf = self.up if up else self.down
                        own[target, y, x] = own[target, y, x] + buf[target]

                    self.line_copy(target, up).start()

        else:
            for target in range(LINE):
                @pl.when((z == target) & (z > 0))
                def _():
                    self.line_copy(target, True).wait_recv()

                @pl.when((z == target) & (z < LINE - 1))
                def _():
                    self.line_copy(target, False).wait_recv()

            self.out[...] = own[z, y, x].astype(jnp.float32)

            @pl.when(z > 0)
            def _():
                self.out[...] = self.out[...] + self.up[z].astype(jnp.float32)

            @pl.when(z < LINE - 1)
            def _():
                self.out[...] = self.out[...] + self.down[z].astype(jnp.float32)

    def drain(self):
        z = self.z
        for name in ("pair", "1a", "1b", "2a", "2b"):
            self.copy(name).wait_send()
        for target in range(LINE):
            @pl.when(z < target)
            def _():
                self.line_copy(target, True).wait_send()

            @pl.when(z > target)
            def _():
                self.line_copy(target, False).wait_send()


SCATTER_LAG = 1.5


def scatter_kernel(count, *refs):
    terms, outs = refs[:count], refs[count : 2 * count]
    bufs = refs[2 * count : 10 * count]
    send, recv, local = refs[10 * count :]
    greet()
    flows = [
        Scatter(terms[t], outs[t], bufs[8 * t : 8 * t + 8], send.at[t], recv.at[t], local.at[t]) for t in range(count)
    ]
    for t, s in wavefront(count, Scatter.STAGES, SCATTER_LAG):
        flows[t].stage(s)
    for flow in flows:
        flow.drain()


def scatter_all(terms):
    count = len(terms)
    shapes = [t.shape[4:] for t in terms]
    scratch = []
    for t, s in zip(terms, shapes):
        scratch += Scatter.scratch(s, t.dtype)
    return pl.pallas_call(
        functools.partial(scatter_kernel, count),
        out_shape=[jax.ShapeDtypeStruct(s, jnp.float32) for s in shapes],
        in_specs=[pl.BlockSpec(memory_space=pl.ANY)] * count,
        out_specs=[pl.BlockSpec(memory_space=pltpu.VMEM)] * count,
        scratch_shapes=scratch
        + [
            pltpu.SemaphoreType.DMA((count, Scatter.SEMS)),
            pltpu.SemaphoreType.DMA((count, Scatter.SEMS)),
            pltpu.SemaphoreType.DMA((count,)),
        ],
        compiler_params=pltpu.CompilerParams(
            collective_id=1, has_side_effects=True, vmem_limit_bytes=56 * 1024 * 1024
        ),
        name="scatter_all",
    )(*terms)

PACK_ROWS, PACK_LANES = 16, 128


def pack_small(vectors, hidden_shift, table):
    lanes = lambda v: jnp.pad(v.astype(jnp.float32), ((0, 0), (0, PACK_LANES - v.shape[1])))
    rows = jnp.concatenate([lanes(jnp.stack(vectors)), lanes(hidden_shift[None]), lanes(table.reshape(3, -1))])
    rows = jnp.pad(rows, ((0, PACK_ROWS - rows.shape[0]), (0, 0)))
    return jnp.concatenate([rows[:8], rows[8:]], axis=1)


def unpack_small(block, count, hidden, table_shape):
    rows = jnp.concatenate([block[:, :, :PACK_LANES], block[:, :, PACK_LANES:]], axis=1)
    devices = rows.shape[0]
    vectors = jnp.transpose(rows[:, :10, :count], (1, 0, 2)).reshape(10, devices * count)
    table = rows[:, 11:14, : table_shape[0] * table_shape[1] // 3].reshape(devices * table_shape[0], table_shape[1])
    return (vectors, rows[:, 10, :hidden].reshape(devices * hidden), table)


def gather_params(devices, vectors, hidden_shift, table, weights):
    if devices != 32:
        whole = lambda v: lax.all_gather(v, "fsdp", axis=0, tiled=True)
        return (
            [as_float(whole(v)) for v in vectors], as_float(whole(hidden_shift)), as_float(whole(table)),
            [whole(w) for w in weights],
        )
    small, *full = gather_all([pack_small(vectors, hidden_shift, table)] + list(weights))
    stacked, hidden_full, table_full = unpack_small(
        small.reshape((devices,) + small.shape[4:]), vectors[0].shape[0], hidden_shift.shape[0], table.shape
    )
    full = [f.reshape((devices * f.shape[4], f.shape[5])) for f in full]
    return ([stacked[k] for k in range(10)], hidden_full, table_full, full)


def scatter_grads(devices, vectors, hidden_shift, table, weights):
    if devices != 32:
        share = lambda v: lax.psum_scatter(as_float(v), "fsdp", scatter_dimension=0, tiled=True)
        return ([share(v) for v in vectors], share(hidden_shift), share(table), [share(w) for w in weights])
    rows = jnp.transpose(jnp.stack(vectors).reshape(10, devices, -1), (1, 0, 2))
    lanes = lambda v: jnp.pad(v, ((0, 0), (0, 0), (0, PACK_LANES - v.shape[2])))
    rows = jnp.concatenate(
        [lanes(rows), lanes(hidden_shift.reshape(devices, 1, -1)), lanes(table.reshape(devices, 3, -1))], axis=1
    )
    rows = jnp.pad(rows, ((0, 0), (0, PACK_ROWS - rows.shape[1]), (0, 0)))
    block = jnp.concatenate([rows[:, :8], rows[:, 8:]], axis=2)
    terms = [block.reshape(GRID + block.shape[1:])] + [
        w.astype(jnp.bfloat16).reshape(GRID + (w.shape[0] // devices, w.shape[1])) for w in weights
    ]
    small, *shares = scatter_all(terms)
    sums, hidden_sum, table_sum = unpack_small(
        small[None], vectors[0].shape[0] // devices, hidden_shift.shape[0] // devices,
        (table.shape[0] // devices, table.shape[1]),
    )
    return ([sums[k] for k in range(10)], hidden_sum, table_sum, shares)


def slot_rows(values, slot, seq):
    crops, length, features = values.shape
    per_pack = seq // slot
    values = jnp.pad(values, ((0, 0), (0, slot - length), (0, 0)))
    values = values.reshape(crops // per_pack, per_pack * slot, features)
    return jnp.pad(values, ((0, 0), (0, seq - per_pack * slot), (0, 0)))


def crop_rows(packed, slot, crops, length):
    packs, seq, features = packed.shape
    per_pack = seq // slot
    return packed[:, : per_pack * slot].reshape(crops, slot, features)[:, :length]


def per_device(
    x_global, x_local, cot_global, cot_local, global_count, local_count, index_global, index_local,
    ln1_gain, ln1_bias, qkv_weight, q_bias, v_bias, proj_weight, proj_bias, gamma1, bias_table,
    ln2_gain, ln2_bias, fc1_weight, fc1_bias, fc2_weight, fc2_bias, gamma2,
):
    glob, glob_len, features = x_global.shape
    loc, loc_len = x_local.shape[:2]
    heads = bias_table.shape[1]
    seq = round_up(glob_len, 16)
    slot = round_up(loc_len, 8)
    per_pack = seq // slot
    packs = glob + loc // per_pack
    devices = lax.axis_size("fsdp")
    small_full, hidden_full, table_full, (qkv_full, proj_full, fc1_full, fc2_full) = gather_params(
        devices,
        [ln1_gain, ln1_bias, q_bias, v_bias, proj_bias, gamma1, ln2_gain, ln2_bias, fc2_bias, gamma2],
        fc1_bias,
        bias_table,
        [qkv_weight, proj_weight, fc1_weight, fc2_weight],
    )
    vectors = jnp.pad(jnp.stack(small_full), ((0, 6), (0, 0)))
    table_rows = table_full.shape[0]
    table = jnp.pad(table_full.T, ((0, round_up(heads, 16) - heads), (0, 0))).astype(jnp.bfloat16)
    sides = (math.isqrt(glob_len - 1), math.isqrt(loc_len - 1))
    grids = ((sides[0], glob_len, 1, seq), (sides[1], loc_len, per_pack, slot))

    glob_keep = jnp.repeat((jnp.arange(glob, dtype=jnp.int32) < global_count[0]).astype(jnp.float32), seq)
    loc_keep = jnp.repeat((jnp.arange(loc, dtype=jnp.int32) < local_count[0]).astype(jnp.float32), slot)
    loc_keep = jnp.pad(loc_keep.reshape(-1, per_pack * slot), ((0, 0), (0, seq - per_pack * slot))).reshape(-1)
    keep = jnp.concatenate([glob_keep, loc_keep])[:, None]
    rows_of = lambda g, l: jnp.concatenate([slot_rows(g, seq, seq), slot_rows(l, slot, seq)]).reshape(-1, features)
    x = rows_of(x_global, x_local)
    cot = rows_of(cot_global, cot_local)

    bias = jnp.stack(expand_bias(table, (index_global, index_local), grids, heads, seq))
    normed, qkv, probs, mixed, attn, resid = attend_forward(
        x, qkv_full, proj_full, vectors, bias, packs, glob, heads
    )
    grad_dtype = jnp.bfloat16
    out, gres, gfc1, gfc2, gfc1_shift, small_two = mlp_both(
        resid, cot, keep, vectors, fc1_full, hidden_full[None], fc2_full, x_global.dtype, grad_dtype
    )
    gx, gqkv, gproj, bias_sums, small_one, gqkv_shift = attend_backward(
        x, normed, qkv, probs, mixed, attn, gres, qkv_full, proj_full, vectors, packs, glob, heads, x_global.dtype,
        grad_dtype, bias.shape[-1],
    )
    gtable = collect_bias((bias_sums[0], bias_sums[1]), (index_global, index_local), grids, table_rows).T
    sums, hidden_sum, table_sum, shares = scatter_grads(
        devices,
        [
            small_one[0], small_one[1], gqkv_shift[0, :features], gqkv_shift[0, 2 * features :], small_one[2],
            small_one[3], small_two[0], small_two[1], small_two[2], small_two[3],
        ],
        gfc1_shift[0],
        gtable,
        [gqkv, gproj, gfc1, gfc2],
    )
    out = out.reshape(packs, seq, features)
    gx = gx.reshape(packs, seq, features)
    return (
        crop_rows(out[:glob], seq, glob, glob_len),
        crop_rows(out[glob:], slot, loc, loc_len),
        crop_rows(gx[:glob], seq, glob, glob_len),
        crop_rows(gx[glob:], slot, loc, loc_len),
        sums[0], sums[1], shares[0], sums[2], sums[3], shares[1], sums[4], sums[5], table_sum,
        sums[6], sums[7], shares[2], hidden_sum, shares[3], sums[8], sums[9],
    )


def solution(mesh):
    placed = (
        P("fsdp", None, None),
        P("fsdp", None, None),
        P("fsdp", None, None),
        P("fsdp", None, None),
        P("fsdp"),
        P("fsdp"),
        P(),
        P(),
        P("fsdp"),
        P("fsdp"),
        P("fsdp", None),
        P("fsdp"),
        P("fsdp"),
        P("fsdp", None),
        P("fsdp"),
        P("fsdp"),
        P("fsdp", None),
        P("fsdp"),
        P("fsdp"),
        P("fsdp", None),
        P("fsdp"),
        P("fsdp", None),
        P("fsdp"),
        P("fsdp"),
    )
    return jax.shard_map(
        per_device,
        mesh=mesh,
        in_specs=placed,
        out_specs=(
            P("fsdp", None, None),
            P("fsdp", None, None),
            P("fsdp", None, None),
            P("fsdp", None, None),
            P("fsdp"),
            P("fsdp"),
            P("fsdp", None),
            P("fsdp"),
            P("fsdp"),
            P("fsdp", None),
            P("fsdp"),
            P("fsdp"),
            P("fsdp", None),
            P("fsdp"),
            P("fsdp"),
            P("fsdp", None),
            P("fsdp"),
            P("fsdp", None),
            P("fsdp"),
            P("fsdp"),
        ),
        check_vma=False,
    )
```

```python
import functools
import math

import jax
import jax.numpy as jnp
from jax import lax
from jax.experimental import pallas as pl
from jax.experimental.pallas import tpu as pltpu
from jax.sharding import PartitionSpec as P

EPSILON = 1e-06
NEG = -1e30
ROWS_IN = (((0,), (0,)), ((), ()))
COLS_IN = (((1,), (1,)), ((), ()))
BIG = 60 * 1024 * 1024


def as_float(values):
    return values.astype(jnp.float32)


def dot(a, b):
    return jnp.dot(a, b, preferred_element_type=jnp.float32)


def dot_tn(a, b):
    return lax.dot_general(a, b, ROWS_IN, preferred_element_type=jnp.float32)


def dot_nt(a, b):
    return lax.dot_general(a, b, COLS_IN, preferred_element_type=jnp.float32)


def round_up(value, unit):
    return (value + unit - 1) // unit * unit


def unit_rows(values):
    average = jnp.mean(values, axis=-1, keepdims=True)
    centered = values - average
    spread = lax.rsqrt(jnp.mean(centered * centered, axis=-1, keepdims=True) + EPSILON)
    return (centered * spread, spread)


def unit_back(grad, unit, spread):
    return spread * (
        grad - jnp.mean(grad, axis=-1, keepdims=True) - unit * jnp.mean(grad * unit, axis=-1, keepdims=True)
    )


def column_sum(values):
    return jnp.sum(values, axis=0, keepdims=True)


V_LN1G, V_LN1B, V_QB, V_VB, V_PB, V_G1, V_LN2G, V_LN2B, V_FB, V_G2 = range(10)


def mlp_kernel(
    steps, blocks, resid_ref, cot_ref, keep_ref, vec_ref, w1_ref, b1_ref, w2_ref,
    out_ref, gres_ref, gw1_ref, gw2_ref, gb1_ref, small_ref,
    normed, gbranch, branch, gnorm, active, ghidden,
):
    step = pl.program_id(0)
    rows, features = resid_ref.shape
    size = rows // blocks
    vec = lambda k: vec_ref[pl.ds(k, 1), :]

    @pl.when(step == 0)
    def _():
        @pl.loop(0, blocks)
        def _(i):
            part = pl.ds(pl.multiple_of(i * size, size), size)
            unit, _ = unit_rows(resid_ref[part, :])
            normed[part, :] = (unit * vec(V_LN2G) + vec(V_LN2B)).astype(jnp.bfloat16)
            grad = as_float(cot_ref[part, :]) * keep_ref[part, :]
            gbranch[part, :] = (vec(V_G2) * grad).astype(jnp.bfloat16)

    w1, w2 = w1_ref[...], w2_ref[...]
    hidden_sum = jnp.zeros_like(b1_ref)

    def block(i, hidden_sum):
        part = pl.ds(pl.multiple_of(i * size, size), size)
        hidden = dot(normed[part, :], w1) + b1_ref[...]
        phi = 0.5 * lax.erf(hidden * (0.5**0.5)) + 0.5
        low = (hidden * phi).astype(jnp.bfloat16)
        active[part, :] = low
        slope = phi + hidden * (jnp.exp(hidden * hidden * -0.5) * 0.3989422804014327)
        add = dot(low, w2)
        grad = dot_nt(gbranch[part, :], w2) * slope
        glow = grad.astype(jnp.bfloat16)
        ghidden[part, :] = glow
        gadd = dot_nt(glow, w1)

        @pl.when(step == 0)
        def _():
            branch[part, :] = add
            gnorm[part, :] = gadd

        @pl.when(step > 0)
        def _():
            branch[part, :] = branch[part, :] + add
            gnorm[part, :] = gnorm[part, :] + gadd

        return hidden_sum + column_sum(as_float(glow))

    gb1_ref[...] = lax.fori_loop(0, blocks, block, jnp.zeros(gb1_ref.shape, jnp.float32))
    gw2_ref[...] = dot_tn(active[...], gbranch[...]).astype(gw2_ref.dtype)
    gw1_ref[...] = dot_tn(normed[...], ghidden[...]).astype(gw1_ref.dtype)

    @pl.when(step == steps - 1)
    def _():
        zero = jnp.zeros((1, features), jnp.float32)

        def block(i, sums):
            part = pl.ds(pl.multiple_of(i * size, size), size)
            keep = keep_ref[part, :]
            resid = resid_ref[part, :]
            full = branch[part, :] + vec(V_FB)
            out_ref[part, :] = ((resid + vec(V_G2) * full) * keep).astype(out_ref.dtype)
            grad = as_float(cot_ref[part, :]) * keep
            unit, spread = unit_rows(resid)
            gn = gnorm[part, :]
            gres_ref[part, :] = grad + unit_back(gn * vec(V_LN2G), unit, spread)
            return (
                sums[0] + column_sum(gn * unit),
                sums[1] + column_sum(gn),
                sums[2] + column_sum(as_float(gbranch[part, :])),
                sums[3] + column_sum(grad * full),
            )

        sums = lax.fori_loop(0, blocks, block, (zero,) * 4)
        small_ref[...] = jnp.zeros_like(small_ref)
        for k in range(4):
            small_ref[pl.ds(k, 1), :] = sums[k]


def mlp_both(resid, cot, keep, vectors, w1, b1, w2, out_dtype, grad_dtype):
    rows, features = resid.shape
    hidden = w1.shape[1]
    chunk = 1024
    steps = hidden // chunk
    whole = lambda shape: pl.BlockSpec(shape, lambda j: (0,) * len(shape), pipeline_mode=pl.Buffered(1))
    return pl.pallas_call(
        functools.partial(mlp_kernel, steps, 3),
        grid=(steps,),
        out_shape=[
            jax.ShapeDtypeStruct((rows, features), out_dtype),
            jax.ShapeDtypeStruct((rows, features), jnp.float32),
            jax.ShapeDtypeStruct((features, hidden), grad_dtype),
            jax.ShapeDtypeStruct((hidden, features), grad_dtype),
            jax.ShapeDtypeStruct((1, hidden), jnp.float32),
            jax.ShapeDtypeStruct((8, features), jnp.float32),
        ],
        in_specs=[
            whole((rows, features)),
            whole((rows, features)),
            whole((rows, 1)),
            whole(vectors.shape),
            pl.BlockSpec((features, chunk), lambda j: (0, j)),
            pl.BlockSpec((1, chunk), lambda j: (0, j)),
            pl.BlockSpec((chunk, features), lambda j: (j, 0)),
        ],
        out_specs=[
            whole((rows, features)),
            whole((rows, features)),
            pl.BlockSpec((features, chunk), lambda j: (0, j)),
            pl.BlockSpec((chunk, features), lambda j: (j, 0)),
            pl.BlockSpec((1, chunk), lambda j: (0, j)),
            whole((8, features)),
        ],
        scratch_shapes=[
            pltpu.VMEM((rows, features), jnp.bfloat16),
            pltpu.VMEM((rows, features), jnp.bfloat16),
            pltpu.VMEM((rows, features), jnp.float32),
            pltpu.VMEM((rows, features), jnp.float32),
            pltpu.VMEM((rows, chunk), jnp.bfloat16),
            pltpu.VMEM((rows, chunk), jnp.bfloat16),
        ],
        compiler_params=pltpu.CompilerParams(vmem_limit_bytes=BIG),
        name="mlp_both",
    )(resid, cot, keep, vectors, w1, b1, w2)


def lane_of(shape):
    return lax.broadcasted_iota(jnp.int32, shape, 1)


def roll_lanes(values, shift):
    shift = shift % values.shape[1]
    return pltpu.roll(values, shift, 1) if shift else values


def corner_rows(side):
    return (1, side, 1 + (side - 1) * side, side * side)


def expand(grids, table_ref, index_refs, bias_refs, row_refs):
    for n, (side, seq, copies, slot) in enumerate(grids):
        index_ref, bias_ref, row_ref = index_refs[n], bias_refs[n], row_refs[n]
        heads, lanes = bias_ref.shape[0], bias_ref.shape[2]
        tables = lax.broadcasted_iota(jnp.int32, (table_ref.shape[1], lanes), 0)

        def pick(row):
            picked = index_ref[pl.ds(row, 1), :] == tables
            return dot(table_ref[...], picked.astype(jnp.bfloat16))

        corners = [pick(row) for row in corner_rows(side)]
        lane = lane_of(corners[0].shape)
        within = (lane + (side - 1)) % side
        for c in range(side):
            for top in range(2):
                left, right = corners[2 * top], corners[2 * top + 1]
                row = jnp.where(within >= c, roll_lanes(left, c), roll_lanes(right, c - (side - 1)))
                row = jnp.where(lane == 0, left, row)
                row_ref[top, :, pl.ds(c, 1), :] = row[:heads].reshape(heads, 1, lanes)
        row_ref[0, :, pl.ds(side, 1), :] = pick(0)[:heads].reshape(heads, 1, lanes)
        lane = lane_of((side, lanes))

        def spread(values, at):
            if copies > 1:
                values = roll_lanes(values, at * slot)
            where = lane_of(values.shape) - at * slot
            return jnp.where((where >= 0) & (where < seq), values, NEG)

        @pl.loop(0, heads)
        def _(h):
            bias_ref[h] = jnp.full(bias_ref.shape[1:], NEG, jnp.float32)
            low, high, first = row_ref[0, h, :side], row_ref[1, h, :side], row_ref[0, h, pl.ds(side, 1)]
            for at in range(copies):
                bias_ref[h, pl.ds(at * slot, 1), :] = spread(first, at)
            for r in range(side):
                rows = jnp.where(
                    lane - 1 < side * (r + 1), roll_lanes(high, -side * (side - 1 - r)), roll_lanes(low, side * r)
                )
                rows = jnp.where(lane == 0, low, rows)
                for at in range(copies):
                    bias_ref[h, pl.ds(at * slot + 1 + side * r, side), :] = spread(rows, at)


def collect(grids, sum_refs, index_refs, row_refs, shape):
    total = jnp.zeros(shape, jnp.float32)
    for n, (side, seq, copies, slot) in enumerate(grids):
        index_ref, sum_ref, row_ref = index_refs[n], sum_refs[n], row_refs[n]
        heads, lanes = sum_ref.shape[0], sum_ref.shape[2]
        lane = lane_of((side, lanes))

        def gathered(h, start, size):
            rows = None
            for at in range(copies):
                piece = roll_lanes(sum_ref[h, pl.ds(at * slot + start, size), :], -at * slot)
                rows = piece if rows is None else rows + piece
            return jnp.where(lane_of((size, lanes)) < seq, rows, 0.0) if copies > 1 else rows

        @pl.loop(0, heads)
        def _(h):
            low = jnp.zeros((side, lanes), jnp.float32)
            high = jnp.zeros((side, lanes), jnp.float32)
            for r in range(side):
                rows = gathered(h, 1 + side * r, side)
                is_low = lane - 1 >= side * (r + 1)
                is_high = (lane >= 1) & (lane - 1 < side * (r + 1))
                low = low + roll_lanes(jnp.where(is_low, rows, 0.0), -side * r) + jnp.where(lane == 0, rows, 0.0)
                high = high + roll_lanes(jnp.where(is_high, rows, 0.0), side * (side - 1 - r))
            row_ref[0, h, :side], row_ref[1, h, :side] = low, high
            row_ref[0, h, pl.ds(side, 1)] = gathered(h, 0, 1)

        flat = lane_of((heads, lanes))
        within = (flat + (side - 1)) % side
        corners = [jnp.zeros((heads, lanes), jnp.float32) for _ in range(4)]
        for c in range(side):
            for top in range(2):
                row = row_ref[top, :, pl.ds(c, 1), :].reshape(heads, lanes)
                is_left = (flat >= 1) & (within >= c)
                is_right = (flat >= 1) & (within < c)
                left = roll_lanes(jnp.where(is_left, row, 0.0), -c) + jnp.where(flat == 0, row, 0.0)
                corners[2 * top] = corners[2 * top] + left
                corners[2 * top + 1] = corners[2 * top + 1] + roll_lanes(jnp.where(is_right, row, 0.0), side - 1 - c)
        tables = lax.broadcasted_iota(jnp.int32, (shape[1], lanes), 0)

        def place_sum(row, values):
            picked = (index_ref[pl.ds(row, 1), :] == tables).astype(jnp.bfloat16)
            top = values.astype(jnp.bfloat16)
            rest = values - as_float(top)
            middle = rest.astype(jnp.bfloat16)
            last = (rest - as_float(middle)).astype(jnp.bfloat16)
            return dot_nt(top, picked) + dot_nt(middle, picked) + dot_nt(last, picked)

        for row, values in zip(corner_rows(side), corners):
            total = total + place_sum(row, values)
        total = total + place_sum(0, row_ref[0, :, pl.ds(side, 1), :].reshape(heads, lanes))
    return total


ROW_SLOTS = 16


def expand_kernel(grids, table_ref, index_g, index_l, bias_ref, rows_g, rows_l):
    expand(grids, table_ref, (index_g, index_l), (bias_ref.at[0], bias_ref.at[1]), (rows_g, rows_l))


def pad_index(indices, lanes):
    return [jnp.pad(i, ((0, 0), (0, lanes - i.shape[1])), constant_values=-1) for i in indices]


def expand_bias(table, indices, grids, heads, seq):
    lanes = round_up(seq, 128)
    return pl.pallas_call(
        functools.partial(expand_kernel, grids),
        out_shape=jax.ShapeDtypeStruct((2, heads, seq, lanes), jnp.float32),
        scratch_shapes=[pltpu.VMEM((2, heads, ROW_SLOTS, lanes), jnp.float32)] * 2,
        compiler_params=pltpu.CompilerParams(vmem_limit_bytes=BIG),
        name="expand_bias",
    )(table, *pad_index(indices, lanes))


def collect_kernel(grids, index_g, index_l, sums_ref, grad_ref, rows_g, rows_l):
    grad_ref[...] = collect(
        grids, (sums_ref.at[0], sums_ref.at[1]), (index_g, index_l), (rows_g, rows_l), grad_ref.shape
    )


def collect_bias(sums, indices, grids, table_rows):
    _, heads, _, lanes = sums.shape
    return pl.pallas_call(
        functools.partial(collect_kernel, grids),
        out_shape=jax.ShapeDtypeStruct((heads, table_rows), jnp.float32),
        scratch_shapes=[pltpu.VMEM((2, heads, ROW_SLOTS, lanes), jnp.float32)] * 2,
        compiler_params=pltpu.CompilerParams(vmem_limit_bytes=BIG),
        name="collect_bias",
    )(*pad_index(indices, lanes), sums)


def head_lanes(shape, width):
    return lax.broadcasted_iota(jnp.int32, shape, 1) < width


def stack_heads(pair, width):
    first = head_lanes(pair.shape, width)
    zero = jnp.zeros_like(pair)
    return jnp.concatenate([jnp.where(first, pair, zero), jnp.where(first, zero, pair)], axis=0)


def merge_heads(stacked, width):
    rows = stacked.shape[0] // 2
    top, low = stacked[:rows], stacked[rows:]
    return jnp.where(head_lanes(top.shape, width), top, low)


def attend_kernel(
    glob, heads, x_ref, wqkv_ref, wproj_ref, vec_ref, bias_ref,
    normed_ref, qkv_ref, probs_ref, mixed_ref, attn_ref, resid_ref,
):
    seq, features = x_ref.shape
    width = features // heads
    vec = lambda k: vec_ref[pl.ds(k, 1), :]
    inputs = as_float(x_ref[...])
    unit, _ = unit_rows(inputs)
    normed = (unit * vec(V_LN1G) + vec(V_LN1B)).astype(jnp.bfloat16)
    normed_ref[...] = normed
    qkv_ref[:, pl.ds(0, features)] = (dot(normed, wqkv_ref[:, pl.ds(0, features)]) + vec(V_QB)).astype(jnp.bfloat16)
    qkv_ref[:, pl.ds(features, features)] = dot(normed, wqkv_ref[:, pl.ds(features, features)]).astype(jnp.bfloat16)
    qkv_ref[:, pl.ds(2 * features, features)] = (
        dot(normed, wqkv_ref[:, pl.ds(2 * features, features)]) + vec(V_VB)
    ).astype(jnp.bfloat16)

    for pair in range(heads // 2):
        at = 2 * width * pair
        queries = stack_heads(qkv_ref[:, pl.ds(at, 2 * width)], width)
        keys = qkv_ref[:, pl.ds(features + at, 2 * width)]
        values = qkv_ref[:, pl.ds(2 * features + at, 2 * width)]
        bias = bias_ref[0, pl.ds(2 * pair, 2), :, pl.ds(0, seq)].reshape(2 * seq, seq)
        scores = dot_nt(queries, keys) * (width**-0.5) + bias
        weights = jnp.exp(scores - jnp.max(scores, axis=-1, keepdims=True))
        probs = (weights * (1.0 / jnp.sum(weights, axis=-1, keepdims=True))).astype(jnp.bfloat16)
        probs_ref[0, pair] = probs
        mixed_ref[:, pl.ds(at, 2 * width)] = merge_heads(dot(probs, values), width).astype(jnp.bfloat16)

    attn = dot(mixed_ref[...], wproj_ref[...]) + vec(V_PB)
    attn_ref[...] = attn.astype(jnp.bfloat16)
    resid_ref[...] = inputs + vec(V_G1) * attn


def attend_forward(x, wqkv, wproj, vectors, bias, packs, glob, heads):
    rows, features = x.shape
    seq = rows // packs
    whole = lambda shape: pl.BlockSpec(shape, lambda p: (0,) * len(shape), pipeline_mode=pl.Buffered(1))
    by_rows = lambda cols: pl.BlockSpec((seq, cols), lambda p: (p, 0))
    return pl.pallas_call(
        functools.partial(attend_kernel, glob, heads),
        grid=(packs,),
        out_shape=[
            jax.ShapeDtypeStruct((rows, features), jnp.bfloat16),
            jax.ShapeDtypeStruct((rows, 3 * features), jnp.bfloat16),
            jax.ShapeDtypeStruct((packs, heads // 2, 2 * seq, seq), jnp.bfloat16),
            jax.ShapeDtypeStruct((rows, features), jnp.bfloat16),
            jax.ShapeDtypeStruct((rows, features), jnp.bfloat16),
            jax.ShapeDtypeStruct((rows, features), jnp.float32),
        ],
        in_specs=[
            by_rows(features),
            whole(wqkv.shape),
            whole(wproj.shape),
            whole(vectors.shape),
            pl.BlockSpec((1,) + bias.shape[1:], lambda p: (jnp.where(p < glob, 0, 1), 0, 0, 0)),
        ],
        out_specs=[
            by_rows(features),
            by_rows(3 * features),
            pl.BlockSpec((1, heads // 2, 2 * seq, seq), lambda p: (p, 0, 0, 0)),
            by_rows(features),
            by_rows(features),
            by_rows(features),
        ],
        compiler_params=pltpu.CompilerParams(vmem_limit_bytes=BIG),
        name="attend_forward",
    )(x, wqkv, wproj, vectors, bias)


def attend_back_kernel(
    packs, glob, heads, chunk, x_ref, normed_ref, qkv_ref, probs_ref, mixed_ref, attn_ref, gres_ref, wqkv_ref, wproj_ref, vec_ref,
    gx_ref, gwqkv_ref, gwproj_ref, bsum_ref, small_ref, gqb_ref,
    normed_all, mixed_all, gattn_all, gqkv_all,
):
    step = pl.program_id(0)
    seq, features = x_ref.shape
    width = features // heads
    vec = lambda k: vec_ref[pl.ds(k, 1), :]
    rows = packs * seq

    @pl.when(step == 0)
    def _():
        small_ref[...] = jnp.zeros_like(small_ref)
        gqb_ref[...] = jnp.zeros_like(gqb_ref)

    @pl.when((step == 0) | (step == glob))
    def _():
        bsum_ref[...] = jnp.zeros_like(bsum_ref)

    @pl.when(step < packs)
    def _():
        part = pl.ds(pl.multiple_of(step * seq, seq), seq)
        gres = gres_ref[...]
        gattn = (vec(V_G1) * gres).astype(jnp.bfloat16)
        gattn_all[part, :] = gattn
        mixed_all[part, :] = mixed_ref[...]
        normed_all[part, :] = normed_ref[...]
        small_ref[pl.ds(2, 1), :] += column_sum(as_float(gattn))
        small_ref[pl.ds(3, 1), :] += column_sum(gres * as_float(attn_ref[...]))
        gmixed = dot_nt(gattn, wproj_ref[...]).astype(jnp.bfloat16)
        scale = width**-0.5
        for pair in range(heads // 2):
            at = 2 * width * pair
            queries = stack_heads(qkv_ref[:, pl.ds(at, 2 * width)], width)
            keys = qkv_ref[:, pl.ds(features + at, 2 * width)]
            values = qkv_ref[:, pl.ds(2 * features + at, 2 * width)]
            grads = stack_heads(gmixed[:, at : at + 2 * width], width)
            mixed = as_float(mixed_ref[:, pl.ds(at, 2 * width)])
            probs = probs_ref[0, pair]
            twice = jnp.concatenate([mixed, mixed], axis=0)
            inner = jnp.sum(as_float(grads) * twice, axis=-1, keepdims=True)
            gscores = as_float(probs) * (dot_nt(grads, values) - inner)
            bsum_ref[0, pl.ds(2 * pair, 2), :, pl.ds(0, seq)] += gscores.reshape(2, seq, seq)
            low = gscores.astype(jnp.bfloat16)
            gqkv_all[part, pl.ds(at, 2 * width)] = (merge_heads(dot(low, keys), width) * scale).astype(jnp.bfloat16)
            gqkv_all[part, pl.ds(features + at, 2 * width)] = (dot_tn(low, queries) * scale).astype(jnp.bfloat16)
            gqkv_all[part, pl.ds(2 * features + at, 2 * width)] = dot_tn(probs, grads).astype(jnp.bfloat16)
        gqkv = gqkv_all[part, :]
        gqb_ref[...] += column_sum(as_float(gqkv))
        gnorm = dot_nt(gqkv, wqkv_ref[...])
        unit, spread = unit_rows(as_float(x_ref[...]))
        small_ref[pl.ds(0, 1), :] += column_sum(gnorm * unit)
        small_ref[pl.ds(1, 1), :] += column_sum(gnorm)
        gx_ref[...] = (gres + unit_back(gnorm * vec(V_LN1G), unit, spread)).astype(gx_ref.dtype)

    @pl.when(step >= packs)
    def _():
        j = step - packs
        wide = 3 * features // chunk

        @pl.when(j < wide)
        def _():
            gwqkv_ref[...] = dot_tn(normed_all[...], gqkv_all[:, pl.ds(pl.multiple_of(j * chunk, chunk), chunk)]).astype(gwqkv_ref.dtype)

        @pl.when(j >= wide)
        def _():
            gwproj_ref[...] = dot_tn(mixed_all[...], gattn_all[:, pl.ds(pl.multiple_of((j - wide) * chunk, chunk), chunk)]).astype(gwproj_ref.dtype)


def attend_backward(x, normed, qkv, probs, mixed, attn, gres, wqkv, wproj, vectors, packs, glob, heads, out_dtype, grad_dtype, lanes):
    rows, features = x.shape
    seq = rows // packs
    chunk = 256
    wide, narrow = 3 * features // chunk, features // chunk
    whole = lambda shape: pl.BlockSpec(shape, lambda s: (0,) * len(shape), pipeline_mode=pl.Buffered(1))
    pack = lambda s: jnp.minimum(s, packs - 1)
    by_rows = lambda cols: pl.BlockSpec((seq, cols), lambda s: (pack(s), 0))
    return pl.pallas_call(
        functools.partial(attend_back_kernel, packs, glob, heads, chunk),
        grid=(packs + wide + narrow,),
        out_shape=[
            jax.ShapeDtypeStruct((rows, features), out_dtype),
            jax.ShapeDtypeStruct((features, 3 * features), grad_dtype),
            jax.ShapeDtypeStruct((features, features), grad_dtype),
            jax.ShapeDtypeStruct((2, heads, seq, lanes), jnp.float32),
            jax.ShapeDtypeStruct((8, features), jnp.float32),
            jax.ShapeDtypeStruct((1, 3 * features), jnp.float32),
        ],
        in_specs=[
            by_rows(features),
            by_rows(features),
            by_rows(3 * features),
            pl.BlockSpec((1, heads // 2, 2 * seq, seq), lambda s: (pack(s), 0, 0, 0)),
            by_rows(features),
            by_rows(features),
            by_rows(features),
            whole(wqkv.shape),
            whole(wproj.shape),
            whole(vectors.shape),
        ],
        out_specs=[
            by_rows(features),
            pl.BlockSpec((features, chunk), lambda s: (0, jnp.clip(s - packs, 0, wide - 1))),
            pl.BlockSpec((features, chunk), lambda s: (0, jnp.clip(s - packs - wide, 0, narrow - 1))),
            pl.BlockSpec((1, heads, seq, lanes), lambda s: (jnp.where(s < glob, 0, 1), 0, 0, 0)),
            whole((8, features)),
            whole((1, 3 * features)),
        ],
        scratch_shapes=[
            pltpu.VMEM((rows, features), jnp.bfloat16),
            pltpu.VMEM((rows, features), jnp.bfloat16),
            pltpu.VMEM((rows, features), jnp.bfloat16),
            pltpu.VMEM((rows, 3 * features), jnp.bfloat16),
        ],
        compiler_params=pltpu.CompilerParams(vmem_limit_bytes=BIG),
        name="attend_backward",
    )(x, normed, qkv, probs, mixed, attn, gres, wqkv, wproj, vectors)


MESH = pl.DeviceIdType.MESH
LINE = 4
GRID = (LINE, 2, 2, 2)
EVERY = slice(None)


def place():
    me = lax.axis_index("fsdp")
    return (me // 8, (me // 4) % 2, (me // 2) % 2, me % 2)


def device_at(z, y, x, c):
    return (((z * 2 + y) * 2 + x) * 2 + c,)


def along(z, k):
    return (z + k) % LINE


def greet():
    z, y, x, c = place()
    barrier = pltpu.get_barrier_semaphore()
    peers = [device_at(z, y, x, 1 - c), device_at(z, y, 1 - x, c), device_at(z, 1 - y, x, c)]
    peers += [device_at(along(z, k), y, x, c) for k in range(1, LINE)]
    for peer in peers:
        pl.semaphore_signal(barrier, inc=1, device_id=peer, device_id_type=MESH)
    pl.semaphore_wait(barrier, len(peers))


def remote(src, dst, send, recv, peer):
    return pltpu.make_async_remote_copy(
        src_ref=src, dst_ref=dst, send_sem=send, recv_sem=recv, device_id=peer, device_id_type=MESH
    )


class Gather:
    STAGES = 5
    SEMS = 12

    def __init__(self, own, full, send, recv):
        self.own, self.full, self.send, self.recv = own, full, send, recv
        self.z, self.y, self.x, self.c = place()
        self.cols = full.shape[-1] // 2

    def line_copy(self, k, source=None):
        z, y, x, c = self.z, self.y, self.x, self.c
        held = z if source is None else source
        peer = device_at(along(z, k), y, x, c)
        return remote(self.own, self.full.at[held, y, x, c], self.send.at[k - 1], self.recv.at[k - 1], peer)

    def copy(self, name):
        z, y, x, c = self.z, self.y, self.x, self.c
        over_x, over_y, pair = device_at(z, y, 1 - x, c), device_at(z, 1 - y, x, c), device_at(z, y, x, 1 - c)
        k, part, half, peer = {
            "near0": (3, (EVERY, y, x, c), 0, over_x),
            "near1": (4, (EVERY, y, x, c), 1, over_y),
            "far0": (5, (EVERY, y, EVERY, c), 0, over_y),
            "far1": (6, (EVERY, EVERY, x, c), 1, over_x),
            "pair": (7, (EVERY, y, x, c), None, pair),
            "pair0": (8, (EVERY, y, 1 - x, c), 0, pair),
            "pair1": (9, (EVERY, 1 - y, x, c), 1, pair),
            "pair2": (10, (EVERY, 1 - y, EVERY, c), 0, pair),
            "pair3": (11, (EVERY, EVERY, 1 - x, c), 1, pair),
        }[name]
        ref = self.full.at[part if half is None else part + (EVERY, pl.ds(half * self.cols, self.cols))]
        return remote(ref, ref, self.send.at[k], self.recv.at[k], peer)

    def mine(self):
        return pltpu.make_async_copy(self.own, self.full.at[self.z, self.y, self.x, self.c], self.recv.at[self.SEMS])

    def stage(self, s):
        if s == 0:
            for k in range(1, LINE):
                self.line_copy(k).start()
            self.mine().start()
        elif s == 1:
            self.mine().wait()
            for k in range(1, LINE):
                self.line_copy(k, along(self.z, LINE - k)).wait_recv()
            for name in ("near0", "near1", "pair"):
                self.copy(name).start()
        elif s == 2:
            for k in ("0", "1"):
                self.copy("near" + k).wait_recv()
                self.copy("far" + k).start()
            self.copy("pair0").start()
            self.copy("pair1").start()
        elif s == 3:
            for k, far in ((2, 0), (3, 1)):
                self.copy("far%d" % far).wait_recv()
                self.copy("pair%d" % k).start()
        else:
            for name in ("pair", "pair0", "pair1", "pair2", "pair3"):
                self.copy(name).wait_recv()

    def drain(self):
        for k in range(1, LINE):
            self.line_copy(k).wait_send()
        for name in ("near0", "near1", "far0", "far1", "pair", "pair0", "pair1", "pair2", "pair3"):
            self.copy(name).wait_send()


def wavefront(count, stages, lag):
    order = [(s + lag * t, t, s) for t in range(count) for s in range(stages)]
    return [(t, s) for _, t, s in sorted(order)]


GATHER_LAG = 0.75


def gather_kernel(count, *refs):
    own, full = refs[:count], refs[count : 2 * count]
    send, recv = refs[2 * count :]
    greet()
    flows = [Gather(own[t], full[t], send.at[t], recv.at[t]) for t in range(count)]
    for t, s in wavefront(count, Gather.STAGES, GATHER_LAG):
        flows[t].stage(s)
    for flow in flows:
        flow.drain()


def gather_all(shards):
    count = len(shards)
    return pl.pallas_call(
        functools.partial(gather_kernel, count),
        out_shape=[jax.ShapeDtypeStruct(GRID + s.shape, s.dtype) for s in shards],
        in_specs=[pl.BlockSpec(memory_space=pltpu.VMEM)] * count,
        out_specs=[pl.BlockSpec(memory_space=pl.ANY)] * count,
        scratch_shapes=[pltpu.SemaphoreType.DMA((count, Gather.SEMS + 1))] * 2,
        compiler_params=pltpu.CompilerParams(collective_id=0, has_side_effects=True),
        name="gather_all",
    )(*shards)


class Scatter:
    STAGES = 5
    SEMS = 9

    def __init__(self, terms, own, bufs, send, recv, finish):
        self.terms, self.loaded = terms, own
        self.pairbuf, self.buf1a, self.buf1b, self.buf2a, self.buf2b, self.line = bufs
        self.send, self.recv, self.finish = send, recv, finish
        self.z, self.y, self.x, self.c = place()
        self.cols = terms.shape[-1] // 2

    BUFS = 6

    @staticmethod
    def scratch(shape, dtype):
        rows, cols = shape
        half = cols // 2
        return [
            pltpu.VMEM((LINE, 2, 2, rows, cols), dtype),
            pltpu.VMEM((LINE, 2, rows, half), dtype),
            pltpu.VMEM((LINE, 2, rows, half), dtype),
            pltpu.VMEM((LINE, rows, half), dtype),
            pltpu.VMEM((LINE, rows, half), dtype),
            pltpu.VMEM((LINE - 1, rows, cols), dtype),
        ]

    def at(self, i, j, k, half=None):
        cols = () if half is None else (EVERY, pl.ds(half * self.cols, self.cols))
        if self.loaded is None:
            return self.terms.at[(i, j, k, self.c) + cols]
        return self.loaded.at[(i, j, k) + cols]

    def load(self):
        return pltpu.make_async_copy(self.terms.at[EVERY, EVERY, EVERY, self.c], self.loaded, self.send.at[8])

    def copy(self, name):
        z, y, x, c = self.z, self.y, self.x, self.c
        over_x, over_y = device_at(z, y, 1 - x, c), device_at(z, 1 - y, x, c)
        k, src, dst, peer = {
            "pair": lambda: (0, self.terms.at[EVERY, EVERY, EVERY, 1 - c], self.pairbuf, device_at(z, y, x, 1 - c)),
            "1a": lambda: (1, self.at(EVERY, 1 - y, EVERY, 0), self.buf1a, over_y),
            "1b": lambda: (2, self.at(EVERY, EVERY, 1 - x, 1), self.buf1b, over_x),
            "2a": lambda: (3, self.at(EVERY, y, 1 - x, 0), self.buf2a, over_x),
            "2b": lambda: (4, self.at(EVERY, 1 - y, x, 1), self.buf2b, over_y),
        }[name]()
        return remote(src, dst, self.send.at[k], self.recv.at[k], peer)

    def line_copy(self, k):
        z, y, x, c = self.z, self.y, self.x, self.c
        target = along(z, k)
        return remote(
            self.at(target, y, x), self.line.at[k - 1], self.send.at[4 + k], self.recv.at[4 + k], device_at(target, y, x, c)
        )

    def add(self, ref, term):
        ref[...] = ref[...] + term

    def stage(self, s):
        z, y, x = self.z, self.y, self.x
        if s == 0:
            self.copy("pair").start()
            if self.loaded is not None:
                self.load().start()
        elif s == 1:
            if self.loaded is not None:
                self.load().wait()
            self.copy("pair").wait_recv()

            @pl.loop(0, LINE)
            def _(i):
                for j in range(2):
                    for k in range(2):
                        self.add(self.at(i, j, k), self.pairbuf[i, j, k])

            self.copy("1a").start()
            self.copy("1b").start()
        elif s == 2:
            self.copy("1a").wait_recv()
            self.copy("1b").wait_recv()

            @pl.loop(0, LINE)
            def _(i):
                for k in range(2):
                    self.add(self.at(i, y, k, 0), self.buf1a[i, k])
                    self.add(self.at(i, k, x, 1), self.buf1b[i, k])

            self.copy("2a").start()
            self.copy("2b").start()
        elif s == 3:
            self.copy("2a").wait_recv()
            self.copy("2b").wait_recv()

            @pl.loop(0, LINE)
            def _(i):
                self.add(self.at(i, y, x, 0), self.buf2a[i])
                self.add(self.at(i, y, x, 1), self.buf2b[i])

            for k in range(1, LINE):
                self.line_copy(k).start()
        else:
            total = as_float(self.at(z, y, x)[...])
            for k in range(1, LINE):
                self.line_copy(k).wait_recv()
                total = total + as_float(self.line[k - 1])
            self.finish(total)

    def drain(self):
        for name in ("pair", "1a", "1b", "2a", "2b"):
            self.copy(name).wait_send()
        for k in range(1, LINE):
            self.line_copy(k).wait_send()


SMALL = (16, 256)


def back_kernel(
    shape, plan, x_ref, normed_ref, q_ref, k_ref, v_ref, probs_ref, mixed_ref, attn_ref, gres_ref, wqkv_ref, wproj_ref, vec_ref,
    two_ref, hidden_ref, index_g, index_l, gfc1_ref, gfc2_ref,
    gx_ref, sqkv_ref, sproj_ref, sfc1_ref, sfc2_ref, ssmall_ref,
    gqkv, gmixed, bsum, vecs, tsum, corner, *scratch,
):
    packs, glob, heads, groups, blocks, grids = shape
    step = pl.program_id(0)
    rows, features = normed_ref.shape
    seq = rows // packs
    width = features // heads
    lanes = features // groups
    scale = width**-0.5
    vec = lambda k: vec_ref[pl.ds(k, 1), :]
    size = rows // blocks
    last = 1 + packs * groups + 1 + blocks

    send, recv = scratch[-2:]
    scratch = scratch[:-2]
    big = 2 * SPLIT
    owns = list(scratch[:big]) + [None] * (groups + 2)
    terms = scratch[big : big + groups + 2]
    bufs = scratch[big + groups + 2 :]

    def put(ref):
        def finish(value):
            ref[...] = value

        return finish

    def put_group(g):
        def finish(value):
            for i in range(3):
                sqkv_ref[:, pl.ds(i * features + g * lanes, lanes)] = value[:, i * lanes : (i + 1) * lanes]

        return finish

    tall, wide = gfc2_ref.shape[4] // SPLIT, gfc1_ref.shape[5] // SPLIT
    sources, ends = [], []
    for k in range(SPLIT):
        sources.append(gfc2_ref.at[EVERY, EVERY, EVERY, EVERY, pl.ds(k * tall, tall)])
        ends.append(put(sfc2_ref.at[pl.ds(k * tall, tall)]))
    for k in range(SPLIT):
        sources.append(gfc1_ref.at[EVERY, EVERY, EVERY, EVERY, EVERY, pl.ds(k * wide, wide)])
        ends.append(put(sfc1_ref.at[EVERY, pl.ds(k * wide, wide)]))
    sources += list(terms)
    ends += [put(sproj_ref)] + [put_group(g) for g in range(groups)] + [put(ssmall_ref)]
    flows = [
        Scatter(sources[t], owns[t], bufs[Scatter.BUFS * t : Scatter.BUFS * (t + 1)], send.at[t], recv.at[t], ends[t]) for t in range(len(ends))
    ]

    def slot(k):
        for t, s in plan[k]:
            flows[t].stage(s)

    def fill(t, value):
        ref = terms[t]
        count = ref.shape[-2]
        for d in range(LINE * 8):
            ref[d // 8, d // 4 % 2, d // 2 % 2, d % 2] = value[d * count : (d + 1) * count].astype(ref.dtype)

    @pl.when(step == 0)
    def _():
        greet()
        slot(0)
        zero = jnp.zeros((1, features), jnp.float32)
        vecs[...] = jnp.zeros_like(vecs)

        def block(i, sums):
            part = pl.ds(pl.multiple_of(i * size, size), size)
            gres = gres_ref[part, :]
            gattn = (vec(V_G1) * gres).astype(jnp.bfloat16)
            gqkv[part, pl.ds(0, features)] = gattn
            gmixed[part, :] = dot_nt(gattn, wproj_ref[...]).astype(jnp.bfloat16)
            return (sums[0] + column_sum(as_float(gattn)), sums[1] + column_sum(gres * as_float(attn_ref[part, :])))

        sums = lax.fori_loop(0, blocks, block, (zero, zero))
        vecs[pl.ds(V_PB, 1), :] = sums[0]
        vecs[pl.ds(V_G1, 1), :] = sums[1]
        bsum[...] = jnp.zeros_like(bsum)
        fill(0, dot_tn(mixed_ref[...], gqkv[:, pl.ds(0, features)]))

    @pl.when((step >= 1) & (step <= packs * groups))
    def _():
        pack = (step - 1) % packs
        group = (step - 1) // packs
        part = pl.ds(pl.multiple_of(pack * seq, seq), seq)
        kind = jnp.where(pack < glob, 0, 1)
        for pair in range(heads // 2 // groups):
            at = 2 * width * pair
            wide = pl.ds(pl.multiple_of(group * lanes + at, 2 * width), 2 * width)
            queries = stack_heads(q_ref[:, pl.ds(at, 2 * width)], width)
            keys = k_ref[:, pl.ds(at, 2 * width)]
            values = v_ref[:, pl.ds(at, 2 * width)]
            grads = stack_heads(gmixed[part, wide], width)
            mixed = as_float(mixed_ref[part, wide])
            probs = probs_ref[0, pair]
            twice = jnp.concatenate([mixed, mixed], axis=0)
            inner = jnp.sum(as_float(grads) * twice, axis=-1, keepdims=True)
            gscores = as_float(probs) * (dot_nt(grads, values) - inner)
            head = group * (heads // groups) + 2 * pair
            bsum[kind, pl.ds(head, 2), :, pl.ds(0, seq)] += gscores.reshape(2, seq, seq)
            low = gscores.astype(jnp.bfloat16)
            gq = (merge_heads(dot(low, keys), width) * scale).astype(jnp.bfloat16)
            gk = (dot_tn(low, queries) * scale).astype(jnp.bfloat16)
            gv = dot_tn(probs, grads).astype(jnp.bfloat16)
            for i, piece in enumerate((gq, gk, gv)):
                at_lane = pl.multiple_of(group * lanes + at + i * features, 2 * width)
                gqkv[part, pl.ds(at_lane, 2 * width)] = piece

    for g in range(groups):
        @pl.when(step == packs * (g + 1))
        def _():
            pieces = [dot_tn(normed_ref[...], gqkv[:, pl.ds(i * features + g * lanes, lanes)]) for i in range(3)]
            fill(1 + g, jnp.concatenate(pieces, axis=1))

    @pl.when(step == packs * groups + 1)
    def _():
        tsum[...] = collect(
            grids, (bsum.at[0], bsum.at[1]), (index_g, index_l), (corner, corner), tsum.shape
        )

    @pl.when(step >= packs * groups + 2)
    def _():
        i = step - packs * groups - 2
        part = pl.ds(pl.multiple_of(i * size, size), size)
        low = gqkv[part, :]
        gnorm = dot_nt(low, wqkv_ref[...])
        unit, spread = unit_rows(as_float(x_ref[...]))
        vecs[pl.ds(V_LN1G, 1), :] += column_sum(gnorm * unit)
        vecs[pl.ds(V_LN1B, 1), :] += column_sum(gnorm)
        total = column_sum(as_float(low))
        vecs[pl.ds(V_QB, 1), :] += total[:, :features]
        vecs[pl.ds(V_VB, 1), :] += total[:, 2 * features :]
        gx_ref[...] = (gres_ref[part, :] + unit_back(gnorm * vec(V_LN1G), unit, spread)).astype(gx_ref.dtype)

    @pl.when(step == last - 1)
    def _():
        for k, row in ((V_LN2G, 0), (V_LN2B, 1), (V_FB, 2), (V_G2, 3)):
            vecs[pl.ds(k, 1), :] = two_ref[pl.ds(row, 1), :]
        ref = terms[-1]
        ref[...] = jnp.zeros_like(ref)
        devices = LINE * 8
        count, wide, table = features // devices, hidden_ref.shape[1] // devices, tsum.shape[1] // devices
        for d in range(devices):
            block = ref.at[d // 8, d // 4 % 2, d // 2 % 2, d % 2]
            block[:, pl.ds(0, count)] = vecs[:, pl.ds(d * count, count)]
            block[pl.ds(10, 1), pl.ds(0, wide)] = hidden_ref[:, pl.ds(d * wide, wide)]
            block[pl.ds(0, heads), pl.ds(128, table)] = tsum[:, pl.ds(d * table, table)]

    for k in range(1, last):
        @pl.when(step == k)
        def _():
            slot(k)

    @pl.when(step == last - 1)
    def _():
        for flow in flows:
            flow.drain()


def back_plan(steps, groups, packs):
    plan = [[] for _ in range(steps)]
    done = steps - 1
    starts = list(PLAN_BIG) + [PLAN_PROJ]
    starts += [[packs * (g + 1) + k for k in PLAN_GROUP[g]] for g in range(groups)] + [[done] * Scatter.STAGES]
    events = []
    for t, at in enumerate(starts):
        for s, k in enumerate(at):
            events.append((min(k, done), s if k >= done else 0, t, s))
    for k, _, t, s in sorted(events):
        plan[k].append((t, s))
    return plan


SPLIT = 2
PLAN_BIG = ([0, 1, 7, 13, 15], [0, 1, 11, 17, 19], [0, 6, 16, 20, 22], [0, 10, 18, 22, 22])
PLAN_PROJ = [1, 3, 9, 14, 17]
PLAN_GROUP = ([0, 2, 8, 13, 15], [0, 2, 7, 10, 10], [0, 1, 4, 4, 4])


def attend_back(
    x, normed, qkv, probs, mixed, attn, gres, wqkv, wproj, vectors, two, hidden, indices, gfc1, gfc2, packs, glob, heads,
    grids, table_rows, out_dtype, lanes,
):
    rows, features = x.shape
    seq = rows // packs
    groups, blocks = 3, 3
    cols = features // groups
    steps = 1 + packs * groups + 1 + blocks
    first_block = packs * groups + 2
    whole = lambda shape: pl.BlockSpec(shape, lambda s: (0,) * len(shape), pipeline_mode=pl.Buffered(1))
    at = lambda s: jnp.clip(s - 1, 0, packs * groups - 1)
    part = lambda i: pl.BlockSpec((seq, cols), lambda s: (at(s) % packs, i * groups + at(s) // packs))
    any_ref = pl.BlockSpec(memory_space=pl.ANY)
    by_block = pl.BlockSpec((rows // blocks, features), lambda s: (jnp.clip(s - first_block, 0, blocks - 1), 0))
    padded = pad_index(indices, lanes)
    shard = lambda t: t.shape[4:]
    term_shapes = [(features // 32, features)] + [(features // 32, 3 * cols)] * groups
    tall, wide = (shard(gfc2)[0] // SPLIT, shard(gfc2)[1]), (shard(gfc1)[0], shard(gfc1)[1] // SPLIT)
    flow_shapes = [(tall, gfc2.dtype)] * SPLIT + [(wide, gfc1.dtype)] * SPLIT
    scratch = [
        pltpu.VMEM((rows, 3 * features), jnp.bfloat16),
        pltpu.VMEM((rows, features), jnp.bfloat16),
        pltpu.VMEM((2, heads, seq, lanes), jnp.float32),
        pltpu.VMEM((16, features), jnp.float32),
        pltpu.VMEM((heads, table_rows), jnp.float32),
        pltpu.VMEM((2, heads, ROW_SLOTS, lanes), jnp.float32),
    ]
    scratch += [pltpu.VMEM((LINE, 2, 2) + s, d) for s, d in flow_shapes]
    flow_shapes += [(s, jnp.bfloat16) for s in term_shapes] + [(SMALL, jnp.float32)]
    scratch += [pltpu.VMEM(GRID + s, jnp.bfloat16) for s in term_shapes] + [pltpu.VMEM(GRID + SMALL, jnp.float32)]
    for s, d in flow_shapes:
        scratch += Scatter.scratch(s, d)
    scratch += [pltpu.SemaphoreType.DMA((len(flow_shapes), Scatter.SEMS))] * 2
    return pl.pallas_call(
        functools.partial(
            back_kernel, (packs, glob, heads, groups, blocks, grids), back_plan(steps, groups, packs)
        ),
        grid=(steps,),
        out_shape=[
            jax.ShapeDtypeStruct((rows, features), out_dtype),
            jax.ShapeDtypeStruct((features // 32, 3 * features), jnp.float32),
            jax.ShapeDtypeStruct((features // 32, features), jnp.float32),
            jax.ShapeDtypeStruct(shard(gfc1), jnp.float32),
            jax.ShapeDtypeStruct(shard(gfc2), jnp.float32),
            jax.ShapeDtypeStruct(SMALL, jnp.float32),
        ],
        in_specs=[
            by_block,
            whole((rows, features)),
            part(0), part(1), part(2),
            pl.BlockSpec((1, heads // 2 // groups, 2 * seq, seq), lambda s: (at(s) % packs, at(s) // packs, 0, 0)),
            whole((rows, features)),
            whole((rows, features)),
            whole((rows, features)),
            whole(wqkv.shape),
            whole(wproj.shape),
            whole(vectors.shape),
            whole(two.shape),
            whole(hidden.shape),
            whole(padded[0].shape),
            whole(padded[1].shape),
            any_ref,
            any_ref,
        ],
        out_specs=[
            by_block,
            whole((features // 32, 3 * features)),
            whole((features // 32, features)),
            whole(shard(gfc1)),
            whole(shard(gfc2)),
            whole(SMALL),
        ],
        scratch_shapes=scratch,
        compiler_params=pltpu.CompilerParams(vmem_limit_bytes=BIG, collective_id=1, has_side_effects=True),
        name="attend_back",
    )(x, normed, qkv, qkv, qkv, probs, mixed, attn, gres, wqkv, wproj, vectors, two, hidden, *padded, gfc1, gfc2)


PACK_ROWS, PACK_LANES = 16, 128


def pack_small(vectors, hidden_shift, table):
    lanes = lambda v: jnp.pad(v.astype(jnp.float32), ((0, 0), (0, PACK_LANES - v.shape[1])))
    rows = jnp.concatenate([lanes(jnp.stack(vectors)), lanes(hidden_shift[None]), lanes(table.reshape(3, -1))])
    rows = jnp.pad(rows, ((0, PACK_ROWS - rows.shape[0]), (0, 0)))
    return jnp.concatenate([rows[:8], rows[8:]], axis=1)


def unpack_small(block, count, hidden, table_shape):
    rows = jnp.concatenate([block[:, :, :PACK_LANES], block[:, :, PACK_LANES:]], axis=1)
    devices = rows.shape[0]
    vectors = jnp.transpose(rows[:, :10, :count], (1, 0, 2)).reshape(10, devices * count)
    table = rows[:, 11:14, : table_shape[0] * table_shape[1] // 3].reshape(devices * table_shape[0], table_shape[1])
    return (vectors, rows[:, 10, :hidden].reshape(devices * hidden), table)


def gather_params(devices, vectors, hidden_shift, table, weights):
    if devices != 32:
        whole = lambda v: lax.all_gather(v, "fsdp", axis=0, tiled=True)
        return (
            [as_float(whole(v)) for v in vectors], as_float(whole(hidden_shift)), as_float(whole(table)),
            [whole(w) for w in weights],
        )
    small, *full = gather_all([pack_small(vectors, hidden_shift, table)] + list(weights))
    stacked, hidden_full, table_full = unpack_small(
        small.reshape((devices,) + small.shape[4:]), vectors[0].shape[0], hidden_shift.shape[0], table.shape
    )
    full = [f.reshape((devices * f.shape[4], f.shape[5])) for f in full]
    return ([stacked[k] for k in range(10)], hidden_full, table_full, full)


def scatter_grads(vectors, hidden_shift, table, weights):
    share = lambda v: lax.psum_scatter(as_float(v), "fsdp", scatter_dimension=0, tiled=True)
    return ([share(v) for v in vectors], share(hidden_shift), share(table), [share(w) for w in weights])


def slot_rows(values, slot, seq):
    crops, length, features = values.shape
    per_pack = seq // slot
    values = jnp.pad(values, ((0, 0), (0, slot - length), (0, 0)))
    values = values.reshape(crops // per_pack, per_pack * slot, features)
    return jnp.pad(values, ((0, 0), (0, seq - per_pack * slot), (0, 0)))


def crop_rows(packed, slot, crops, length):
    packs, seq, features = packed.shape
    per_pack = seq // slot
    return packed[:, : per_pack * slot].reshape(crops, slot, features)[:, :length]


def per_device(
    x_global, x_local, cot_global, cot_local, global_count, local_count, index_global, index_local,
    ln1_gain, ln1_bias, qkv_weight, q_bias, v_bias, proj_weight, proj_bias, gamma1, bias_table,
    ln2_gain, ln2_bias, fc1_weight, fc1_bias, fc2_weight, fc2_bias, gamma2,
):
    glob, glob_len, features = x_global.shape
    loc, loc_len = x_local.shape[:2]
    heads = bias_table.shape[1]
    seq = round_up(glob_len, 16)
    slot = round_up(loc_len, 8)
    per_pack = seq // slot
    packs = glob + loc // per_pack
    devices = lax.axis_size("fsdp")
    small_full, hidden_full, table_full, (qkv_full, proj_full, fc1_full, fc2_full) = gather_params(
        devices,
        [ln1_gain, ln1_bias, q_bias, v_bias, proj_bias, gamma1, ln2_gain, ln2_bias, fc2_bias, gamma2],
        fc1_bias,
        bias_table,
        [qkv_weight, proj_weight, fc1_weight, fc2_weight],
    )
    vectors = jnp.pad(jnp.stack(small_full), ((0, 6), (0, 0)))
    table_rows = table_full.shape[0]
    table = jnp.pad(table_full.T, ((0, round_up(heads, 16) - heads), (0, 0))).astype(jnp.bfloat16)
    sides = (math.isqrt(glob_len - 1), math.isqrt(loc_len - 1))
    grids = ((sides[0], glob_len, 1, seq), (sides[1], loc_len, per_pack, slot))

    glob_keep = jnp.repeat((jnp.arange(glob, dtype=jnp.int32) < global_count[0]).astype(jnp.float32), seq)
    loc_keep = jnp.repeat((jnp.arange(loc, dtype=jnp.int32) < local_count[0]).astype(jnp.float32), slot)
    loc_keep = jnp.pad(loc_keep.reshape(-1, per_pack * slot), ((0, 0), (0, seq - per_pack * slot))).reshape(-1)
    keep = jnp.concatenate([glob_keep, loc_keep])[:, None]
    rows_of = lambda g, l: jnp.concatenate([slot_rows(g, seq, seq), slot_rows(l, slot, seq)]).reshape(-1, features)
    x = rows_of(x_global, x_local)
    cot = rows_of(cot_global, cot_local)

    indices = (index_global, index_local)
    bias = expand_bias(table, indices, grids, heads, seq)
    lanes = bias.shape[-1]
    normed, qkv, probs, mixed, attn, resid = attend_forward(
        x, qkv_full, proj_full, vectors, bias, packs, glob, heads
    )
    out, gres, gfc1, gfc2, gfc1_shift, small_two = mlp_both(
        resid, cot, keep, vectors, fc1_full, hidden_full[None], fc2_full, x_global.dtype, jnp.bfloat16
    )
    if devices == 32:
        shaped = lambda g: g.reshape(GRID + (g.shape[0] // devices, g.shape[1]))
        gx, *shares, small = attend_back(
            x, normed, qkv, probs, mixed, attn, gres, qkv_full, proj_full, vectors, small_two, gfc1_shift, indices,
            shaped(gfc1), shaped(gfc2), packs, glob, heads, grids, table_rows, x_global.dtype, lanes,
        )
        sums = [small[k, : features // devices] for k in range(10)]
        hidden_sum = small[10, : fc1_bias.shape[0]]
        table_sum = small[:heads, 128 : 128 + table_rows // devices].T
    else:
        gx, gqkv, gproj, bias_sums, small_one, gqkv_shift = attend_backward(
            x, normed, qkv, probs, mixed, attn, gres, qkv_full, proj_full, vectors, packs, glob, heads,
            x_global.dtype, jnp.bfloat16, lanes,
        )
        gtable = collect_bias(bias_sums, indices, grids, table_rows).T
        vector_grads = [
            small_one[0], small_one[1], gqkv_shift[0, :features], gqkv_shift[0, 2 * features :], small_one[2],
            small_one[3], small_two[0], small_two[1], small_two[2], small_two[3],
        ]
        sums, hidden_sum, table_sum, shares = scatter_grads(
            vector_grads, gfc1_shift[0], gtable, [gqkv, gproj, gfc1, gfc2]
        )
    out = out.reshape(packs, seq, features)
    gx = gx.reshape(packs, seq, features)
    return (
        crop_rows(out[:glob], seq, glob, glob_len),
        crop_rows(out[glob:], slot, loc, loc_len),
        crop_rows(gx[:glob], seq, glob, glob_len),
        crop_rows(gx[glob:], slot, loc, loc_len),
        sums[0], sums[1], shares[0], sums[2], sums[3], shares[1], sums[4], sums[5], table_sum,
        sums[6], sums[7], shares[2], hidden_sum, shares[3], sums[8], sums[9],
    )


def solution(mesh):
    placed = (
        P("fsdp", None, None),
        P("fsdp", None, None),
        P("fsdp", None, None),
        P("fsdp", None, None),
        P("fsdp"),
        P("fsdp"),
        P(),
        P(),
        P("fsdp"),
        P("fsdp"),
        P("fsdp", None),
        P("fsdp"),
        P("fsdp"),
        P("fsdp", None),
        P("fsdp"),
        P("fsdp"),
        P("fsdp", None),
        P("fsdp"),
        P("fsdp"),
        P("fsdp", None),
        P("fsdp"),
        P("fsdp", None),
        P("fsdp"),
        P("fsdp"),
    )
    return jax.shard_map(
        per_device,
        mesh=mesh,
        in_specs=placed,
        out_specs=(
            P("fsdp", None, None),
            P("fsdp", None, None),
            P("fsdp", None, None),
            P("fsdp", None, None),
            P("fsdp"),
            P("fsdp"),
            P("fsdp", None),
            P("fsdp"),
            P("fsdp"),
            P("fsdp", None),
            P("fsdp"),
            P("fsdp"),
            P("fsdp", None),
            P("fsdp"),
            P("fsdp"),
            P("fsdp", None),
            P("fsdp"),
            P("fsdp", None),
            P("fsdp"),
            P("fsdp"),
        ),
        check_vma=False,
    )
```

```python
import functools
import math

import jax
import jax.numpy as jnp
from jax import lax
from jax.experimental import pallas as pl
from jax.experimental.pallas import tpu as pltpu
from jax.sharding import PartitionSpec as P

EPSILON = 1e-06
NEG = -1e30
ROWS_IN = (((0,), (0,)), ((), ()))
COLS_IN = (((1,), (1,)), ((), ()))
BIG = 60 * 1024 * 1024


def as_float(values):
    return values.astype(jnp.float32)


def dot(a, b):
    return jnp.dot(a, b, preferred_element_type=jnp.float32)


def dot_tn(a, b):
    return lax.dot_general(a, b, ROWS_IN, preferred_element_type=jnp.float32)


def dot_nt(a, b):
    return lax.dot_general(a, b, COLS_IN, preferred_element_type=jnp.float32)


def round_up(value, unit):
    return (value + unit - 1) // unit * unit


def unit_rows(values):
    average = jnp.mean(values, axis=-1, keepdims=True)
    centered = values - average
    spread = lax.rsqrt(jnp.mean(centered * centered, axis=-1, keepdims=True) + EPSILON)
    return (centered * spread, spread)


def unit_back(grad, unit, spread):
    return spread * (
        grad - jnp.mean(grad, axis=-1, keepdims=True) - unit * jnp.mean(grad * unit, axis=-1, keepdims=True)
    )


def column_sum(values):
    return jnp.sum(values, axis=0, keepdims=True)


V_LN1G, V_LN1B, V_QB, V_VB, V_PB, V_G1, V_LN2G, V_LN2B, V_FB, V_G2 = range(10)


def mlp_kernel(
    steps, blocks, resid_ref, cot_ref, keep_ref, vec_ref, w1_ref, b1_ref, w2_ref,
    out_ref, gres_ref, gw1_ref, gw2_ref, gb1_ref, small_ref,
    normed, gbranch, branch, gnorm, active, ghidden,
):
    step = pl.program_id(0)
    rows, features = resid_ref.shape
    size = rows // blocks
    vec = lambda k: vec_ref[pl.ds(k, 1), :]

    @pl.when(step == 0)
    def _():
        @pl.loop(0, blocks)
        def _(i):
            part = pl.ds(pl.multiple_of(i * size, size), size)
            unit, _ = unit_rows(resid_ref[part, :])
            normed[part, :] = (unit * vec(V_LN2G) + vec(V_LN2B)).astype(jnp.bfloat16)
            grad = as_float(cot_ref[part, :]) * keep_ref[part, :]
            gbranch[part, :] = (vec(V_G2) * grad).astype(jnp.bfloat16)

    w1, w2 = w1_ref[...], w2_ref[...]
    hidden_sum = jnp.zeros_like(b1_ref)

    def block(i, hidden_sum):
        part = pl.ds(pl.multiple_of(i * size, size), size)
        hidden = dot(normed[part, :], w1) + b1_ref[...]
        phi = 0.5 * lax.erf(hidden * (0.5**0.5)) + 0.5
        low = (hidden * phi).astype(jnp.bfloat16)
        active[part, :] = low
        slope = phi + hidden * (jnp.exp(hidden * hidden * -0.5) * 0.3989422804014327)
        add = dot(low, w2)
        grad = dot_nt(gbranch[part, :], w2) * slope
        glow = grad.astype(jnp.bfloat16)
        ghidden[part, :] = glow
        gadd = dot_nt(glow, w1)

        @pl.when(step == 0)
        def _():
            branch[part, :] = add
            gnorm[part, :] = gadd

        @pl.when(step > 0)
        def _():
            branch[part, :] = branch[part, :] + add
            gnorm[part, :] = gnorm[part, :] + gadd

        return hidden_sum + column_sum(as_float(glow))

    gb1_ref[...] = lax.fori_loop(0, blocks, block, jnp.zeros(gb1_ref.shape, jnp.float32))
    gw2_ref[...] = dot_tn(active[...], gbranch[...]).astype(gw2_ref.dtype)
    gw1_ref[...] = dot_tn(normed[...], ghidden[...]).astype(gw1_ref.dtype)

    @pl.when(step == steps - 1)
    def _():
        zero = jnp.zeros((1, features), jnp.float32)

        def block(i, sums):
            part = pl.ds(pl.multiple_of(i * size, size), size)
            keep = keep_ref[part, :]
            resid = resid_ref[part, :]
            full = branch[part, :] + vec(V_FB)
            out_ref[part, :] = ((resid + vec(V_G2) * full) * keep).astype(out_ref.dtype)
            grad = as_float(cot_ref[part, :]) * keep
            unit, spread = unit_rows(resid)
            gn = gnorm[part, :]
            gres_ref[part, :] = grad + unit_back(gn * vec(V_LN2G), unit, spread)
            return (
                sums[0] + column_sum(gn * unit),
                sums[1] + column_sum(gn),
                sums[2] + column_sum(as_float(gbranch[part, :])),
                sums[3] + column_sum(grad * full),
            )

        sums = lax.fori_loop(0, blocks, block, (zero,) * 4)
        small_ref[...] = jnp.zeros_like(small_ref)
        for k in range(4):
            small_ref[pl.ds(k, 1), :] = sums[k]


def mlp_both(resid, cot, keep, vectors, w1, b1, w2, out_dtype, grad_dtype):
    rows, features = resid.shape
    hidden = w1.shape[1]
    chunk = 1024
    steps = hidden // chunk
    whole = lambda shape: pl.BlockSpec(shape, lambda j: (0,) * len(shape), pipeline_mode=pl.Buffered(1))
    return pl.pallas_call(
        functools.partial(mlp_kernel, steps, 3),
        grid=(steps,),
        out_shape=[
            jax.ShapeDtypeStruct((rows, features), out_dtype),
            jax.ShapeDtypeStruct((rows, features), jnp.float32),
            jax.ShapeDtypeStruct((features, hidden), grad_dtype),
            jax.ShapeDtypeStruct((hidden, features), grad_dtype),
            jax.ShapeDtypeStruct((1, hidden), jnp.float32),
            jax.ShapeDtypeStruct((8, features), jnp.float32),
        ],
        in_specs=[
            whole((rows, features)),
            whole((rows, features)),
            whole((rows, 1)),
            whole(vectors.shape),
            pl.BlockSpec((features, chunk), lambda j: (0, j)),
            pl.BlockSpec((1, chunk), lambda j: (0, j)),
            pl.BlockSpec((chunk, features), lambda j: (j, 0)),
        ],
        out_specs=[
            whole((rows, features)),
            whole((rows, features)),
            pl.BlockSpec((features, chunk), lambda j: (0, j)),
            pl.BlockSpec((chunk, features), lambda j: (j, 0)),
            pl.BlockSpec((1, chunk), lambda j: (0, j)),
            whole((8, features)),
        ],
        scratch_shapes=[
            pltpu.VMEM((rows, features), jnp.bfloat16),
            pltpu.VMEM((rows, features), jnp.bfloat16),
            pltpu.VMEM((rows, features), jnp.float32),
            pltpu.VMEM((rows, features), jnp.float32),
            pltpu.VMEM((rows, chunk), jnp.bfloat16),
            pltpu.VMEM((rows, chunk), jnp.bfloat16),
        ],
        compiler_params=pltpu.CompilerParams(vmem_limit_bytes=BIG),
        name="mlp_both",
    )(resid, cot, keep, vectors, w1, b1, w2)


def lane_of(shape):
    return lax.broadcasted_iota(jnp.int32, shape, 1)


def roll_lanes(values, shift):
    shift = shift % values.shape[1]
    return pltpu.roll(values, shift, 1) if shift else values


def corner_rows(side):
    return (1, side, 1 + (side - 1) * side, side * side)


def expand(grids, table_ref, index_refs, bias_refs, row_refs):
    for n, (side, seq, copies, slot) in enumerate(grids):
        index_ref, bias_ref, row_ref = index_refs[n], bias_refs[n], row_refs[n]
        heads, lanes = bias_ref.shape[0], bias_ref.shape[2]
        tables = lax.broadcasted_iota(jnp.int32, (table_ref.shape[1], lanes), 0)

        def pick(row):
            picked = index_ref[pl.ds(row, 1), :] == tables
            return dot(table_ref[...].astype(jnp.bfloat16), picked.astype(jnp.bfloat16))

        corners = [pick(row) for row in corner_rows(side)]
        lane = lane_of(corners[0].shape)
        within = (lane + (side - 1)) % side
        for c in range(side):
            for top in range(2):
                left, right = corners[2 * top], corners[2 * top + 1]
                row = jnp.where(within >= c, roll_lanes(left, c), roll_lanes(right, c - (side - 1)))
                row = jnp.where(lane == 0, left, row)
                row_ref[top, :, pl.ds(c, 1), :] = row[:heads].reshape(heads, 1, lanes)
        row_ref[0, :, pl.ds(side, 1), :] = pick(0)[:heads].reshape(heads, 1, lanes)
        lane = lane_of((side, lanes))

        def spread(values, at):
            if copies > 1:
                values = roll_lanes(values, at * slot)
            where = lane_of(values.shape) - at * slot
            return jnp.where((where >= 0) & (where < seq), values, NEG)

        @pl.loop(0, heads)
        def _(h):
            bias_ref[h] = jnp.full(bias_ref.shape[1:], NEG, jnp.float32)
            low, high, first = row_ref[0, h, :side], row_ref[1, h, :side], row_ref[0, h, pl.ds(side, 1)]
            for at in range(copies):
                bias_ref[h, pl.ds(at * slot, 1), :] = spread(first, at)
            for r in range(side):
                rows = jnp.where(
                    lane - 1 < side * (r + 1), roll_lanes(high, -side * (side - 1 - r)), roll_lanes(low, side * r)
                )
                rows = jnp.where(lane == 0, low, rows)
                for at in range(copies):
                    bias_ref[h, pl.ds(at * slot + 1 + side * r, side), :] = spread(rows, at)


def collect(grids, sum_refs, index_refs, row_refs, shape):
    total = jnp.zeros(shape, jnp.float32)
    for n, (side, seq, copies, slot) in enumerate(grids):
        index_ref, sum_ref, row_ref = index_refs[n], sum_refs[n], row_refs[n]
        heads, lanes = sum_ref.shape[0], sum_ref.shape[2]
        lane = lane_of((side, lanes))

        def gathered(h, start, size):
            rows = None
            for at in range(copies):
                piece = roll_lanes(sum_ref[h, pl.ds(at * slot + start, size), :], -at * slot)
                rows = piece if rows is None else rows + piece
            return jnp.where(lane_of((size, lanes)) < seq, rows, 0.0) if copies > 1 else rows

        @pl.loop(0, heads)
        def _(h):
            low = jnp.zeros((side, lanes), jnp.float32)
            high = jnp.zeros((side, lanes), jnp.float32)
            for r in range(side):
                rows = gathered(h, 1 + side * r, side)
                is_low = lane - 1 >= side * (r + 1)
                is_high = (lane >= 1) & (lane - 1 < side * (r + 1))
                low = low + roll_lanes(jnp.where(is_low, rows, 0.0), -side * r) + jnp.where(lane == 0, rows, 0.0)
                high = high + roll_lanes(jnp.where(is_high, rows, 0.0), side * (side - 1 - r))
            row_ref[0, h, :side], row_ref[1, h, :side] = low, high
            row_ref[0, h, pl.ds(side, 1)] = gathered(h, 0, 1)

        flat = lane_of((heads, lanes))
        within = (flat + (side - 1)) % side
        corners = [jnp.zeros((heads, lanes), jnp.float32) for _ in range(4)]
        for c in range(side):
            for top in range(2):
                row = row_ref[top, :, pl.ds(c, 1), :].reshape(heads, lanes)
                is_left = (flat >= 1) & (within >= c)
                is_right = (flat >= 1) & (within < c)
                left = roll_lanes(jnp.where(is_left, row, 0.0), -c) + jnp.where(flat == 0, row, 0.0)
                corners[2 * top] = corners[2 * top] + left
                corners[2 * top + 1] = corners[2 * top + 1] + roll_lanes(jnp.where(is_right, row, 0.0), side - 1 - c)
        tables = lax.broadcasted_iota(jnp.int32, (shape[1], lanes), 0)

        def place_sum(row, values):
            picked = (index_ref[pl.ds(row, 1), :] == tables).astype(jnp.bfloat16)
            top = values.astype(jnp.bfloat16)
            rest = values - as_float(top)
            middle = rest.astype(jnp.bfloat16)
            last = (rest - as_float(middle)).astype(jnp.bfloat16)
            return dot_nt(top, picked) + dot_nt(middle, picked) + dot_nt(last, picked)

        for row, values in zip(corner_rows(side), corners):
            total = total + place_sum(row, values)
        total = total + place_sum(0, row_ref[0, :, pl.ds(side, 1), :].reshape(heads, lanes))
    return total


ROW_SLOTS = 16


def expand_kernel(grids, table_ref, index_g, index_l, bias_ref, rows_g, rows_l):
    expand(grids, table_ref, (index_g, index_l), (bias_ref.at[0], bias_ref.at[1]), (rows_g, rows_l))


def pad_index(indices, lanes):
    return [jnp.pad(i, ((0, 0), (0, lanes - i.shape[1])), constant_values=-1) for i in indices]


def expand_bias(table, indices, grids, heads, seq):
    lanes = round_up(seq, 128)
    return pl.pallas_call(
        functools.partial(expand_kernel, grids),
        out_shape=jax.ShapeDtypeStruct((2, heads, seq, lanes), jnp.float32),
        scratch_shapes=[pltpu.VMEM((2, heads, ROW_SLOTS, lanes), jnp.float32)] * 2,
        compiler_params=pltpu.CompilerParams(vmem_limit_bytes=BIG),
        name="expand_bias",
    )(table, *pad_index(indices, lanes))


def collect_kernel(grids, index_g, index_l, sums_ref, grad_ref, rows_g, rows_l):
    grad_ref[...] = collect(
        grids, (sums_ref.at[0], sums_ref.at[1]), (index_g, index_l), (rows_g, rows_l), grad_ref.shape
    )


def collect_bias(sums, indices, grids, table_rows):
    _, heads, _, lanes = sums.shape
    return pl.pallas_call(
        functools.partial(collect_kernel, grids),
        out_shape=jax.ShapeDtypeStruct((heads, table_rows), jnp.float32),
        scratch_shapes=[pltpu.VMEM((2, heads, ROW_SLOTS, lanes), jnp.float32)] * 2,
        compiler_params=pltpu.CompilerParams(vmem_limit_bytes=BIG),
        name="collect_bias",
    )(*pad_index(indices, lanes), sums)


def head_lanes(shape, width):
    return lax.broadcasted_iota(jnp.int32, shape, 1) < width


def stack_heads(pair, width):
    first = head_lanes(pair.shape, width)
    zero = jnp.zeros_like(pair)
    return jnp.concatenate([jnp.where(first, pair, zero), jnp.where(first, zero, pair)], axis=0)


def merge_heads(stacked, width):
    rows = stacked.shape[0] // 2
    top, low = stacked[:rows], stacked[rows:]
    return jnp.where(head_lanes(top.shape, width), top, low)


def attend_kernel(
    glob, heads, x_ref, wqkv_ref, wproj_ref, vec_ref, bias_ref,
    normed_ref, qkv_ref, probs_ref, mixed_ref, attn_ref, resid_ref,
):
    seq, features = x_ref.shape
    width = features // heads
    vec = lambda k: vec_ref[pl.ds(k, 1), :]
    inputs = as_float(x_ref[...])
    unit, _ = unit_rows(inputs)
    normed = (unit * vec(V_LN1G) + vec(V_LN1B)).astype(jnp.bfloat16)
    normed_ref[...] = normed
    qkv_ref[:, pl.ds(0, features)] = (dot(normed, wqkv_ref[:, pl.ds(0, features)]) + vec(V_QB)).astype(jnp.bfloat16)
    qkv_ref[:, pl.ds(features, features)] = dot(normed, wqkv_ref[:, pl.ds(features, features)]).astype(jnp.bfloat16)
    qkv_ref[:, pl.ds(2 * features, features)] = (
        dot(normed, wqkv_ref[:, pl.ds(2 * features, features)]) + vec(V_VB)
    ).astype(jnp.bfloat16)

    for pair in range(heads // 2):
        at = 2 * width * pair
        queries = stack_heads(qkv_ref[:, pl.ds(at, 2 * width)], width)
        keys = qkv_ref[:, pl.ds(features + at, 2 * width)]
        values = qkv_ref[:, pl.ds(2 * features + at, 2 * width)]
        bias = bias_ref[0, pl.ds(2 * pair, 2), :, pl.ds(0, seq)].reshape(2 * seq, seq)
        scores = dot_nt(queries, keys) * (width**-0.5) + bias
        weights = jnp.exp(scores - jnp.max(scores, axis=-1, keepdims=True))
        probs = (weights * (1.0 / jnp.sum(weights, axis=-1, keepdims=True))).astype(jnp.bfloat16)
        probs_ref[0, pair] = probs
        mixed_ref[:, pl.ds(at, 2 * width)] = merge_heads(dot(probs, values), width).astype(jnp.bfloat16)

    attn = dot(mixed_ref[...], wproj_ref[...]) + vec(V_PB)
    attn_ref[...] = attn.astype(jnp.bfloat16)
    resid_ref[...] = inputs + vec(V_G1) * attn


def attend_forward(x, wqkv, wproj, vectors, bias, packs, glob, heads):
    rows, features = x.shape
    seq = rows // packs
    whole = lambda shape: pl.BlockSpec(shape, lambda p: (0,) * len(shape), pipeline_mode=pl.Buffered(1))
    by_rows = lambda cols: pl.BlockSpec((seq, cols), lambda p: (p, 0))
    return pl.pallas_call(
        functools.partial(attend_kernel, glob, heads),
        grid=(packs,),
        out_shape=[
            jax.ShapeDtypeStruct((rows, features), jnp.bfloat16),
            jax.ShapeDtypeStruct((rows, 3 * features), jnp.bfloat16),
            jax.ShapeDtypeStruct((packs, heads // 2, 2 * seq, seq), jnp.bfloat16),
            jax.ShapeDtypeStruct((rows, features), jnp.bfloat16),
            jax.ShapeDtypeStruct((rows, features), jnp.bfloat16),
            jax.ShapeDtypeStruct((rows, features), jnp.float32),
        ],
        in_specs=[
            by_rows(features),
            whole(wqkv.shape),
            whole(wproj.shape),
            whole(vectors.shape),
            pl.BlockSpec((1,) + bias.shape[1:], lambda p: (jnp.where(p < glob, 0, 1), 0, 0, 0)),
        ],
        out_specs=[
            by_rows(features),
            by_rows(3 * features),
            pl.BlockSpec((1, heads // 2, 2 * seq, seq), lambda p: (p, 0, 0, 0)),
            by_rows(features),
            by_rows(features),
            by_rows(features),
        ],
        compiler_params=pltpu.CompilerParams(vmem_limit_bytes=BIG),
        name="attend_forward",
    )(x, wqkv, wproj, vectors, bias)


def attend_back_kernel(
    packs, glob, heads, chunk, x_ref, normed_ref, qkv_ref, probs_ref, mixed_ref, attn_ref, gres_ref, wqkv_ref, wproj_ref, vec_ref,
    gx_ref, gwqkv_ref, gwproj_ref, bsum_ref, small_ref, gqb_ref,
    normed_all, mixed_all, gattn_all, gqkv_all,
):
    step = pl.program_id(0)
    seq, features = x_ref.shape
    width = features // heads
    vec = lambda k: vec_ref[pl.ds(k, 1), :]
    rows = packs * seq

    @pl.when(step == 0)
    def _():
        small_ref[...] = jnp.zeros_like(small_ref)
        gqb_ref[...] = jnp.zeros_like(gqb_ref)

    @pl.when((step == 0) | (step == glob))
    def _():
        bsum_ref[...] = jnp.zeros_like(bsum_ref)

    @pl.when(step < packs)
    def _():
        part = pl.ds(pl.multiple_of(step * seq, seq), seq)
        gres = gres_ref[...]
        gattn = (vec(V_G1) * gres).astype(jnp.bfloat16)
        gattn_all[part, :] = gattn
        mixed_all[part, :] = mixed_ref[...]
        normed_all[part, :] = normed_ref[...]
        small_ref[pl.ds(2, 1), :] += column_sum(as_float(gattn))
        small_ref[pl.ds(3, 1), :] += column_sum(gres * as_float(attn_ref[...]))
        gmixed = dot_nt(gattn, wproj_ref[...]).astype(jnp.bfloat16)
        scale = width**-0.5
        for pair in range(heads // 2):
            at = 2 * width * pair
            queries = stack_heads(qkv_ref[:, pl.ds(at, 2 * width)], width)
            keys = qkv_ref[:, pl.ds(features + at, 2 * width)]
            values = qkv_ref[:, pl.ds(2 * features + at, 2 * width)]
            grads = stack_heads(gmixed[:, at : at + 2 * width], width)
            mixed = as_float(mixed_ref[:, pl.ds(at, 2 * width)])
            probs = probs_ref[0, pair]
            twice = jnp.concatenate([mixed, mixed], axis=0)
            inner = jnp.sum(as_float(grads) * twice, axis=-1, keepdims=True)
            gscores = as_float(probs) * (dot_nt(grads, values) - inner)
            bsum_ref[0, pl.ds(2 * pair, 2), :, pl.ds(0, seq)] += gscores.reshape(2, seq, seq)
            low = gscores.astype(jnp.bfloat16)
            gqkv_all[part, pl.ds(at, 2 * width)] = (merge_heads(dot(low, keys), width) * scale).astype(jnp.bfloat16)
            gqkv_all[part, pl.ds(features + at, 2 * width)] = (dot_tn(low, queries) * scale).astype(jnp.bfloat16)
            gqkv_all[part, pl.ds(2 * features + at, 2 * width)] = dot_tn(probs, grads).astype(jnp.bfloat16)
        gqkv = gqkv_all[part, :]
        gqb_ref[...] += column_sum(as_float(gqkv))
        gnorm = dot_nt(gqkv, wqkv_ref[...])
        unit, spread = unit_rows(as_float(x_ref[...]))
        small_ref[pl.ds(0, 1), :] += column_sum(gnorm * unit)
        small_ref[pl.ds(1, 1), :] += column_sum(gnorm)
        gx_ref[...] = (gres + unit_back(gnorm * vec(V_LN1G), unit, spread)).astype(gx_ref.dtype)

    @pl.when(step >= packs)
    def _():
        j = step - packs
        wide = 3 * features // chunk

        @pl.when(j < wide)
        def _():
            gwqkv_ref[...] = dot_tn(normed_all[...], gqkv_all[:, pl.ds(pl.multiple_of(j * chunk, chunk), chunk)]).astype(gwqkv_ref.dtype)

        @pl.when(j >= wide)
        def _():
            gwproj_ref[...] = dot_tn(mixed_all[...], gattn_all[:, pl.ds(pl.multiple_of((j - wide) * chunk, chunk), chunk)]).astype(gwproj_ref.dtype)


def attend_backward(x, normed, qkv, probs, mixed, attn, gres, wqkv, wproj, vectors, packs, glob, heads, out_dtype, grad_dtype, lanes):
    rows, features = x.shape
    seq = rows // packs
    chunk = 256
    wide, narrow = 3 * features // chunk, features // chunk
    whole = lambda shape: pl.BlockSpec(shape, lambda s: (0,) * len(shape), pipeline_mode=pl.Buffered(1))
    pack = lambda s: jnp.minimum(s, packs - 1)
    by_rows = lambda cols: pl.BlockSpec((seq, cols), lambda s: (pack(s), 0))
    return pl.pallas_call(
        functools.partial(attend_back_kernel, packs, glob, heads, chunk),
        grid=(packs + wide + narrow,),
        out_shape=[
            jax.ShapeDtypeStruct((rows, features), out_dtype),
            jax.ShapeDtypeStruct((features, 3 * features), grad_dtype),
            jax.ShapeDtypeStruct((features, features), grad_dtype),
            jax.ShapeDtypeStruct((2, heads, seq, lanes), jnp.float32),
            jax.ShapeDtypeStruct((8, features), jnp.float32),
            jax.ShapeDtypeStruct((1, 3 * features), jnp.float32),
        ],
        in_specs=[
            by_rows(features),
            by_rows(features),
            by_rows(3 * features),
            pl.BlockSpec((1, heads // 2, 2 * seq, seq), lambda s: (pack(s), 0, 0, 0)),
            by_rows(features),
            by_rows(features),
            by_rows(features),
            whole(wqkv.shape),
            whole(wproj.shape),
            whole(vectors.shape),
        ],
        out_specs=[
            by_rows(features),
            pl.BlockSpec((features, chunk), lambda s: (0, jnp.clip(s - packs, 0, wide - 1))),
            pl.BlockSpec((features, chunk), lambda s: (0, jnp.clip(s - packs - wide, 0, narrow - 1))),
            pl.BlockSpec((1, heads, seq, lanes), lambda s: (jnp.where(s < glob, 0, 1), 0, 0, 0)),
            whole((8, features)),
            whole((1, 3 * features)),
        ],
        scratch_shapes=[
            pltpu.VMEM((rows, features), jnp.bfloat16),
            pltpu.VMEM((rows, features), jnp.bfloat16),
            pltpu.VMEM((rows, features), jnp.bfloat16),
            pltpu.VMEM((rows, 3 * features), jnp.bfloat16),
        ],
        compiler_params=pltpu.CompilerParams(vmem_limit_bytes=BIG),
        name="attend_backward",
    )(x, normed, qkv, probs, mixed, attn, gres, wqkv, wproj, vectors)


MESH = pl.DeviceIdType.MESH
LINE = 4
GRID = (LINE, 2, 2, 2)
EVERY = slice(None)


def place():
    me = lax.axis_index("fsdp")
    return (me // 8, (me // 4) % 2, (me // 2) % 2, me % 2)


def device_at(z, y, x, c):
    return (((z * 2 + y) * 2 + x) * 2 + c,)


def along(z, k):
    return (z + k) % LINE


def greet():
    z, y, x, c = place()
    barrier = pltpu.get_barrier_semaphore()
    peers = [device_at(z, y, x, 1 - c), device_at(z, y, 1 - x, c), device_at(z, 1 - y, x, c)]
    peers += [device_at(along(z, k), y, x, c) for k in range(1, LINE)]
    for peer in peers:
        pl.semaphore_signal(barrier, inc=1, device_id=peer, device_id_type=MESH)
    pl.semaphore_wait(barrier, len(peers))


def remote(src, dst, send, recv, peer):
    return pltpu.make_async_remote_copy(
        src_ref=src, dst_ref=dst, send_sem=send, recv_sem=recv, device_id=peer, device_id_type=MESH
    )


class Gather:
    STAGES = 5
    SEMS = 12

    def __init__(self, own, full, send, recv):
        self.own, self.full, self.send, self.recv = own, full, send, recv
        self.z, self.y, self.x, self.c = place()
        self.cols = full.shape[-1] // 2

    def line_copy(self, k, source=None):
        z, y, x, c = self.z, self.y, self.x, self.c
        held = z if source is None else source
        peer = device_at(along(z, k), y, x, c)
        return remote(self.own, self.full.at[held, y, x, c], self.send.at[k - 1], self.recv.at[k - 1], peer)

    def copy(self, name):
        z, y, x, c = self.z, self.y, self.x, self.c
        over_x, over_y, pair = device_at(z, y, 1 - x, c), device_at(z, 1 - y, x, c), device_at(z, y, x, 1 - c)
        k, part, half, peer = {
            "near0": (3, (EVERY, y, x, c), 0, over_x),
            "near1": (4, (EVERY, y, x, c), 1, over_y),
            "far0": (5, (EVERY, y, EVERY, c), 0, over_y),
            "far1": (6, (EVERY, EVERY, x, c), 1, over_x),
            "pair": (7, (EVERY, y, x, c), None, pair),
            "pair0": (8, (EVERY, y, 1 - x, c), 0, pair),
            "pair1": (9, (EVERY, 1 - y, x, c), 1, pair),
            "pair2": (10, (EVERY, 1 - y, EVERY, c), 0, pair),
            "pair3": (11, (EVERY, EVERY, 1 - x, c), 1, pair),
        }[name]
        ref = self.full.at[part if half is None else part + (EVERY, pl.ds(half * self.cols, self.cols))]
        return remote(ref, ref, self.send.at[k], self.recv.at[k], peer)

    def mine(self):
        return pltpu.make_async_copy(self.own, self.full.at[self.z, self.y, self.x, self.c], self.recv.at[self.SEMS])

    def stage(self, s):
        if s == 0:
            for k in range(1, LINE):
                self.line_copy(k).start()
            self.mine().start()
        elif s == 1:
            self.mine().wait()
            for k in range(1, LINE):
                self.line_copy(k, along(self.z, LINE - k)).wait_recv()
            for name in ("near0", "near1", "pair"):
                self.copy(name).start()
        elif s == 2:
            for k in ("0", "1"):
                self.copy("near" + k).wait_recv()
                self.copy("far" + k).start()
            self.copy("pair0").start()
            self.copy("pair1").start()
        elif s == 3:
            for k, far in ((2, 0), (3, 1)):
                self.copy("far%d" % far).wait_recv()
                self.copy("pair%d" % k).start()
        else:
            for name in ("pair", "pair0", "pair1", "pair2", "pair3"):
                self.copy(name).wait_recv()

    def drain(self):
        for k in range(1, LINE):
            self.line_copy(k).wait_send()
        for name in ("near0", "near1", "far0", "far1", "pair", "pair0", "pair1", "pair2", "pair3"):
            self.copy(name).wait_send()


class Scatter:
    STAGES = 5
    SEMS = 9

    def __init__(self, terms, own, bufs, send, recv, finish):
        self.terms, self.loaded = terms, own
        self.pairbuf, self.buf1a, self.buf1b, self.buf2a, self.buf2b, self.line = bufs
        self.send, self.recv, self.finish = send, recv, finish
        self.z, self.y, self.x, self.c = place()
        self.cols = terms.shape[-1] // 2

    BUFS = 6

    @staticmethod
    def scratch(shape, dtype):
        rows, cols = shape
        half = cols // 2
        return [
            pltpu.VMEM((LINE, 2, 2, rows, cols), dtype),
            pltpu.VMEM((LINE, 2, rows, half), dtype),
            pltpu.VMEM((LINE, 2, rows, half), dtype),
            pltpu.VMEM((LINE, rows, half), dtype),
            pltpu.VMEM((LINE, rows, half), dtype),
            pltpu.VMEM((LINE - 1, rows, cols), dtype),
        ]

    def at(self, i, j, k, half=None):
        cols = () if half is None else (EVERY, pl.ds(half * self.cols, self.cols))
        if self.loaded is None:
            return self.terms.at[(i, j, k, self.c) + cols]
        return self.loaded.at[(i, j, k) + cols]

    def load(self):
        return pltpu.make_async_copy(self.terms.at[EVERY, EVERY, EVERY, self.c], self.loaded, self.send.at[8])

    def copy(self, name):
        z, y, x, c = self.z, self.y, self.x, self.c
        over_x, over_y = device_at(z, y, 1 - x, c), device_at(z, 1 - y, x, c)
        k, src, dst, peer = {
            "pair": lambda: (0, self.terms.at[EVERY, EVERY, EVERY, 1 - c], self.pairbuf, device_at(z, y, x, 1 - c)),
            "1a": lambda: (1, self.at(EVERY, 1 - y, EVERY, 0), self.buf1a, over_y),
            "1b": lambda: (2, self.at(EVERY, EVERY, 1 - x, 1), self.buf1b, over_x),
            "2a": lambda: (3, self.at(EVERY, y, 1 - x, 0), self.buf2a, over_x),
            "2b": lambda: (4, self.at(EVERY, 1 - y, x, 1), self.buf2b, over_y),
        }[name]()
        return remote(src, dst, self.send.at[k], self.recv.at[k], peer)

    def line_copy(self, k):
        z, y, x, c = self.z, self.y, self.x, self.c
        target = along(z, k)
        return remote(
            self.at(target, y, x), self.line.at[k - 1], self.send.at[4 + k], self.recv.at[4 + k], device_at(target, y, x, c)
        )

    def add(self, ref, term):
        ref[...] = ref[...] + term

    def stage(self, s):
        z, y, x = self.z, self.y, self.x
        if s == 0:
            self.copy("pair").start()
            if self.loaded is not None:
                self.load().start()
        elif s == 1:
            if self.loaded is not None:
                self.load().wait()
            self.copy("pair").wait_recv()

            @pl.loop(0, LINE)
            def _(i):
                for j in range(2):
                    for k in range(2):
                        self.add(self.at(i, j, k), self.pairbuf[i, j, k])

            self.copy("1a").start()
            self.copy("1b").start()
        elif s == 2:
            self.copy("1a").wait_recv()
            self.copy("1b").wait_recv()

            @pl.loop(0, LINE)
            def _(i):
                for k in range(2):
                    self.add(self.at(i, y, k, 0), self.buf1a[i, k])
                    self.add(self.at(i, k, x, 1), self.buf1b[i, k])

            self.copy("2a").start()
            self.copy("2b").start()
        elif s == 3:
            self.copy("2a").wait_recv()
            self.copy("2b").wait_recv()

            @pl.loop(0, LINE)
            def _(i):
                self.add(self.at(i, y, x, 0), self.buf2a[i])
                self.add(self.at(i, y, x, 1), self.buf2b[i])

            for k in range(1, LINE):
                self.line_copy(k).start()
        else:
            total = as_float(self.at(z, y, x)[...])
            for k in range(1, LINE):
                self.line_copy(k).wait_recv()
                total = total + as_float(self.line[k - 1])
            self.finish(total)

    def drain(self):
        for name in ("pair", "1a", "1b", "2a", "2b"):
            self.copy(name).wait_send()
        for k in range(1, LINE):
            self.line_copy(k).wait_send()


SMALL = (16, 256)


def back_kernel(
    shape, plan, x_ref, normed_ref, q_ref, k_ref, v_ref, probs_ref, mixed_ref, attn_ref, gres_ref, wqkv_ref, wproj_ref, vec_ref,
    two_ref, hidden_ref, index_g, index_l, gfc1_ref, gfc2_ref,
    gx_ref, sqkv_ref, sproj_ref, sfc1_ref, sfc2_ref, ssmall_ref,
    gqkv, gmixed, bsum, vecs, tsum, corner, *scratch,
):
    packs, glob, heads, groups, blocks, grids = shape
    step = pl.program_id(0)
    rows, features = normed_ref.shape
    seq = rows // packs
    width = features // heads
    lanes = features // groups
    scale = width**-0.5
    vec = lambda k: vec_ref[pl.ds(k, 1), :]
    size = rows // blocks
    last = 1 + packs * groups + 1 + blocks

    send, recv = scratch[-2:]
    scratch = scratch[:-2]
    big = 2 * SPLIT
    owns = list(scratch[:big]) + [None] * (groups + 2)
    terms = scratch[big : big + groups + 2]
    bufs = scratch[big + groups + 2 :]

    def put(ref):
        def finish(value):
            ref[...] = value

        return finish

    def put_group(g):
        def finish(value):
            for i in range(3):
                sqkv_ref[:, pl.ds(i * features + g * lanes, lanes)] = value[:, i * lanes : (i + 1) * lanes]

        return finish

    tall, wide = gfc2_ref.shape[4] // SPLIT, gfc1_ref.shape[5] // SPLIT
    sources, ends = [], []
    for k in range(SPLIT):
        sources.append(gfc2_ref.at[EVERY, EVERY, EVERY, EVERY, pl.ds(k * tall, tall)])
        ends.append(put(sfc2_ref.at[pl.ds(k * tall, tall)]))
    for k in range(SPLIT):
        sources.append(gfc1_ref.at[EVERY, EVERY, EVERY, EVERY, EVERY, pl.ds(k * wide, wide)])
        ends.append(put(sfc1_ref.at[EVERY, pl.ds(k * wide, wide)]))
    sources += list(terms)
    ends += [put(sproj_ref)] + [put_group(g) for g in range(groups)] + [put(ssmall_ref)]
    flows = [
        Scatter(sources[t], owns[t], bufs[Scatter.BUFS * t : Scatter.BUFS * (t + 1)], send.at[t], recv.at[t], ends[t]) for t in range(len(ends))
    ]

    def slot(k):
        for t, s in plan[k]:
            flows[t].stage(s)

    def fill(t, value):
        ref = terms[t]
        count = ref.shape[-2]
        for d in range(LINE * 8):
            ref[d // 8, d // 4 % 2, d // 2 % 2, d % 2] = value[d * count : (d + 1) * count].astype(ref.dtype)

    @pl.when(step == 0)
    def _():
        greet()
        slot(0)
        zero = jnp.zeros((1, features), jnp.float32)
        vecs[...] = jnp.zeros_like(vecs)

        def block(i, sums):
            part = pl.ds(pl.multiple_of(i * size, size), size)
            gres = gres_ref[part, :]
            gattn = (vec(V_G1) * gres).astype(jnp.bfloat16)
            gqkv[part, pl.ds(0, features)] = gattn
            gmixed[part, :] = dot_nt(gattn, wproj_ref[...]).astype(jnp.bfloat16)
            return (sums[0] + column_sum(as_float(gattn)), sums[1] + column_sum(gres * as_float(attn_ref[part, :])))

        sums = lax.fori_loop(0, blocks, block, (zero, zero))
        vecs[pl.ds(V_PB, 1), :] = sums[0]
        vecs[pl.ds(V_G1, 1), :] = sums[1]
        bsum[...] = jnp.zeros_like(bsum)
        fill(0, dot_tn(mixed_ref[...], gqkv[:, pl.ds(0, features)]))

    @pl.when((step >= 1) & (step <= packs * groups))
    def _():
        pack = (step - 1) % packs
        group = (step - 1) // packs
        part = pl.ds(pl.multiple_of(pack * seq, seq), seq)
        kind = jnp.where(pack < glob, 0, 1)
        for pair in range(heads // 2 // groups):
            at = 2 * width * pair
            wide = pl.ds(pl.multiple_of(group * lanes + at, 2 * width), 2 * width)
            queries = stack_heads(q_ref[:, pl.ds(at, 2 * width)], width)
            keys = k_ref[:, pl.ds(at, 2 * width)]
            values = v_ref[:, pl.ds(at, 2 * width)]
            grads = stack_heads(gmixed[part, wide], width)
            mixed = as_float(mixed_ref[part, wide])
            probs = probs_ref[0, pair]
            twice = jnp.concatenate([mixed, mixed], axis=0)
            inner = jnp.sum(as_float(grads) * twice, axis=-1, keepdims=True)
            gscores = as_float(probs) * (dot_nt(grads, values) - inner)
            head = group * (heads // groups) + 2 * pair
            bsum[kind, pl.ds(head, 2), :, pl.ds(0, seq)] += gscores.reshape(2, seq, seq)
            low = gscores.astype(jnp.bfloat16)
            gq = (merge_heads(dot(low, keys), width) * scale).astype(jnp.bfloat16)
            gk = (dot_tn(low, queries) * scale).astype(jnp.bfloat16)
            gv = dot_tn(probs, grads).astype(jnp.bfloat16)
            for i, piece in enumerate((gq, gk, gv)):
                at_lane = pl.multiple_of(group * lanes + at + i * features, 2 * width)
                gqkv[part, pl.ds(at_lane, 2 * width)] = piece

    for g in range(groups):
        @pl.when(step == packs * (g + 1))
        def _():
            pieces = [dot_tn(normed_ref[...], gqkv[:, pl.ds(i * features + g * lanes, lanes)]) for i in range(3)]
            fill(1 + g, jnp.concatenate(pieces, axis=1))

    @pl.when(step == packs * groups + 1)
    def _():
        tsum[...] = collect(
            grids, (bsum.at[0], bsum.at[1]), (index_g, index_l), (corner, corner), tsum.shape
        )

    @pl.when(step >= packs * groups + 2)
    def _():
        i = step - packs * groups - 2
        part = pl.ds(pl.multiple_of(i * size, size), size)
        low = gqkv[part, :]
        gnorm = dot_nt(low, wqkv_ref[...])
        unit, spread = unit_rows(as_float(x_ref[...]))
        vecs[pl.ds(V_LN1G, 1), :] += column_sum(gnorm * unit)
        vecs[pl.ds(V_LN1B, 1), :] += column_sum(gnorm)
        total = column_sum(as_float(low))
        vecs[pl.ds(V_QB, 1), :] += total[:, :features]
        vecs[pl.ds(V_VB, 1), :] += total[:, 2 * features :]
        gx_ref[...] = (gres_ref[part, :] + unit_back(gnorm * vec(V_LN1G), unit, spread)).astype(gx_ref.dtype)

    @pl.when(step == last - 1)
    def _():
        for k, row in ((V_LN2G, 0), (V_LN2B, 1), (V_FB, 2), (V_G2, 3)):
            vecs[pl.ds(k, 1), :] = two_ref[pl.ds(row, 1), :]
        ref = terms[-1]
        ref[...] = jnp.zeros_like(ref)
        devices = LINE * 8
        count, wide, table = features // devices, hidden_ref.shape[1] // devices, tsum.shape[1] // devices
        for d in range(devices):
            block = ref.at[d // 8, d // 4 % 2, d // 2 % 2, d % 2]
            block[:, pl.ds(0, count)] = vecs[:, pl.ds(d * count, count)]
            block[pl.ds(10, 1), pl.ds(0, wide)] = hidden_ref[:, pl.ds(d * wide, wide)]
            block[pl.ds(0, heads), pl.ds(128, table)] = tsum[:, pl.ds(d * table, table)]

    for k in range(1, last):
        @pl.when(step == k)
        def _():
            slot(k)

    @pl.when(step == last - 1)
    def _():
        for flow in flows:
            flow.drain()


def back_plan(steps, groups, packs):
    plan = [[] for _ in range(steps)]
    done = steps - 1
    starts = list(PLAN_BIG) + [PLAN_PROJ]
    starts += [[packs * (g + 1) + k for k in PLAN_GROUP[g]] for g in range(groups)] + [[done] * Scatter.STAGES]
    events = []
    for t, at in enumerate(starts):
        for s, k in enumerate(at):
            events.append((min(k, done), s if k >= done else 0, t, s))
    for k, _, t, s in sorted(events):
        plan[k].append((t, s))
    return plan


SPLIT = 2
PLAN_BIG = ([0, 1, 7, 13, 15], [0, 1, 11, 17, 19], [0, 6, 16, 20, 22], [0, 10, 18, 22, 22])
PLAN_PROJ = [1, 3, 9, 14, 17]
PLAN_GROUP = ([0, 2, 8, 13, 15], [0, 2, 7, 10, 10], [0, 1, 4, 4, 4])


def attend_back(
    x, normed, qkv, probs, mixed, attn, gres, wqkv, wproj, vectors, two, hidden, indices, gfc1, gfc2, packs, glob, heads,
    grids, table_rows, out_dtype, lanes,
):
    rows, features = x.shape
    seq = rows // packs
    groups, blocks = 3, 3
    cols = features // groups
    steps = 1 + packs * groups + 1 + blocks
    first_block = packs * groups + 2
    whole = lambda shape: pl.BlockSpec(shape, lambda s: (0,) * len(shape), pipeline_mode=pl.Buffered(1))
    at = lambda s: jnp.clip(s - 1, 0, packs * groups - 1)
    part = lambda i: pl.BlockSpec((seq, cols), lambda s: (at(s) % packs, i * groups + at(s) // packs))
    any_ref = pl.BlockSpec(memory_space=pl.ANY)
    by_block = pl.BlockSpec((rows // blocks, features), lambda s: (jnp.clip(s - first_block, 0, blocks - 1), 0))
    padded = pad_index(indices, lanes)
    shard = lambda t: t.shape[4:]
    term_shapes = [(features // 32, features)] + [(features // 32, 3 * cols)] * groups
    tall, wide = (shard(gfc2)[0] // SPLIT, shard(gfc2)[1]), (shard(gfc1)[0], shard(gfc1)[1] // SPLIT)
    flow_shapes = [(tall, gfc2.dtype)] * SPLIT + [(wide, gfc1.dtype)] * SPLIT
    scratch = [
        pltpu.VMEM((rows, 3 * features), jnp.bfloat16),
        pltpu.VMEM((rows, features), jnp.bfloat16),
        pltpu.VMEM((2, heads, seq, lanes), jnp.float32),
        pltpu.VMEM((16, features), jnp.float32),
        pltpu.VMEM((heads, table_rows), jnp.float32),
        pltpu.VMEM((2, heads, ROW_SLOTS, lanes), jnp.float32),
    ]
    scratch += [pltpu.VMEM((LINE, 2, 2) + s, d) for s, d in flow_shapes]
    flow_shapes += [(s, jnp.bfloat16) for s in term_shapes] + [(SMALL, jnp.float32)]
    scratch += [pltpu.VMEM(GRID + s, jnp.bfloat16) for s in term_shapes] + [pltpu.VMEM(GRID + SMALL, jnp.float32)]
    for s, d in flow_shapes:
        scratch += Scatter.scratch(s, d)
    scratch += [pltpu.SemaphoreType.DMA((len(flow_shapes), Scatter.SEMS))] * 2
    return pl.pallas_call(
        functools.partial(
            back_kernel, (packs, glob, heads, groups, blocks, grids), back_plan(steps, groups, packs)
        ),
        grid=(steps,),
        out_shape=[
            jax.ShapeDtypeStruct((rows, features), out_dtype),
            jax.ShapeDtypeStruct((features // 32, 3 * features), jnp.float32),
            jax.ShapeDtypeStruct((features // 32, features), jnp.float32),
            jax.ShapeDtypeStruct(shard(gfc1), jnp.float32),
            jax.ShapeDtypeStruct(shard(gfc2), jnp.float32),
            jax.ShapeDtypeStruct(SMALL, jnp.float32),
        ],
        in_specs=[
            by_block,
            whole((rows, features)),
            part(0), part(1), part(2),
            pl.BlockSpec((1, heads // 2 // groups, 2 * seq, seq), lambda s: (at(s) % packs, at(s) // packs, 0, 0)),
            whole((rows, features)),
            whole((rows, features)),
            whole((rows, features)),
            whole(wqkv.shape),
            whole(wproj.shape),
            whole(vectors.shape),
            whole(two.shape),
            whole(hidden.shape),
            whole(padded[0].shape),
            whole(padded[1].shape),
            any_ref,
            any_ref,
        ],
        out_specs=[
            by_block,
            whole((features // 32, 3 * features)),
            whole((features // 32, features)),
            whole(shard(gfc1)),
            whole(shard(gfc2)),
            whole(SMALL),
        ],
        scratch_shapes=scratch,
        compiler_params=pltpu.CompilerParams(vmem_limit_bytes=BIG, collective_id=1, has_side_effects=True),
        name="attend_back",
    )(x, normed, qkv, qkv, qkv, probs, mixed, attn, gres, wqkv, wproj, vectors, two, hidden, *padded, gfc1, gfc2)


def gather_order():
    small, qkv, proj, one, two = range(5)
    head = [(small, 0), (qkv, 0), (proj, 0), (small, 1), (small, 2), (small, 3), (small, 4), "unpack"]
    head += [(qkv, 1), (one, 0), (proj, 1), "expand global", (qkv, 2), (two, 0), (one, 1), (proj, 2), "expand local"]
    head += [(qkv, 3), (two, 1), (one, 2), (proj, 3), (qkv, 4), (proj, 4)]
    return head, {1: [], 2: [(two, 2), (one, 3)], 3: [], 4: [], 5: [(two, 3)], 6: [(one, 4)], 7: [(two, 4)]}


def front_kernel(
    shape, xg_ref, xl_ref, small_ref, oqkv_ref, oproj_ref, ofc1_ref, ofc2_ref, index_g, index_l,
    x_ref, normed_ref, qkv_ref, probs_ref, mixed_ref, attn_ref, resid_ref, vec_ref, hidden_ref,
    fqkv_ref, fproj_ref, ffc1_ref, ffc2_ref,
    table, bias, rows_g, rows_l, padded, wqkv, wproj, small_full, load, send, recv,
):
    packs, glob, heads, grids = shape
    step = pl.program_id(0)
    seq, features = x_ref.shape
    width = features // heads
    devices = LINE * 8
    vec = lambda k: vec_ref[pl.ds(k, 1), :]
    owns = (small_ref, oqkv_ref, oproj_ref, ofc1_ref, ofc2_ref)
    fulls = (small_full, fqkv_ref, fproj_ref, ffc1_ref, ffc2_ref)
    flows = [Gather(o, f, send.at[t], recv.at[t]) for t, (o, f) in enumerate(zip(owns, fulls))]
    head, later = gather_order()

    def each_shard(act):
        @pl.loop(0, devices)
        def _(d):
            for k, (ref, held) in enumerate(((fqkv_ref, wqkv), (fproj_ref, wproj))):
                count = held.shape[0] // devices
                part = held.at[pl.ds(pl.multiple_of(d * count, 8), count)]
                act(pltpu.make_async_copy(ref.at[d // 8, d // 4 % 2, d // 2 % 2, d % 2], part, load.at[k, d]))

    @pl.when(step == 0)
    def _():
        greet()
        table[...] = jnp.zeros_like(table)
        for item in head:
            if item == "unpack":
                count, wide = features // devices, hidden_ref.shape[1] // devices
                lines = table.shape[1] // devices
                for d in range(devices):
                    block = small_full.at[d // 8, d // 4 % 2, d // 2 % 2, d % 2]
                    vec_ref[:, pl.ds(d * count, count)] = block[:, pl.ds(0, count)]
                    hidden_ref[:, pl.ds(d * wide, wide)] = block[pl.ds(10, 1), pl.ds(0, wide)]
                    table[pl.ds(0, heads), pl.ds(d * lines, lines)] = block[pl.ds(0, heads), pl.ds(128, lines)]
            elif item == "expand global":
                expand(grids[:1], table, (index_g,), (bias.at[0],), (rows_g,))
            elif item == "expand local":
                expand(grids[1:], table, (index_l,), (bias.at[1],), (rows_l,))
            else:
                flows[item[0]].stage(item[1])
        each_shard(lambda copy: copy.start())
        each_shard(lambda copy: copy.wait())

    @pl.when((step >= 1) & (step <= packs))
    def _():
        padded[...] = jnp.zeros_like(padded)

        @pl.when(step <= glob)
        def _():
            padded[pl.ds(0, xg_ref.shape[1]), :] = as_float(xg_ref[0])

        @pl.when(step > glob)
        def _():
            for k in range(xl_ref.shape[0]):
                padded[pl.ds(k * grids[1][3], xl_ref.shape[1]), :] = as_float(xl_ref[k])

        inputs = padded[...]
        x_ref[...] = inputs.astype(jnp.bfloat16)
        unit, _ = unit_rows(inputs)
        normed = (unit * vec(V_LN1G) + vec(V_LN1B)).astype(jnp.bfloat16)
        normed_ref[...] = normed
        qkv_ref[:, pl.ds(0, features)] = (dot(normed, wqkv[:, pl.ds(0, features)]) + vec(V_QB)).astype(jnp.bfloat16)
        qkv_ref[:, pl.ds(features, features)] = dot(normed, wqkv[:, pl.ds(features, features)]).astype(jnp.bfloat16)
        qkv_ref[:, pl.ds(2 * features, features)] = (
            dot(normed, wqkv[:, pl.ds(2 * features, features)]) + vec(V_VB)
        ).astype(jnp.bfloat16)
        kind = jnp.where(step <= glob, 0, 1)
        for pair in range(heads // 2):
            at = 2 * width * pair
            queries = stack_heads(qkv_ref[:, pl.ds(at, 2 * width)], width)
            keys = qkv_ref[:, pl.ds(features + at, 2 * width)]
            values = qkv_ref[:, pl.ds(2 * features + at, 2 * width)]
            part = bias[kind, pl.ds(2 * pair, 2), :, pl.ds(0, seq)].reshape(2 * seq, seq)
            scores = dot_nt(queries, keys) * (width**-0.5) + part
            weights = jnp.exp(scores - jnp.max(scores, axis=-1, keepdims=True))
            probs = (weights * (1.0 / jnp.sum(weights, axis=-1, keepdims=True))).astype(jnp.bfloat16)
            probs_ref[0, pair] = probs
            mixed_ref[:, pl.ds(at, 2 * width)] = merge_heads(dot(probs, values), width).astype(jnp.bfloat16)

        attn = dot(mixed_ref[...], wproj[...]) + vec(V_PB)
        attn_ref[...] = attn.astype(jnp.bfloat16)
        resid_ref[...] = inputs + vec(V_G1) * attn

    for k, items in later.items():
        if items:
            @pl.when(step == k)
            def _():
                for t, s in items:
                    flows[t].stage(s)

    @pl.when(step == packs + 1)
    def _():
        for flow in flows:
            flow.drain()


def attend_front(xg, xl, small, shards, indices, packs, heads, grids, seq, table_rows):
    glob, glob_len, features = xg.shape
    loc, loc_len, _ = xl.shape
    per_pack = loc // (packs - glob)
    rows, lanes = packs * seq, round_up(seq, 128)
    hidden = shards[2].shape[1]
    padded = pad_index(indices, lanes)
    whole = lambda shape: pl.BlockSpec(shape, lambda s: (0,) * len(shape), pipeline_mode=pl.Buffered(1))
    at = lambda s: jnp.clip(s - 1, 0, packs - 1)
    by_rows = lambda cols: pl.BlockSpec((seq, cols), lambda s: (at(s), 0))
    any_ref = pl.BlockSpec(memory_space=pl.ANY)
    owns = [small] + list(shards)
    return pl.pallas_call(
        functools.partial(front_kernel, (packs, glob, heads, grids)),
        grid=(packs + 2,),
        out_shape=[
            jax.ShapeDtypeStruct((rows, features), jnp.bfloat16),
            jax.ShapeDtypeStruct((rows, features), jnp.bfloat16),
            jax.ShapeDtypeStruct((rows, 3 * features), jnp.bfloat16),
            jax.ShapeDtypeStruct((packs, heads // 2, 2 * seq, seq), jnp.bfloat16),
            jax.ShapeDtypeStruct((rows, features), jnp.bfloat16),
            jax.ShapeDtypeStruct((rows, features), jnp.bfloat16),
            jax.ShapeDtypeStruct((rows, features), jnp.float32),
            jax.ShapeDtypeStruct((16, features), jnp.float32),
            jax.ShapeDtypeStruct((1, hidden), jnp.float32),
        ]
        + [jax.ShapeDtypeStruct(GRID + s.shape, s.dtype) for s in shards],
        in_specs=[
            pl.BlockSpec((1, glob_len, features), lambda s: (jnp.minimum(at(s), glob - 1), 0, 0)),
            pl.BlockSpec((per_pack, loc_len, features), lambda s: (jnp.maximum(at(s) - glob, 0), 0, 0)),
        ]
        + [whole(o.shape) for o in owns]
        + [whole(padded[0].shape), whole(padded[1].shape)],
        out_specs=[
            by_rows(features),
            by_rows(features),
            by_rows(3 * features),
            pl.BlockSpec((1, heads // 2, 2 * seq, seq), lambda s: (at(s), 0, 0, 0)),
            by_rows(features),
            by_rows(features),
            by_rows(features),
            whole((16, features)),
            whole((1, hidden)),
        ]
        + [any_ref] * 4,
        scratch_shapes=[
            pltpu.VMEM((16, table_rows), jnp.float32),
            pltpu.VMEM((2, heads, seq, lanes), jnp.float32),
            pltpu.VMEM((2, heads, ROW_SLOTS, lanes), jnp.float32),
            pltpu.VMEM((2, heads, ROW_SLOTS, lanes), jnp.float32),
            pltpu.VMEM((seq, features), jnp.float32),
            pltpu.VMEM((features, 3 * features), jnp.bfloat16),
            pltpu.VMEM((features, features), jnp.bfloat16),
            pltpu.VMEM(GRID + SMALL, jnp.float32),
            pltpu.SemaphoreType.DMA((2, LINE * 8)),
            pltpu.SemaphoreType.DMA((len(owns), Gather.SEMS + 1)),
            pltpu.SemaphoreType.DMA((len(owns), Gather.SEMS + 1)),
        ],
        compiler_params=pltpu.CompilerParams(vmem_limit_bytes=BIG, collective_id=0, has_side_effects=True),
        name="attend_front",
    )(xg, xl, *owns, *padded)


def gather_params(vectors, hidden_shift, table, weights):
    whole = lambda v: lax.all_gather(v, "fsdp", axis=0, tiled=True)
    return ([as_float(whole(v)) for v in vectors], as_float(whole(hidden_shift)), as_float(whole(table)), [whole(w) for w in weights])


def pack_small(vectors, hidden_shift, table):
    rows, lanes = SMALL[0], SMALL[1] // 2
    fit = lambda v: jnp.pad(as_float(v), ((0, 0), (0, lanes - v.shape[1])))
    left = jnp.concatenate([fit(jnp.stack(vectors)), fit(hidden_shift[None])])
    fill = lambda v: jnp.pad(v, ((0, rows - v.shape[0]), (0, 0)))
    return jnp.concatenate([fill(left), fill(fit(table.T))], axis=1)


def scatter_grads(vectors, hidden_shift, table, weights):
    share = lambda v: lax.psum_scatter(as_float(v), "fsdp", scatter_dimension=0, tiled=True)
    return ([share(v) for v in vectors], share(hidden_shift), share(table), [share(w) for w in weights])


def slot_rows(values, slot, seq):
    crops, length, features = values.shape
    per_pack = seq // slot
    values = jnp.pad(values, ((0, 0), (0, slot - length), (0, 0)))
    values = values.reshape(crops // per_pack, per_pack * slot, features)
    return jnp.pad(values, ((0, 0), (0, seq - per_pack * slot), (0, 0)))


def crop_rows(packed, slot, crops, length):
    packs, seq, features = packed.shape
    per_pack = seq // slot
    return packed[:, : per_pack * slot].reshape(crops, slot, features)[:, :length]


def per_device(
    x_global, x_local, cot_global, cot_local, global_count, local_count, index_global, index_local,
    ln1_gain, ln1_bias, qkv_weight, q_bias, v_bias, proj_weight, proj_bias, gamma1, bias_table,
    ln2_gain, ln2_bias, fc1_weight, fc1_bias, fc2_weight, fc2_bias, gamma2,
):
    glob, glob_len, features = x_global.shape
    loc, loc_len = x_local.shape[:2]
    heads = bias_table.shape[1]
    seq = round_up(glob_len, 16)
    slot = round_up(loc_len, 8)
    per_pack = seq // slot
    packs = glob + loc // per_pack
    devices = lax.axis_size("fsdp")
    vector_args = [ln1_gain, ln1_bias, q_bias, v_bias, proj_bias, gamma1, ln2_gain, ln2_bias, fc2_bias, gamma2]
    weights = [qkv_weight, proj_weight, fc1_weight, fc2_weight]
    table_rows = bias_table.shape[0] * devices
    indices = (index_global, index_local)
    sides = (math.isqrt(glob_len - 1), math.isqrt(loc_len - 1))
    grids = ((sides[0], glob_len, 1, seq), (sides[1], loc_len, per_pack, slot))

    glob_keep = jnp.repeat((jnp.arange(glob, dtype=jnp.int32) < global_count[0]).astype(jnp.float32), seq)
    loc_keep = jnp.repeat((jnp.arange(loc, dtype=jnp.int32) < local_count[0]).astype(jnp.float32), slot)
    loc_keep = jnp.pad(loc_keep.reshape(-1, per_pack * slot), ((0, 0), (0, seq - per_pack * slot))).reshape(-1)
    keep = jnp.concatenate([glob_keep, loc_keep])[:, None]
    rows_of = lambda g, l: jnp.concatenate([slot_rows(g, seq, seq), slot_rows(l, slot, seq)]).reshape(-1, features)
    cot = rows_of(cot_global, cot_local)
    if devices == 32:
        x, normed, qkv, probs, mixed, attn, resid, vectors, hidden_row, *full = attend_front(
            x_global, x_local, pack_small(vector_args, fc1_bias, bias_table), weights, indices, packs, heads, grids, seq,
            table_rows,
        )
        qkv_full, proj_full, fc1_full, fc2_full = [f.reshape(devices * f.shape[4], f.shape[5]) for f in full]
        lanes = round_up(seq, 128)
    else:
        small_full, hidden_full, table_full, (qkv_full, proj_full, fc1_full, fc2_full) = gather_params(
            vector_args, fc1_bias, bias_table, weights
        )
        vectors = jnp.pad(jnp.stack(small_full), ((0, 6), (0, 0)))
        hidden_row = hidden_full[None]
        table = jnp.pad(table_full.T, ((0, round_up(heads, 16) - heads), (0, 0))).astype(jnp.bfloat16)
        x = rows_of(x_global, x_local)
        bias = expand_bias(table, indices, grids, heads, seq)
        lanes = bias.shape[-1]
        normed, qkv, probs, mixed, attn, resid = attend_forward(
            x, qkv_full, proj_full, vectors, bias, packs, glob, heads
        )
    out, gres, gfc1, gfc2, gfc1_shift, small_two = mlp_both(
        resid, cot, keep, vectors, fc1_full, hidden_row, fc2_full, x_global.dtype, jnp.bfloat16
    )
    if devices == 32:
        shaped = lambda g: g.reshape(GRID + (g.shape[0] // devices, g.shape[1]))
        gx, *shares, small = attend_back(
            x, normed, qkv, probs, mixed, attn, gres, qkv_full, proj_full, vectors, small_two, gfc1_shift, indices,
            shaped(gfc1), shaped(gfc2), packs, glob, heads, grids, table_rows, x_global.dtype, lanes,
        )
        sums = [small[k, : features // devices] for k in range(10)]
        hidden_sum = small[10, : fc1_bias.shape[0]]
        table_sum = small[:heads, 128 : 128 + table_rows // devices].T
    else:
        gx, gqkv, gproj, bias_sums, small_one, gqkv_shift = attend_backward(
            x, normed, qkv, probs, mixed, attn, gres, qkv_full, proj_full, vectors, packs, glob, heads,
            x_global.dtype, jnp.bfloat16, lanes,
        )
        gtable = collect_bias(bias_sums, indices, grids, table_rows).T
        vector_grads = [
            small_one[0], small_one[1], gqkv_shift[0, :features], gqkv_shift[0, 2 * features :], small_one[2],
            small_one[3], small_two[0], small_two[1], small_two[2], small_two[3],
        ]
        sums, hidden_sum, table_sum, shares = scatter_grads(
            vector_grads, gfc1_shift[0], gtable, [gqkv, gproj, gfc1, gfc2]
        )
    out = out.reshape(packs, seq, features)
    gx = gx.reshape(packs, seq, features)
    return (
        crop_rows(out[:glob], seq, glob, glob_len),
        crop_rows(out[glob:], slot, loc, loc_len),
        crop_rows(gx[:glob], seq, glob, glob_len),
        crop_rows(gx[glob:], slot, loc, loc_len),
        sums[0], sums[1], shares[0], sums[2], sums[3], shares[1], sums[4], sums[5], table_sum,
        sums[6], sums[7], shares[2], hidden_sum, shares[3], sums[8], sums[9],
    )


def solution(mesh):
    placed = (
        P("fsdp", None, None),
        P("fsdp", None, None),
        P("fsdp", None, None),
        P("fsdp", None, None),
        P("fsdp"),
        P("fsdp"),
        P(),
        P(),
        P("fsdp"),
        P("fsdp"),
        P("fsdp", None),
        P("fsdp"),
        P("fsdp"),
        P("fsdp", None),
        P("fsdp"),
        P("fsdp"),
        P("fsdp", None),
        P("fsdp"),
        P("fsdp"),
        P("fsdp", None),
        P("fsdp"),
        P("fsdp", None),
        P("fsdp"),
        P("fsdp"),
    )
    return jax.shard_map(
        per_device,
        mesh=mesh,
        in_specs=placed,
        out_specs=(
            P("fsdp", None, None),
            P("fsdp", None, None),
            P("fsdp", None, None),
            P("fsdp", None, None),
            P("fsdp"),
            P("fsdp"),
            P("fsdp", None),
            P("fsdp"),
            P("fsdp"),
            P("fsdp", None),
            P("fsdp"),
            P("fsdp"),
            P("fsdp", None),
            P("fsdp"),
            P("fsdp"),
            P("fsdp", None),
            P("fsdp"),
            P("fsdp", None),
            P("fsdp"),
            P("fsdp"),
        ),
        check_vma=False,
    )
```

```python
import functools
import math

import jax
import jax.numpy as jnp
from jax import lax
from jax.experimental import pallas as pl
from jax.experimental.pallas import tpu as pltpu
from jax.sharding import PartitionSpec as P

EPSILON = 1e-06
NEG = -1e30
ROWS_IN = (((0,), (0,)), ((), ()))
COLS_IN = (((1,), (1,)), ((), ()))
BIG = 60 * 1024 * 1024


def as_float(values):
    return values.astype(jnp.float32)


def dot(a, b):
    return jnp.dot(a, b, preferred_element_type=jnp.float32)


def dot_tn(a, b):
    return lax.dot_general(a, b, ROWS_IN, preferred_element_type=jnp.float32)


def dot_nt(a, b):
    return lax.dot_general(a, b, COLS_IN, preferred_element_type=jnp.float32)


def round_up(value, unit):
    return (value + unit - 1) // unit * unit


def unit_rows(values):
    average = jnp.mean(values, axis=-1, keepdims=True)
    centered = values - average
    spread = lax.rsqrt(jnp.mean(centered * centered, axis=-1, keepdims=True) + EPSILON)
    return (centered * spread, spread)


def unit_back(grad, unit, spread):
    return spread * (
        grad - jnp.mean(grad, axis=-1, keepdims=True) - unit * jnp.mean(grad * unit, axis=-1, keepdims=True)
    )


def column_sum(values):
    return jnp.sum(values, axis=0, keepdims=True)


V_LN1G, V_LN1B, V_QB, V_VB, V_PB, V_G1, V_LN2G, V_LN2B, V_FB, V_G2 = range(10)


def mlp_kernel(
    steps, blocks, seq, slot, gcount_ref, lcount_ref, resid_ref, cg_ref, cl_ref, vec_ref, w1_ref, b1_ref, w2_ref,
    outg_ref, outl_ref, gres_ref, gw1_ref, gw2_ref, gb1_ref, small_ref,
    cot, normed, gbranch, branch, gnorm, active, ghidden,
):
    step = pl.program_id(0)
    rows, features = resid_ref.shape
    size = rows // blocks
    vec = lambda k: vec_ref[pl.ds(k, 1), :]
    glob, glob_len, _ = cg_ref.shape
    loc, loc_len, _ = cl_ref.shape
    per_pack = seq // slot
    packs = glob + loc // per_pack

    def kept(k, count_ref):
        return jnp.where(k < count_ref[0], 1.0, 0.0)

    @pl.when(step == 0)
    def _():
        cot[...] = jnp.zeros_like(cot)

        @pl.loop(0, glob)
        def _(p):
            rows_of = pl.ds(pl.multiple_of(p * seq, seq), glob_len)
            cot[rows_of, :] = (as_float(cg_ref[p]) * kept(p, gcount_ref)).astype(jnp.bfloat16)

        @pl.loop(0, packs - glob)
        def _(p):
            for k in range(per_pack):
                crop = p * per_pack + k
                rows_of = pl.ds(pl.multiple_of((glob + p) * seq + k * slot, 8), loc_len)
                cot[rows_of, :] = (as_float(cl_ref[crop]) * kept(crop, lcount_ref)).astype(jnp.bfloat16)

        @pl.loop(0, blocks)
        def _(i):
            part = pl.ds(pl.multiple_of(i * size, size), size)
            unit, _ = unit_rows(resid_ref[part, :])
            normed[part, :] = (unit * vec(V_LN2G) + vec(V_LN2B)).astype(jnp.bfloat16)
            gbranch[part, :] = (vec(V_G2) * as_float(cot[part, :])).astype(jnp.bfloat16)

    w1, w2 = w1_ref[...], w2_ref[...]

    def block(i, hidden_sum):
        part = pl.ds(pl.multiple_of(i * size, size), size)
        hidden = dot(normed[part, :], w1) + b1_ref[...]
        phi = 0.5 * lax.erf(hidden * (0.5**0.5)) + 0.5
        low = (hidden * phi).astype(jnp.bfloat16)
        active[part, :] = low
        slope = phi + hidden * (jnp.exp(hidden * hidden * -0.5) * 0.3989422804014327)
        add = dot(low, w2)
        grad = dot_nt(gbranch[part, :], w2) * slope
        glow = grad.astype(jnp.bfloat16)
        ghidden[part, :] = glow
        gadd = dot_nt(glow, w1)

        @pl.when(step == 0)
        def _():
            branch[part, :] = add
            gnorm[part, :] = gadd

        @pl.when(step > 0)
        def _():
            branch[part, :] = branch[part, :] + add
            gnorm[part, :] = gnorm[part, :] + gadd

        return hidden_sum + column_sum(as_float(glow))

    gb1_ref[...] = lax.fori_loop(0, blocks, block, jnp.zeros(gb1_ref.shape, jnp.float32))
    gw2_ref[...] = dot_tn(active[...], gbranch[...]).astype(gw2_ref.dtype)
    gw1_ref[...] = dot_tn(normed[...], ghidden[...]).astype(gw1_ref.dtype)

    @pl.when(step == steps - 1)
    def _():
        zero = jnp.zeros((1, features), jnp.float32)

        def pack(p, sums, write):
            part = pl.ds(pl.multiple_of(p * seq, seq), seq)
            resid = resid_ref[part, :]
            full = branch[part, :] + vec(V_FB)
            write(p, resid + vec(V_G2) * full)
            grad = as_float(cot[part, :])
            unit, spread = unit_rows(resid)
            gn = gnorm[part, :]
            gres_ref[part, :] = grad + unit_back(gn * vec(V_LN2G), unit, spread)
            return (
                sums[0] + column_sum(gn * unit),
                sums[1] + column_sum(gn),
                sums[2] + column_sum(as_float(gbranch[part, :])),
                sums[3] + column_sum(grad * full),
            )

        def write_glob(p, value):
            outg_ref[p] = (value[:glob_len] * kept(p, gcount_ref)).astype(outg_ref.dtype)

        def write_loc(p, value):
            for k in range(per_pack):
                crop = (p - glob) * per_pack + k
                piece = value[k * slot : k * slot + loc_len] * kept(crop, lcount_ref)
                outl_ref[crop] = piece.astype(outl_ref.dtype)

        sums = lax.fori_loop(0, glob, lambda p, s: pack(p, s, write_glob), (zero,) * 4)
        sums = lax.fori_loop(glob, packs, lambda p, s: pack(p, s, write_loc), sums)
        small_ref[...] = jnp.zeros_like(small_ref)
        for k in range(4):
            small_ref[pl.ds(k, 1), :] = sums[k]


def mlp_both(gcount, lcount, resid, cg, cl, vectors, w1, b1, w2, seq, slot, out_dtype, grad_dtype):
    rows, features = resid.shape
    hidden = w1.shape[1]
    chunk = 1024
    steps = hidden // chunk
    whole = lambda shape: pl.BlockSpec(shape, lambda j: (0,) * len(shape), pipeline_mode=pl.Buffered(1))
    scalar = pl.BlockSpec(memory_space=pltpu.SMEM)
    return pl.pallas_call(
        functools.partial(mlp_kernel, steps, 3, seq, slot),
        grid=(steps,),
        out_shape=[
            jax.ShapeDtypeStruct(cg.shape, out_dtype),
            jax.ShapeDtypeStruct(cl.shape, out_dtype),
            jax.ShapeDtypeStruct((rows, features), jnp.float32),
            jax.ShapeDtypeStruct((features, hidden), grad_dtype),
            jax.ShapeDtypeStruct((hidden, features), grad_dtype),
            jax.ShapeDtypeStruct((1, hidden), jnp.float32),
            jax.ShapeDtypeStruct((8, features), jnp.float32),
        ],
        in_specs=[
            scalar,
            scalar,
            whole((rows, features)),
            whole(cg.shape),
            whole(cl.shape),
            whole(vectors.shape),
            pl.BlockSpec((features, chunk), lambda j: (0, j)),
            pl.BlockSpec((1, chunk), lambda j: (0, j)),
            pl.BlockSpec((chunk, features), lambda j: (j, 0)),
        ],
        out_specs=[
            whole(cg.shape),
            whole(cl.shape),
            whole((rows, features)),
            pl.BlockSpec((features, chunk), lambda j: (0, j)),
            pl.BlockSpec((chunk, features), lambda j: (j, 0)),
            pl.BlockSpec((1, chunk), lambda j: (0, j)),
            whole((8, features)),
        ],
        scratch_shapes=[
            pltpu.VMEM((rows, features), jnp.bfloat16),
            pltpu.VMEM((rows, features), jnp.bfloat16),
            pltpu.VMEM((rows, features), jnp.bfloat16),
            pltpu.VMEM((rows, features), jnp.float32),
            pltpu.VMEM((rows, features), jnp.float32),
            pltpu.VMEM((rows, chunk), jnp.bfloat16),
            pltpu.VMEM((rows, chunk), jnp.bfloat16),
        ],
        compiler_params=pltpu.CompilerParams(vmem_limit_bytes=BIG),
        name="mlp_both",
    )(gcount, lcount, resid, cg, cl, vectors, w1, b1, w2)


def lane_of(shape):
    return lax.broadcasted_iota(jnp.int32, shape, 1)


def roll_lanes(values, shift):
    shift = shift % values.shape[1]
    return pltpu.roll(values, shift, 1) if shift else values


def corner_rows(side):
    return (1, side, 1 + (side - 1) * side, side * side)


def expand(grids, table_ref, index_refs, bias_refs, row_refs):
    for n, (side, seq, copies, slot) in enumerate(grids):
        index_ref, bias_ref, row_ref = index_refs[n], bias_refs[n], row_refs[n]
        heads, lanes = bias_ref.shape[0], bias_ref.shape[2]
        tables = lax.broadcasted_iota(jnp.int32, (table_ref.shape[1], lanes), 0)

        def pick(row):
            picked = index_ref[pl.ds(row, 1), :] == tables
            return dot(table_ref[...].astype(jnp.bfloat16), picked.astype(jnp.bfloat16))

        corners = [pick(k) for k in range(4)]
        lane = lane_of(corners[0].shape)
        within = (lane + (side - 1)) % side
        for c in range(side):
            for top in range(2):
                left, right = corners[2 * top], corners[2 * top + 1]
                row = jnp.where(within >= c, roll_lanes(left, c), roll_lanes(right, c - (side - 1)))
                row = jnp.where(lane == 0, left, row)
                row_ref[top, :, pl.ds(c, 1), :] = row[:heads].reshape(heads, 1, lanes)
        row_ref[0, :, pl.ds(side, 1), :] = pick(4)[:heads].reshape(heads, 1, lanes)
        lane = lane_of((side, lanes))

        def spread(values, at):
            if copies > 1:
                values = roll_lanes(values, at * slot)
            where = lane_of(values.shape) - at * slot
            return jnp.where((where >= 0) & (where < seq), values, NEG)

        @pl.loop(0, heads)
        def _(h):
            bias_ref[h] = jnp.full(bias_ref.shape[1:], NEG, jnp.float32)
            low, high, first = row_ref[0, h, :side], row_ref[1, h, :side], row_ref[0, h, pl.ds(side, 1)]
            for at in range(copies):
                bias_ref[h, pl.ds(at * slot, 1), :] = spread(first, at)
            for r in range(side):
                rows = jnp.where(
                    lane - 1 < side * (r + 1), roll_lanes(high, -side * (side - 1 - r)), roll_lanes(low, side * r)
                )
                rows = jnp.where(lane == 0, low, rows)
                for at in range(copies):
                    bias_ref[h, pl.ds(at * slot + 1 + side * r, side), :] = spread(rows, at)


def collect(grids, sum_refs, index_refs, row_refs, shape):
    total = jnp.zeros(shape, jnp.float32)
    for n, (side, seq, copies, slot) in enumerate(grids):
        index_ref, sum_ref, row_ref = index_refs[n], sum_refs[n], row_refs[n]
        heads, lanes = sum_ref.shape[0], sum_ref.shape[2]
        lane = lane_of((side, lanes))

        def gathered(h, start, size):
            rows = None
            for at in range(copies):
                piece = roll_lanes(sum_ref[h, pl.ds(at * slot + start, size), :], -at * slot)
                rows = piece if rows is None else rows + piece
            return jnp.where(lane_of((size, lanes)) < seq, rows, 0.0) if copies > 1 else rows

        @pl.loop(0, heads)
        def _(h):
            low = jnp.zeros((side, lanes), jnp.float32)
            high = jnp.zeros((side, lanes), jnp.float32)
            for r in range(side):
                rows = gathered(h, 1 + side * r, side)
                is_low = lane - 1 >= side * (r + 1)
                is_high = (lane >= 1) & (lane - 1 < side * (r + 1))
                low = low + roll_lanes(jnp.where(is_low, rows, 0.0), -side * r) + jnp.where(lane == 0, rows, 0.0)
                high = high + roll_lanes(jnp.where(is_high, rows, 0.0), side * (side - 1 - r))
            row_ref[0, h, :side], row_ref[1, h, :side] = low, high
            row_ref[0, h, pl.ds(side, 1)] = gathered(h, 0, 1)

        flat = lane_of((heads, lanes))
        within = (flat + (side - 1)) % side
        corners = [jnp.zeros((heads, lanes), jnp.float32) for _ in range(4)]
        for c in range(side):
            for top in range(2):
                row = row_ref[top, :, pl.ds(c, 1), :].reshape(heads, lanes)
                is_left = (flat >= 1) & (within >= c)
                is_right = (flat >= 1) & (within < c)
                left = roll_lanes(jnp.where(is_left, row, 0.0), -c) + jnp.where(flat == 0, row, 0.0)
                corners[2 * top] = corners[2 * top] + left
                corners[2 * top + 1] = corners[2 * top + 1] + roll_lanes(jnp.where(is_right, row, 0.0), side - 1 - c)
        tables = lax.broadcasted_iota(jnp.int32, (shape[1], lanes), 0)

        def place_sum(row, values):
            picked = (index_ref[pl.ds(row, 1), :] == tables).astype(jnp.bfloat16)
            top = values.astype(jnp.bfloat16)
            rest = values - as_float(top)
            middle = rest.astype(jnp.bfloat16)
            last = (rest - as_float(middle)).astype(jnp.bfloat16)
            return dot_nt(top, picked) + dot_nt(middle, picked) + dot_nt(last, picked)

        for k, values in enumerate(corners):
            total = total + place_sum(k, values)
        total = total + place_sum(4, row_ref[0, :, pl.ds(side, 1), :].reshape(heads, lanes))
    return total


ROW_SLOTS = 16


def expand_kernel(grids, table_ref, index_g, index_l, bias_ref, rows_g, rows_l):
    expand(grids, table_ref, (index_g, index_l), (bias_ref.at[0], bias_ref.at[1]), (rows_g, rows_l))


def pad_index(indices, lanes):
    picked = []
    for index in indices:
        rows = corner_rows(math.isqrt(index.shape[0] - 1)) + (0,)
        rows = jnp.concatenate([index[r : r + 1] for r in rows])
        picked.append(jnp.pad(rows, ((0, 8 - len(rows)), (0, lanes - index.shape[1])), constant_values=-1))
    return picked


def expand_bias(table, indices, grids, heads, seq):
    lanes = round_up(seq, 128)
    return pl.pallas_call(
        functools.partial(expand_kernel, grids),
        out_shape=jax.ShapeDtypeStruct((2, heads, seq, lanes), jnp.float32),
        scratch_shapes=[pltpu.VMEM((2, heads, ROW_SLOTS, lanes), jnp.float32)] * 2,
        compiler_params=pltpu.CompilerParams(vmem_limit_bytes=BIG),
        name="expand_bias",
    )(table, *pad_index(indices, lanes))


def collect_kernel(grids, index_g, index_l, sums_ref, grad_ref, rows_g, rows_l):
    grad_ref[...] = collect(
        grids, (sums_ref.at[0], sums_ref.at[1]), (index_g, index_l), (rows_g, rows_l), grad_ref.shape
    )


def collect_bias(sums, indices, grids, table_rows):
    _, heads, _, lanes = sums.shape
    return pl.pallas_call(
        functools.partial(collect_kernel, grids),
        out_shape=jax.ShapeDtypeStruct((heads, table_rows), jnp.float32),
        scratch_shapes=[pltpu.VMEM((2, heads, ROW_SLOTS, lanes), jnp.float32)] * 2,
        compiler_params=pltpu.CompilerParams(vmem_limit_bytes=BIG),
        name="collect_bias",
    )(*pad_index(indices, lanes), sums)


def head_lanes(shape, width):
    return lax.broadcasted_iota(jnp.int32, shape, 1) < width


def stack_heads(pair, width):
    first = head_lanes(pair.shape, width)
    zero = jnp.zeros_like(pair)
    return jnp.concatenate([jnp.where(first, pair, zero), jnp.where(first, zero, pair)], axis=0)


def merge_heads(stacked, width):
    rows = stacked.shape[0] // 2
    top, low = stacked[:rows], stacked[rows:]
    return jnp.where(head_lanes(top.shape, width), top, low)


def attend_kernel(
    glob, heads, x_ref, wqkv_ref, wproj_ref, vec_ref, bias_ref,
    normed_ref, qkv_ref, probs_ref, mixed_ref, attn_ref, resid_ref,
):
    seq, features = x_ref.shape
    width = features // heads
    vec = lambda k: vec_ref[pl.ds(k, 1), :]
    inputs = as_float(x_ref[...])
    unit, _ = unit_rows(inputs)
    normed = (unit * vec(V_LN1G) + vec(V_LN1B)).astype(jnp.bfloat16)
    normed_ref[...] = normed
    qkv_ref[:, pl.ds(0, features)] = (dot(normed, wqkv_ref[:, pl.ds(0, features)]) + vec(V_QB)).astype(jnp.bfloat16)
    qkv_ref[:, pl.ds(features, features)] = dot(normed, wqkv_ref[:, pl.ds(features, features)]).astype(jnp.bfloat16)
    qkv_ref[:, pl.ds(2 * features, features)] = (
        dot(normed, wqkv_ref[:, pl.ds(2 * features, features)]) + vec(V_VB)
    ).astype(jnp.bfloat16)

    for pair in range(heads // 2):
        at = 2 * width * pair
        queries = stack_heads(qkv_ref[:, pl.ds(at, 2 * width)], width)
        keys = qkv_ref[:, pl.ds(features + at, 2 * width)]
        values = qkv_ref[:, pl.ds(2 * features + at, 2 * width)]
        bias = bias_ref[0, pl.ds(2 * pair, 2), :, pl.ds(0, seq)].reshape(2 * seq, seq)
        scores = dot_nt(queries, keys) * (width**-0.5) + bias
        weights = jnp.exp(scores - jnp.max(scores, axis=-1, keepdims=True))
        probs = (weights * (1.0 / jnp.sum(weights, axis=-1, keepdims=True))).astype(jnp.bfloat16)
        probs_ref[0, pair] = probs
        mixed_ref[:, pl.ds(at, 2 * width)] = merge_heads(dot(probs, values), width).astype(jnp.bfloat16)

    attn = dot(mixed_ref[...], wproj_ref[...]) + vec(V_PB)
    attn_ref[...] = attn.astype(jnp.bfloat16)
    resid_ref[...] = inputs + vec(V_G1) * attn


def attend_forward(x, wqkv, wproj, vectors, bias, packs, glob, heads):
    rows, features = x.shape
    seq = rows // packs
    whole = lambda shape: pl.BlockSpec(shape, lambda p: (0,) * len(shape), pipeline_mode=pl.Buffered(1))
    by_rows = lambda cols: pl.BlockSpec((seq, cols), lambda p: (p, 0))
    return pl.pallas_call(
        functools.partial(attend_kernel, glob, heads),
        grid=(packs,),
        out_shape=[
            jax.ShapeDtypeStruct((rows, features), jnp.bfloat16),
            jax.ShapeDtypeStruct((rows, 3 * features), jnp.bfloat16),
            jax.ShapeDtypeStruct((packs, heads // 2, 2 * seq, seq), jnp.bfloat16),
            jax.ShapeDtypeStruct((rows, features), jnp.bfloat16),
            jax.ShapeDtypeStruct((rows, features), jnp.bfloat16),
            jax.ShapeDtypeStruct((rows, features), jnp.float32),
        ],
        in_specs=[
            by_rows(features),
            whole(wqkv.shape),
            whole(wproj.shape),
            whole(vectors.shape),
            pl.BlockSpec((1,) + bias.shape[1:], lambda p: (jnp.where(p < glob, 0, 1), 0, 0, 0)),
        ],
        out_specs=[
            by_rows(features),
            by_rows(3 * features),
            pl.BlockSpec((1, heads // 2, 2 * seq, seq), lambda p: (p, 0, 0, 0)),
            by_rows(features),
            by_rows(features),
            by_rows(features),
        ],
        compiler_params=pltpu.CompilerParams(vmem_limit_bytes=BIG),
        name="attend_forward",
    )(x, wqkv, wproj, vectors, bias)


def attend_back_kernel(
    packs, glob, heads, chunk, x_ref, normed_ref, qkv_ref, probs_ref, mixed_ref, attn_ref, gres_ref, wqkv_ref, wproj_ref, vec_ref,
    gx_ref, gwqkv_ref, gwproj_ref, bsum_ref, small_ref, gqb_ref,
    normed_all, mixed_all, gattn_all, gqkv_all,
):
    step = pl.program_id(0)
    seq, features = x_ref.shape
    width = features // heads
    vec = lambda k: vec_ref[pl.ds(k, 1), :]
    rows = packs * seq

    @pl.when(step == 0)
    def _():
        small_ref[...] = jnp.zeros_like(small_ref)
        gqb_ref[...] = jnp.zeros_like(gqb_ref)

    @pl.when((step == 0) | (step == glob))
    def _():
        bsum_ref[...] = jnp.zeros_like(bsum_ref)

    @pl.when(step < packs)
    def _():
        part = pl.ds(pl.multiple_of(step * seq, seq), seq)
        gres = gres_ref[...]
        gattn = (vec(V_G1) * gres).astype(jnp.bfloat16)
        gattn_all[part, :] = gattn
        mixed_all[part, :] = mixed_ref[...]
        normed_all[part, :] = normed_ref[...]
        small_ref[pl.ds(2, 1), :] += column_sum(as_float(gattn))
        small_ref[pl.ds(3, 1), :] += column_sum(gres * as_float(attn_ref[...]))
        gmixed = dot_nt(gattn, wproj_ref[...]).astype(jnp.bfloat16)
        scale = width**-0.5
        for pair in range(heads // 2):
            at = 2 * width * pair
            queries = stack_heads(qkv_ref[:, pl.ds(at, 2 * width)], width)
            keys = qkv_ref[:, pl.ds(features + at, 2 * width)]
            values = qkv_ref[:, pl.ds(2 * features + at, 2 * width)]
            grads = stack_heads(gmixed[:, at : at + 2 * width], width)
            mixed = as_float(mixed_ref[:, pl.ds(at, 2 * width)])
            probs = probs_ref[0, pair]
            twice = jnp.concatenate([mixed, mixed], axis=0)
            inner = jnp.sum(as_float(grads) * twice, axis=-1, keepdims=True)
            gscores = as_float(probs) * (dot_nt(grads, values) - inner)
            bsum_ref[0, pl.ds(2 * pair, 2), :, pl.ds(0, seq)] += gscores.reshape(2, seq, seq)
            low = gscores.astype(jnp.bfloat16)
            gqkv_all[part, pl.ds(at, 2 * width)] = (merge_heads(dot(low, keys), width) * scale).astype(jnp.bfloat16)
            gqkv_all[part, pl.ds(features + at, 2 * width)] = (dot_tn(low, queries) * scale).astype(jnp.bfloat16)
            gqkv_all[part, pl.ds(2 * features + at, 2 * width)] = dot_tn(probs, grads).astype(jnp.bfloat16)
        gqkv = gqkv_all[part, :]
        gqb_ref[...] += column_sum(as_float(gqkv))
        gnorm = dot_nt(gqkv, wqkv_ref[...])
        unit, spread = unit_rows(as_float(x_ref[...]))
        small_ref[pl.ds(0, 1), :] += column_sum(gnorm * unit)
        small_ref[pl.ds(1, 1), :] += column_sum(gnorm)
        gx_ref[...] = (gres + unit_back(gnorm * vec(V_LN1G), unit, spread)).astype(gx_ref.dtype)

    @pl.when(step >= packs)
    def _():
        j = step - packs
        wide = 3 * features // chunk

        @pl.when(j < wide)
        def _():
            gwqkv_ref[...] = dot_tn(normed_all[...], gqkv_all[:, pl.ds(pl.multiple_of(j * chunk, chunk), chunk)]).astype(gwqkv_ref.dtype)

        @pl.when(j >= wide)
        def _():
            gwproj_ref[...] = dot_tn(mixed_all[...], gattn_all[:, pl.ds(pl.multiple_of((j - wide) * chunk, chunk), chunk)]).astype(gwproj_ref.dtype)


def attend_backward(x, normed, qkv, probs, mixed, attn, gres, wqkv, wproj, vectors, packs, glob, heads, out_dtype, grad_dtype, lanes):
    rows, features = x.shape
    seq = rows // packs
    chunk = 256
    wide, narrow = 3 * features // chunk, features // chunk
    whole = lambda shape: pl.BlockSpec(shape, lambda s: (0,) * len(shape), pipeline_mode=pl.Buffered(1))
    pack = lambda s: jnp.minimum(s, packs - 1)
    by_rows = lambda cols: pl.BlockSpec((seq, cols), lambda s: (pack(s), 0))
    return pl.pallas_call(
        functools.partial(attend_back_kernel, packs, glob, heads, chunk),
        grid=(packs + wide + narrow,),
        out_shape=[
            jax.ShapeDtypeStruct((rows, features), out_dtype),
            jax.ShapeDtypeStruct((features, 3 * features), grad_dtype),
            jax.ShapeDtypeStruct((features, features), grad_dtype),
            jax.ShapeDtypeStruct((2, heads, seq, lanes), jnp.float32),
            jax.ShapeDtypeStruct((8, features), jnp.float32),
            jax.ShapeDtypeStruct((1, 3 * features), jnp.float32),
        ],
        in_specs=[
            by_rows(features),
            by_rows(features),
            by_rows(3 * features),
            pl.BlockSpec((1, heads // 2, 2 * seq, seq), lambda s: (pack(s), 0, 0, 0)),
            by_rows(features),
            by_rows(features),
            by_rows(features),
            whole(wqkv.shape),
            whole(wproj.shape),
            whole(vectors.shape),
        ],
        out_specs=[
            by_rows(features),
            pl.BlockSpec((features, chunk), lambda s: (0, jnp.clip(s - packs, 0, wide - 1))),
            pl.BlockSpec((features, chunk), lambda s: (0, jnp.clip(s - packs - wide, 0, narrow - 1))),
            pl.BlockSpec((1, heads, seq, lanes), lambda s: (jnp.where(s < glob, 0, 1), 0, 0, 0)),
            whole((8, features)),
            whole((1, 3 * features)),
        ],
        scratch_shapes=[
            pltpu.VMEM((rows, features), jnp.bfloat16),
            pltpu.VMEM((rows, features), jnp.bfloat16),
            pltpu.VMEM((rows, features), jnp.bfloat16),
            pltpu.VMEM((rows, 3 * features), jnp.bfloat16),
        ],
        compiler_params=pltpu.CompilerParams(vmem_limit_bytes=BIG),
        name="attend_backward",
    )(x, normed, qkv, probs, mixed, attn, gres, wqkv, wproj, vectors)


MESH = pl.DeviceIdType.MESH
LINE = 4
GRID = (LINE, 2, 2, 2)
EVERY = slice(None)


def place():
    me = lax.axis_index("fsdp")
    return (me // 8, (me // 4) % 2, (me // 2) % 2, me % 2)


def device_at(z, y, x, c):
    return (((z * 2 + y) * 2 + x) * 2 + c,)


def along(z, k):
    return (z + k) % LINE


def greet():
    z, y, x, c = place()
    barrier = pltpu.get_barrier_semaphore()
    peers = [device_at(z, y, x, 1 - c), device_at(z, y, 1 - x, c), device_at(z, 1 - y, x, c)]
    peers += [device_at(along(z, k), y, x, c) for k in range(1, LINE)]
    for peer in peers:
        pl.semaphore_signal(barrier, inc=1, device_id=peer, device_id_type=MESH)
    pl.semaphore_wait(barrier, len(peers))


def remote(src, dst, send, recv, peer):
    return pltpu.make_async_remote_copy(
        src_ref=src, dst_ref=dst, send_sem=send, recv_sem=recv, device_id=peer, device_id_type=MESH
    )


class Gather:
    STAGES = 5
    SEMS = 12

    def __init__(self, own, full, send, recv):
        self.own, self.full, self.send, self.recv = own, full, send, recv
        self.z, self.y, self.x, self.c = place()
        self.cols = full.shape[-1] // 2

    def line_copy(self, k, source=None):
        z, y, x, c = self.z, self.y, self.x, self.c
        held = z if source is None else source
        peer = device_at(along(z, k), y, x, c)
        return remote(self.own, self.full.at[held, y, x, c], self.send.at[k - 1], self.recv.at[k - 1], peer)

    def copy(self, name):
        z, y, x, c = self.z, self.y, self.x, self.c
        over_x, over_y, pair = device_at(z, y, 1 - x, c), device_at(z, 1 - y, x, c), device_at(z, y, x, 1 - c)
        k, part, half, peer = {
            "near0": (3, (EVERY, y, x, c), 0, over_x),
            "near1": (4, (EVERY, y, x, c), 1, over_y),
            "far0": (5, (EVERY, y, EVERY, c), 0, over_y),
            "far1": (6, (EVERY, EVERY, x, c), 1, over_x),
            "pair": (7, (EVERY, y, x, c), None, pair),
            "pair0": (8, (EVERY, y, 1 - x, c), 0, pair),
            "pair1": (9, (EVERY, 1 - y, x, c), 1, pair),
            "pair2": (10, (EVERY, 1 - y, EVERY, c), 0, pair),
            "pair3": (11, (EVERY, EVERY, 1 - x, c), 1, pair),
        }[name]
        ref = self.full.at[part if half is None else part + (EVERY, pl.ds(half * self.cols, self.cols))]
        return remote(ref, ref, self.send.at[k], self.recv.at[k], peer)

    def mine(self):
        return pltpu.make_async_copy(self.own, self.full.at[self.z, self.y, self.x, self.c], self.recv.at[self.SEMS])

    def stage(self, s):
        if s == 0:
            for k in range(1, LINE):
                self.line_copy(k).start()
            self.mine().start()
        elif s == 1:
            self.mine().wait()
            for k in range(1, LINE):
                self.line_copy(k, along(self.z, LINE - k)).wait_recv()
            for name in ("near0", "near1", "pair"):
                self.copy(name).start()
        elif s == 2:
            for k in ("0", "1"):
                self.copy("near" + k).wait_recv()
                self.copy("far" + k).start()
            self.copy("pair0").start()
            self.copy("pair1").start()
        elif s == 3:
            for k, far in ((2, 0), (3, 1)):
                self.copy("far%d" % far).wait_recv()
                self.copy("pair%d" % k).start()
        else:
            for name in ("pair", "pair0", "pair1", "pair2", "pair3"):
                self.copy(name).wait_recv()

    def drain(self):
        for k in range(1, LINE):
            self.line_copy(k).wait_send()
        for name in ("near0", "near1", "far0", "far1", "pair", "pair0", "pair1", "pair2", "pair3"):
            self.copy(name).wait_send()


class Scatter:
    STAGES = 5
    SEMS = 9

    def __init__(self, terms, own, bufs, send, recv, finish):
        self.terms, self.loaded = terms, own
        self.pairbuf, self.buf1a, self.buf1b, self.buf2a, self.buf2b, self.line = bufs
        self.send, self.recv, self.finish = send, recv, finish
        self.z, self.y, self.x, self.c = place()
        self.cols = terms.shape[-1] // 2

    BUFS = 6

    @staticmethod
    def scratch(shape, dtype):
        rows, cols = shape
        half = cols // 2
        return [
            pltpu.VMEM((LINE, 2, 2, rows, cols), dtype),
            pltpu.VMEM((LINE, 2, rows, half), dtype),
            pltpu.VMEM((LINE, 2, rows, half), dtype),
            pltpu.VMEM((LINE, rows, half), dtype),
            pltpu.VMEM((LINE, rows, half), dtype),
            pltpu.VMEM((LINE - 1, rows, cols), dtype),
        ]

    def at(self, i, j, k, half=None):
        cols = () if half is None else (EVERY, pl.ds(half * self.cols, self.cols))
        if self.loaded is None:
            return self.terms.at[(i, j, k, self.c) + cols]
        return self.loaded.at[(i, j, k) + cols]

    def load(self):
        return pltpu.make_async_copy(self.terms.at[EVERY, EVERY, EVERY, self.c], self.loaded, self.send.at[8])

    def copy(self, name):
        z, y, x, c = self.z, self.y, self.x, self.c
        over_x, over_y = device_at(z, y, 1 - x, c), device_at(z, 1 - y, x, c)
        k, src, dst, peer = {
            "pair": lambda: (0, self.terms.at[EVERY, EVERY, EVERY, 1 - c], self.pairbuf, device_at(z, y, x, 1 - c)),
            "1a": lambda: (1, self.at(EVERY, 1 - y, EVERY, 0), self.buf1a, over_y),
            "1b": lambda: (2, self.at(EVERY, EVERY, 1 - x, 1), self.buf1b, over_x),
            "2a": lambda: (3, self.at(EVERY, y, 1 - x, 0), self.buf2a, over_x),
            "2b": lambda: (4, self.at(EVERY, 1 - y, x, 1), self.buf2b, over_y),
        }[name]()
        return remote(src, dst, self.send.at[k], self.recv.at[k], peer)

    def line_copy(self, k):
        z, y, x, c = self.z, self.y, self.x, self.c
        target = along(z, k)
        return remote(
            self.at(target, y, x), self.line.at[k - 1], self.send.at[4 + k], self.recv.at[4 + k], device_at(target, y, x, c)
        )

    def add(self, ref, term):
        ref[...] = ref[...] + term

    def stage(self, s):
        z, y, x = self.z, self.y, self.x
        if s == 0:
            self.copy("pair").start()
            if self.loaded is not None:
                self.load().start()
        elif s == 1:
            if self.loaded is not None:
                self.load().wait()
            self.copy("pair").wait_recv()

            @pl.loop(0, LINE)
            def _(i):
                for j in range(2):
                    for k in range(2):
                        self.add(self.at(i, j, k), self.pairbuf[i, j, k])

            self.copy("1a").start()
            self.copy("1b").start()
        elif s == 2:
            self.copy("1a").wait_recv()
            self.copy("1b").wait_recv()

            @pl.loop(0, LINE)
            def _(i):
                for k in range(2):
                    self.add(self.at(i, y, k, 0), self.buf1a[i, k])
                    self.add(self.at(i, k, x, 1), self.buf1b[i, k])

            self.copy("2a").start()
            self.copy("2b").start()
        elif s == 3:
            self.copy("2a").wait_recv()
            self.copy("2b").wait_recv()

            @pl.loop(0, LINE)
            def _(i):
                self.add(self.at(i, y, x, 0), self.buf2a[i])
                self.add(self.at(i, y, x, 1), self.buf2b[i])

            for k in range(1, LINE):
                self.line_copy(k).start()
        else:
            total = as_float(self.at(z, y, x)[...])
            for k in range(1, LINE):
                self.line_copy(k).wait_recv()
                total = total + as_float(self.line[k - 1])
            self.finish(total)

    def drain(self):
        for name in ("pair", "1a", "1b", "2a", "2b"):
            self.copy(name).wait_send()
        for k in range(1, LINE):
            self.line_copy(k).wait_send()


SMALL = (16, 256)


def back_kernel(
    shape, plan, x_ref, normed_ref, q_ref, k_ref, v_ref, probs_ref, mixed_ref, attn_ref, gres_ref, wqkv_ref, wproj_ref, vec_ref,
    two_ref, hidden_ref, index_g, index_l, gfc1_ref, gfc2_ref,
    gxg_ref, gxl_ref, sqkv_ref, sproj_ref, sfc1_ref, sfc2_ref, ssmall_ref,
    gqkv, gmixed, bsum, vecs, tsum, corner, *scratch,
):
    packs, glob, heads, groups, blocks, grids = shape
    step = pl.program_id(0)
    rows, features = normed_ref.shape
    seq = rows // packs
    width = features // heads
    lanes = features // groups
    scale = width**-0.5
    vec = lambda k: vec_ref[pl.ds(k, 1), :]
    size = rows // blocks
    last = 1 + packs * groups + 1 + blocks

    send, recv = scratch[-2:]
    scratch = scratch[:-2]
    big = 2 * SPLIT
    owns = list(scratch[:big]) + [None] * (groups + 2)
    terms = scratch[big : big + groups + 2]
    bufs = scratch[big + groups + 2 :]

    def put(ref):
        def finish(value):
            ref[...] = value

        return finish

    def put_group(g):
        def finish(value):
            for i in range(3):
                sqkv_ref[:, pl.ds(i * features + g * lanes, lanes)] = value[:, i * lanes : (i + 1) * lanes]

        return finish

    tall, wide = gfc2_ref.shape[4] // SPLIT, gfc1_ref.shape[5] // SPLIT
    sources, ends = [], []
    for k in range(SPLIT):
        sources.append(gfc2_ref.at[EVERY, EVERY, EVERY, EVERY, pl.ds(k * tall, tall)])
        ends.append(put(sfc2_ref.at[pl.ds(k * tall, tall)]))
    for k in range(SPLIT):
        sources.append(gfc1_ref.at[EVERY, EVERY, EVERY, EVERY, EVERY, pl.ds(k * wide, wide)])
        ends.append(put(sfc1_ref.at[EVERY, pl.ds(k * wide, wide)]))
    sources += list(terms)
    ends += [put(sproj_ref)] + [put_group(g) for g in range(groups)] + [put(ssmall_ref)]
    flows = [
        Scatter(sources[t], owns[t], bufs[Scatter.BUFS * t : Scatter.BUFS * (t + 1)], send.at[t], recv.at[t], ends[t]) for t in range(len(ends))
    ]

    def slot(k):
        for t, s in plan[k]:
            flows[t].stage(s)

    def fill(t, value):
        ref = terms[t]
        count = ref.shape[-2]
        for d in range(LINE * 8):
            ref[d // 8, d // 4 % 2, d // 2 % 2, d % 2] = value[d * count : (d + 1) * count].astype(ref.dtype)

    @pl.when(step == 0)
    def _():
        greet()
        slot(0)
        zero = jnp.zeros((1, features), jnp.float32)
        vecs[...] = jnp.zeros_like(vecs)

        def block(i, sums):
            part = pl.ds(pl.multiple_of(i * size, size), size)
            gres = gres_ref[part, :]
            gattn = (vec(V_G1) * gres).astype(jnp.bfloat16)
            gqkv[part, pl.ds(0, features)] = gattn
            gmixed[part, :] = dot_nt(gattn, wproj_ref[...]).astype(jnp.bfloat16)
            return (sums[0] + column_sum(as_float(gattn)), sums[1] + column_sum(gres * as_float(attn_ref[part, :])))

        sums = lax.fori_loop(0, blocks, block, (zero, zero))
        vecs[pl.ds(V_PB, 1), :] = sums[0]
        vecs[pl.ds(V_G1, 1), :] = sums[1]
        bsum[...] = jnp.zeros_like(bsum)
        fill(0, dot_tn(mixed_ref[...], gqkv[:, pl.ds(0, features)]))

    @pl.when((step >= 1) & (step <= packs * groups))
    def _():
        pack = (step - 1) % packs
        group = (step - 1) // packs
        part = pl.ds(pl.multiple_of(pack * seq, seq), seq)
        kind = jnp.where(pack < glob, 0, 1)
        for pair in range(heads // 2 // groups):
            at = 2 * width * pair
            wide = pl.ds(pl.multiple_of(group * lanes + at, 2 * width), 2 * width)
            queries = stack_heads(q_ref[:, pl.ds(at, 2 * width)], width)
            keys = k_ref[:, pl.ds(at, 2 * width)]
            values = v_ref[:, pl.ds(at, 2 * width)]
            grads = stack_heads(gmixed[part, wide], width)
            mixed = as_float(mixed_ref[part, wide])
            probs = probs_ref[0, pair]
            twice = jnp.concatenate([mixed, mixed], axis=0)
            inner = jnp.sum(as_float(grads) * twice, axis=-1, keepdims=True)
            gscores = as_float(probs) * (dot_nt(grads, values) - inner)
            head = group * (heads // groups) + 2 * pair
            bsum[kind, pl.ds(head, 2), :, pl.ds(0, seq)] += gscores.reshape(2, seq, seq)
            low = gscores.astype(jnp.bfloat16)
            gq = (merge_heads(dot(low, keys), width) * scale).astype(jnp.bfloat16)
            gk = (dot_tn(low, queries) * scale).astype(jnp.bfloat16)
            gv = dot_tn(probs, grads).astype(jnp.bfloat16)
            for i, piece in enumerate((gq, gk, gv)):
                at_lane = pl.multiple_of(group * lanes + at + i * features, 2 * width)
                gqkv[part, pl.ds(at_lane, 2 * width)] = piece

    for g in range(groups):
        @pl.when(step == packs * (g + 1))
        def _():
            pieces = [dot_tn(normed_ref[...], gqkv[:, pl.ds(i * features + g * lanes, lanes)]) for i in range(3)]
            fill(1 + g, jnp.concatenate(pieces, axis=1))

    @pl.when(step == packs * groups + 1)
    def _():
        tsum[...] = collect(
            grids, (bsum.at[0], bsum.at[1]), (index_g, index_l), (corner, corner), tsum.shape
        )

    @pl.when(step >= packs * groups + 2)
    def _():
        i = step - packs * groups - 2
        part = pl.ds(pl.multiple_of(i * size, size), size)
        low = gqkv[part, :]
        gnorm = dot_nt(low, wqkv_ref[...])
        unit, spread = unit_rows(as_float(x_ref[...]))
        vecs[pl.ds(V_LN1G, 1), :] += column_sum(gnorm * unit)
        vecs[pl.ds(V_LN1B, 1), :] += column_sum(gnorm)
        total = column_sum(as_float(low))
        vecs[pl.ds(V_QB, 1), :] += total[:, :features]
        vecs[pl.ds(V_VB, 1), :] += total[:, 2 * features :]
        value = gres_ref[part, :] + unit_back(gnorm * vec(V_LN1G), unit, spread)
        per_block = packs // blocks
        glob_len, loc_len, per_pack, slot = grids[0][1], grids[1][1], grids[1][2], grids[1][3]

        @pl.when(i < glob // per_block)
        def _():
            for n in range(per_block):
                gxg_ref[n] = value[n * seq : n * seq + glob_len].astype(gxg_ref.dtype)

        @pl.when(i >= glob // per_block)
        def _():
            for n in range(per_block):
                for k in range(per_pack):
                    start = n * seq + k * slot
                    gxl_ref[n * per_pack + k] = value[start : start + loc_len].astype(gxl_ref.dtype)

    @pl.when(step == last - 1)
    def _():
        for k, row in ((V_LN2G, 0), (V_LN2B, 1), (V_FB, 2), (V_G2, 3)):
            vecs[pl.ds(k, 1), :] = two_ref[pl.ds(row, 1), :]
        ref = terms[-1]
        ref[...] = jnp.zeros_like(ref)
        devices = LINE * 8
        count, wide, table = features // devices, hidden_ref.shape[1] // devices, tsum.shape[1] // devices
        for d in range(devices):
            block = ref.at[d // 8, d // 4 % 2, d // 2 % 2, d % 2]
            block[:, pl.ds(0, count)] = vecs[:, pl.ds(d * count, count)]
            block[pl.ds(10, 1), pl.ds(0, wide)] = hidden_ref[:, pl.ds(d * wide, wide)]
            block[pl.ds(0, heads), pl.ds(128, table)] = tsum[:, pl.ds(d * table, table)]

    for k in range(1, last):
        @pl.when(step == k)
        def _():
            slot(k)

    @pl.when(step == last - 1)
    def _():
        for flow in flows:
            flow.drain()


def back_plan(steps, groups, packs):
    plan = [[] for _ in range(steps)]
    done = steps - 1
    starts = list(PLAN_BIG) + [PLAN_PROJ]
    starts += [[packs * (g + 1) + k for k in PLAN_GROUP[g]] for g in range(groups)] + [[done] * Scatter.STAGES]
    events = []
    for t, at in enumerate(starts):
        for s, k in enumerate(at):
            events.append((min(k, done), s if k >= done else 0, t, s))
    for k, _, t, s in sorted(events):
        plan[k].append((t, s))
    return plan


SPLIT = 2
PLAN_BIG = ([0, 1, 9, 14, 18], [0, 1, 13, 18, 20], [0, 9, 17, 20, 22], [0, 13, 19, 21, 22])
PLAN_PROJ = [1, 2, 10, 14, 17]
PLAN_GROUP = ([0, 2, 9, 13, 14], [0, 2, 7, 9, 10], [0, 1, 3, 4, 4])


def attend_back(
    x, normed, qkv, probs, mixed, attn, gres, wqkv, wproj, vectors, two, hidden, indices, gfc1, gfc2, packs, glob, heads,
    grids, table_rows, out_dtype, lanes,
):
    rows, features = x.shape
    seq = rows // packs
    groups, blocks = 3, 3
    per_block = packs // blocks
    cols = features // groups
    steps = 1 + packs * groups + 1 + blocks
    first_block = packs * groups + 2
    whole = lambda shape: pl.BlockSpec(shape, lambda s: (0,) * len(shape), pipeline_mode=pl.Buffered(1))
    at = lambda s: jnp.clip(s - 1, 0, packs * groups - 1)
    part = lambda i: pl.BlockSpec((seq, cols), lambda s: (at(s) % packs, i * groups + at(s) // packs))
    any_ref = pl.BlockSpec(memory_space=pl.ANY)
    by_block = pl.BlockSpec((rows // blocks, features), lambda s: (jnp.clip(s - first_block, 0, blocks - 1), 0))
    padded = pad_index(indices, lanes)
    shard = lambda t: t.shape[4:]
    term_shapes = [(features // 32, features)] + [(features // 32, 3 * cols)] * groups
    tall, wide = (shard(gfc2)[0] // SPLIT, shard(gfc2)[1]), (shard(gfc1)[0], shard(gfc1)[1] // SPLIT)
    flow_shapes = [(tall, gfc2.dtype)] * SPLIT + [(wide, gfc1.dtype)] * SPLIT
    scratch = [
        pltpu.VMEM((rows, 3 * features), jnp.bfloat16),
        pltpu.VMEM((rows, features), jnp.bfloat16),
        pltpu.VMEM((2, heads, seq, lanes), jnp.float32),
        pltpu.VMEM((16, features), jnp.float32),
        pltpu.VMEM((heads, table_rows), jnp.float32),
        pltpu.VMEM((2, heads, ROW_SLOTS, lanes), jnp.float32),
    ]
    scratch += [pltpu.VMEM((LINE, 2, 2) + s, d) for s, d in flow_shapes]
    flow_shapes += [(s, jnp.bfloat16) for s in term_shapes] + [(SMALL, jnp.float32)]
    scratch += [pltpu.VMEM(GRID + s, jnp.bfloat16) for s in term_shapes] + [pltpu.VMEM(GRID + SMALL, jnp.float32)]
    for s, d in flow_shapes:
        scratch += Scatter.scratch(s, d)
    scratch += [pltpu.SemaphoreType.DMA((len(flow_shapes), Scatter.SEMS))] * 2
    return pl.pallas_call(
        functools.partial(
            back_kernel, (packs, glob, heads, groups, blocks, grids), back_plan(steps, groups, packs)
        ),
        grid=(steps,),
        out_shape=[
            jax.ShapeDtypeStruct((glob, grids[0][1], features), out_dtype),
            jax.ShapeDtypeStruct(((packs - glob) * grids[1][2], grids[1][1], features), out_dtype),
            jax.ShapeDtypeStruct((features // 32, 3 * features), jnp.float32),
            jax.ShapeDtypeStruct((features // 32, features), jnp.float32),
            jax.ShapeDtypeStruct(shard(gfc1), jnp.float32),
            jax.ShapeDtypeStruct(shard(gfc2), jnp.float32),
            jax.ShapeDtypeStruct(SMALL, jnp.float32),
        ],
        in_specs=[
            by_block,
            whole((rows, features)),
            part(0), part(1), part(2),
            pl.BlockSpec((1, heads // 2 // groups, 2 * seq, seq), lambda s: (at(s) % packs, at(s) // packs, 0, 0)),
            whole((rows, features)),
            whole((rows, features)),
            whole((rows, features)),
            whole(wqkv.shape),
            whole(wproj.shape),
            whole(vectors.shape),
            whole(two.shape),
            whole(hidden.shape),
            whole(padded[0].shape),
            whole(padded[1].shape),
            any_ref,
            any_ref,
        ],
        out_specs=[
            pl.BlockSpec(
                (per_block, grids[0][1], features),
                lambda s: (jnp.clip(s - first_block, 0, glob // per_block - 1), 0, 0),
            ),
            pl.BlockSpec(
                (per_block * grids[1][2], grids[1][1], features),
                lambda s: (jnp.maximum(s - first_block - glob // per_block, 0), 0, 0),
            ),
            whole((features // 32, 3 * features)),
            whole((features // 32, features)),
            whole(shard(gfc1)),
            whole(shard(gfc2)),
            whole(SMALL),
        ],
        scratch_shapes=scratch,
        compiler_params=pltpu.CompilerParams(vmem_limit_bytes=BIG, collective_id=1, has_side_effects=True),
        name="attend_back",
    )(x, normed, qkv, qkv, qkv, probs, mixed, attn, gres, wqkv, wproj, vectors, two, hidden, *padded, gfc1, gfc2)


def gather_order():
    small, qkv, proj, one, two = range(5)
    head = [(small, 0), (qkv, 0), (proj, 0), (small, 1), (small, 2), (small, 3), (small, 4), "unpack"]
    head += [(qkv, 1), (one, 0), (proj, 1), "expand global", (qkv, 2), (two, 0), (one, 1), (proj, 2), "expand local"]
    head += [(qkv, 3), (two, 1), (one, 2), (proj, 3), (qkv, 4), (proj, 4)]
    return head, {1: [], 2: [(two, 2), (one, 3)], 3: [], 4: [], 5: [(two, 3)], 6: [(one, 4)], 7: [(two, 4)]}


def front_kernel(
    shape, xg_ref, xl_ref, small_ref, oqkv_ref, oproj_ref, ofc1_ref, ofc2_ref, index_g, index_l,
    x_ref, normed_ref, qkv_ref, probs_ref, mixed_ref, attn_ref, resid_ref, vec_ref, hidden_ref,
    fqkv_ref, fproj_ref, ffc1_ref, ffc2_ref,
    table, bias, rows_g, rows_l, padded, wqkv, wproj, small_full, load, send, recv,
):
    packs, glob, heads, grids = shape
    step = pl.program_id(0)
    seq, features = x_ref.shape
    width = features // heads
    devices = LINE * 8
    vec = lambda k: vec_ref[pl.ds(k, 1), :]
    owns = (small_ref, oqkv_ref, oproj_ref, ofc1_ref, ofc2_ref)
    fulls = (small_full, fqkv_ref, fproj_ref, ffc1_ref, ffc2_ref)
    flows = [Gather(o, f, send.at[t], recv.at[t]) for t, (o, f) in enumerate(zip(owns, fulls))]
    head, later = gather_order()

    def each_shard(act):
        @pl.loop(0, devices)
        def _(d):
            for k, (ref, held) in enumerate(((fqkv_ref, wqkv), (fproj_ref, wproj))):
                count = held.shape[0] // devices
                part = held.at[pl.ds(pl.multiple_of(d * count, 8), count)]
                act(pltpu.make_async_copy(ref.at[d // 8, d // 4 % 2, d // 2 % 2, d % 2], part, load.at[k, d]))

    @pl.when(step == 0)
    def _():
        greet()
        table[...] = jnp.zeros_like(table)
        for item in head:
            if item == "unpack":
                count, wide = features // devices, hidden_ref.shape[1] // devices
                lines = table.shape[1] // devices
                for d in range(devices):
                    block = small_full.at[d // 8, d // 4 % 2, d // 2 % 2, d % 2]
                    vec_ref[:, pl.ds(d * count, count)] = block[:, pl.ds(0, count)]
                    hidden_ref[:, pl.ds(d * wide, wide)] = block[pl.ds(10, 1), pl.ds(0, wide)]
                    table[pl.ds(0, heads), pl.ds(d * lines, lines)] = block[pl.ds(0, heads), pl.ds(128, lines)]
            elif item == "expand global":
                expand(grids[:1], table, (index_g,), (bias.at[0],), (rows_g,))
            elif item == "expand local":
                expand(grids[1:], table, (index_l,), (bias.at[1],), (rows_l,))
            else:
                flows[item[0]].stage(item[1])
        each_shard(lambda copy: copy.start())
        each_shard(lambda copy: copy.wait())

    @pl.when((step >= 1) & (step <= packs))
    def _():
        padded[...] = jnp.zeros_like(padded)

        @pl.when(step <= glob)
        def _():
            padded[pl.ds(0, xg_ref.shape[1]), :] = as_float(xg_ref[0])

        @pl.when(step > glob)
        def _():
            for k in range(xl_ref.shape[0]):
                padded[pl.ds(k * grids[1][3], xl_ref.shape[1]), :] = as_float(xl_ref[k])

        inputs = padded[...]
        x_ref[...] = inputs.astype(jnp.bfloat16)
        unit, _ = unit_rows(inputs)
        normed = (unit * vec(V_LN1G) + vec(V_LN1B)).astype(jnp.bfloat16)
        normed_ref[...] = normed
        qkv_ref[:, pl.ds(0, features)] = (dot(normed, wqkv[:, pl.ds(0, features)]) + vec(V_QB)).astype(jnp.bfloat16)
        qkv_ref[:, pl.ds(features, features)] = dot(normed, wqkv[:, pl.ds(features, features)]).astype(jnp.bfloat16)
        qkv_ref[:, pl.ds(2 * features, features)] = (
            dot(normed, wqkv[:, pl.ds(2 * features, features)]) + vec(V_VB)
        ).astype(jnp.bfloat16)
        kind = jnp.where(step <= glob, 0, 1)
        for pair in range(heads // 2):
            at = 2 * width * pair
            queries = stack_heads(qkv_ref[:, pl.ds(at, 2 * width)], width)
            keys = qkv_ref[:, pl.ds(features + at, 2 * width)]
            values = qkv_ref[:, pl.ds(2 * features + at, 2 * width)]
            part = bias[kind, pl.ds(2 * pair, 2), :, pl.ds(0, seq)].reshape(2 * seq, seq)
            scores = dot_nt(queries, keys) * (width**-0.5) + part
            weights = jnp.exp(scores - jnp.max(scores, axis=-1, keepdims=True))
            probs = (weights * (1.0 / jnp.sum(weights, axis=-1, keepdims=True))).astype(jnp.bfloat16)
            probs_ref[0, pair] = probs
            mixed_ref[:, pl.ds(at, 2 * width)] = merge_heads(dot(probs, values), width).astype(jnp.bfloat16)

        attn = dot(mixed_ref[...], wproj[...]) + vec(V_PB)
        attn_ref[...] = attn.astype(jnp.bfloat16)
        resid_ref[...] = inputs + vec(V_G1) * attn

    for k, items in later.items():
        if items:
            @pl.when(step == k)
            def _():
                for t, s in items:
                    flows[t].stage(s)

    @pl.when(step == packs + 1)
    def _():
        for flow in flows:
            flow.drain()


def attend_front(xg, xl, small, shards, indices, packs, heads, grids, seq, table_rows):
    glob, glob_len, features = xg.shape
    loc, loc_len, _ = xl.shape
    per_pack = loc // (packs - glob)
    rows, lanes = packs * seq, round_up(seq, 128)
    hidden = shards[2].shape[1]
    padded = pad_index(indices, lanes)
    whole = lambda shape: pl.BlockSpec(shape, lambda s: (0,) * len(shape), pipeline_mode=pl.Buffered(1))
    at = lambda s: jnp.clip(s - 1, 0, packs - 1)
    by_rows = lambda cols: pl.BlockSpec((seq, cols), lambda s: (at(s), 0))
    any_ref = pl.BlockSpec(memory_space=pl.ANY)
    owns = [small] + list(shards)
    return pl.pallas_call(
        functools.partial(front_kernel, (packs, glob, heads, grids)),
        grid=(packs + 2,),
        out_shape=[
            jax.ShapeDtypeStruct((rows, features), jnp.bfloat16),
            jax.ShapeDtypeStruct((rows, features), jnp.bfloat16),
            jax.ShapeDtypeStruct((rows, 3 * features), jnp.bfloat16),
            jax.ShapeDtypeStruct((packs, heads // 2, 2 * seq, seq), jnp.bfloat16),
            jax.ShapeDtypeStruct((rows, features), jnp.bfloat16),
            jax.ShapeDtypeStruct((rows, features), jnp.bfloat16),
            jax.ShapeDtypeStruct((rows, features), jnp.float32),
            jax.ShapeDtypeStruct((16, features), jnp.float32),
            jax.ShapeDtypeStruct((1, hidden), jnp.float32),
        ]
        + [jax.ShapeDtypeStruct(GRID + s.shape, s.dtype) for s in shards],
        in_specs=[
            pl.BlockSpec((1, glob_len, features), lambda s: (jnp.minimum(at(s), glob - 1), 0, 0)),
            pl.BlockSpec((per_pack, loc_len, features), lambda s: (jnp.maximum(at(s) - glob, 0), 0, 0)),
        ]
        + [whole(o.shape) for o in owns]
        + [whole(padded[0].shape), whole(padded[1].shape)],
        out_specs=[
            by_rows(features),
            by_rows(features),
            by_rows(3 * features),
            pl.BlockSpec((1, heads // 2, 2 * seq, seq), lambda s: (at(s), 0, 0, 0)),
            by_rows(features),
            by_rows(features),
            by_rows(features),
            whole((16, features)),
            whole((1, hidden)),
        ]
        + [any_ref] * 4,
        scratch_shapes=[
            pltpu.VMEM((16, table_rows), jnp.float32),
            pltpu.VMEM((2, heads, seq, lanes), jnp.float32),
            pltpu.VMEM((2, heads, ROW_SLOTS, lanes), jnp.float32),
            pltpu.VMEM((2, heads, ROW_SLOTS, lanes), jnp.float32),
            pltpu.VMEM((seq, features), jnp.float32),
            pltpu.VMEM((features, 3 * features), jnp.bfloat16),
            pltpu.VMEM((features, features), jnp.bfloat16),
            pltpu.VMEM(GRID + SMALL, jnp.float32),
            pltpu.SemaphoreType.DMA((2, LINE * 8)),
            pltpu.SemaphoreType.DMA((len(owns), Gather.SEMS + 1)),
            pltpu.SemaphoreType.DMA((len(owns), Gather.SEMS + 1)),
        ],
        compiler_params=pltpu.CompilerParams(vmem_limit_bytes=BIG, collective_id=0, has_side_effects=True),
        name="attend_front",
    )(xg, xl, *owns, *padded)


def gather_params(vectors, hidden_shift, table, weights):
    whole = lambda v: lax.all_gather(v, "fsdp", axis=0, tiled=True)
    return ([as_float(whole(v)) for v in vectors], as_float(whole(hidden_shift)), as_float(whole(table)), [whole(w) for w in weights])


def pack_small(vectors, hidden_shift, table):
    rows, lanes = SMALL[0], SMALL[1] // 2
    fit = lambda v: jnp.pad(as_float(v), ((0, 0), (0, lanes - v.shape[1])))
    left = jnp.concatenate([fit(jnp.stack(vectors)), fit(hidden_shift[None])])
    fill = lambda v: jnp.pad(v, ((0, rows - v.shape[0]), (0, 0)))
    return jnp.concatenate([fill(left), fill(fit(table.T))], axis=1)


def scatter_grads(vectors, hidden_shift, table, weights):
    share = lambda v: lax.psum_scatter(as_float(v), "fsdp", scatter_dimension=0, tiled=True)
    return ([share(v) for v in vectors], share(hidden_shift), share(table), [share(w) for w in weights])


def slot_rows(values, slot, seq):
    crops, length, features = values.shape
    per_pack = seq // slot
    values = jnp.pad(values, ((0, 0), (0, slot - length), (0, 0)))
    values = values.reshape(crops // per_pack, per_pack * slot, features)
    return jnp.pad(values, ((0, 0), (0, seq - per_pack * slot), (0, 0)))


def crop_rows(packed, slot, crops, length):
    packs, seq, features = packed.shape
    per_pack = seq // slot
    return packed[:, : per_pack * slot].reshape(crops, slot, features)[:, :length]


def per_device(
    x_global, x_local, cot_global, cot_local, global_count, local_count, index_global, index_local,
    ln1_gain, ln1_bias, qkv_weight, q_bias, v_bias, proj_weight, proj_bias, gamma1, bias_table,
    ln2_gain, ln2_bias, fc1_weight, fc1_bias, fc2_weight, fc2_bias, gamma2,
):
    glob, glob_len, features = x_global.shape
    loc, loc_len = x_local.shape[:2]
    heads = bias_table.shape[1]
    seq = round_up(glob_len, 16)
    slot = round_up(loc_len, 8)
    per_pack = seq // slot
    packs = glob + loc // per_pack
    devices = lax.axis_size("fsdp")
    vector_args = [ln1_gain, ln1_bias, q_bias, v_bias, proj_bias, gamma1, ln2_gain, ln2_bias, fc2_bias, gamma2]
    weights = [qkv_weight, proj_weight, fc1_weight, fc2_weight]
    table_rows = bias_table.shape[0] * devices
    indices = (index_global, index_local)
    sides = (math.isqrt(glob_len - 1), math.isqrt(loc_len - 1))
    grids = ((sides[0], glob_len, 1, seq), (sides[1], loc_len, per_pack, slot))

    rows_of = lambda g, l: jnp.concatenate([slot_rows(g, seq, seq), slot_rows(l, slot, seq)]).reshape(-1, features)
    if devices == 32:
        x, normed, qkv, probs, mixed, attn, resid, vectors, hidden_row, *full = attend_front(
            x_global, x_local, pack_small(vector_args, fc1_bias, bias_table), weights, indices, packs, heads, grids, seq,
            table_rows,
        )
        qkv_full, proj_full, fc1_full, fc2_full = [f.reshape(devices * f.shape[4], f.shape[5]) for f in full]
        lanes = round_up(seq, 128)
    else:
        small_full, hidden_full, table_full, (qkv_full, proj_full, fc1_full, fc2_full) = gather_params(
            vector_args, fc1_bias, bias_table, weights
        )
        vectors = jnp.pad(jnp.stack(small_full), ((0, 6), (0, 0)))
        hidden_row = hidden_full[None]
        table = jnp.pad(table_full.T, ((0, round_up(heads, 16) - heads), (0, 0))).astype(jnp.bfloat16)
        x = rows_of(x_global, x_local)
        bias = expand_bias(table, indices, grids, heads, seq)
        lanes = bias.shape[-1]
        normed, qkv, probs, mixed, attn, resid = attend_forward(
            x, qkv_full, proj_full, vectors, bias, packs, glob, heads
        )
    out_global, out_local, gres, gfc1, gfc2, gfc1_shift, small_two = mlp_both(
        global_count, local_count, resid, cot_global, cot_local, vectors, fc1_full, hidden_row, fc2_full, seq, slot,
        x_global.dtype, jnp.bfloat16,
    )
    if devices == 32:
        shaped = lambda g: g.reshape(GRID + (g.shape[0] // devices, g.shape[1]))
        gx_global, gx_local, *shares, small = attend_back(
            x, normed, qkv, probs, mixed, attn, gres, qkv_full, proj_full, vectors, small_two, gfc1_shift, indices,
            shaped(gfc1), shaped(gfc2), packs, glob, heads, grids, table_rows, x_global.dtype, lanes,
        )
        sums = [small[k, : features // devices] for k in range(10)]
        hidden_sum = small[10, : fc1_bias.shape[0]]
        table_sum = small[:heads, 128 : 128 + table_rows // devices].T
    else:
        gx, gqkv, gproj, bias_sums, small_one, gqkv_shift = attend_backward(
            x, normed, qkv, probs, mixed, attn, gres, qkv_full, proj_full, vectors, packs, glob, heads,
            x_global.dtype, jnp.bfloat16, lanes,
        )
        gx = gx.reshape(packs, seq, features)
        gx_global, gx_local = crop_rows(gx[:glob], seq, glob, glob_len), crop_rows(gx[glob:], slot, loc, loc_len)
        gtable = collect_bias(bias_sums, indices, grids, table_rows).T
        vector_grads = [
            small_one[0], small_one[1], gqkv_shift[0, :features], gqkv_shift[0, 2 * features :], small_one[2],
            small_one[3], small_two[0], small_two[1], small_two[2], small_two[3],
        ]
        sums, hidden_sum, table_sum, shares = scatter_grads(
            vector_grads, gfc1_shift[0], gtable, [gqkv, gproj, gfc1, gfc2]
        )
    return (
        out_global, out_local, gx_global, gx_local,
        sums[0], sums[1], shares[0], sums[2], sums[3], shares[1], sums[4], sums[5], table_sum,
        sums[6], sums[7], shares[2], hidden_sum, shares[3], sums[8], sums[9],
    )


def solution(mesh):
    placed = (
        P("fsdp", None, None),
        P("fsdp", None, None),
        P("fsdp", None, None),
        P("fsdp", None, None),
        P("fsdp"),
        P("fsdp"),
        P(),
        P(),
        P("fsdp"),
        P("fsdp"),
        P("fsdp", None),
        P("fsdp"),
        P("fsdp"),
        P("fsdp", None),
        P("fsdp"),
        P("fsdp"),
        P("fsdp", None),
        P("fsdp"),
        P("fsdp"),
        P("fsdp", None),
        P("fsdp"),
        P("fsdp", None),
        P("fsdp"),
        P("fsdp"),
    )
    return jax.shard_map(
        per_device,
        mesh=mesh,
        in_specs=placed,
        out_specs=(
            P("fsdp", None, None),
            P("fsdp", None, None),
            P("fsdp", None, None),
            P("fsdp", None, None),
            P("fsdp"),
            P("fsdp"),
            P("fsdp", None),
            P("fsdp"),
            P("fsdp"),
            P("fsdp", None),
            P("fsdp"),
            P("fsdp"),
            P("fsdp", None),
            P("fsdp"),
            P("fsdp"),
            P("fsdp", None),
            P("fsdp"),
            P("fsdp", None),
            P("fsdp"),
            P("fsdp"),
        ),
        check_vma=False,
    )
```

```python
import functools
import math

import jax
import jax.numpy as jnp
from jax import lax
from jax.experimental import pallas as pl
from jax.experimental.pallas import tpu as pltpu
from jax.sharding import PartitionSpec as P

EPSILON = 1e-06
NEG = -1e30
ROWS_IN = (((0,), (0,)), ((), ()))
COLS_IN = (((1,), (1,)), ((), ()))
BIG = 60 * 1024 * 1024


def as_float(values):
    return values.astype(jnp.float32)


def dot(a, b):
    return jnp.dot(a, b, preferred_element_type=jnp.float32)


def dot_tn(a, b):
    return lax.dot_general(a, b, ROWS_IN, preferred_element_type=jnp.float32)


def dot_nt(a, b):
    return lax.dot_general(a, b, COLS_IN, preferred_element_type=jnp.float32)


def round_up(value, unit):
    return (value + unit - 1) // unit * unit


def unit_rows(values):
    average = jnp.mean(values, axis=-1, keepdims=True)
    centered = values - average
    spread = lax.rsqrt(jnp.mean(centered * centered, axis=-1, keepdims=True) + EPSILON)
    return (centered * spread, spread)


def unit_back(grad, unit, spread):
    return spread * (
        grad - jnp.mean(grad, axis=-1, keepdims=True) - unit * jnp.mean(grad * unit, axis=-1, keepdims=True)
    )


def column_sum(values):
    return jnp.sum(values, axis=0, keepdims=True)


V_LN1G, V_LN1B, V_QB, V_VB, V_PB, V_G1, V_LN2G, V_LN2B, V_FB, V_G2 = range(10)


MLP_PLAN = {
    (0, "end"): ((0, 0),), (1, 0): ((0, 1),), (1, 2): ((0, 2),), (1, "end"): ((0, 3), (1, 0)), (2, 0): ((1, 1),),
    (2, 1): ((0, 4),), (2, 2): ((1, 2),), (2, "end"): ((1, 3),), (2, "last"): ((1, 4),),
}


def fill_terms(ref, value):
    count = ref.shape[-2]
    for d in range(LINE * 8):
        ref[d // 8, d // 4 % 2, d // 2 % 2, d % 2] = value[d * count : (d + 1) * count].astype(ref.dtype)


def put(ref):
    def finish(value):
        ref[...] = value

    return finish


def mlp_kernel(
    steps, blocks, seq, slot, shared, gcount_ref, lcount_ref, resid_ref, cg_ref, cl_ref, vec_ref, w1_ref, b1_ref, w2_ref,
    outg_ref, outl_ref, gres_ref, gw1_ref, gw2_ref, gb1_ref, small_ref, *rest,
):
    step = pl.program_id(0)
    flows = []
    if shared:
        share_ref, *rest = rest
        send, recv = rest[-2:]
        terms, bufs = rest[7 : 7 + shared], rest[7 + shared : -2]
        wide = w1_ref.shape[1]
        for t in range(shared):
            pieces = bufs[Scatter.BUFS * t : Scatter.BUFS * (t + 1)]
            finish = put(share_ref.at[EVERY, pl.ds(t * wide, wide)])
            flows.append(Scatter(terms[t], None, pieces, send.at[t], recv.at[t], finish))
    cot, normed, gbranch, branch, gnorm, active, ghidden = rest[:7]

    def slot_at(where):
        for (s, at), items in MLP_PLAN.items() if shared else ():
            if at == where if isinstance(where, str) else isinstance(at, int):
                @pl.when((step == s) if isinstance(where, str) else ((step == s) & (where == at)))
                def _():
                    for t, n in items:
                        flows[t].stage(n)

    rows, features = resid_ref.shape
    size = rows // blocks
    vec = lambda k: vec_ref[pl.ds(k, 1), :]
    glob, glob_len, _ = cg_ref.shape
    loc, loc_len, _ = cl_ref.shape
    per_pack = seq // slot
    packs = glob + loc // per_pack

    def kept(k, count_ref):
        return jnp.where(k < count_ref[0], 1.0, 0.0)

    @pl.when(step == 0)
    def _():
        if shared:
            greet()
        cot[...] = jnp.zeros_like(cot)

        @pl.loop(0, glob)
        def _(p):
            rows_of = pl.ds(pl.multiple_of(p * seq, seq), glob_len)
            cot[rows_of, :] = (as_float(cg_ref[p]) * kept(p, gcount_ref)).astype(jnp.bfloat16)

        @pl.loop(0, packs - glob)
        def _(p):
            for k in range(per_pack):
                crop = p * per_pack + k
                rows_of = pl.ds(pl.multiple_of((glob + p) * seq + k * slot, 8), loc_len)
                cot[rows_of, :] = (as_float(cl_ref[crop]) * kept(crop, lcount_ref)).astype(jnp.bfloat16)

        @pl.loop(0, blocks)
        def _(i):
            part = pl.ds(pl.multiple_of(i * size, size), size)
            unit, _ = unit_rows(resid_ref[part, :])
            normed[part, :] = (unit * vec(V_LN2G) + vec(V_LN2B)).astype(jnp.bfloat16)
            gbranch[part, :] = (vec(V_G2) * as_float(cot[part, :])).astype(jnp.bfloat16)

    w1, w2 = w1_ref[...], w2_ref[...]

    def block(i, hidden_sum):
        part = pl.ds(pl.multiple_of(i * size, size), size)
        hidden = dot(normed[part, :], w1) + b1_ref[...]
        phi = 0.5 * lax.erf(hidden * (0.5**0.5)) + 0.5
        low = (hidden * phi).astype(jnp.bfloat16)
        active[part, :] = low
        slope = phi + hidden * (jnp.exp(hidden * hidden * -0.5) * 0.3989422804014327)
        add = dot(low, w2)
        grad = dot_nt(gbranch[part, :], w2) * slope
        glow = grad.astype(jnp.bfloat16)
        ghidden[part, :] = glow
        gadd = dot_nt(glow, w1)

        @pl.when(step == 0)
        def _():
            branch[part, :] = add
            gnorm[part, :] = gadd

        @pl.when(step > 0)
        def _():
            branch[part, :] = branch[part, :] + add
            gnorm[part, :] = gnorm[part, :] + gadd

        slot_at(i)
        return hidden_sum + column_sum(as_float(glow))

    gb1_ref[...] = lax.fori_loop(0, blocks, block, jnp.zeros(gb1_ref.shape, jnp.float32))
    gw2_ref[...] = dot_tn(active[...], gbranch[...]).astype(gw2_ref.dtype)
    for t in range(shared):
        @pl.when(step == t)
        def _():
            fill_terms(terms[t], dot_tn(normed[...], ghidden[...]))

    @pl.when(step >= shared)
    def _():
        gw1_ref[...] = dot_tn(normed[...], ghidden[...]).astype(gw1_ref.dtype)

    slot_at("end")

    @pl.when(step == steps - 1)
    def _():
        zero = jnp.zeros((1, features), jnp.float32)

        def pack(p, sums, write):
            part = pl.ds(pl.multiple_of(p * seq, seq), seq)
            resid = resid_ref[part, :]
            full = branch[part, :] + vec(V_FB)
            write(p, resid + vec(V_G2) * full)
            grad = as_float(cot[part, :])
            unit, spread = unit_rows(resid)
            gn = gnorm[part, :]
            gres_ref[part, :] = grad + unit_back(gn * vec(V_LN2G), unit, spread)
            return (
                sums[0] + column_sum(gn * unit),
                sums[1] + column_sum(gn),
                sums[2] + column_sum(as_float(gbranch[part, :])),
                sums[3] + column_sum(grad * full),
            )

        def write_glob(p, value):
            outg_ref[p] = (value[:glob_len] * kept(p, gcount_ref)).astype(outg_ref.dtype)

        def write_loc(p, value):
            for k in range(per_pack):
                crop = (p - glob) * per_pack + k
                piece = value[k * slot : k * slot + loc_len] * kept(crop, lcount_ref)
                outl_ref[crop] = piece.astype(outl_ref.dtype)

        sums = lax.fori_loop(0, glob, lambda p, s: pack(p, s, write_glob), (zero,) * 4)
        sums = lax.fori_loop(glob, packs, lambda p, s: pack(p, s, write_loc), sums)
        small_ref[...] = jnp.zeros_like(small_ref)
        for k in range(4):
            small_ref[pl.ds(k, 1), :] = sums[k]

    slot_at("last")

    if shared:
        @pl.when(step == steps - 1)
        def _():
            for flow in flows:
                flow.drain()


def mlp_both(gcount, lcount, resid, cg, cl, vectors, w1, b1, w2, seq, slot, out_dtype, grad_dtype, shared):
    rows, features = resid.shape
    hidden = w1.shape[1]
    chunk = 1024
    steps = hidden // chunk
    whole = lambda shape: pl.BlockSpec(shape, lambda j: (0,) * len(shape), pipeline_mode=pl.Buffered(1))
    scalar = pl.BlockSpec(memory_space=pltpu.SMEM)
    shares, extra, params = [], [], {}
    if shared:
        share = (features // (LINE * 8), chunk)
        shares = [jax.ShapeDtypeStruct((share[0], shared * chunk), jnp.float32)]
        extra = [pltpu.VMEM(GRID + share, jnp.bfloat16)] * shared
        extra += Scatter.scratch(share, jnp.bfloat16) * shared
        extra += [pltpu.SemaphoreType.DMA((shared, Scatter.SEMS))] * 2
        params = dict(collective_id=2, has_side_effects=True)
    return pl.pallas_call(
        functools.partial(mlp_kernel, steps, 3, seq, slot, shared),
        grid=(steps,),
        out_shape=[
            jax.ShapeDtypeStruct(cg.shape, out_dtype),
            jax.ShapeDtypeStruct(cl.shape, out_dtype),
            jax.ShapeDtypeStruct((rows, features), jnp.float32),
            jax.ShapeDtypeStruct((features, hidden - shared * chunk), grad_dtype),
            jax.ShapeDtypeStruct((hidden, features), grad_dtype),
            jax.ShapeDtypeStruct((1, hidden), jnp.float32),
            jax.ShapeDtypeStruct((8, features), jnp.float32),
        ]
        + shares,
        in_specs=[
            scalar,
            scalar,
            whole((rows, features)),
            whole(cg.shape),
            whole(cl.shape),
            whole(vectors.shape),
            pl.BlockSpec((features, chunk), lambda j: (0, j)),
            pl.BlockSpec((1, chunk), lambda j: (0, j)),
            pl.BlockSpec((chunk, features), lambda j: (j, 0)),
        ],
        out_specs=[
            whole(cg.shape),
            whole(cl.shape),
            whole((rows, features)),
            pl.BlockSpec((features, chunk), lambda j: (0, jnp.maximum(j - shared, 0))),
            pl.BlockSpec((chunk, features), lambda j: (j, 0)),
            pl.BlockSpec((1, chunk), lambda j: (0, j)),
            whole((8, features)),
        ]
        + [whole(s.shape) for s in shares],
        scratch_shapes=[
            pltpu.VMEM((rows, features), jnp.bfloat16),
            pltpu.VMEM((rows, features), jnp.bfloat16),
            pltpu.VMEM((rows, features), jnp.bfloat16),
            pltpu.VMEM((rows, features), jnp.float32),
            pltpu.VMEM((rows, features), jnp.float32),
            pltpu.VMEM((rows, chunk), jnp.bfloat16),
            pltpu.VMEM((rows, chunk), jnp.bfloat16),
        ]
        + extra,
        compiler_params=pltpu.CompilerParams(vmem_limit_bytes=BIG, **params),
        name="mlp_both",
    )(gcount, lcount, resid, cg, cl, vectors, w1, b1, w2)


def lane_of(shape):
    return lax.broadcasted_iota(jnp.int32, shape, 1)


def roll_lanes(values, shift):
    shift = shift % values.shape[1]
    return pltpu.roll(values, shift, 1) if shift else values


def corner_rows(side):
    return (1, side, 1 + (side - 1) * side, side * side)


def expand(grids, table_ref, index_refs, bias_refs, row_refs):
    for n, (side, seq, copies, slot) in enumerate(grids):
        index_ref, bias_ref, row_ref = index_refs[n], bias_refs[n], row_refs[n]
        heads, lanes = bias_ref.shape[0], bias_ref.shape[2]
        tables = lax.broadcasted_iota(jnp.int32, (table_ref.shape[1], lanes), 0)

        def pick(row):
            picked = index_ref[pl.ds(row, 1), :] == tables
            return dot(table_ref[...].astype(jnp.bfloat16), picked.astype(jnp.bfloat16))

        corners = [pick(k) for k in range(4)]
        lane = lane_of(corners[0].shape)
        within = (lane + (side - 1)) % side
        for c in range(side):
            for top in range(2):
                left, right = corners[2 * top], corners[2 * top + 1]
                row = jnp.where(within >= c, roll_lanes(left, c), roll_lanes(right, c - (side - 1)))
                row = jnp.where(lane == 0, left, row)
                row_ref[top, :, pl.ds(c, 1), :] = row[:heads].reshape(heads, 1, lanes)
        row_ref[0, :, pl.ds(side, 1), :] = pick(4)[:heads].reshape(heads, 1, lanes)
        lane = lane_of((side, lanes))

        def spread(values, at):
            if copies > 1:
                values = roll_lanes(values, at * slot)
            where = lane_of(values.shape) - at * slot
            return jnp.where((where >= 0) & (where < seq), values, NEG)

        @pl.loop(0, heads)
        def _(h):
            bias_ref[h] = jnp.full(bias_ref.shape[1:], NEG, jnp.float32)
            low, high, first = row_ref[0, h, :side], row_ref[1, h, :side], row_ref[0, h, pl.ds(side, 1)]
            for at in range(copies):
                bias_ref[h, pl.ds(at * slot, 1), :] = spread(first, at)
            for r in range(side):
                rows = jnp.where(
                    lane - 1 < side * (r + 1), roll_lanes(high, -side * (side - 1 - r)), roll_lanes(low, side * r)
                )
                rows = jnp.where(lane == 0, low, rows)
                for at in range(copies):
                    bias_ref[h, pl.ds(at * slot + 1 + side * r, side), :] = spread(rows, at)


def collect(grids, sum_refs, index_refs, row_refs, shape):
    total = jnp.zeros(shape, jnp.float32)
    for n, (side, seq, copies, slot) in enumerate(grids):
        index_ref, sum_ref, row_ref = index_refs[n], sum_refs[n], row_refs[n]
        heads, lanes = sum_ref.shape[0], sum_ref.shape[2]
        lane = lane_of((side, lanes))

        def gathered(h, start, size):
            rows = None
            for at in range(copies):
                piece = roll_lanes(sum_ref[h, pl.ds(at * slot + start, size), :], -at * slot)
                rows = piece if rows is None else rows + piece
            return jnp.where(lane_of((size, lanes)) < seq, rows, 0.0) if copies > 1 else rows

        @pl.loop(0, heads)
        def _(h):
            low = jnp.zeros((side, lanes), jnp.float32)
            high = jnp.zeros((side, lanes), jnp.float32)
            for r in range(side):
                rows = gathered(h, 1 + side * r, side)
                is_low = lane - 1 >= side * (r + 1)
                is_high = (lane >= 1) & (lane - 1 < side * (r + 1))
                low = low + roll_lanes(jnp.where(is_low, rows, 0.0), -side * r) + jnp.where(lane == 0, rows, 0.0)
                high = high + roll_lanes(jnp.where(is_high, rows, 0.0), side * (side - 1 - r))
            row_ref[0, h, :side], row_ref[1, h, :side] = low, high
            row_ref[0, h, pl.ds(side, 1)] = gathered(h, 0, 1)

        flat = lane_of((heads, lanes))
        within = (flat + (side - 1)) % side
        corners = [jnp.zeros((heads, lanes), jnp.float32) for _ in range(4)]
        for c in range(side):
            for top in range(2):
                row = row_ref[top, :, pl.ds(c, 1), :].reshape(heads, lanes)
                is_left = (flat >= 1) & (within >= c)
                is_right = (flat >= 1) & (within < c)
                left = roll_lanes(jnp.where(is_left, row, 0.0), -c) + jnp.where(flat == 0, row, 0.0)
                corners[2 * top] = corners[2 * top] + left
                corners[2 * top + 1] = corners[2 * top + 1] + roll_lanes(jnp.where(is_right, row, 0.0), side - 1 - c)
        tables = lax.broadcasted_iota(jnp.int32, (shape[1], lanes), 0)

        def place_sum(row, values):
            picked = (index_ref[pl.ds(row, 1), :] == tables).astype(jnp.bfloat16)
            top = values.astype(jnp.bfloat16)
            rest = values - as_float(top)
            middle = rest.astype(jnp.bfloat16)
            last = (rest - as_float(middle)).astype(jnp.bfloat16)
            return dot_nt(top, picked) + dot_nt(middle, picked) + dot_nt(last, picked)

        for k, values in enumerate(corners):
            total = total + place_sum(k, values)
        total = total + place_sum(4, row_ref[0, :, pl.ds(side, 1), :].reshape(heads, lanes))
    return total


ROW_SLOTS = 16


def expand_kernel(grids, table_ref, index_g, index_l, bias_ref, rows_g, rows_l):
    expand(grids, table_ref, (index_g, index_l), (bias_ref.at[0], bias_ref.at[1]), (rows_g, rows_l))


def pad_index(indices, lanes):
    picked = []
    for index in indices:
        rows = corner_rows(math.isqrt(index.shape[0] - 1)) + (0,)
        rows = jnp.concatenate([index[r : r + 1] for r in rows])
        picked.append(jnp.pad(rows, ((0, 8 - len(rows)), (0, lanes - index.shape[1])), constant_values=-1))
    return picked


def expand_bias(table, indices, grids, heads, seq):
    lanes = round_up(seq, 128)
    return pl.pallas_call(
        functools.partial(expand_kernel, grids),
        out_shape=jax.ShapeDtypeStruct((2, heads, seq, lanes), jnp.float32),
        scratch_shapes=[pltpu.VMEM((2, heads, ROW_SLOTS, lanes), jnp.float32)] * 2,
        compiler_params=pltpu.CompilerParams(vmem_limit_bytes=BIG),
        name="expand_bias",
    )(table, *pad_index(indices, lanes))


def collect_kernel(grids, index_g, index_l, sums_ref, grad_ref, rows_g, rows_l):
    grad_ref[...] = collect(
        grids, (sums_ref.at[0], sums_ref.at[1]), (index_g, index_l), (rows_g, rows_l), grad_ref.shape
    )


def collect_bias(sums, indices, grids, table_rows):
    _, heads, _, lanes = sums.shape
    return pl.pallas_call(
        functools.partial(collect_kernel, grids),
        out_shape=jax.ShapeDtypeStruct((heads, table_rows), jnp.float32),
        scratch_shapes=[pltpu.VMEM((2, heads, ROW_SLOTS, lanes), jnp.float32)] * 2,
        compiler_params=pltpu.CompilerParams(vmem_limit_bytes=BIG),
        name="collect_bias",
    )(*pad_index(indices, lanes), sums)


def head_lanes(shape, width):
    return lax.broadcasted_iota(jnp.int32, shape, 1) < width


def stack_heads(pair, width):
    first = head_lanes(pair.shape, width)
    zero = jnp.zeros_like(pair)
    return jnp.concatenate([jnp.where(first, pair, zero), jnp.where(first, zero, pair)], axis=0)


def merge_heads(stacked, width):
    rows = stacked.shape[0] // 2
    top, low = stacked[:rows], stacked[rows:]
    return jnp.where(head_lanes(top.shape, width), top, low)


def attend_kernel(
    glob, heads, x_ref, wqkv_ref, wproj_ref, vec_ref, bias_ref,
    normed_ref, qkv_ref, probs_ref, mixed_ref, attn_ref, resid_ref,
):
    seq, features = x_ref.shape
    width = features // heads
    vec = lambda k: vec_ref[pl.ds(k, 1), :]
    inputs = as_float(x_ref[...])
    unit, _ = unit_rows(inputs)
    normed = (unit * vec(V_LN1G) + vec(V_LN1B)).astype(jnp.bfloat16)
    normed_ref[...] = normed
    qkv_ref[:, pl.ds(0, features)] = (dot(normed, wqkv_ref[:, pl.ds(0, features)]) + vec(V_QB)).astype(jnp.bfloat16)
    qkv_ref[:, pl.ds(features, features)] = dot(normed, wqkv_ref[:, pl.ds(features, features)]).astype(jnp.bfloat16)
    qkv_ref[:, pl.ds(2 * features, features)] = (
        dot(normed, wqkv_ref[:, pl.ds(2 * features, features)]) + vec(V_VB)
    ).astype(jnp.bfloat16)

    for pair in range(heads // 2):
        at = 2 * width * pair
        queries = stack_heads(qkv_ref[:, pl.ds(at, 2 * width)], width)
        keys = qkv_ref[:, pl.ds(features + at, 2 * width)]
        values = qkv_ref[:, pl.ds(2 * features + at, 2 * width)]
        bias = bias_ref[0, pl.ds(2 * pair, 2), :, pl.ds(0, seq)].reshape(2 * seq, seq)
        scores = dot_nt(queries, keys) * (width**-0.5) + bias
        weights = jnp.exp(scores - jnp.max(scores, axis=-1, keepdims=True))
        probs = (weights * (1.0 / jnp.sum(weights, axis=-1, keepdims=True))).astype(jnp.bfloat16)
        probs_ref[0, pair] = probs
        mixed_ref[:, pl.ds(at, 2 * width)] = merge_heads(dot(probs, values), width).astype(jnp.bfloat16)

    attn = dot(mixed_ref[...], wproj_ref[...]) + vec(V_PB)
    attn_ref[...] = attn.astype(jnp.bfloat16)
    resid_ref[...] = inputs + vec(V_G1) * attn


def attend_forward(x, wqkv, wproj, vectors, bias, packs, glob, heads):
    rows, features = x.shape
    seq = rows // packs
    whole = lambda shape: pl.BlockSpec(shape, lambda p: (0,) * len(shape), pipeline_mode=pl.Buffered(1))
    by_rows = lambda cols: pl.BlockSpec((seq, cols), lambda p: (p, 0))
    return pl.pallas_call(
        functools.partial(attend_kernel, glob, heads),
        grid=(packs,),
        out_shape=[
            jax.ShapeDtypeStruct((rows, features), jnp.bfloat16),
            jax.ShapeDtypeStruct((rows, 3 * features), jnp.bfloat16),
            jax.ShapeDtypeStruct((packs, heads // 2, 2 * seq, seq), jnp.bfloat16),
            jax.ShapeDtypeStruct((rows, features), jnp.bfloat16),
            jax.ShapeDtypeStruct((rows, features), jnp.bfloat16),
            jax.ShapeDtypeStruct((rows, features), jnp.float32),
        ],
        in_specs=[
            by_rows(features),
            whole(wqkv.shape),
            whole(wproj.shape),
            whole(vectors.shape),
            pl.BlockSpec((1,) + bias.shape[1:], lambda p: (jnp.where(p < glob, 0, 1), 0, 0, 0)),
        ],
        out_specs=[
            by_rows(features),
            by_rows(3 * features),
            pl.BlockSpec((1, heads // 2, 2 * seq, seq), lambda p: (p, 0, 0, 0)),
            by_rows(features),
            by_rows(features),
            by_rows(features),
        ],
        compiler_params=pltpu.CompilerParams(vmem_limit_bytes=BIG),
        name="attend_forward",
    )(x, wqkv, wproj, vectors, bias)


def attend_back_kernel(
    packs, glob, heads, chunk, x_ref, normed_ref, qkv_ref, probs_ref, mixed_ref, attn_ref, gres_ref, wqkv_ref, wproj_ref, vec_ref,
    gx_ref, gwqkv_ref, gwproj_ref, bsum_ref, small_ref, gqb_ref,
    normed_all, mixed_all, gattn_all, gqkv_all,
):
    step = pl.program_id(0)
    seq, features = x_ref.shape
    width = features // heads
    vec = lambda k: vec_ref[pl.ds(k, 1), :]
    rows = packs * seq

    @pl.when(step == 0)
    def _():
        small_ref[...] = jnp.zeros_like(small_ref)
        gqb_ref[...] = jnp.zeros_like(gqb_ref)

    @pl.when((step == 0) | (step == glob))
    def _():
        bsum_ref[...] = jnp.zeros_like(bsum_ref)

    @pl.when(step < packs)
    def _():
        part = pl.ds(pl.multiple_of(step * seq, seq), seq)
        gres = gres_ref[...]
        gattn = (vec(V_G1) * gres).astype(jnp.bfloat16)
        gattn_all[part, :] = gattn
        mixed_all[part, :] = mixed_ref[...]
        normed_all[part, :] = normed_ref[...]
        small_ref[pl.ds(2, 1), :] += column_sum(as_float(gattn))
        small_ref[pl.ds(3, 1), :] += column_sum(gres * as_float(attn_ref[...]))
        gmixed = dot_nt(gattn, wproj_ref[...]).astype(jnp.bfloat16)
        scale = width**-0.5
        for pair in range(heads // 2):
            at = 2 * width * pair
            queries = stack_heads(qkv_ref[:, pl.ds(at, 2 * width)], width)
            keys = qkv_ref[:, pl.ds(features + at, 2 * width)]
            values = qkv_ref[:, pl.ds(2 * features + at, 2 * width)]
            grads = stack_heads(gmixed[:, at : at + 2 * width], width)
            mixed = as_float(mixed_ref[:, pl.ds(at, 2 * width)])
            probs = probs_ref[0, pair]
            twice = jnp.concatenate([mixed, mixed], axis=0)
            inner = jnp.sum(as_float(grads) * twice, axis=-1, keepdims=True)
            gscores = as_float(probs) * (dot_nt(grads, values) - inner)
            bsum_ref[0, pl.ds(2 * pair, 2), :, pl.ds(0, seq)] += gscores.reshape(2, seq, seq)
            low = gscores.astype(jnp.bfloat16)
            gqkv_all[part, pl.ds(at, 2 * width)] = (merge_heads(dot(low, keys), width) * scale).astype(jnp.bfloat16)
            gqkv_all[part, pl.ds(features + at, 2 * width)] = (dot_tn(low, queries) * scale).astype(jnp.bfloat16)
            gqkv_all[part, pl.ds(2 * features + at, 2 * width)] = dot_tn(probs, grads).astype(jnp.bfloat16)
        gqkv = gqkv_all[part, :]
        gqb_ref[...] += column_sum(as_float(gqkv))
        gnorm = dot_nt(gqkv, wqkv_ref[...])
        unit, spread = unit_rows(as_float(x_ref[...]))
        small_ref[pl.ds(0, 1), :] += column_sum(gnorm * unit)
        small_ref[pl.ds(1, 1), :] += column_sum(gnorm)
        gx_ref[...] = (gres + unit_back(gnorm * vec(V_LN1G), unit, spread)).astype(gx_ref.dtype)

    @pl.when(step >= packs)
    def _():
        j = step - packs
        wide = 3 * features // chunk

        @pl.when(j < wide)
        def _():
            gwqkv_ref[...] = dot_tn(normed_all[...], gqkv_all[:, pl.ds(pl.multiple_of(j * chunk, chunk), chunk)]).astype(gwqkv_ref.dtype)

        @pl.when(j >= wide)
        def _():
            gwproj_ref[...] = dot_tn(mixed_all[...], gattn_all[:, pl.ds(pl.multiple_of((j - wide) * chunk, chunk), chunk)]).astype(gwproj_ref.dtype)


def attend_backward(x, normed, qkv, probs, mixed, attn, gres, wqkv, wproj, vectors, packs, glob, heads, out_dtype, grad_dtype, lanes):
    rows, features = x.shape
    seq = rows // packs
    chunk = 256
    wide, narrow = 3 * features // chunk, features // chunk
    whole = lambda shape: pl.BlockSpec(shape, lambda s: (0,) * len(shape), pipeline_mode=pl.Buffered(1))
    pack = lambda s: jnp.minimum(s, packs - 1)
    by_rows = lambda cols: pl.BlockSpec((seq, cols), lambda s: (pack(s), 0))
    return pl.pallas_call(
        functools.partial(attend_back_kernel, packs, glob, heads, chunk),
        grid=(packs + wide + narrow,),
        out_shape=[
            jax.ShapeDtypeStruct((rows, features), out_dtype),
            jax.ShapeDtypeStruct((features, 3 * features), grad_dtype),
            jax.ShapeDtypeStruct((features, features), grad_dtype),
            jax.ShapeDtypeStruct((2, heads, seq, lanes), jnp.float32),
            jax.ShapeDtypeStruct((8, features), jnp.float32),
            jax.ShapeDtypeStruct((1, 3 * features), jnp.float32),
        ],
        in_specs=[
            by_rows(features),
            by_rows(features),
            by_rows(3 * features),
            pl.BlockSpec((1, heads // 2, 2 * seq, seq), lambda s: (pack(s), 0, 0, 0)),
            by_rows(features),
            by_rows(features),
            by_rows(features),
            whole(wqkv.shape),
            whole(wproj.shape),
            whole(vectors.shape),
        ],
        out_specs=[
            by_rows(features),
            pl.BlockSpec((features, chunk), lambda s: (0, jnp.clip(s - packs, 0, wide - 1))),
            pl.BlockSpec((features, chunk), lambda s: (0, jnp.clip(s - packs - wide, 0, narrow - 1))),
            pl.BlockSpec((1, heads, seq, lanes), lambda s: (jnp.where(s < glob, 0, 1), 0, 0, 0)),
            whole((8, features)),
            whole((1, 3 * features)),
        ],
        scratch_shapes=[
            pltpu.VMEM((rows, features), jnp.bfloat16),
            pltpu.VMEM((rows, features), jnp.bfloat16),
            pltpu.VMEM((rows, features), jnp.bfloat16),
            pltpu.VMEM((rows, 3 * features), jnp.bfloat16),
        ],
        compiler_params=pltpu.CompilerParams(vmem_limit_bytes=BIG),
        name="attend_backward",
    )(x, normed, qkv, probs, mixed, attn, gres, wqkv, wproj, vectors)


MESH = pl.DeviceIdType.MESH
LINE = 4
GRID = (LINE, 2, 2, 2)
EVERY = slice(None)


def place():
    me = lax.axis_index("fsdp")
    return (me // 8, (me // 4) % 2, (me // 2) % 2, me % 2)


def device_at(z, y, x, c):
    return (((z * 2 + y) * 2 + x) * 2 + c,)


def along(z, k):
    return (z + k) % LINE


def greet():
    z, y, x, c = place()
    barrier = pltpu.get_barrier_semaphore()
    peers = [device_at(z, y, x, 1 - c), device_at(z, y, 1 - x, c), device_at(z, 1 - y, x, c)]
    peers += [device_at(along(z, k), y, x, c) for k in range(1, LINE)]
    for peer in peers:
        pl.semaphore_signal(barrier, inc=1, device_id=peer, device_id_type=MESH)
    pl.semaphore_wait(barrier, len(peers))


def remote(src, dst, send, recv, peer):
    return pltpu.make_async_remote_copy(
        src_ref=src, dst_ref=dst, send_sem=send, recv_sem=recv, device_id=peer, device_id_type=MESH
    )


class Gather:
    SEMS = 24

    def __init__(self, own, full, send, recv):
        self.own, self.full, self.send, self.recv = own, full, send, recv
        self.z, self.y, self.x, self.c = place()
        self.cols = full.shape[-1] // 2

    def half(self, ref, part, half):
        cols = (EVERY, pl.ds(half * self.cols, self.cols))
        return ref.at[part + cols]

    def line_copy(self, k, source=None):
        z, y, x, c = self.z, self.y, self.x, self.c
        held = z if source is None else source
        peer = device_at(along(z, k), y, x, c)
        return remote(self.own, self.full.at[held, y, x, c], self.send.at[k - 1], self.recv.at[k - 1], peer)

    def over(self, half, near):
        z, y, x, c = self.z, self.y, self.x, self.c
        return device_at(z, y, 1 - x, c) if (half == 0) == near else device_at(z, 1 - y, x, c)

    def first(self, half):
        z, y, x, c = self.z, self.y, self.x, self.c
        k = 3 + half
        return remote(
            self.half(self.own, (), half), self.half(self.full, (z, y, x, c), half), self.send.at[k], self.recv.at[k],
            self.over(half, True),
        )

    def hop(self, half, k, near):
        z, y, x, c = self.z, self.y, self.x, self.c
        held = along(z, LINE - k) if k else z
        if near:
            part, sem = (held, y, x, c), 7 + 3 * half + k - 1
        else:
            part = (held, y, EVERY, c) if half == 0 else (held, EVERY, x, c)
            sem = 13 + 3 * half + k - 1 if k else 5 + half
        ref = self.half(self.full, part, half)
        return remote(ref, ref, self.send.at[sem], self.recv.at[sem], self.over(half, near))

    def pair(self, k):
        z, y, x, c = self.z, self.y, self.x, self.c
        part, half = (
            ((EVERY, y, x, c), None),
            ((EVERY, y, 1 - x, c), 0),
            ((EVERY, 1 - y, x, c), 1),
            ((EVERY, 1 - y, EVERY, c), 0),
            ((EVERY, EVERY, 1 - x, c), 1),
        )[k]
        ref = self.full.at[part] if half is None else self.half(self.full, part, half)
        return remote(ref, ref, self.send.at[19 + k], self.recv.at[19 + k], device_at(z, y, x, 1 - c))

    def mine(self):
        return pltpu.make_async_copy(self.own, self.full.at[self.z, self.y, self.x, self.c], self.recv.at[self.SEMS])

    def stage(self, name):
        away = range(1, LINE)
        if name == "a":
            for k in away:
                self.line_copy(k).start()
            for half in range(2):
                self.first(half).start()
            self.mine().start()
        elif name == "n":
            self.mine().wait()
            for half in range(2):
                self.first(half).wait_recv()
                self.hop(half, 0, False).start()
        elif name == "z":
            for k in away:
                self.line_copy(k, along(self.z, LINE - k)).wait_recv()
                for half in range(2):
                    self.hop(half, k, True).start()
            self.pair(0).start()
        elif name == "f":
            for k in away:
                for half in range(2):
                    self.hop(half, k, True).wait_recv()
                    self.hop(half, k, False).start()
            self.pair(1).start()
            self.pair(2).start()
        elif name == "q":
            for half in range(2):
                for k in range(LINE):
                    self.hop(half, k, False).wait_recv()
                self.pair(3 + half).start()
        else:
            for k in range(5):
                self.pair(k).wait_recv()

    def drain(self):
        away = range(1, LINE)
        for k in away:
            self.line_copy(k).wait_send()
        for half in range(2):
            self.first(half).wait_send()
            self.hop(half, 0, False).wait_send()
            for k in away:
                self.hop(half, k, True).wait_send()
                self.hop(half, k, False).wait_send()
        for k in range(5):
            self.pair(k).wait_send()


class Scatter:
    STAGES = 5
    SEMS = 9

    def __init__(self, terms, own, bufs, send, recv, finish):
        self.terms, self.loaded = terms, own
        self.pairbuf, self.buf1a, self.buf1b, self.buf2a, self.buf2b, self.line = bufs
        self.send, self.recv, self.finish = send, recv, finish
        self.z, self.y, self.x, self.c = place()
        self.cols = terms.shape[-1] // 2

    BUFS = 6

    @staticmethod
    def scratch(shape, dtype):
        rows, cols = shape
        half = cols // 2
        return [
            pltpu.VMEM((LINE, 2, 2, rows, cols), dtype),
            pltpu.VMEM((LINE, 2, rows, half), dtype),
            pltpu.VMEM((LINE, 2, rows, half), dtype),
            pltpu.VMEM((LINE, rows, half), dtype),
            pltpu.VMEM((LINE, rows, half), dtype),
            pltpu.VMEM((LINE - 1, rows, cols), dtype),
        ]

    def at(self, i, j, k, half=None):
        cols = () if half is None else (EVERY, pl.ds(half * self.cols, self.cols))
        if self.loaded is None:
            return self.terms.at[(i, j, k, self.c) + cols]
        return self.loaded.at[(i, j, k) + cols]

    def load(self):
        return pltpu.make_async_copy(self.terms.at[EVERY, EVERY, EVERY, self.c], self.loaded, self.send.at[8])

    def copy(self, name):
        z, y, x, c = self.z, self.y, self.x, self.c
        over_x, over_y = device_at(z, y, 1 - x, c), device_at(z, 1 - y, x, c)
        k, src, dst, peer = {
            "pair": lambda: (0, self.terms.at[EVERY, EVERY, EVERY, 1 - c], self.pairbuf, device_at(z, y, x, 1 - c)),
            "1a": lambda: (1, self.at(EVERY, 1 - y, EVERY, 0), self.buf1a, over_y),
            "1b": lambda: (2, self.at(EVERY, EVERY, 1 - x, 1), self.buf1b, over_x),
            "2a": lambda: (3, self.at(EVERY, y, 1 - x, 0), self.buf2a, over_x),
            "2b": lambda: (4, self.at(EVERY, 1 - y, x, 1), self.buf2b, over_y),
        }[name]()
        return remote(src, dst, self.send.at[k], self.recv.at[k], peer)

    def line_copy(self, k):
        z, y, x, c = self.z, self.y, self.x, self.c
        target = along(z, k)
        return remote(
            self.at(target, y, x), self.line.at[k - 1], self.send.at[4 + k], self.recv.at[4 + k], device_at(target, y, x, c)
        )

    def add(self, ref, term):
        ref[...] = ref[...] + term

    def stage(self, s):
        z, y, x = self.z, self.y, self.x
        if s == 0:
            self.copy("pair").start()
            if self.loaded is not None:
                self.load().start()
        elif s == 1:
            if self.loaded is not None:
                self.load().wait()
            self.copy("pair").wait_recv()

            @pl.loop(0, LINE)
            def _(i):
                for j in range(2):
                    for k in range(2):
                        self.add(self.at(i, j, k), self.pairbuf[i, j, k])

            self.copy("1a").start()
            self.copy("1b").start()
        elif s == 2:
            self.copy("1a").wait_recv()
            self.copy("1b").wait_recv()

            @pl.loop(0, LINE)
            def _(i):
                for k in range(2):
                    self.add(self.at(i, y, k, 0), self.buf1a[i, k])
                    self.add(self.at(i, k, x, 1), self.buf1b[i, k])

            self.copy("2a").start()
            self.copy("2b").start()
        elif s == 3:
            self.copy("2a").wait_recv()
            self.copy("2b").wait_recv()

            @pl.loop(0, LINE)
            def _(i):
                self.add(self.at(i, y, x, 0), self.buf2a[i])
                self.add(self.at(i, y, x, 1), self.buf2b[i])

            for k in range(1, LINE):
                self.line_copy(k).start()
        else:
            total = as_float(self.at(z, y, x)[...])
            for k in range(1, LINE):
                self.line_copy(k).wait_recv()
                total = total + as_float(self.line[k - 1])
            self.finish(total)

    def drain(self):
        for name in ("pair", "1a", "1b", "2a", "2b"):
            self.copy(name).wait_send()
        for k in range(1, LINE):
            self.line_copy(k).wait_send()


SMALL = (16, 256)


def back_kernel(
    shape, plan, x_ref, normed_ref, q_ref, k_ref, v_ref, probs_ref, mixed_ref, attn_ref, gres_ref, wqkv_ref, wproj_ref, vec_ref,
    two_ref, hidden_ref, index_g, index_l, gfc1_ref, gfc2_ref,
    gxg_ref, gxl_ref, sqkv_ref, sproj_ref, sfc1_ref, sfc2_ref, ssmall_ref,
    gqkv, gmixed, bsum, vecs, tsum, corner, *scratch,
):
    packs, glob, heads, groups, blocks, grids = shape
    step = pl.program_id(0)
    rows, features = normed_ref.shape
    seq = rows // packs
    width = features // heads
    lanes = features // groups
    scale = width**-0.5
    vec = lambda k: vec_ref[pl.ds(k, 1), :]
    size = rows // blocks
    last = 1 + packs * groups + 1 + blocks

    send, recv = scratch[-2:]
    scratch = scratch[:-2]
    big = SPLIT + 1
    owns = list(scratch[:big]) + [None] * (groups + 2)
    terms = scratch[big : big + groups + 2]
    bufs = scratch[big + groups + 2 :]

    def put_group(g):
        def finish(value):
            for i in range(3):
                sqkv_ref[:, pl.ds(i * features + g * lanes, lanes)] = value[:, i * lanes : (i + 1) * lanes]

        return finish

    tall = gfc2_ref.shape[4] // SPLIT
    sources, ends = [], []
    for k in range(SPLIT):
        sources.append(gfc2_ref.at[EVERY, EVERY, EVERY, EVERY, pl.ds(k * tall, tall)])
        ends.append(put(sfc2_ref.at[pl.ds(k * tall, tall)]))
    sources.append(gfc1_ref)
    ends.append(put(sfc1_ref))
    sources += list(terms)
    ends += [put(sproj_ref)] + [put_group(g) for g in range(groups)] + [put(ssmall_ref)]
    flows = [
        Scatter(sources[t], owns[t], bufs[Scatter.BUFS * t : Scatter.BUFS * (t + 1)], send.at[t], recv.at[t], ends[t]) for t in range(len(ends))
    ]

    def slot(k):
        for t, s in plan.get(k, ()):
            flows[t].stage(s)

    @pl.when(step == 0)
    def _():
        greet()
        slot(0)
        zero = jnp.zeros((1, features), jnp.float32)
        vecs[...] = jnp.zeros_like(vecs)

        def block(i, sums):
            part = pl.ds(pl.multiple_of(i * size, size), size)
            gres = gres_ref[part, :]
            gattn = (vec(V_G1) * gres).astype(jnp.bfloat16)
            gqkv[part, pl.ds(0, features)] = gattn
            gmixed[part, :] = dot_nt(gattn, wproj_ref[...]).astype(jnp.bfloat16)
            return (sums[0] + column_sum(as_float(gattn)), sums[1] + column_sum(gres * as_float(attn_ref[part, :])))

        sums = lax.fori_loop(0, blocks, block, (zero, zero))
        vecs[pl.ds(V_PB, 1), :] = sums[0]
        vecs[pl.ds(V_G1, 1), :] = sums[1]
        bsum[...] = jnp.zeros_like(bsum)
        fill_terms(terms[0], dot_tn(mixed_ref[...], gqkv[:, pl.ds(0, features)]))

    @pl.when((step >= 1) & (step <= packs * groups))
    def _():
        pack = (step - 1) % packs
        group = (step - 1) // packs
        part = pl.ds(pl.multiple_of(pack * seq, seq), seq)
        kind = jnp.where(pack < glob, 0, 1)
        for pair in range(heads // 2 // groups):
            at = 2 * width * pair
            wide = pl.ds(pl.multiple_of(group * lanes + at, 2 * width), 2 * width)
            queries = stack_heads(q_ref[:, pl.ds(at, 2 * width)], width)
            keys = k_ref[:, pl.ds(at, 2 * width)]
            values = v_ref[:, pl.ds(at, 2 * width)]
            grads = stack_heads(gmixed[part, wide], width)
            mixed = as_float(mixed_ref[part, wide])
            probs = probs_ref[0, pair]
            twice = jnp.concatenate([mixed, mixed], axis=0)
            inner = jnp.sum(as_float(grads) * twice, axis=-1, keepdims=True)
            gscores = as_float(probs) * (dot_nt(grads, values) - inner)
            head = group * (heads // groups) + 2 * pair
            bsum[kind, pl.ds(head, 2), :, pl.ds(0, seq)] += gscores.reshape(2, seq, seq)
            low = gscores.astype(jnp.bfloat16)
            gq = (merge_heads(dot(low, keys), width) * scale).astype(jnp.bfloat16)
            gk = (dot_tn(low, queries) * scale).astype(jnp.bfloat16)
            gv = dot_tn(probs, grads).astype(jnp.bfloat16)
            for i, piece in enumerate((gq, gk, gv)):
                at_lane = pl.multiple_of(group * lanes + at + i * features, 2 * width)
                gqkv[part, pl.ds(at_lane, 2 * width)] = piece

    for g in range(groups):
        @pl.when(step == packs * (g + 1))
        def _():
            pieces = [dot_tn(normed_ref[...], gqkv[:, pl.ds(i * features + g * lanes, lanes)]) for i in range(3)]
            fill_terms(terms[1 + g], jnp.concatenate(pieces, axis=1))

    @pl.when(step == packs * groups + 1)
    def _():
        tsum[...] = collect(
            grids, (bsum.at[0], bsum.at[1]), (index_g, index_l), (corner, corner), tsum.shape
        )

    @pl.when(step >= packs * groups + 2)
    def _():
        i = step - packs * groups - 2
        part = pl.ds(pl.multiple_of(i * size, size), size)
        low = gqkv[part, :]
        gnorm = dot_nt(low, wqkv_ref[...])
        unit, spread = unit_rows(as_float(x_ref[...]))
        vecs[pl.ds(V_LN1G, 1), :] += column_sum(gnorm * unit)
        vecs[pl.ds(V_LN1B, 1), :] += column_sum(gnorm)
        total = column_sum(as_float(low))
        vecs[pl.ds(V_QB, 1), :] += total[:, :features]
        vecs[pl.ds(V_VB, 1), :] += total[:, 2 * features :]
        value = gres_ref[part, :] + unit_back(gnorm * vec(V_LN1G), unit, spread)
        per_block = packs // blocks
        glob_len, loc_len, per_pack, slot = grids[0][1], grids[1][1], grids[1][2], grids[1][3]

        @pl.when(i < glob // per_block)
        def _():
            for n in range(per_block):
                gxg_ref[n] = value[n * seq : n * seq + glob_len].astype(gxg_ref.dtype)

        @pl.when(i >= glob // per_block)
        def _():
            for n in range(per_block):
                for k in range(per_pack):
                    start = n * seq + k * slot
                    gxl_ref[n * per_pack + k] = value[start : start + loc_len].astype(gxl_ref.dtype)

    @pl.when(step == last - 1)
    def _():
        for k, row in ((V_LN2G, 0), (V_LN2B, 1), (V_FB, 2), (V_G2, 3)):
            vecs[pl.ds(k, 1), :] = two_ref[pl.ds(row, 1), :]
        ref = terms[-1]
        ref[...] = jnp.zeros_like(ref)
        devices = LINE * 8
        count, wide, table = features // devices, hidden_ref.shape[1] // devices, tsum.shape[1] // devices
        for d in range(devices):
            block = ref.at[d // 8, d // 4 % 2, d // 2 % 2, d % 2]
            block[:, pl.ds(0, count)] = vecs[:, pl.ds(d * count, count)]
            block[pl.ds(10, 1), pl.ds(0, wide)] = hidden_ref[:, pl.ds(d * wide, wide)]
            block[pl.ds(0, heads), pl.ds(128, table)] = tsum[:, pl.ds(d * table, table)]

    for k in sorted(plan):
        if k:
            @pl.when(step == k)
            def _():
                slot(k)

    @pl.when(step == last - 1)
    def _():
        for flow in flows:
            flow.drain()


BACK_PLAN = {
    0: ((0, 0), (1, 0),),
    1: ((0, 1),),
    4: ((2, 0),),
    5: ((1, 1),),
    7: ((3, 0), (4, 0), (2, 1),),
    11: ((0, 2),),
    12: ((1, 2),),
    13: ((5, 0), (2, 2),),
    16: ((0, 3), (5, 1),),
    18: ((6, 0), (4, 1), (1, 3), (3, 1),),
    19: ((4, 2), (2, 3), (5, 2), (6, 1),),
    20: ((3, 2),),
    21: ((4, 3),),
    22: (
        (7, 0), (1, 4), (5, 3), (6, 2), (7, 1), (4, 4), (2, 4), (3, 3),
        (5, 4), (6, 3), (7, 2), (0, 4), (7, 3), (6, 4), (3, 4), (7, 4),
    ),
}
SPLIT = 2


def attend_back(
    x, normed, qkv, probs, mixed, attn, gres, wqkv, wproj, vectors, two, hidden, indices, gfc1, gfc2, packs, glob, heads,
    grids, table_rows, out_dtype, lanes,
):
    rows, features = x.shape
    seq = rows // packs
    groups, blocks = 3, 3
    per_block = packs // blocks
    cols = features // groups
    steps = 1 + packs * groups + 1 + blocks
    first_block = packs * groups + 2
    whole = lambda shape: pl.BlockSpec(shape, lambda s: (0,) * len(shape), pipeline_mode=pl.Buffered(1))
    at = lambda s: jnp.clip(s - 1, 0, packs * groups - 1)
    part = lambda i: pl.BlockSpec((seq, cols), lambda s: (at(s) % packs, i * groups + at(s) // packs))
    any_ref = pl.BlockSpec(memory_space=pl.ANY)
    by_block = pl.BlockSpec((rows // blocks, features), lambda s: (jnp.clip(s - first_block, 0, blocks - 1), 0))
    padded = pad_index(indices, lanes)
    shard = lambda t: t.shape[4:]
    term_shapes = [(features // 32, features)] + [(features // 32, 3 * cols)] * groups
    tall = (shard(gfc2)[0] // SPLIT, shard(gfc2)[1])
    flow_shapes = [(tall, gfc2.dtype)] * SPLIT + [(shard(gfc1), gfc1.dtype)]
    scratch = [
        pltpu.VMEM((rows, 3 * features), jnp.bfloat16),
        pltpu.VMEM((rows, features), jnp.bfloat16),
        pltpu.VMEM((2, heads, seq, lanes), jnp.float32),
        pltpu.VMEM((16, features), jnp.float32),
        pltpu.VMEM((heads, table_rows), jnp.float32),
        pltpu.VMEM((2, heads, ROW_SLOTS, lanes), jnp.float32),
    ]
    scratch += [pltpu.VMEM((LINE, 2, 2) + s, d) for s, d in flow_shapes]
    flow_shapes += [(s, jnp.bfloat16) for s in term_shapes] + [(SMALL, jnp.float32)]
    scratch += [pltpu.VMEM(GRID + s, jnp.bfloat16) for s in term_shapes] + [pltpu.VMEM(GRID + SMALL, jnp.float32)]
    for s, d in flow_shapes:
        scratch += Scatter.scratch(s, d)
    scratch += [pltpu.SemaphoreType.DMA((len(flow_shapes), Scatter.SEMS))] * 2
    return pl.pallas_call(
        functools.partial(
            back_kernel, (packs, glob, heads, groups, blocks, grids), BACK_PLAN
        ),
        grid=(steps,),
        out_shape=[
            jax.ShapeDtypeStruct((glob, grids[0][1], features), out_dtype),
            jax.ShapeDtypeStruct(((packs - glob) * grids[1][2], grids[1][1], features), out_dtype),
            jax.ShapeDtypeStruct((features // 32, 3 * features), jnp.float32),
            jax.ShapeDtypeStruct((features // 32, features), jnp.float32),
            jax.ShapeDtypeStruct(shard(gfc1), jnp.float32),
            jax.ShapeDtypeStruct(shard(gfc2), jnp.float32),
            jax.ShapeDtypeStruct(SMALL, jnp.float32),
        ],
        in_specs=[
            by_block,
            whole((rows, features)),
            part(0), part(1), part(2),
            pl.BlockSpec((1, heads // 2 // groups, 2 * seq, seq), lambda s: (at(s) % packs, at(s) // packs, 0, 0)),
            whole((rows, features)),
            whole((rows, features)),
            whole((rows, features)),
            whole(wqkv.shape),
            whole(wproj.shape),
            whole(vectors.shape),
            whole(two.shape),
            whole(hidden.shape),
            whole(padded[0].shape),
            whole(padded[1].shape),
            any_ref,
            any_ref,
        ],
        out_specs=[
            pl.BlockSpec(
                (per_block, grids[0][1], features),
                lambda s: (jnp.clip(s - first_block, 0, glob // per_block - 1), 0, 0),
            ),
            pl.BlockSpec(
                (per_block * grids[1][2], grids[1][1], features),
                lambda s: (jnp.maximum(s - first_block - glob // per_block, 0), 0, 0),
            ),
            whole((features // 32, 3 * features)),
            whole((features // 32, features)),
            whole(shard(gfc1)),
            whole(shard(gfc2)),
            whole(SMALL),
        ],
        scratch_shapes=scratch,
        compiler_params=pltpu.CompilerParams(vmem_limit_bytes=BIG, collective_id=1, has_side_effects=True),
        name="attend_back",
    )(x, normed, qkv, qkv, qkv, probs, mixed, attn, gres, wqkv, wproj, vectors, two, hidden, *padded, gfc1, gfc2)


GATHER_HEAD = (
    (0, "a"), (2, "a"), (1, "a"), (4, "a"), (0, "n"), (6, "a"), (0, "z"), (5, "a"), (1, "n"), (2, "n"), (0, "f"),
    (4, "n"), (6, "n"), (2, "z"), (5, "n"), (0, "q"), (3, "a"), (1, "z"), (0, "e"), (3, "n"), "unpack", (2, "f"),
    (1, "f"), "expand global", (6, "z"), (2, "q"), "expand local", (1, "q"), (4, "z"), (5, "z"), (2, "e"), (6, "f"),
    (1, "e"),
)
GATHER_LATER = {
    1: ((3, "z"), (4, "f")),
    2: ((6, "q"), (5, "f")),
    4: ((3, "f"), (4, "q")),
    5: ((4, "e"), (5, "q")),
    7: ((3, "q"), (6, "e"), (5, "e"), (3, "e")),
}


def front_kernel(
    shape, xg_ref, xl_ref, small_ref, oqkv_ref, oproj_ref, ofc1_ref, ofc2_ref, index_g, index_l,
    x_ref, normed_ref, qkv_ref, probs_ref, mixed_ref, attn_ref, resid_ref, vec_ref, hidden_ref,
    fqkv_ref, fproj_ref, ffc1_ref, ffc2_ref,
    table, bias, rows_g, rows_l, padded, wqkv, wproj, small_full, load, send, recv,
):
    packs, glob, heads, grids = shape
    step = pl.program_id(0)
    seq, features = x_ref.shape
    width = features // heads
    devices = LINE * 8
    vec = lambda k: vec_ref[pl.ds(k, 1), :]
    wide, tall = ofc1_ref.shape[1] // 2, ofc2_ref.shape[0] // 2
    ends = [(small_ref, small_full), (oqkv_ref, fqkv_ref), (oproj_ref, fproj_ref)]
    lead = (EVERY,) * 4
    for k in range(2):
        cols = (EVERY, pl.ds(k * wide, wide))
        ends.append((ofc1_ref.at[cols], ffc1_ref.at[lead + cols]))
    for k in range(2):
        lines = (pl.ds(k * tall, tall),)
        ends.append((ofc2_ref.at[lines], ffc2_ref.at[lead + lines]))
    flows = [Gather(o, f, send.at[t], recv.at[t]) for t, (o, f) in enumerate(ends)]

    def each_shard(act):
        @pl.loop(0, devices)
        def _(d):
            for k, (ref, held) in enumerate(((fqkv_ref, wqkv), (fproj_ref, wproj))):
                count = held.shape[0] // devices
                part = held.at[pl.ds(pl.multiple_of(d * count, 8), count)]
                act(pltpu.make_async_copy(ref.at[d // 8, d // 4 % 2, d // 2 % 2, d % 2], part, load.at[k, d]))

    @pl.when(step == 0)
    def _():
        greet()
        table[...] = jnp.zeros_like(table)
        for item in GATHER_HEAD:
            if item == "unpack":
                count, wide = features // devices, hidden_ref.shape[1] // devices
                lines = table.shape[1] // devices
                for d in range(devices):
                    block = small_full.at[d // 8, d // 4 % 2, d // 2 % 2, d % 2]
                    vec_ref[:, pl.ds(d * count, count)] = block[:, pl.ds(0, count)]
                    hidden_ref[:, pl.ds(d * wide, wide)] = block[pl.ds(10, 1), pl.ds(0, wide)]
                    table[pl.ds(0, heads), pl.ds(d * lines, lines)] = block[pl.ds(0, heads), pl.ds(128, lines)]
            elif item == "expand global":
                expand(grids[:1], table, (index_g,), (bias.at[0],), (rows_g,))
            elif item == "expand local":
                expand(grids[1:], table, (index_l,), (bias.at[1],), (rows_l,))
            else:
                flows[item[0]].stage(item[1])
        each_shard(lambda copy: copy.start())
        each_shard(lambda copy: copy.wait())

    @pl.when((step >= 1) & (step <= packs))
    def _():
        padded[...] = jnp.zeros_like(padded)

        @pl.when(step <= glob)
        def _():
            padded[pl.ds(0, xg_ref.shape[1]), :] = as_float(xg_ref[0])

        @pl.when(step > glob)
        def _():
            for k in range(xl_ref.shape[0]):
                padded[pl.ds(k * grids[1][3], xl_ref.shape[1]), :] = as_float(xl_ref[k])

        inputs = padded[...]
        x_ref[...] = inputs.astype(jnp.bfloat16)
        unit, _ = unit_rows(inputs)
        normed = (unit * vec(V_LN1G) + vec(V_LN1B)).astype(jnp.bfloat16)
        normed_ref[...] = normed
        qkv_ref[:, pl.ds(0, features)] = (dot(normed, wqkv[:, pl.ds(0, features)]) + vec(V_QB)).astype(jnp.bfloat16)
        qkv_ref[:, pl.ds(features, features)] = dot(normed, wqkv[:, pl.ds(features, features)]).astype(jnp.bfloat16)
        qkv_ref[:, pl.ds(2 * features, features)] = (
            dot(normed, wqkv[:, pl.ds(2 * features, features)]) + vec(V_VB)
        ).astype(jnp.bfloat16)
        kind = jnp.where(step <= glob, 0, 1)
        for pair in range(heads // 2):
            at = 2 * width * pair
            queries = stack_heads(qkv_ref[:, pl.ds(at, 2 * width)], width)
            keys = qkv_ref[:, pl.ds(features + at, 2 * width)]
            values = qkv_ref[:, pl.ds(2 * features + at, 2 * width)]
            part = bias[kind, pl.ds(2 * pair, 2), :, pl.ds(0, seq)].reshape(2 * seq, seq)
            scores = dot_nt(queries, keys) * (width**-0.5) + part
            weights = jnp.exp(scores - jnp.max(scores, axis=-1, keepdims=True))
            probs = (weights * (1.0 / jnp.sum(weights, axis=-1, keepdims=True))).astype(jnp.bfloat16)
            probs_ref[0, pair] = probs
            mixed_ref[:, pl.ds(at, 2 * width)] = merge_heads(dot(probs, values), width).astype(jnp.bfloat16)

        attn = dot(mixed_ref[...], wproj[...]) + vec(V_PB)
        attn_ref[...] = attn.astype(jnp.bfloat16)
        resid_ref[...] = inputs + vec(V_G1) * attn

    for k, items in GATHER_LATER.items():
        @pl.when(step == k)
        def _():
            for t, s in items:
                flows[t].stage(s)

    @pl.when(step == packs + 1)
    def _():
        for flow in flows:
            flow.drain()


def attend_front(xg, xl, small, shards, indices, packs, heads, grids, seq, table_rows):
    glob, glob_len, features = xg.shape
    loc, loc_len, _ = xl.shape
    per_pack = loc // (packs - glob)
    rows, lanes = packs * seq, round_up(seq, 128)
    hidden = shards[2].shape[1]
    padded = pad_index(indices, lanes)
    whole = lambda shape: pl.BlockSpec(shape, lambda s: (0,) * len(shape), pipeline_mode=pl.Buffered(1))
    at = lambda s: jnp.clip(s - 1, 0, packs - 1)
    by_rows = lambda cols: pl.BlockSpec((seq, cols), lambda s: (at(s), 0))
    any_ref = pl.BlockSpec(memory_space=pl.ANY)
    owns = [small] + list(shards)
    return pl.pallas_call(
        functools.partial(front_kernel, (packs, glob, heads, grids)),
        grid=(packs + 2,),
        out_shape=[
            jax.ShapeDtypeStruct((rows, features), jnp.bfloat16),
            jax.ShapeDtypeStruct((rows, features), jnp.bfloat16),
            jax.ShapeDtypeStruct((rows, 3 * features), jnp.bfloat16),
            jax.ShapeDtypeStruct((packs, heads // 2, 2 * seq, seq), jnp.bfloat16),
            jax.ShapeDtypeStruct((rows, features), jnp.bfloat16),
            jax.ShapeDtypeStruct((rows, features), jnp.bfloat16),
            jax.ShapeDtypeStruct((rows, features), jnp.float32),
            jax.ShapeDtypeStruct((16, features), jnp.float32),
            jax.ShapeDtypeStruct((1, hidden), jnp.float32),
        ]
        + [jax.ShapeDtypeStruct(GRID + s.shape, s.dtype) for s in shards],
        in_specs=[
            pl.BlockSpec((1, glob_len, features), lambda s: (jnp.minimum(at(s), glob - 1), 0, 0)),
            pl.BlockSpec((per_pack, loc_len, features), lambda s: (jnp.maximum(at(s) - glob, 0), 0, 0)),
        ]
        + [whole(o.shape) for o in owns]
        + [whole(padded[0].shape), whole(padded[1].shape)],
        out_specs=[
            by_rows(features),
            by_rows(features),
            by_rows(3 * features),
            pl.BlockSpec((1, heads // 2, 2 * seq, seq), lambda s: (at(s), 0, 0, 0)),
            by_rows(features),
            by_rows(features),
            by_rows(features),
            whole((16, features)),
            whole((1, hidden)),
        ]
        + [any_ref] * 4,
        scratch_shapes=[
            pltpu.VMEM((16, table_rows), jnp.float32),
            pltpu.VMEM((2, heads, seq, lanes), jnp.float32),
            pltpu.VMEM((2, heads, ROW_SLOTS, lanes), jnp.float32),
            pltpu.VMEM((2, heads, ROW_SLOTS, lanes), jnp.float32),
            pltpu.VMEM((seq, features), jnp.float32),
            pltpu.VMEM((features, 3 * features), jnp.bfloat16),
            pltpu.VMEM((features, features), jnp.bfloat16),
            pltpu.VMEM(GRID + SMALL, jnp.float32),
            pltpu.SemaphoreType.DMA((2, LINE * 8)),
            pltpu.SemaphoreType.DMA((len(owns) + 2, Gather.SEMS + 1)),
            pltpu.SemaphoreType.DMA((len(owns) + 2, Gather.SEMS + 1)),
        ],
        compiler_params=pltpu.CompilerParams(vmem_limit_bytes=BIG, collective_id=0, has_side_effects=True),
        name="attend_front",
    )(xg, xl, *owns, *padded)


def gather_params(vectors, hidden_shift, table, weights):
    whole = lambda v: lax.all_gather(v, "fsdp", axis=0, tiled=True)
    return ([as_float(whole(v)) for v in vectors], as_float(whole(hidden_shift)), as_float(whole(table)), [whole(w) for w in weights])


def pack_small(vectors, hidden_shift, table):
    rows, lanes = SMALL[0], SMALL[1] // 2
    fit = lambda v: jnp.pad(as_float(v), ((0, 0), (0, lanes - v.shape[1])))
    left = jnp.concatenate([fit(jnp.stack(vectors)), fit(hidden_shift[None])])
    fill = lambda v: jnp.pad(v, ((0, rows - v.shape[0]), (0, 0)))
    return jnp.concatenate([fill(left), fill(fit(table.T))], axis=1)


def scatter_grads(vectors, hidden_shift, table, weights):
    share = lambda v: lax.psum_scatter(as_float(v), "fsdp", scatter_dimension=0, tiled=True)
    return ([share(v) for v in vectors], share(hidden_shift), share(table), [share(w) for w in weights])


def slot_rows(values, slot, seq):
    crops, length, features = values.shape
    per_pack = seq // slot
    values = jnp.pad(values, ((0, 0), (0, slot - length), (0, 0)))
    values = values.reshape(crops // per_pack, per_pack * slot, features)
    return jnp.pad(values, ((0, 0), (0, seq - per_pack * slot), (0, 0)))


def crop_rows(packed, slot, crops, length):
    packs, seq, features = packed.shape
    per_pack = seq // slot
    return packed[:, : per_pack * slot].reshape(crops, slot, features)[:, :length]


def per_device(
    x_global, x_local, cot_global, cot_local, global_count, local_count, index_global, index_local,
    ln1_gain, ln1_bias, qkv_weight, q_bias, v_bias, proj_weight, proj_bias, gamma1, bias_table,
    ln2_gain, ln2_bias, fc1_weight, fc1_bias, fc2_weight, fc2_bias, gamma2,
):
    glob, glob_len, features = x_global.shape
    loc, loc_len = x_local.shape[:2]
    heads = bias_table.shape[1]
    seq = round_up(glob_len, 16)
    slot = round_up(loc_len, 8)
    per_pack = seq // slot
    packs = glob + loc // per_pack
    devices = lax.axis_size("fsdp")
    vector_args = [ln1_gain, ln1_bias, q_bias, v_bias, proj_bias, gamma1, ln2_gain, ln2_bias, fc2_bias, gamma2]
    weights = [qkv_weight, proj_weight, fc1_weight, fc2_weight]
    table_rows = bias_table.shape[0] * devices
    indices = (index_global, index_local)
    sides = (math.isqrt(glob_len - 1), math.isqrt(loc_len - 1))
    grids = ((sides[0], glob_len, 1, seq), (sides[1], loc_len, per_pack, slot))

    rows_of = lambda g, l: jnp.concatenate([slot_rows(g, seq, seq), slot_rows(l, slot, seq)]).reshape(-1, features)
    if devices == 32:
        x, normed, qkv, probs, mixed, attn, resid, vectors, hidden_row, *full = attend_front(
            x_global, x_local, pack_small(vector_args, fc1_bias, bias_table), weights, indices, packs, heads, grids, seq,
            table_rows,
        )
        qkv_full, proj_full, fc1_full, fc2_full = [f.reshape(devices * f.shape[4], f.shape[5]) for f in full]
        lanes = round_up(seq, 128)
    else:
        small_full, hidden_full, table_full, (qkv_full, proj_full, fc1_full, fc2_full) = gather_params(
            vector_args, fc1_bias, bias_table, weights
        )
        vectors = jnp.pad(jnp.stack(small_full), ((0, 6), (0, 0)))
        hidden_row = hidden_full[None]
        table = jnp.pad(table_full.T, ((0, round_up(heads, 16) - heads), (0, 0))).astype(jnp.bfloat16)
        x = rows_of(x_global, x_local)
        bias = expand_bias(table, indices, grids, heads, seq)
        lanes = bias.shape[-1]
        normed, qkv, probs, mixed, attn, resid = attend_forward(
            x, qkv_full, proj_full, vectors, bias, packs, glob, heads
        )
    out_global, out_local, gres, gfc1, gfc2, gfc1_shift, small_two, *early = mlp_both(
        global_count, local_count, resid, cot_global, cot_local, vectors, fc1_full, hidden_row, fc2_full, seq, slot,
        x_global.dtype, jnp.bfloat16, 2 if devices == 32 else 0,
    )
    if devices == 32:
        shaped = lambda g: g.reshape(GRID + (g.shape[0] // devices, g.shape[1]))
        gx_global, gx_local, *shares, small = attend_back(
            x, normed, qkv, probs, mixed, attn, gres, qkv_full, proj_full, vectors, small_two, gfc1_shift, indices,
            shaped(gfc1), shaped(gfc2), packs, glob, heads, grids, table_rows, x_global.dtype, lanes,
        )
        shares[2] = jnp.concatenate(early + [shares[2]], axis=1)
        sums = [small[k, : features // devices] for k in range(10)]
        hidden_sum = small[10, : fc1_bias.shape[0]]
        table_sum = small[:heads, 128 : 128 + table_rows // devices].T
    else:
        gx, gqkv, gproj, bias_sums, small_one, gqkv_shift = attend_backward(
            x, normed, qkv, probs, mixed, attn, gres, qkv_full, proj_full, vectors, packs, glob, heads,
            x_global.dtype, jnp.bfloat16, lanes,
        )
        gx = gx.reshape(packs, seq, features)
        gx_global, gx_local = crop_rows(gx[:glob], seq, glob, glob_len), crop_rows(gx[glob:], slot, loc, loc_len)
        gtable = collect_bias(bias_sums, indices, grids, table_rows).T
        vector_grads = [
            small_one[0], small_one[1], gqkv_shift[0, :features], gqkv_shift[0, 2 * features :], small_one[2],
            small_one[3], small_two[0], small_two[1], small_two[2], small_two[3],
        ]
        sums, hidden_sum, table_sum, shares = scatter_grads(
            vector_grads, gfc1_shift[0], gtable, [gqkv, gproj, gfc1, gfc2]
        )
    return (
        out_global, out_local, gx_global, gx_local,
        sums[0], sums[1], shares[0], sums[2], sums[3], shares[1], sums[4], sums[5], table_sum,
        sums[6], sums[7], shares[2], hidden_sum, shares[3], sums[8], sums[9],
    )


def solution(mesh):
    placed = (
        P("fsdp", None, None),
        P("fsdp", None, None),
        P("fsdp", None, None),
        P("fsdp", None, None),
        P("fsdp"),
        P("fsdp"),
        P(),
        P(),
        P("fsdp"),
        P("fsdp"),
        P("fsdp", None),
        P("fsdp"),
        P("fsdp"),
        P("fsdp", None),
        P("fsdp"),
        P("fsdp"),
        P("fsdp", None),
        P("fsdp"),
        P("fsdp"),
        P("fsdp", None),
        P("fsdp"),
        P("fsdp", None),
        P("fsdp"),
        P("fsdp"),
    )
    return jax.shard_map(
        per_device,
        mesh=mesh,
        in_specs=placed,
        out_specs=(
            P("fsdp", None, None),
            P("fsdp", None, None),
            P("fsdp", None, None),
            P("fsdp", None, None),
            P("fsdp"),
            P("fsdp"),
            P("fsdp", None),
            P("fsdp"),
            P("fsdp"),
            P("fsdp", None),
            P("fsdp"),
            P("fsdp"),
            P("fsdp", None),
            P("fsdp"),
            P("fsdp"),
            P("fsdp", None),
            P("fsdp"),
            P("fsdp", None),
            P("fsdp"),
            P("fsdp"),
        ),
        check_vma=False,
    )
```

```python
import functools
import math

import jax
import jax.numpy as jnp
from jax import lax
from jax.experimental import pallas as pl
from jax.experimental.pallas import tpu as pltpu
from jax.sharding import PartitionSpec as P

EPSILON = 1e-06
NEG = -1e30
ROWS_IN = (((0,), (0,)), ((), ()))
COLS_IN = (((1,), (1,)), ((), ()))
BIG = 60 * 1024 * 1024


def as_float(values):
    return values.astype(jnp.float32)


def dot(a, b):
    return jnp.dot(a, b, preferred_element_type=jnp.float32)


def dot_tn(a, b):
    return lax.dot_general(a, b, ROWS_IN, preferred_element_type=jnp.float32)


def dot_nt(a, b):
    return lax.dot_general(a, b, COLS_IN, preferred_element_type=jnp.float32)


def round_up(value, unit):
    return (value + unit - 1) // unit * unit


def unit_rows(values):
    average = jnp.mean(values, axis=-1, keepdims=True)
    centered = values - average
    spread = lax.rsqrt(jnp.mean(centered * centered, axis=-1, keepdims=True) + EPSILON)
    return (centered * spread, spread)


def unit_back(grad, unit, spread):
    return spread * (
        grad - jnp.mean(grad, axis=-1, keepdims=True) - unit * jnp.mean(grad * unit, axis=-1, keepdims=True)
    )


def column_sum(values):
    return jnp.sum(values, axis=0, keepdims=True)


V_LN1G, V_LN1B, V_QB, V_VB, V_PB, V_G1, V_LN2G, V_LN2B, V_FB, V_G2 = range(10)


MLP_PLAN = {
    (0, "end"): ((0, 0),), (1, 0): ((0, 1),), (1, 2): ((0, 2),), (1, "end"): ((0, 3), (1, 0)), (2, 0): ((1, 1),),
    (2, 1): ((0, 4),), (2, 2): ((1, 2),), (2, "end"): ((1, 3),), (2, "last"): ((1, 4),),
}


def fill_terms(ref, value):
    count = ref.shape[-2]
    for d in range(LINE * 8):
        ref[d // 8, d // 4 % 2, d // 2 % 2, d % 2] = value[d * count : (d + 1) * count].astype(ref.dtype)


def put(ref):
    def finish(value):
        ref[...] = value

    return finish


def mlp_kernel(
    steps, blocks, seq, slot, shared, gcount_ref, lcount_ref, resid_ref, cg_ref, cl_ref, vec_ref, w1_ref, b1_ref, w2_ref,
    outg_ref, outl_ref, gres_ref, gw1_ref, gw2_ref, gb1_ref, small_ref, *rest,
):
    step = pl.program_id(0)
    flows = []
    if shared:
        share_ref, *rest = rest
        send, recv = rest[-2:]
        terms, bufs = rest[7 : 7 + shared], rest[7 + shared : -2]
        wide = w1_ref.shape[1]
        for t in range(shared):
            pieces = bufs[Scatter.BUFS * t : Scatter.BUFS * (t + 1)]
            finish = put(share_ref.at[EVERY, pl.ds(t * wide, wide)])
            flows.append(Scatter(terms[t], None, pieces, send.at[t], recv.at[t], finish))
    cot, normed, gbranch, branch, gnorm, active, ghidden = rest[:7]

    def slot_at(where):
        for (s, at), items in MLP_PLAN.items() if shared else ():
            if at == where if isinstance(where, str) else isinstance(at, int):
                @pl.when((step == s) if isinstance(where, str) else ((step == s) & (where == at)))
                def _():
                    for t, n in items:
                        flows[t].stage(n)

    rows, features = resid_ref.shape
    size = rows // blocks
    vec = lambda k: vec_ref[pl.ds(k, 1), :]
    glob, glob_len, _ = cg_ref.shape
    loc, loc_len, _ = cl_ref.shape
    per_pack = seq // slot
    packs = glob + loc // per_pack

    def kept(k, count_ref):
        return jnp.where(k < count_ref[0], 1.0, 0.0)

    @pl.when(step == 0)
    def _():
        if shared:
            greet()
        cot[...] = jnp.zeros_like(cot)

        @pl.loop(0, glob)
        def _(p):
            rows_of = pl.ds(pl.multiple_of(p * seq, seq), glob_len)
            cot[rows_of, :] = (as_float(cg_ref[p]) * kept(p, gcount_ref)).astype(jnp.bfloat16)

        @pl.loop(0, packs - glob)
        def _(p):
            for k in range(per_pack):
                crop = p * per_pack + k
                rows_of = pl.ds(pl.multiple_of((glob + p) * seq + k * slot, 8), loc_len)
                cot[rows_of, :] = (as_float(cl_ref[crop]) * kept(crop, lcount_ref)).astype(jnp.bfloat16)

        @pl.loop(0, blocks)
        def _(i):
            part = pl.ds(pl.multiple_of(i * size, size), size)
            unit, _ = unit_rows(resid_ref[part, :])
            normed[part, :] = (unit * vec(V_LN2G) + vec(V_LN2B)).astype(jnp.bfloat16)
            gbranch[part, :] = (vec(V_G2) * as_float(cot[part, :])).astype(jnp.bfloat16)

    w1, w2 = w1_ref[...], w2_ref[...]

    def block(i, hidden_sum):
        part = pl.ds(pl.multiple_of(i * size, size), size)
        hidden = dot(normed[part, :], w1) + b1_ref[...]
        phi = 0.5 * lax.erf(hidden * (0.5**0.5)) + 0.5
        low = (hidden * phi).astype(jnp.bfloat16)
        active[part, :] = low
        slope = phi + hidden * (jnp.exp(hidden * hidden * -0.5) * 0.3989422804014327)
        add = dot(low, w2)
        grad = dot_nt(gbranch[part, :], w2) * slope
        glow = grad.astype(jnp.bfloat16)
        ghidden[part, :] = glow
        gadd = dot_nt(glow, w1)

        @pl.when(step == 0)
        def _():
            branch[part, :] = add
            gnorm[part, :] = gadd

        @pl.when(step > 0)
        def _():
            branch[part, :] = branch[part, :] + add
            gnorm[part, :] = gnorm[part, :] + gadd

        slot_at(i)
        return hidden_sum + column_sum(as_float(glow))

    gb1_ref[...] = lax.fori_loop(0, blocks, block, jnp.zeros(gb1_ref.shape, jnp.float32))
    gw2_ref[...] = dot_tn(active[...], gbranch[...]).astype(gw2_ref.dtype)
    for t in range(shared):
        @pl.when(step == t)
        def _():
            fill_terms(terms[t], dot_tn(normed[...], ghidden[...]))

    @pl.when(step >= shared)
    def _():
        gw1_ref[...] = dot_tn(normed[...], ghidden[...]).astype(gw1_ref.dtype)

    slot_at("end")

    @pl.when(step == steps - 1)
    def _():
        zero = jnp.zeros((1, features), jnp.float32)

        def pack(p, sums, write):
            part = pl.ds(pl.multiple_of(p * seq, seq), seq)
            resid = resid_ref[part, :]
            full = branch[part, :] + vec(V_FB)
            write(p, resid + vec(V_G2) * full)
            grad = as_float(cot[part, :])
            unit, spread = unit_rows(resid)
            gn = gnorm[part, :]
            gres_ref[part, :] = grad + unit_back(gn * vec(V_LN2G), unit, spread)
            return (
                sums[0] + column_sum(gn * unit),
                sums[1] + column_sum(gn),
                sums[2] + column_sum(as_float(gbranch[part, :])),
                sums[3] + column_sum(grad * full),
            )

        def write_glob(p, value):
            outg_ref[p] = (value[:glob_len] * kept(p, gcount_ref)).astype(outg_ref.dtype)

        def write_loc(p, value):
            for k in range(per_pack):
                crop = (p - glob) * per_pack + k
                piece = value[k * slot : k * slot + loc_len] * kept(crop, lcount_ref)
                outl_ref[crop] = piece.astype(outl_ref.dtype)

        sums = lax.fori_loop(0, glob, lambda p, s: pack(p, s, write_glob), (zero,) * 4)
        sums = lax.fori_loop(glob, packs, lambda p, s: pack(p, s, write_loc), sums)
        small_ref[...] = jnp.zeros_like(small_ref)
        for k in range(4):
            small_ref[pl.ds(k, 1), :] = sums[k]

    slot_at("last")

    if shared:
        @pl.when(step == steps - 1)
        def _():
            for flow in flows:
                flow.drain()


def mlp_both(gcount, lcount, resid, cg, cl, vectors, w1, b1, w2, seq, slot, out_dtype, grad_dtype, shared):
    rows, features = resid.shape
    hidden = w1.shape[1]
    chunk = 1024
    steps = hidden // chunk
    whole = lambda shape: pl.BlockSpec(shape, lambda j: (0,) * len(shape), pipeline_mode=pl.Buffered(1))
    scalar = pl.BlockSpec(memory_space=pltpu.SMEM)
    shares, extra, params = [], [], {}
    if shared:
        share = (features // (LINE * 8), chunk)
        shares = [jax.ShapeDtypeStruct((share[0], shared * chunk), jnp.float32)]
        extra = [pltpu.VMEM(GRID + share, jnp.bfloat16)] * shared
        extra += Scatter.scratch(share, jnp.bfloat16) * shared
        extra += [pltpu.SemaphoreType.DMA((shared, Scatter.SEMS))] * 2
        params = dict(collective_id=2, has_side_effects=True)
    return pl.pallas_call(
        functools.partial(mlp_kernel, steps, 3, seq, slot, shared),
        grid=(steps,),
        out_shape=[
            jax.ShapeDtypeStruct(cg.shape, out_dtype),
            jax.ShapeDtypeStruct(cl.shape, out_dtype),
            jax.ShapeDtypeStruct((rows, features), jnp.float32),
            jax.ShapeDtypeStruct((features, hidden - shared * chunk), grad_dtype),
            jax.ShapeDtypeStruct((hidden, features), grad_dtype),
            jax.ShapeDtypeStruct((1, hidden), jnp.float32),
            jax.ShapeDtypeStruct((8, features), jnp.float32),
        ]
        + shares,
        in_specs=[
            scalar,
            scalar,
            whole((rows, features)),
            whole(cg.shape),
            whole(cl.shape),
            whole(vectors.shape),
            pl.BlockSpec((features, chunk), lambda j: (0, j)),
            pl.BlockSpec((1, chunk), lambda j: (0, j)),
            pl.BlockSpec((chunk, features), lambda j: (j, 0)),
        ],
        out_specs=[
            whole(cg.shape),
            whole(cl.shape),
            whole((rows, features)),
            pl.BlockSpec((features, chunk), lambda j: (0, jnp.maximum(j - shared, 0))),
            pl.BlockSpec((chunk, features), lambda j: (j, 0)),
            pl.BlockSpec((1, chunk), lambda j: (0, j)),
            whole((8, features)),
        ]
        + [whole(s.shape) for s in shares],
        scratch_shapes=[
            pltpu.VMEM((rows, features), jnp.bfloat16),
            pltpu.VMEM((rows, features), jnp.bfloat16),
            pltpu.VMEM((rows, features), jnp.bfloat16),
            pltpu.VMEM((rows, features), jnp.float32),
            pltpu.VMEM((rows, features), jnp.float32),
            pltpu.VMEM((rows, chunk), jnp.bfloat16),
            pltpu.VMEM((rows, chunk), jnp.bfloat16),
        ]
        + extra,
        compiler_params=pltpu.CompilerParams(vmem_limit_bytes=BIG, **params),
        name="mlp_both",
    )(gcount, lcount, resid, cg, cl, vectors, w1, b1, w2)


def lane_of(shape):
    return lax.broadcasted_iota(jnp.int32, shape, 1)


def roll_lanes(values, shift):
    shift = shift % values.shape[1]
    return pltpu.roll(values, shift, 1) if shift else values


def corner_rows(side):
    return (1, side, 1 + (side - 1) * side, side * side)


def expand(grids, table_ref, index_refs, bias_refs, row_refs):
    for n, (side, seq, copies, slot) in enumerate(grids):
        index_ref, bias_ref, row_ref = index_refs[n], bias_refs[n], row_refs[n]
        heads, lanes = bias_ref.shape[0], bias_ref.shape[2]
        tables = lax.broadcasted_iota(jnp.int32, (table_ref.shape[1], lanes), 0)

        def pick(row):
            picked = index_ref[pl.ds(row, 1), :] == tables
            return dot(table_ref[...].astype(jnp.bfloat16), picked.astype(jnp.bfloat16))

        corners = [pick(k) for k in range(4)]
        lane = lane_of(corners[0].shape)
        within = (lane + (side - 1)) % side
        for c in range(side):
            for top in range(2):
                left, right = corners[2 * top], corners[2 * top + 1]
                row = jnp.where(within >= c, roll_lanes(left, c), roll_lanes(right, c - (side - 1)))
                row = jnp.where(lane == 0, left, row)
                row_ref[top, :, pl.ds(c, 1), :] = row[:heads].reshape(heads, 1, lanes)
        row_ref[0, :, pl.ds(side, 1), :] = pick(4)[:heads].reshape(heads, 1, lanes)
        lane = lane_of((side, lanes))

        def spread(values, at):
            if copies > 1:
                values = roll_lanes(values, at * slot)
            where = lane_of(values.shape) - at * slot
            return jnp.where((where >= 0) & (where < seq), values, NEG)

        @pl.loop(0, heads)
        def _(h):
            bias_ref[h] = jnp.full(bias_ref.shape[1:], NEG, jnp.float32)
            low, high, first = row_ref[0, h, :side], row_ref[1, h, :side], row_ref[0, h, pl.ds(side, 1)]
            for at in range(copies):
                bias_ref[h, pl.ds(at * slot, 1), :] = spread(first, at)
            for r in range(side):
                rows = jnp.where(
                    lane - 1 < side * (r + 1), roll_lanes(high, -side * (side - 1 - r)), roll_lanes(low, side * r)
                )
                rows = jnp.where(lane == 0, low, rows)
                for at in range(copies):
                    bias_ref[h, pl.ds(at * slot + 1 + side * r, side), :] = spread(rows, at)


def collect(grids, sum_refs, index_refs, row_refs, shape):
    total = jnp.zeros(shape, jnp.float32)
    for n, (side, seq, copies, slot) in enumerate(grids):
        index_ref, sum_ref, row_ref = index_refs[n], sum_refs[n], row_refs[n]
        heads, lanes = sum_ref.shape[0], sum_ref.shape[2]
        lane = lane_of((side, lanes))

        def gathered(h, start, size):
            rows = None
            for at in range(copies):
                piece = roll_lanes(sum_ref[h, pl.ds(at * slot + start, size), :], -at * slot)
                rows = piece if rows is None else rows + piece
            return jnp.where(lane_of((size, lanes)) < seq, rows, 0.0) if copies > 1 else rows

        @pl.loop(0, heads)
        def _(h):
            low = jnp.zeros((side, lanes), jnp.float32)
            high = jnp.zeros((side, lanes), jnp.float32)
            for r in range(side):
                rows = gathered(h, 1 + side * r, side)
                is_low = lane - 1 >= side * (r + 1)
                is_high = (lane >= 1) & (lane - 1 < side * (r + 1))
                low = low + roll_lanes(jnp.where(is_low, rows, 0.0), -side * r) + jnp.where(lane == 0, rows, 0.0)
                high = high + roll_lanes(jnp.where(is_high, rows, 0.0), side * (side - 1 - r))
            row_ref[0, h, :side], row_ref[1, h, :side] = low, high
            row_ref[0, h, pl.ds(side, 1)] = gathered(h, 0, 1)

        flat = lane_of((heads, lanes))
        within = (flat + (side - 1)) % side
        corners = [jnp.zeros((heads, lanes), jnp.float32) for _ in range(4)]
        for c in range(side):
            for top in range(2):
                row = row_ref[top, :, pl.ds(c, 1), :].reshape(heads, lanes)
                is_left = (flat >= 1) & (within >= c)
                is_right = (flat >= 1) & (within < c)
                left = roll_lanes(jnp.where(is_left, row, 0.0), -c) + jnp.where(flat == 0, row, 0.0)
                corners[2 * top] = corners[2 * top] + left
                corners[2 * top + 1] = corners[2 * top + 1] + roll_lanes(jnp.where(is_right, row, 0.0), side - 1 - c)
        tables = lax.broadcasted_iota(jnp.int32, (shape[1], lanes), 0)

        def place_sum(row, values):
            picked = (index_ref[pl.ds(row, 1), :] == tables).astype(jnp.bfloat16)
            top = values.astype(jnp.bfloat16)
            rest = values - as_float(top)
            middle = rest.astype(jnp.bfloat16)
            last = (rest - as_float(middle)).astype(jnp.bfloat16)
            return dot_nt(top, picked) + dot_nt(middle, picked) + dot_nt(last, picked)

        for k, values in enumerate(corners):
            total = total + place_sum(k, values)
        total = total + place_sum(4, row_ref[0, :, pl.ds(side, 1), :].reshape(heads, lanes))
    return total


ROW_SLOTS = 16


def expand_kernel(grids, table_ref, index_g, index_l, bias_ref, rows_g, rows_l):
    expand(grids, table_ref, (index_g, index_l), (bias_ref.at[0], bias_ref.at[1]), (rows_g, rows_l))


def pad_index(indices, lanes):
    picked = []
    for index in indices:
        rows = corner_rows(math.isqrt(index.shape[0] - 1)) + (0,)
        rows = jnp.concatenate([index[r : r + 1] for r in rows])
        picked.append(jnp.pad(rows, ((0, 8 - len(rows)), (0, lanes - index.shape[1])), constant_values=-1))
    return picked


def expand_bias(table, indices, grids, heads, seq):
    lanes = round_up(seq, 128)
    return pl.pallas_call(
        functools.partial(expand_kernel, grids),
        out_shape=jax.ShapeDtypeStruct((2, heads, seq, lanes), jnp.float32),
        scratch_shapes=[pltpu.VMEM((2, heads, ROW_SLOTS, lanes), jnp.float32)] * 2,
        compiler_params=pltpu.CompilerParams(vmem_limit_bytes=BIG),
        name="expand_bias",
    )(table, *pad_index(indices, lanes))


def collect_kernel(grids, index_g, index_l, sums_ref, grad_ref, rows_g, rows_l):
    grad_ref[...] = collect(
        grids, (sums_ref.at[0], sums_ref.at[1]), (index_g, index_l), (rows_g, rows_l), grad_ref.shape
    )


def collect_bias(sums, indices, grids, table_rows):
    _, heads, _, lanes = sums.shape
    return pl.pallas_call(
        functools.partial(collect_kernel, grids),
        out_shape=jax.ShapeDtypeStruct((heads, table_rows), jnp.float32),
        scratch_shapes=[pltpu.VMEM((2, heads, ROW_SLOTS, lanes), jnp.float32)] * 2,
        compiler_params=pltpu.CompilerParams(vmem_limit_bytes=BIG),
        name="collect_bias",
    )(*pad_index(indices, lanes), sums)


def head_lanes(shape, width):
    return lax.broadcasted_iota(jnp.int32, shape, 1) < width


def stack_heads(pair, width):
    first = head_lanes(pair.shape, width)
    zero = jnp.zeros_like(pair)
    return jnp.concatenate([jnp.where(first, pair, zero), jnp.where(first, zero, pair)], axis=0)


def merge_heads(stacked, width):
    rows = stacked.shape[0] // 2
    top, low = stacked[:rows], stacked[rows:]
    return jnp.where(head_lanes(top.shape, width), top, low)


def attend_kernel(
    glob, heads, x_ref, wqkv_ref, wproj_ref, vec_ref, bias_ref,
    normed_ref, qkv_ref, probs_ref, mixed_ref, attn_ref, resid_ref,
):
    seq, features = x_ref.shape
    width = features // heads
    vec = lambda k: vec_ref[pl.ds(k, 1), :]
    inputs = as_float(x_ref[...])
    unit, _ = unit_rows(inputs)
    normed = (unit * vec(V_LN1G) + vec(V_LN1B)).astype(jnp.bfloat16)
    normed_ref[...] = normed
    qkv_ref[:, pl.ds(0, features)] = (dot(normed, wqkv_ref[:, pl.ds(0, features)]) + vec(V_QB)).astype(jnp.bfloat16)
    qkv_ref[:, pl.ds(features, features)] = dot(normed, wqkv_ref[:, pl.ds(features, features)]).astype(jnp.bfloat16)
    qkv_ref[:, pl.ds(2 * features, features)] = (
        dot(normed, wqkv_ref[:, pl.ds(2 * features, features)]) + vec(V_VB)
    ).astype(jnp.bfloat16)

    for pair in range(heads // 2):
        at = 2 * width * pair
        queries = stack_heads(qkv_ref[:, pl.ds(at, 2 * width)], width)
        keys = qkv_ref[:, pl.ds(features + at, 2 * width)]
        values = qkv_ref[:, pl.ds(2 * features + at, 2 * width)]
        bias = bias_ref[0, pl.ds(2 * pair, 2), :, pl.ds(0, seq)].reshape(2 * seq, seq)
        scores = dot_nt(queries, keys) * (width**-0.5) + bias
        weights = jnp.exp(scores - jnp.max(scores, axis=-1, keepdims=True))
        probs = (weights * (1.0 / jnp.sum(weights, axis=-1, keepdims=True))).astype(jnp.bfloat16)
        probs_ref[0, pair] = probs
        mixed_ref[:, pl.ds(at, 2 * width)] = merge_heads(dot(probs, values), width).astype(jnp.bfloat16)

    attn = dot(mixed_ref[...], wproj_ref[...]) + vec(V_PB)
    attn_ref[...] = attn.astype(jnp.bfloat16)
    resid_ref[...] = inputs + vec(V_G1) * attn


def attend_forward(x, wqkv, wproj, vectors, bias, packs, glob, heads):
    rows, features = x.shape
    seq = rows // packs
    whole = lambda shape: pl.BlockSpec(shape, lambda p: (0,) * len(shape), pipeline_mode=pl.Buffered(1))
    by_rows = lambda cols: pl.BlockSpec((seq, cols), lambda p: (p, 0))
    return pl.pallas_call(
        functools.partial(attend_kernel, glob, heads),
        grid=(packs,),
        out_shape=[
            jax.ShapeDtypeStruct((rows, features), jnp.bfloat16),
            jax.ShapeDtypeStruct((rows, 3 * features), jnp.bfloat16),
            jax.ShapeDtypeStruct((packs, heads // 2, 2 * seq, seq), jnp.bfloat16),
            jax.ShapeDtypeStruct((rows, features), jnp.bfloat16),
            jax.ShapeDtypeStruct((rows, features), jnp.bfloat16),
            jax.ShapeDtypeStruct((rows, features), jnp.float32),
        ],
        in_specs=[
            by_rows(features),
            whole(wqkv.shape),
            whole(wproj.shape),
            whole(vectors.shape),
            pl.BlockSpec((1,) + bias.shape[1:], lambda p: (jnp.where(p < glob, 0, 1), 0, 0, 0)),
        ],
        out_specs=[
            by_rows(features),
            by_rows(3 * features),
            pl.BlockSpec((1, heads // 2, 2 * seq, seq), lambda p: (p, 0, 0, 0)),
            by_rows(features),
            by_rows(features),
            by_rows(features),
        ],
        compiler_params=pltpu.CompilerParams(vmem_limit_bytes=BIG),
        name="attend_forward",
    )(x, wqkv, wproj, vectors, bias)


def attend_back_kernel(
    packs, glob, heads, chunk, x_ref, normed_ref, qkv_ref, probs_ref, mixed_ref, attn_ref, gres_ref, wqkv_ref, wproj_ref, vec_ref,
    gx_ref, gwqkv_ref, gwproj_ref, bsum_ref, small_ref, gqb_ref,
    normed_all, mixed_all, gattn_all, gqkv_all,
):
    step = pl.program_id(0)
    seq, features = x_ref.shape
    width = features // heads
    vec = lambda k: vec_ref[pl.ds(k, 1), :]
    rows = packs * seq

    @pl.when(step == 0)
    def _():
        small_ref[...] = jnp.zeros_like(small_ref)
        gqb_ref[...] = jnp.zeros_like(gqb_ref)

    @pl.when((step == 0) | (step == glob))
    def _():
        bsum_ref[...] = jnp.zeros_like(bsum_ref)

    @pl.when(step < packs)
    def _():
        part = pl.ds(pl.multiple_of(step * seq, seq), seq)
        gres = gres_ref[...]
        gattn = (vec(V_G1) * gres).astype(jnp.bfloat16)
        gattn_all[part, :] = gattn
        mixed_all[part, :] = mixed_ref[...]
        normed_all[part, :] = normed_ref[...]
        small_ref[pl.ds(2, 1), :] += column_sum(as_float(gattn))
        small_ref[pl.ds(3, 1), :] += column_sum(gres * as_float(attn_ref[...]))
        gmixed = dot_nt(gattn, wproj_ref[...]).astype(jnp.bfloat16)
        scale = width**-0.5
        for pair in range(heads // 2):
            at = 2 * width * pair
            queries = stack_heads(qkv_ref[:, pl.ds(at, 2 * width)], width)
            keys = qkv_ref[:, pl.ds(features + at, 2 * width)]
            values = qkv_ref[:, pl.ds(2 * features + at, 2 * width)]
            grads = stack_heads(gmixed[:, at : at + 2 * width], width)
            mixed = as_float(mixed_ref[:, pl.ds(at, 2 * width)])
            probs = probs_ref[0, pair]
            twice = jnp.concatenate([mixed, mixed], axis=0)
            inner = jnp.sum(as_float(grads) * twice, axis=-1, keepdims=True)
            gscores = as_float(probs) * (dot_nt(grads, values) - inner)
            bsum_ref[0, pl.ds(2 * pair, 2), :, pl.ds(0, seq)] += gscores.reshape(2, seq, seq)
            low = gscores.astype(jnp.bfloat16)
            gqkv_all[part, pl.ds(at, 2 * width)] = (merge_heads(dot(low, keys), width) * scale).astype(jnp.bfloat16)
            gqkv_all[part, pl.ds(features + at, 2 * width)] = (dot_tn(low, queries) * scale).astype(jnp.bfloat16)
            gqkv_all[part, pl.ds(2 * features + at, 2 * width)] = dot_tn(probs, grads).astype(jnp.bfloat16)
        gqkv = gqkv_all[part, :]
        gqb_ref[...] += column_sum(as_float(gqkv))
        gnorm = dot_nt(gqkv, wqkv_ref[...])
        unit, spread = unit_rows(as_float(x_ref[...]))
        small_ref[pl.ds(0, 1), :] += column_sum(gnorm * unit)
        small_ref[pl.ds(1, 1), :] += column_sum(gnorm)
        gx_ref[...] = (gres + unit_back(gnorm * vec(V_LN1G), unit, spread)).astype(gx_ref.dtype)

    @pl.when(step >= packs)
    def _():
        j = step - packs
        wide = 3 * features // chunk

        @pl.when(j < wide)
        def _():
            gwqkv_ref[...] = dot_tn(normed_all[...], gqkv_all[:, pl.ds(pl.multiple_of(j * chunk, chunk), chunk)]).astype(gwqkv_ref.dtype)

        @pl.when(j >= wide)
        def _():
            gwproj_ref[...] = dot_tn(mixed_all[...], gattn_all[:, pl.ds(pl.multiple_of((j - wide) * chunk, chunk), chunk)]).astype(gwproj_ref.dtype)


def attend_backward(x, normed, qkv, probs, mixed, attn, gres, wqkv, wproj, vectors, packs, glob, heads, out_dtype, grad_dtype, lanes):
    rows, features = x.shape
    seq = rows // packs
    chunk = 256
    wide, narrow = 3 * features // chunk, features // chunk
    whole = lambda shape: pl.BlockSpec(shape, lambda s: (0,) * len(shape), pipeline_mode=pl.Buffered(1))
    pack = lambda s: jnp.minimum(s, packs - 1)
    by_rows = lambda cols: pl.BlockSpec((seq, cols), lambda s: (pack(s), 0))
    return pl.pallas_call(
        functools.partial(attend_back_kernel, packs, glob, heads, chunk),
        grid=(packs + wide + narrow,),
        out_shape=[
            jax.ShapeDtypeStruct((rows, features), out_dtype),
            jax.ShapeDtypeStruct((features, 3 * features), grad_dtype),
            jax.ShapeDtypeStruct((features, features), grad_dtype),
            jax.ShapeDtypeStruct((2, heads, seq, lanes), jnp.float32),
            jax.ShapeDtypeStruct((8, features), jnp.float32),
            jax.ShapeDtypeStruct((1, 3 * features), jnp.float32),
        ],
        in_specs=[
            by_rows(features),
            by_rows(features),
            by_rows(3 * features),
            pl.BlockSpec((1, heads // 2, 2 * seq, seq), lambda s: (pack(s), 0, 0, 0)),
            by_rows(features),
            by_rows(features),
            by_rows(features),
            whole(wqkv.shape),
            whole(wproj.shape),
            whole(vectors.shape),
        ],
        out_specs=[
            by_rows(features),
            pl.BlockSpec((features, chunk), lambda s: (0, jnp.clip(s - packs, 0, wide - 1))),
            pl.BlockSpec((features, chunk), lambda s: (0, jnp.clip(s - packs - wide, 0, narrow - 1))),
            pl.BlockSpec((1, heads, seq, lanes), lambda s: (jnp.where(s < glob, 0, 1), 0, 0, 0)),
            whole((8, features)),
            whole((1, 3 * features)),
        ],
        scratch_shapes=[
            pltpu.VMEM((rows, features), jnp.bfloat16),
            pltpu.VMEM((rows, features), jnp.bfloat16),
            pltpu.VMEM((rows, features), jnp.bfloat16),
            pltpu.VMEM((rows, 3 * features), jnp.bfloat16),
        ],
        compiler_params=pltpu.CompilerParams(vmem_limit_bytes=BIG),
        name="attend_backward",
    )(x, normed, qkv, probs, mixed, attn, gres, wqkv, wproj, vectors)


MESH = pl.DeviceIdType.MESH
LINE = 4
GRID = (LINE, 2, 2, 2)
EVERY = slice(None)


def place():
    me = lax.axis_index("fsdp")
    return (me // 8, (me // 4) % 2, (me // 2) % 2, me % 2)


def device_at(z, y, x, c):
    return (((z * 2 + y) * 2 + x) * 2 + c,)


def along(z, k):
    return (z + k) % LINE


def greet():
    z, y, x, c = place()
    barrier = pltpu.get_barrier_semaphore()
    peers = [device_at(z, y, x, 1 - c), device_at(z, y, 1 - x, c), device_at(z, 1 - y, x, c)]
    peers += [device_at(along(z, k), y, x, c) for k in range(1, LINE)]
    for peer in peers:
        pl.semaphore_signal(barrier, inc=1, device_id=peer, device_id_type=MESH)
    pl.semaphore_wait(barrier, len(peers))


def remote(src, dst, send, recv, peer):
    return pltpu.make_async_remote_copy(
        src_ref=src, dst_ref=dst, send_sem=send, recv_sem=recv, device_id=peer, device_id_type=MESH
    )


class Gather:
    SEMS = 24

    def __init__(self, own, full, send, recv):
        self.own, self.full, self.send, self.recv = own, full, send, recv
        self.z, self.y, self.x, self.c = place()
        self.cols = full.shape[-1] // 2

    def half(self, ref, part, half):
        cols = (EVERY, pl.ds(half * self.cols, self.cols))
        return ref.at[part + cols]

    def line_copy(self, k, source=None):
        z, y, x, c = self.z, self.y, self.x, self.c
        held = z if source is None else source
        peer = device_at(along(z, k), y, x, c)
        return remote(self.own, self.full.at[held, y, x, c], self.send.at[k - 1], self.recv.at[k - 1], peer)

    def over(self, half, near):
        z, y, x, c = self.z, self.y, self.x, self.c
        return device_at(z, y, 1 - x, c) if (half == 0) == near else device_at(z, 1 - y, x, c)

    def first(self, half):
        z, y, x, c = self.z, self.y, self.x, self.c
        k = 3 + half
        return remote(
            self.half(self.own, (), half), self.half(self.full, (z, y, x, c), half), self.send.at[k], self.recv.at[k],
            self.over(half, True),
        )

    def hop(self, half, k, near):
        z, y, x, c = self.z, self.y, self.x, self.c
        held = along(z, LINE - k) if k else z
        if near:
            part, sem = (held, y, x, c), 7 + 3 * half + k - 1
        else:
            part = (held, y, EVERY, c) if half == 0 else (held, EVERY, x, c)
            sem = 13 + 3 * half + k - 1 if k else 5 + half
        ref = self.half(self.full, part, half)
        return remote(ref, ref, self.send.at[sem], self.recv.at[sem], self.over(half, near))

    def pair(self, k):
        z, y, x, c = self.z, self.y, self.x, self.c
        part, half = (
            ((EVERY, y, x, c), None),
            ((EVERY, y, 1 - x, c), 0),
            ((EVERY, 1 - y, x, c), 1),
            ((EVERY, 1 - y, EVERY, c), 0),
            ((EVERY, EVERY, 1 - x, c), 1),
        )[k]
        ref = self.full.at[part] if half is None else self.half(self.full, part, half)
        return remote(ref, ref, self.send.at[19 + k], self.recv.at[19 + k], device_at(z, y, x, 1 - c))

    def mine(self):
        return pltpu.make_async_copy(self.own, self.full.at[self.z, self.y, self.x, self.c], self.recv.at[self.SEMS])

    def stage(self, name):
        away = range(1, LINE)
        if name == "a":
            for k in away:
                self.line_copy(k).start()
            for half in range(2):
                self.first(half).start()
            self.mine().start()
        elif name == "n":
            self.mine().wait()
            for half in range(2):
                self.first(half).wait_recv()
                self.hop(half, 0, False).start()
        elif name == "z":
            for k in away:
                self.line_copy(k, along(self.z, LINE - k)).wait_recv()
                for half in range(2):
                    self.hop(half, k, True).start()
            self.pair(0).start()
        elif name == "f":
            for k in away:
                for half in range(2):
                    self.hop(half, k, True).wait_recv()
                    self.hop(half, k, False).start()
            self.pair(1).start()
            self.pair(2).start()
        elif name == "q":
            for half in range(2):
                for k in range(LINE):
                    self.hop(half, k, False).wait_recv()
                self.pair(3 + half).start()
        else:
            for k in range(5):
                self.pair(k).wait_recv()

    def drain(self):
        away = range(1, LINE)
        for k in away:
            self.line_copy(k).wait_send()
        for half in range(2):
            self.first(half).wait_send()
            self.hop(half, 0, False).wait_send()
            for k in away:
                self.hop(half, k, True).wait_send()
                self.hop(half, k, False).wait_send()
        for k in range(5):
            self.pair(k).wait_send()


class Scatter:
    STAGES = 5
    SEMS = 9

    def __init__(self, terms, own, bufs, send, recv, finish):
        self.terms, self.loaded = terms, own
        self.pairbuf, self.buf1a, self.buf1b, self.buf2a, self.buf2b, self.line = bufs
        self.send, self.recv, self.finish = send, recv, finish
        self.z, self.y, self.x, self.c = place()
        self.cols = terms.shape[-1] // 2

    BUFS = 6

    @staticmethod
    def scratch(shape, dtype):
        rows, cols = shape
        half = cols // 2
        return [
            pltpu.VMEM((LINE, 2, 2, rows, cols), dtype),
            pltpu.VMEM((LINE, 2, rows, half), dtype),
            pltpu.VMEM((LINE, 2, rows, half), dtype),
            pltpu.VMEM((LINE, rows, half), dtype),
            pltpu.VMEM((LINE, rows, half), dtype),
            pltpu.VMEM((LINE - 1, rows, cols), dtype),
        ]

    def at(self, i, j, k, half=None):
        cols = () if half is None else (EVERY, pl.ds(half * self.cols, self.cols))
        if self.loaded is None:
            return self.terms.at[(i, j, k, self.c) + cols]
        return self.loaded.at[(i, j, k) + cols]

    def load(self):
        return pltpu.make_async_copy(self.terms.at[EVERY, EVERY, EVERY, self.c], self.loaded, self.send.at[8])

    def copy(self, name):
        z, y, x, c = self.z, self.y, self.x, self.c
        over_x, over_y = device_at(z, y, 1 - x, c), device_at(z, 1 - y, x, c)
        k, src, dst, peer = {
            "pair": lambda: (0, self.terms.at[EVERY, EVERY, EVERY, 1 - c], self.pairbuf, device_at(z, y, x, 1 - c)),
            "1a": lambda: (1, self.at(EVERY, 1 - y, EVERY, 0), self.buf1a, over_y),
            "1b": lambda: (2, self.at(EVERY, EVERY, 1 - x, 1), self.buf1b, over_x),
            "2a": lambda: (3, self.at(EVERY, y, 1 - x, 0), self.buf2a, over_x),
            "2b": lambda: (4, self.at(EVERY, 1 - y, x, 1), self.buf2b, over_y),
        }[name]()
        return remote(src, dst, self.send.at[k], self.recv.at[k], peer)

    def line_copy(self, k):
        z, y, x, c = self.z, self.y, self.x, self.c
        target = along(z, k)
        return remote(
            self.at(target, y, x), self.line.at[k - 1], self.send.at[4 + k], self.recv.at[4 + k], device_at(target, y, x, c)
        )

    def add(self, ref, term):
        ref[...] = ref[...] + term

    def stage(self, s):
        z, y, x = self.z, self.y, self.x
        if s == 0:
            self.copy("pair").start()
            if self.loaded is not None:
                self.load().start()
        elif s == 1:
            if self.loaded is not None:
                self.load().wait()
            self.copy("pair").wait_recv()

            @pl.loop(0, LINE)
            def _(i):
                for j in range(2):
                    for k in range(2):
                        self.add(self.at(i, j, k), self.pairbuf[i, j, k])

            self.copy("1a").start()
            self.copy("1b").start()
        elif s == 2:
            self.copy("1a").wait_recv()
            self.copy("1b").wait_recv()

            @pl.loop(0, LINE)
            def _(i):
                for k in range(2):
                    self.add(self.at(i, y, k, 0), self.buf1a[i, k])
                    self.add(self.at(i, k, x, 1), self.buf1b[i, k])

            self.copy("2a").start()
            self.copy("2b").start()
        elif s == 3:
            self.copy("2a").wait_recv()
            self.copy("2b").wait_recv()

            @pl.loop(0, LINE)
            def _(i):
                self.add(self.at(i, y, x, 0), self.buf2a[i])
                self.add(self.at(i, y, x, 1), self.buf2b[i])

            for k in range(1, LINE):
                self.line_copy(k).start()
        else:
            total = as_float(self.at(z, y, x)[...])
            for k in range(1, LINE):
                self.line_copy(k).wait_recv()
                total = total + as_float(self.line[k - 1])
            self.finish(total)

    def drain(self):
        for name in ("pair", "1a", "1b", "2a", "2b"):
            self.copy(name).wait_send()
        for k in range(1, LINE):
            self.line_copy(k).wait_send()


SMALL = (16, 256)


def back_kernel(
    shape, plan, x_ref, normed_ref, q_ref, k_ref, v_ref, probs_ref, mixed_ref, attn_ref, gres_ref, wqkv_ref, wproj_ref, vec_ref,
    two_ref, hidden_ref, raw_g, raw_l, gfc1_ref, gfc2_ref,
    gxg_ref, gxl_ref, sqkv_ref, sproj_ref, sfc1_ref, sfc2_ref, ssmall_ref,
    gqkv, gmixed, bsum, vecs, tsum, corner, index_g, index_l, *scratch,
):
    packs, glob, heads, groups, blocks, grids = shape
    step = pl.program_id(0)
    rows, features = normed_ref.shape
    seq = rows // packs
    width = features // heads
    lanes = features // groups
    scale = width**-0.5
    vec = lambda k: vec_ref[pl.ds(k, 1), :]
    size = rows // blocks
    last = 1 + packs * groups + 1 + blocks

    send, recv = scratch[-2:]
    scratch = scratch[:-2]
    big = SPLIT + 1
    owns = list(scratch[:big]) + [None] * (groups + 2)
    terms = scratch[big : big + groups + 2]
    bufs = scratch[big + groups + 2 :]

    def put_group(g):
        def finish(value):
            for i in range(3):
                sqkv_ref[:, pl.ds(i * features + g * lanes, lanes)] = value[:, i * lanes : (i + 1) * lanes]

        return finish

    tall = gfc2_ref.shape[4] // SPLIT
    sources, ends = [], []
    for k in range(SPLIT):
        sources.append(gfc2_ref.at[EVERY, EVERY, EVERY, EVERY, pl.ds(k * tall, tall)])
        ends.append(put(sfc2_ref.at[pl.ds(k * tall, tall)]))
    sources.append(gfc1_ref)
    ends.append(put(sfc1_ref))
    sources += list(terms)
    ends += [put(sproj_ref)] + [put_group(g) for g in range(groups)] + [put(ssmall_ref)]
    flows = [
        Scatter(sources[t], owns[t], bufs[Scatter.BUFS * t : Scatter.BUFS * (t + 1)], send.at[t], recv.at[t], ends[t]) for t in range(len(ends))
    ]

    def slot(k):
        for t, s in plan.get(k, ()):
            flows[t].stage(s)

    @pl.when(step == 0)
    def _():
        greet()
        slot(0)
        zero = jnp.zeros((1, features), jnp.float32)
        vecs[...] = jnp.zeros_like(vecs)

        def block(i, sums):
            part = pl.ds(pl.multiple_of(i * size, size), size)
            gres = gres_ref[part, :]
            gattn = (vec(V_G1) * gres).astype(jnp.bfloat16)
            gqkv[part, pl.ds(0, features)] = gattn
            gmixed[part, :] = dot_nt(gattn, wproj_ref[...]).astype(jnp.bfloat16)
            return (sums[0] + column_sum(as_float(gattn)), sums[1] + column_sum(gres * as_float(attn_ref[part, :])))

        sums = lax.fori_loop(0, blocks, block, (zero, zero))
        vecs[pl.ds(V_PB, 1), :] = sums[0]
        vecs[pl.ds(V_G1, 1), :] = sums[1]
        bsum[...] = jnp.zeros_like(bsum)
        fill_terms(terms[0], dot_tn(mixed_ref[...], gqkv[:, pl.ds(0, features)]))

    @pl.when((step >= 1) & (step <= packs * groups))
    def _():
        pack = (step - 1) % packs
        group = (step - 1) // packs
        part = pl.ds(pl.multiple_of(pack * seq, seq), seq)
        kind = jnp.where(pack < glob, 0, 1)
        for pair in range(heads // 2 // groups):
            at = 2 * width * pair
            wide = pl.ds(pl.multiple_of(group * lanes + at, 2 * width), 2 * width)
            queries = stack_heads(q_ref[:, pl.ds(at, 2 * width)], width)
            keys = k_ref[:, pl.ds(at, 2 * width)]
            values = v_ref[:, pl.ds(at, 2 * width)]
            grads = stack_heads(gmixed[part, wide], width)
            mixed = as_float(mixed_ref[part, wide])
            probs = probs_ref[0, pair]
            twice = jnp.concatenate([mixed, mixed], axis=0)
            inner = jnp.sum(as_float(grads) * twice, axis=-1, keepdims=True)
            gscores = as_float(probs) * (dot_nt(grads, values) - inner)
            head = group * (heads // groups) + 2 * pair
            bsum[kind, pl.ds(head, 2), :, pl.ds(0, seq)] += gscores.reshape(2, seq, seq)
            low = gscores.astype(jnp.bfloat16)
            gq = (merge_heads(dot(low, keys), width) * scale).astype(jnp.bfloat16)
            gk = (dot_tn(low, queries) * scale).astype(jnp.bfloat16)
            gv = dot_tn(probs, grads).astype(jnp.bfloat16)
            for i, piece in enumerate((gq, gk, gv)):
                at_lane = pl.multiple_of(group * lanes + at + i * features, 2 * width)
                gqkv[part, pl.ds(at_lane, 2 * width)] = piece

    for g in range(groups):
        @pl.when(step == packs * (g + 1))
        def _():
            pieces = [dot_tn(normed_ref[...], gqkv[:, pl.ds(i * features + g * lanes, lanes)]) for i in range(3)]
            fill_terms(terms[1 + g], jnp.concatenate(pieces, axis=1))

    @pl.when(step == packs * groups + 1)
    def _():
        pick_rows(raw_g, index_g)
        pick_rows(raw_l, index_l)
        tsum[...] = collect(
            grids, (bsum.at[0], bsum.at[1]), (index_g, index_l), (corner, corner), tsum.shape
        )

    @pl.when(step >= packs * groups + 2)
    def _():
        i = step - packs * groups - 2
        part = pl.ds(pl.multiple_of(i * size, size), size)
        low = gqkv[part, :]
        gnorm = dot_nt(low, wqkv_ref[...])
        unit, spread = unit_rows(as_float(x_ref[...]))
        vecs[pl.ds(V_LN1G, 1), :] += column_sum(gnorm * unit)
        vecs[pl.ds(V_LN1B, 1), :] += column_sum(gnorm)
        total = column_sum(as_float(low))
        vecs[pl.ds(V_QB, 1), :] += total[:, :features]
        vecs[pl.ds(V_VB, 1), :] += total[:, 2 * features :]
        value = gres_ref[part, :] + unit_back(gnorm * vec(V_LN1G), unit, spread)
        per_block = packs // blocks
        glob_len, loc_len, per_pack, slot = grids[0][1], grids[1][1], grids[1][2], grids[1][3]

        @pl.when(i < glob // per_block)
        def _():
            for n in range(per_block):
                gxg_ref[n] = value[n * seq : n * seq + glob_len].astype(gxg_ref.dtype)

        @pl.when(i >= glob // per_block)
        def _():
            for n in range(per_block):
                for k in range(per_pack):
                    start = n * seq + k * slot
                    gxl_ref[n * per_pack + k] = value[start : start + loc_len].astype(gxl_ref.dtype)

    @pl.when(step == last - 1)
    def _():
        for k, row in ((V_LN2G, 0), (V_LN2B, 1), (V_FB, 2), (V_G2, 3)):
            vecs[pl.ds(k, 1), :] = two_ref[pl.ds(row, 1), :]
        ref = terms[-1]
        ref[...] = jnp.zeros_like(ref)
        devices = LINE * 8
        count, wide, table = features // devices, hidden_ref.shape[1] // devices, tsum.shape[1] // devices
        for d in range(devices):
            block = ref.at[d // 8, d // 4 % 2, d // 2 % 2, d % 2]
            block[:, pl.ds(0, count)] = vecs[:, pl.ds(d * count, count)]
            block[pl.ds(10, 1), pl.ds(0, wide)] = hidden_ref[:, pl.ds(d * wide, wide)]
            block[pl.ds(0, heads), pl.ds(128, table)] = tsum[:, pl.ds(d * table, table)]

    for k in sorted(plan):
        if k:
            @pl.when(step == k)
            def _():
                slot(k)

    @pl.when(step == last - 1)
    def _():
        for flow in flows:
            flow.drain()


BACK_PLAN = {
    0: ((0, 0), (1, 0),),
    1: ((0, 1),),
    4: ((2, 0),),
    5: ((1, 1),),
    7: ((3, 0), (4, 0), (2, 1),),
    11: ((0, 2),),
    12: ((1, 2),),
    13: ((5, 0), (2, 2),),
    16: ((0, 3), (5, 1),),
    18: ((6, 0), (4, 1), (1, 3), (3, 1),),
    19: ((4, 2), (2, 3), (5, 2), (6, 1),),
    20: ((3, 2),),
    21: ((4, 3),),
    22: (
        (7, 0), (1, 4), (5, 3), (6, 2), (7, 1), (4, 4), (2, 4), (3, 3),
        (5, 4), (6, 3), (7, 2), (0, 4), (7, 3), (6, 4), (3, 4), (7, 4),
    ),
}
SPLIT = 2


def attend_back(
    x, normed, qkv, probs, mixed, attn, gres, wqkv, wproj, vectors, two, hidden, indices, gfc1, gfc2, packs, glob, heads,
    grids, table_rows, out_dtype, lanes,
):
    rows, features = x.shape
    seq = rows // packs
    groups, blocks = 3, 3
    per_block = packs // blocks
    cols = features // groups
    steps = 1 + packs * groups + 1 + blocks
    first_block = packs * groups + 2
    whole = lambda shape: pl.BlockSpec(shape, lambda s: (0,) * len(shape), pipeline_mode=pl.Buffered(1))
    at = lambda s: jnp.clip(s - 1, 0, packs * groups - 1)
    part = lambda i: pl.BlockSpec((seq, cols), lambda s: (at(s) % packs, i * groups + at(s) // packs))
    any_ref = pl.BlockSpec(memory_space=pl.ANY)
    by_block = pl.BlockSpec((rows // blocks, features), lambda s: (jnp.clip(s - first_block, 0, blocks - 1), 0))
    shard = lambda t: t.shape[4:]
    term_shapes = [(features // 32, features)] + [(features // 32, 3 * cols)] * groups
    tall = (shard(gfc2)[0] // SPLIT, shard(gfc2)[1])
    flow_shapes = [(tall, gfc2.dtype)] * SPLIT + [(shard(gfc1), gfc1.dtype)]
    scratch = [
        pltpu.VMEM((rows, 3 * features), jnp.bfloat16),
        pltpu.VMEM((rows, features), jnp.bfloat16),
        pltpu.VMEM((2, heads, seq, lanes), jnp.float32),
        pltpu.VMEM((16, features), jnp.float32),
        pltpu.VMEM((heads, table_rows), jnp.float32),
        pltpu.VMEM((2, heads, ROW_SLOTS, lanes), jnp.float32),
        pltpu.VMEM((8, lanes), jnp.int32),
        pltpu.VMEM((8, lanes), jnp.int32),
    ]
    scratch += [pltpu.VMEM((LINE, 2, 2) + s, d) for s, d in flow_shapes]
    flow_shapes += [(s, jnp.bfloat16) for s in term_shapes] + [(SMALL, jnp.float32)]
    scratch += [pltpu.VMEM(GRID + s, jnp.bfloat16) for s in term_shapes] + [pltpu.VMEM(GRID + SMALL, jnp.float32)]
    for s, d in flow_shapes:
        scratch += Scatter.scratch(s, d)
    scratch += [pltpu.SemaphoreType.DMA((len(flow_shapes), Scatter.SEMS))] * 2
    return pl.pallas_call(
        functools.partial(
            back_kernel, (packs, glob, heads, groups, blocks, grids), BACK_PLAN
        ),
        grid=(steps,),
        out_shape=[
            jax.ShapeDtypeStruct((glob, grids[0][1], features), out_dtype),
            jax.ShapeDtypeStruct(((packs - glob) * grids[1][2], grids[1][1], features), out_dtype),
            jax.ShapeDtypeStruct((features // 32, 3 * features), jnp.float32),
            jax.ShapeDtypeStruct((features // 32, features), jnp.float32),
            jax.ShapeDtypeStruct(shard(gfc1), jnp.float32),
            jax.ShapeDtypeStruct(shard(gfc2), jnp.float32),
            jax.ShapeDtypeStruct(SMALL, jnp.float32),
        ],
        in_specs=[
            by_block,
            whole((rows, features)),
            part(0), part(1), part(2),
            pl.BlockSpec((1, heads // 2 // groups, 2 * seq, seq), lambda s: (at(s) % packs, at(s) // packs, 0, 0)),
            whole((rows, features)),
            whole((rows, features)),
            whole((rows, features)),
            whole(wqkv.shape),
            whole(wproj.shape),
            whole(vectors.shape),
            whole(two.shape),
            whole(hidden.shape),
            whole(indices[0].shape),
            whole(indices[1].shape),
            any_ref,
            any_ref,
        ],
        out_specs=[
            pl.BlockSpec(
                (per_block, grids[0][1], features),
                lambda s: (jnp.clip(s - first_block, 0, glob // per_block - 1), 0, 0),
            ),
            pl.BlockSpec(
                (per_block * grids[1][2], grids[1][1], features),
                lambda s: (jnp.maximum(s - first_block - glob // per_block, 0), 0, 0),
            ),
            whole((features // 32, 3 * features)),
            whole((features // 32, features)),
            whole(shard(gfc1)),
            whole(shard(gfc2)),
            whole(SMALL),
        ],
        scratch_shapes=scratch,
        compiler_params=pltpu.CompilerParams(vmem_limit_bytes=BIG, collective_id=1, has_side_effects=True),
        name="attend_back",
    )(x, normed, qkv, qkv, qkv, probs, mixed, attn, gres, wqkv, wproj, vectors, two, hidden, *indices, gfc1, gfc2)


GATHER_HEAD = (
    (0, "a"), (2, "a"), (1, "a"), (4, "a"), (0, "n"), (6, "a"), (0, "z"), (5, "a"), (1, "n"), (2, "n"), (0, "f"),
    (4, "n"), (6, "n"), (2, "z"), (5, "n"), (0, "q"), (3, "a"), (1, "z"), (0, "e"), (3, "n"), "unpack", (2, "f"),
    (1, "f"), "expand global", (6, "z"), (2, "q"), "expand local", (1, "q"), (4, "z"), (5, "z"), (2, "e"), (6, "f"),
    (1, "e"),
)
GATHER_LATER = {
    1: ((3, "z"), (4, "f")),
    2: ((6, "q"), (5, "f")),
    4: ((3, "f"), (4, "q")),
    5: ((4, "e"), (5, "q")),
    7: ((3, "q"), (6, "e"), (5, "e"), (3, "e")),
}


def pick_rows(index_ref, rows_ref):
    length = index_ref.shape[0]
    rows_ref[...] = jnp.full(rows_ref.shape, -1, jnp.int32)
    for k, row in enumerate(corner_rows(math.isqrt(length - 1)) + (0,)):
        rows_ref[pl.ds(k, 1), pl.ds(0, length)] = index_ref[pl.ds(row, 1), :]


def front_kernel(
    shape, xg_ref, xl_ref, vecs_ref, shift_ref, table_ref, oqkv_ref, oproj_ref, ofc1_ref, ofc2_ref, raw_g, raw_l,
    x_ref, normed_ref, qkv_ref, probs_ref, mixed_ref, attn_ref, resid_ref, vec_ref, hidden_ref,
    fqkv_ref, fproj_ref, ffc1_ref, ffc2_ref,
    table, bias, rows_g, rows_l, padded, wqkv, wproj, small_ref, small_full, index_g, index_l, load, send, recv,
):
    packs, glob, heads, grids = shape
    step = pl.program_id(0)
    seq, features = x_ref.shape
    width = features // heads
    devices = LINE * 8
    vec = lambda k: vec_ref[pl.ds(k, 1), :]
    wide, tall = ofc1_ref.shape[1] // 2, ofc2_ref.shape[0] // 2
    ends = [(small_ref, small_full), (oqkv_ref, fqkv_ref), (oproj_ref, fproj_ref)]
    lead = (EVERY,) * 4
    for k in range(2):
        cols = (EVERY, pl.ds(k * wide, wide))
        ends.append((ofc1_ref.at[cols], ffc1_ref.at[lead + cols]))
    for k in range(2):
        lines = (pl.ds(k * tall, tall),)
        ends.append((ofc2_ref.at[lines], ffc2_ref.at[lead + lines]))
    flows = [Gather(o, f, send.at[t], recv.at[t]) for t, (o, f) in enumerate(ends)]

    def each_shard(act):
        @pl.loop(0, devices)
        def _(d):
            for k, (ref, held) in enumerate(((fqkv_ref, wqkv), (fproj_ref, wproj))):
                count = held.shape[0] // devices
                part = held.at[pl.ds(pl.multiple_of(d * count, 8), count)]
                act(pltpu.make_async_copy(ref.at[d // 8, d // 4 % 2, d // 2 % 2, d % 2], part, load.at[k, d]))

    @pl.when(step == 0)
    def _():
        greet()
        small_ref[...] = jnp.zeros_like(small_ref)
        small_ref[pl.ds(0, vecs_ref.shape[0]), pl.ds(0, vecs_ref.shape[1])] = as_float(vecs_ref[...])
        small_ref[pl.ds(10, 1), pl.ds(0, shift_ref.shape[1])] = as_float(shift_ref[...])
        small_ref[pl.ds(0, heads), pl.ds(128, table_ref.shape[1])] = as_float(table_ref[...])
        pick_rows(raw_g, index_g)
        pick_rows(raw_l, index_l)
        table[...] = jnp.zeros_like(table)
        for item in GATHER_HEAD:
            if item == "unpack":
                count, wide = features // devices, hidden_ref.shape[1] // devices
                lines = table.shape[1] // devices
                for d in range(devices):
                    block = small_full.at[d // 8, d // 4 % 2, d // 2 % 2, d % 2]
                    vec_ref[:, pl.ds(d * count, count)] = block[:, pl.ds(0, count)]
                    hidden_ref[:, pl.ds(d * wide, wide)] = block[pl.ds(10, 1), pl.ds(0, wide)]
                    table[pl.ds(0, heads), pl.ds(d * lines, lines)] = block[pl.ds(0, heads), pl.ds(128, lines)]
            elif item == "expand global":
                expand(grids[:1], table, (index_g,), (bias.at[0],), (rows_g,))
            elif item == "expand local":
                expand(grids[1:], table, (index_l,), (bias.at[1],), (rows_l,))
            else:
                flows[item[0]].stage(item[1])
        each_shard(lambda copy: copy.start())
        each_shard(lambda copy: copy.wait())

    @pl.when((step >= 1) & (step <= packs))
    def _():
        padded[...] = jnp.zeros_like(padded)

        @pl.when(step <= glob)
        def _():
            padded[pl.ds(0, xg_ref.shape[1]), :] = as_float(xg_ref[0])

        @pl.when(step > glob)
        def _():
            for k in range(xl_ref.shape[0]):
                padded[pl.ds(k * grids[1][3], xl_ref.shape[1]), :] = as_float(xl_ref[k])

        inputs = padded[...]
        x_ref[...] = inputs.astype(jnp.bfloat16)
        unit, _ = unit_rows(inputs)
        normed = (unit * vec(V_LN1G) + vec(V_LN1B)).astype(jnp.bfloat16)
        normed_ref[...] = normed
        qkv_ref[:, pl.ds(0, features)] = (dot(normed, wqkv[:, pl.ds(0, features)]) + vec(V_QB)).astype(jnp.bfloat16)
        qkv_ref[:, pl.ds(features, features)] = dot(normed, wqkv[:, pl.ds(features, features)]).astype(jnp.bfloat16)
        qkv_ref[:, pl.ds(2 * features, features)] = (
            dot(normed, wqkv[:, pl.ds(2 * features, features)]) + vec(V_VB)
        ).astype(jnp.bfloat16)
        kind = jnp.where(step <= glob, 0, 1)
        for pair in range(heads // 2):
            at = 2 * width * pair
            queries = stack_heads(qkv_ref[:, pl.ds(at, 2 * width)], width)
            keys = qkv_ref[:, pl.ds(features + at, 2 * width)]
            values = qkv_ref[:, pl.ds(2 * features + at, 2 * width)]
            part = bias[kind, pl.ds(2 * pair, 2), :, pl.ds(0, seq)].reshape(2 * seq, seq)
            scores = dot_nt(queries, keys) * (width**-0.5) + part
            weights = jnp.exp(scores - jnp.max(scores, axis=-1, keepdims=True))
            probs = (weights * (1.0 / jnp.sum(weights, axis=-1, keepdims=True))).astype(jnp.bfloat16)
            probs_ref[0, pair] = probs
            mixed_ref[:, pl.ds(at, 2 * width)] = merge_heads(dot(probs, values), width).astype(jnp.bfloat16)

        attn = dot(mixed_ref[...], wproj[...]) + vec(V_PB)
        attn_ref[...] = attn.astype(jnp.bfloat16)
        resid_ref[...] = inputs + vec(V_G1) * attn

    for k, items in GATHER_LATER.items():
        @pl.when(step == k)
        def _():
            for t, s in items:
                flows[t].stage(s)

    @pl.when(step == packs + 1)
    def _():
        for flow in flows:
            flow.drain()


def attend_front(xg, xl, smalls, shards, indices, packs, heads, grids, seq, table_rows):
    glob, glob_len, features = xg.shape
    loc, loc_len, _ = xl.shape
    per_pack = loc // (packs - glob)
    rows, lanes = packs * seq, round_up(seq, 128)
    hidden = shards[2].shape[1]
    whole = lambda shape: pl.BlockSpec(shape, lambda s: (0,) * len(shape), pipeline_mode=pl.Buffered(1))
    at = lambda s: jnp.clip(s - 1, 0, packs - 1)
    by_rows = lambda cols: pl.BlockSpec((seq, cols), lambda s: (at(s), 0))
    any_ref = pl.BlockSpec(memory_space=pl.ANY)
    owns = list(smalls) + list(shards)
    return pl.pallas_call(
        functools.partial(front_kernel, (packs, glob, heads, grids)),
        grid=(packs + 2,),
        out_shape=[
            jax.ShapeDtypeStruct((rows, features), jnp.bfloat16),
            jax.ShapeDtypeStruct((rows, features), jnp.bfloat16),
            jax.ShapeDtypeStruct((rows, 3 * features), jnp.bfloat16),
            jax.ShapeDtypeStruct((packs, heads // 2, 2 * seq, seq), jnp.bfloat16),
            jax.ShapeDtypeStruct((rows, features), jnp.bfloat16),
            jax.ShapeDtypeStruct((rows, features), jnp.bfloat16),
            jax.ShapeDtypeStruct((rows, features), jnp.float32),
            jax.ShapeDtypeStruct((16, features), jnp.float32),
            jax.ShapeDtypeStruct((1, hidden), jnp.float32),
        ]
        + [jax.ShapeDtypeStruct(GRID + s.shape, s.dtype) for s in shards],
        in_specs=[
            pl.BlockSpec((1, glob_len, features), lambda s: (jnp.minimum(at(s), glob - 1), 0, 0)),
            pl.BlockSpec((per_pack, loc_len, features), lambda s: (jnp.maximum(at(s) - glob, 0), 0, 0)),
        ]
        + [whole(o.shape) for o in owns]
        + [whole(i.shape) for i in indices],
        out_specs=[
            by_rows(features),
            by_rows(features),
            by_rows(3 * features),
            pl.BlockSpec((1, heads // 2, 2 * seq, seq), lambda s: (at(s), 0, 0, 0)),
            by_rows(features),
            by_rows(features),
            by_rows(features),
            whole((16, features)),
            whole((1, hidden)),
        ]
        + [any_ref] * 4,
        scratch_shapes=[
            pltpu.VMEM((16, table_rows), jnp.float32),
            pltpu.VMEM((2, heads, seq, lanes), jnp.float32),
            pltpu.VMEM((2, heads, ROW_SLOTS, lanes), jnp.float32),
            pltpu.VMEM((2, heads, ROW_SLOTS, lanes), jnp.float32),
            pltpu.VMEM((seq, features), jnp.float32),
            pltpu.VMEM((features, 3 * features), jnp.bfloat16),
            pltpu.VMEM((features, features), jnp.bfloat16),
            pltpu.VMEM(SMALL, jnp.float32),
            pltpu.VMEM(GRID + SMALL, jnp.float32),
            pltpu.VMEM((8, lanes), jnp.int32),
            pltpu.VMEM((8, lanes), jnp.int32),
            pltpu.SemaphoreType.DMA((2, LINE * 8)),
            pltpu.SemaphoreType.DMA((len(shards) + 3, Gather.SEMS + 1)),
            pltpu.SemaphoreType.DMA((len(shards) + 3, Gather.SEMS + 1)),
        ],
        compiler_params=pltpu.CompilerParams(vmem_limit_bytes=BIG, collective_id=0, has_side_effects=True),
        name="attend_front",
    )(xg, xl, *owns, *indices)


def gather_params(vectors, hidden_shift, table, weights):
    whole = lambda v: lax.all_gather(v, "fsdp", axis=0, tiled=True)
    return ([as_float(whole(v)) for v in vectors], as_float(whole(hidden_shift)), as_float(whole(table)), [whole(w) for w in weights])


def scatter_grads(vectors, hidden_shift, table, weights):
    share = lambda v: lax.psum_scatter(as_float(v), "fsdp", scatter_dimension=0, tiled=True)
    return ([share(v) for v in vectors], share(hidden_shift), share(table), [share(w) for w in weights])


def slot_rows(values, slot, seq):
    crops, length, features = values.shape
    per_pack = seq // slot
    values = jnp.pad(values, ((0, 0), (0, slot - length), (0, 0)))
    values = values.reshape(crops // per_pack, per_pack * slot, features)
    return jnp.pad(values, ((0, 0), (0, seq - per_pack * slot), (0, 0)))


def crop_rows(packed, slot, crops, length):
    packs, seq, features = packed.shape
    per_pack = seq // slot
    return packed[:, : per_pack * slot].reshape(crops, slot, features)[:, :length]


def per_device(
    x_global, x_local, cot_global, cot_local, global_count, local_count, index_global, index_local,
    ln1_gain, ln1_bias, qkv_weight, q_bias, v_bias, proj_weight, proj_bias, gamma1, bias_table,
    ln2_gain, ln2_bias, fc1_weight, fc1_bias, fc2_weight, fc2_bias, gamma2,
):
    glob, glob_len, features = x_global.shape
    loc, loc_len = x_local.shape[:2]
    heads = bias_table.shape[1]
    seq = round_up(glob_len, 16)
    slot = round_up(loc_len, 8)
    per_pack = seq // slot
    packs = glob + loc // per_pack
    devices = lax.axis_size("fsdp")
    vector_args = [ln1_gain, ln1_bias, q_bias, v_bias, proj_bias, gamma1, ln2_gain, ln2_bias, fc2_bias, gamma2]
    weights = [qkv_weight, proj_weight, fc1_weight, fc2_weight]
    table_rows = bias_table.shape[0] * devices
    indices = (index_global, index_local)
    sides = (math.isqrt(glob_len - 1), math.isqrt(loc_len - 1))
    grids = ((sides[0], glob_len, 1, seq), (sides[1], loc_len, per_pack, slot))

    rows_of = lambda g, l: jnp.concatenate([slot_rows(g, seq, seq), slot_rows(l, slot, seq)]).reshape(-1, features)
    if devices == 32:
        x, normed, qkv, probs, mixed, attn, resid, vectors, hidden_row, *full = attend_front(
            x_global, x_local, (jnp.stack(vector_args), fc1_bias[None], bias_table.T), weights, indices, packs, heads, grids, seq,
            table_rows,
        )
        qkv_full, proj_full, fc1_full, fc2_full = [f.reshape(devices * f.shape[4], f.shape[5]) for f in full]
        lanes = round_up(seq, 128)
    else:
        small_full, hidden_full, table_full, (qkv_full, proj_full, fc1_full, fc2_full) = gather_params(
            vector_args, fc1_bias, bias_table, weights
        )
        vectors = jnp.pad(jnp.stack(small_full), ((0, 6), (0, 0)))
        hidden_row = hidden_full[None]
        table = jnp.pad(table_full.T, ((0, round_up(heads, 16) - heads), (0, 0))).astype(jnp.bfloat16)
        x = rows_of(x_global, x_local)
        bias = expand_bias(table, indices, grids, heads, seq)
        lanes = bias.shape[-1]
        normed, qkv, probs, mixed, attn, resid = attend_forward(
            x, qkv_full, proj_full, vectors, bias, packs, glob, heads
        )
    out_global, out_local, gres, gfc1, gfc2, gfc1_shift, small_two, *early = mlp_both(
        global_count, local_count, resid, cot_global, cot_local, vectors, fc1_full, hidden_row, fc2_full, seq, slot,
        x_global.dtype, jnp.bfloat16, 2 if devices == 32 else 0,
    )
    if devices == 32:
        shaped = lambda g: g.reshape(GRID + (g.shape[0] // devices, g.shape[1]))
        gx_global, gx_local, *shares, small = attend_back(
            x, normed, qkv, probs, mixed, attn, gres, qkv_full, proj_full, vectors, small_two, gfc1_shift, indices,
            shaped(gfc1), shaped(gfc2), packs, glob, heads, grids, table_rows, x_global.dtype, lanes,
        )
        shares[2] = jnp.concatenate(early + [shares[2]], axis=1)
        sums = [small[k, : features // devices] for k in range(10)]
        hidden_sum = small[10, : fc1_bias.shape[0]]
        table_sum = small[:heads, 128 : 128 + table_rows // devices].T
    else:
        gx, gqkv, gproj, bias_sums, small_one, gqkv_shift = attend_backward(
            x, normed, qkv, probs, mixed, attn, gres, qkv_full, proj_full, vectors, packs, glob, heads,
            x_global.dtype, jnp.bfloat16, lanes,
        )
        gx = gx.reshape(packs, seq, features)
        gx_global, gx_local = crop_rows(gx[:glob], seq, glob, glob_len), crop_rows(gx[glob:], slot, loc, loc_len)
        gtable = collect_bias(bias_sums, indices, grids, table_rows).T
        vector_grads = [
            small_one[0], small_one[1], gqkv_shift[0, :features], gqkv_shift[0, 2 * features :], small_one[2],
            small_one[3], small_two[0], small_two[1], small_two[2], small_two[3],
        ]
        sums, hidden_sum, table_sum, shares = scatter_grads(
            vector_grads, gfc1_shift[0], gtable, [gqkv, gproj, gfc1, gfc2]
        )
    return (
        out_global, out_local, gx_global, gx_local,
        sums[0], sums[1], shares[0], sums[2], sums[3], shares[1], sums[4], sums[5], table_sum,
        sums[6], sums[7], shares[2], hidden_sum, shares[3], sums[8], sums[9],
    )


def solution(mesh):
    placed = (
        P("fsdp", None, None),
        P("fsdp", None, None),
        P("fsdp", None, None),
        P("fsdp", None, None),
        P("fsdp"),
        P("fsdp"),
        P(),
        P(),
        P("fsdp"),
        P("fsdp"),
        P("fsdp", None),
        P("fsdp"),
        P("fsdp"),
        P("fsdp", None),
        P("fsdp"),
        P("fsdp"),
        P("fsdp", None),
        P("fsdp"),
        P("fsdp"),
        P("fsdp", None),
        P("fsdp"),
        P("fsdp", None),
        P("fsdp"),
        P("fsdp"),
    )
    return jax.shard_map(
        per_device,
        mesh=mesh,
        in_specs=placed,
        out_specs=(
            P("fsdp", None, None),
            P("fsdp", None, None),
            P("fsdp", None, None),
            P("fsdp", None, None),
            P("fsdp"),
            P("fsdp"),
            P("fsdp", None),
            P("fsdp"),
            P("fsdp"),
            P("fsdp", None),
            P("fsdp"),
            P("fsdp"),
            P("fsdp", None),
            P("fsdp"),
            P("fsdp"),
            P("fsdp", None),
            P("fsdp"),
            P("fsdp", None),
            P("fsdp"),
            P("fsdp"),
        ),
        check_vma=False,
    )
```

```python
import functools
import math

import jax
import jax.numpy as jnp
from jax import lax
from jax.experimental import pallas as pl
from jax.experimental.pallas import tpu as pltpu
from jax.sharding import PartitionSpec as P

EPSILON = 1e-06
NEG = -1e30
ROWS_IN = (((0,), (0,)), ((), ()))
COLS_IN = (((1,), (1,)), ((), ()))
BIG = 60 * 1024 * 1024


def as_float(values):
    return values.astype(jnp.float32)


def dot(a, b):
    return jnp.dot(a, b, preferred_element_type=jnp.float32)


def dot_tn(a, b):
    return lax.dot_general(a, b, ROWS_IN, preferred_element_type=jnp.float32)


def dot_nt(a, b):
    return lax.dot_general(a, b, COLS_IN, preferred_element_type=jnp.float32)


def round_up(value, unit):
    return (value + unit - 1) // unit * unit


def unit_rows(values):
    average = jnp.mean(values, axis=-1, keepdims=True)
    centered = values - average
    spread = lax.rsqrt(jnp.mean(centered * centered, axis=-1, keepdims=True) + EPSILON)
    return (centered * spread, spread)


def unit_back(grad, unit, spread):
    return spread * (
        grad - jnp.mean(grad, axis=-1, keepdims=True) - unit * jnp.mean(grad * unit, axis=-1, keepdims=True)
    )


def column_sum(values):
    return jnp.sum(values, axis=0, keepdims=True)


V_LN1G, V_LN1B, V_QB, V_VB, V_PB, V_G1, V_LN2G, V_LN2B, V_FB, V_G2 = range(10)


MLP_PLAN = {
    (0, "end"): ((0, 0),), (1, 0): ((0, 1),), (1, 2): ((0, 2),), (1, "end"): ((0, 3), (1, 0)), (2, 0): ((1, 1),),
    (2, 1): ((0, 4),), (2, 2): ((1, 2),), (2, "end"): ((1, 3),), (2, "last"): ((1, 4),),
}


def fill_terms(ref, value):
    count = ref.shape[-2]
    for d in range(LINE * 8):
        ref[d // 8, d // 4 % 2, d // 2 % 2, d % 2] = value[d * count : (d + 1) * count].astype(ref.dtype)


def put(ref):
    def finish(value):
        ref[...] = value

    return finish


def mlp_kernel(
    steps, blocks, seq, slot, shared, gcount_ref, lcount_ref, resid_ref, cg_ref, cl_ref, vec_ref, w1_ref, b1_ref, w2_ref,
    outg_ref, outl_ref, gres_ref, gw1_ref, gw2_ref, gb1_ref, small_ref, *rest,
):
    step = pl.program_id(0)
    flows = []
    if shared:
        share_ref, *rest = rest
        send, recv = rest[-2:]
        terms, bufs = rest[7 : 7 + shared], rest[7 + shared : -2]
        wide = w1_ref.shape[1]
        for t in range(shared):
            pieces = bufs[Scatter.BUFS * t : Scatter.BUFS * (t + 1)]
            finish = put(share_ref.at[EVERY, pl.ds(t * wide, wide)])
            flows.append(Scatter(terms[t], None, pieces, send.at[t], recv.at[t], finish))
    cot, normed, gbranch, branch, gnorm, active, ghidden = rest[:7]

    def slot_at(where):
        for (s, at), items in MLP_PLAN.items() if shared else ():
            if at == where if isinstance(where, str) else isinstance(at, int):
                @pl.when((step == s) if isinstance(where, str) else ((step == s) & (where == at)))
                def _():
                    for t, n in items:
                        flows[t].stage(n)

    rows, features = resid_ref.shape
    size = rows // blocks
    vec = lambda k: vec_ref[pl.ds(k, 1), :]
    glob, glob_len, _ = cg_ref.shape
    loc, loc_len, _ = cl_ref.shape
    per_pack = seq // slot
    packs = glob + loc // per_pack

    def kept(k, count_ref):
        return jnp.where(k < count_ref[0], 1.0, 0.0)

    @pl.when(step == 0)
    def _():
        if shared:
            greet()
        cot[...] = jnp.zeros_like(cot)

        @pl.loop(0, glob)
        def _(p):
            rows_of = pl.ds(pl.multiple_of(p * seq, seq), glob_len)
            cot[rows_of, :] = (as_float(cg_ref[p]) * kept(p, gcount_ref)).astype(jnp.bfloat16)

        @pl.loop(0, packs - glob)
        def _(p):
            for k in range(per_pack):
                crop = p * per_pack + k
                rows_of = pl.ds(pl.multiple_of((glob + p) * seq + k * slot, 8), loc_len)
                cot[rows_of, :] = (as_float(cl_ref[crop]) * kept(crop, lcount_ref)).astype(jnp.bfloat16)

        @pl.loop(0, blocks)
        def _(i):
            part = pl.ds(pl.multiple_of(i * size, size), size)
            unit, _ = unit_rows(resid_ref[part, :])
            normed[part, :] = (unit * vec(V_LN2G) + vec(V_LN2B)).astype(jnp.bfloat16)
            gbranch[part, :] = (vec(V_G2) * as_float(cot[part, :])).astype(jnp.bfloat16)

    w1, w2 = w1_ref[...], w2_ref[...]

    def block(i, hidden_sum):
        part = pl.ds(pl.multiple_of(i * size, size), size)
        hidden = dot(normed[part, :], w1) + b1_ref[...]
        phi = 0.5 * lax.erf(hidden * (0.5**0.5)) + 0.5
        low = (hidden * phi).astype(jnp.bfloat16)
        active[part, :] = low
        slope = phi + hidden * (jnp.exp(hidden * hidden * -0.5) * 0.3989422804014327)
        add = dot(low, w2)
        grad = dot_nt(gbranch[part, :], w2) * slope
        glow = grad.astype(jnp.bfloat16)
        ghidden[part, :] = glow
        gadd = dot_nt(glow, w1)

        @pl.when(step == 0)
        def _():
            branch[part, :] = add
            gnorm[part, :] = gadd

        @pl.when(step > 0)
        def _():
            branch[part, :] = branch[part, :] + add
            gnorm[part, :] = gnorm[part, :] + gadd

        slot_at(i)
        return hidden_sum + column_sum(as_float(glow))

    gb1_ref[...] = lax.fori_loop(0, blocks, block, jnp.zeros(gb1_ref.shape, jnp.float32))
    gw2_ref[...] = dot_tn(active[...], gbranch[...]).astype(gw2_ref.dtype)
    for t in range(shared):
        @pl.when(step == t)
        def _():
            fill_terms(terms[t], dot_tn(normed[...], ghidden[...]))

    @pl.when(step >= shared)
    def _():
        gw1_ref[...] = dot_tn(normed[...], ghidden[...]).astype(gw1_ref.dtype)

    slot_at("end")

    @pl.when(step == steps - 1)
    def _():
        zero = jnp.zeros((1, features), jnp.float32)

        def pack(p, sums, write):
            part = pl.ds(pl.multiple_of(p * seq, seq), seq)
            resid = resid_ref[part, :]
            full = branch[part, :] + vec(V_FB)
            write(p, resid + vec(V_G2) * full)
            grad = as_float(cot[part, :])
            unit, spread = unit_rows(resid)
            gn = gnorm[part, :]
            gres_ref[part, :] = grad + unit_back(gn * vec(V_LN2G), unit, spread)
            return (
                sums[0] + column_sum(gn * unit),
                sums[1] + column_sum(gn),
                sums[2] + column_sum(as_float(gbranch[part, :])),
                sums[3] + column_sum(grad * full),
            )

        def write_glob(p, value):
            outg_ref[p] = (value[:glob_len] * kept(p, gcount_ref)).astype(outg_ref.dtype)

        def write_loc(p, value):
            for k in range(per_pack):
                crop = (p - glob) * per_pack + k
                piece = value[k * slot : k * slot + loc_len] * kept(crop, lcount_ref)
                outl_ref[crop] = piece.astype(outl_ref.dtype)

        sums = lax.fori_loop(0, glob, lambda p, s: pack(p, s, write_glob), (zero,) * 4)
        sums = lax.fori_loop(glob, packs, lambda p, s: pack(p, s, write_loc), sums)
        small_ref[...] = jnp.zeros_like(small_ref)
        for k in range(4):
            small_ref[pl.ds(k, 1), :] = sums[k]

    slot_at("last")

    if shared:
        @pl.when(step == steps - 1)
        def _():
            for flow in flows:
                flow.drain()


def mlp_both(gcount, lcount, resid, cg, cl, vectors, w1, b1, w2, seq, slot, out_dtype, grad_dtype, shared):
    rows, features = resid.shape
    hidden = w1.shape[1]
    chunk = 1024
    steps = hidden // chunk
    whole = lambda shape: pl.BlockSpec(shape, lambda j: (0,) * len(shape), pipeline_mode=pl.Buffered(1))
    scalar = pl.BlockSpec(memory_space=pltpu.SMEM)
    shares, extra, params = [], [], {}
    if shared:
        share = (features // (LINE * 8), chunk)
        shares = [jax.ShapeDtypeStruct((share[0], shared * chunk), jnp.float32)]
        extra = [pltpu.VMEM(GRID + share, jnp.bfloat16)] * shared
        extra += Scatter.scratch(share, jnp.bfloat16) * shared
        extra += [pltpu.SemaphoreType.DMA((shared, Scatter.SEMS))] * 2
        params = dict(collective_id=2, has_side_effects=True)
    return pl.pallas_call(
        functools.partial(mlp_kernel, steps, 3, seq, slot, shared),
        grid=(steps,),
        out_shape=[
            jax.ShapeDtypeStruct(cg.shape, out_dtype),
            jax.ShapeDtypeStruct(cl.shape, out_dtype),
            jax.ShapeDtypeStruct((rows, features), jnp.float32),
            jax.ShapeDtypeStruct((features, hidden - shared * chunk), grad_dtype),
            jax.ShapeDtypeStruct((hidden, features), grad_dtype),
            jax.ShapeDtypeStruct((1, hidden), jnp.float32),
            jax.ShapeDtypeStruct((8, features), jnp.float32),
        ]
        + shares,
        in_specs=[
            scalar,
            scalar,
            whole((rows, features)),
            whole(cg.shape),
            whole(cl.shape),
            whole(vectors.shape),
            pl.BlockSpec((features, chunk), lambda j: (0, j)),
            pl.BlockSpec((1, chunk), lambda j: (0, j)),
            pl.BlockSpec((chunk, features), lambda j: (j, 0)),
        ],
        out_specs=[
            whole(cg.shape),
            whole(cl.shape),
            whole((rows, features)),
            pl.BlockSpec((features, chunk), lambda j: (0, jnp.maximum(j - shared, 0))),
            pl.BlockSpec((chunk, features), lambda j: (j, 0)),
            pl.BlockSpec((1, chunk), lambda j: (0, j)),
            whole((8, features)),
        ]
        + [whole(s.shape) for s in shares],
        scratch_shapes=[
            pltpu.VMEM((rows, features), jnp.bfloat16),
            pltpu.VMEM((rows, features), jnp.bfloat16),
            pltpu.VMEM((rows, features), jnp.bfloat16),
            pltpu.VMEM((rows, features), jnp.float32),
            pltpu.VMEM((rows, features), jnp.float32),
            pltpu.VMEM((rows, chunk), jnp.bfloat16),
            pltpu.VMEM((rows, chunk), jnp.bfloat16),
        ]
        + extra,
        compiler_params=pltpu.CompilerParams(vmem_limit_bytes=BIG, **params),
        name="mlp_both",
    )(gcount, lcount, resid, cg, cl, vectors, w1, b1, w2)


def lane_of(shape):
    return lax.broadcasted_iota(jnp.int32, shape, 1)


def roll_lanes(values, shift):
    shift = shift % values.shape[1]
    return pltpu.roll(values, shift, 1) if shift else values


def corner_rows(side):
    return (1, side, 1 + (side - 1) * side, side * side)


def expand(grids, table_ref, index_refs, bias_refs, row_refs):
    for n, (side, seq, copies, slot) in enumerate(grids):
        index_ref, bias_ref, row_ref = index_refs[n], bias_refs[n], row_refs[n]
        heads, lanes = bias_ref.shape[0], bias_ref.shape[2]
        tables = lax.broadcasted_iota(jnp.int32, (table_ref.shape[1], lanes), 0)

        def pick(row):
            picked = index_ref[pl.ds(row, 1), :] == tables
            return dot(table_ref[...].astype(jnp.bfloat16), picked.astype(jnp.bfloat16))

        corners = [pick(k) for k in range(4)]
        lane = lane_of(corners[0].shape)
        within = (lane + (side - 1)) % side
        for c in range(side):
            for top in range(2):
                left, right = corners[2 * top], corners[2 * top + 1]
                row = jnp.where(within >= c, roll_lanes(left, c), roll_lanes(right, c - (side - 1)))
                row = jnp.where(lane == 0, left, row)
                row_ref[top, :, pl.ds(c, 1), :] = row[:heads].reshape(heads, 1, lanes)
        row_ref[0, :, pl.ds(side, 1), :] = pick(4)[:heads].reshape(heads, 1, lanes)
        lane = lane_of((side, lanes))

        def spread(values, at):
            if copies > 1:
                values = roll_lanes(values, at * slot)
            where = lane_of(values.shape) - at * slot
            return jnp.where((where >= 0) & (where < seq), values, NEG)

        @pl.loop(0, heads)
        def _(h):
            bias_ref[h] = jnp.full(bias_ref.shape[1:], NEG, jnp.float32)
            low, high, first = row_ref[0, h, :side], row_ref[1, h, :side], row_ref[0, h, pl.ds(side, 1)]
            for at in range(copies):
                bias_ref[h, pl.ds(at * slot, 1), :] = spread(first, at)
            for r in range(side):
                rows = jnp.where(
                    lane - 1 < side * (r + 1), roll_lanes(high, -side * (side - 1 - r)), roll_lanes(low, side * r)
                )
                rows = jnp.where(lane == 0, low, rows)
                for at in range(copies):
                    bias_ref[h, pl.ds(at * slot + 1 + side * r, side), :] = spread(rows, at)


def collect(grids, sum_refs, index_refs, row_refs, shape):
    total = jnp.zeros(shape, jnp.float32)
    for n, (side, seq, copies, slot) in enumerate(grids):
        index_ref, sum_ref, row_ref = index_refs[n], sum_refs[n], row_refs[n]
        heads, lanes = sum_ref.shape[0], sum_ref.shape[2]
        lane = lane_of((side, lanes))

        def gathered(h, start, size):
            rows = None
            for at in range(copies):
                piece = roll_lanes(sum_ref[h, pl.ds(at * slot + start, size), :], -at * slot)
                rows = piece if rows is None else rows + piece
            return jnp.where(lane_of((size, lanes)) < seq, rows, 0.0) if copies > 1 else rows

        @pl.loop(0, heads)
        def _(h):
            low = jnp.zeros((side, lanes), jnp.float32)
            high = jnp.zeros((side, lanes), jnp.float32)
            for r in range(side):
                rows = gathered(h, 1 + side * r, side)
                is_low = lane - 1 >= side * (r + 1)
                is_high = (lane >= 1) & (lane - 1 < side * (r + 1))
                low = low + roll_lanes(jnp.where(is_low, rows, 0.0), -side * r) + jnp.where(lane == 0, rows, 0.0)
                high = high + roll_lanes(jnp.where(is_high, rows, 0.0), side * (side - 1 - r))
            row_ref[0, h, :side], row_ref[1, h, :side] = low, high
            row_ref[0, h, pl.ds(side, 1)] = gathered(h, 0, 1)

        flat = lane_of((heads, lanes))
        within = (flat + (side - 1)) % side
        corners = [jnp.zeros((heads, lanes), jnp.float32) for _ in range(4)]
        for c in range(side):
            for top in range(2):
                row = row_ref[top, :, pl.ds(c, 1), :].reshape(heads, lanes)
                is_left = (flat >= 1) & (within >= c)
                is_right = (flat >= 1) & (within < c)
                left = roll_lanes(jnp.where(is_left, row, 0.0), -c) + jnp.where(flat == 0, row, 0.0)
                corners[2 * top] = corners[2 * top] + left
                corners[2 * top + 1] = corners[2 * top + 1] + roll_lanes(jnp.where(is_right, row, 0.0), side - 1 - c)
        tables = lax.broadcasted_iota(jnp.int32, (shape[1], lanes), 0)

        def place_sum(row, values):
            picked = (index_ref[pl.ds(row, 1), :] == tables).astype(jnp.bfloat16)
            top = values.astype(jnp.bfloat16)
            rest = values - as_float(top)
            middle = rest.astype(jnp.bfloat16)
            last = (rest - as_float(middle)).astype(jnp.bfloat16)
            return dot_nt(top, picked) + dot_nt(middle, picked) + dot_nt(last, picked)

        for k, values in enumerate(corners):
            total = total + place_sum(k, values)
        total = total + place_sum(4, row_ref[0, :, pl.ds(side, 1), :].reshape(heads, lanes))
    return total


ROW_SLOTS = 16


def expand_kernel(grids, table_ref, index_g, index_l, bias_ref, rows_g, rows_l):
    expand(grids, table_ref, (index_g, index_l), (bias_ref.at[0], bias_ref.at[1]), (rows_g, rows_l))


def pad_index(indices, lanes):
    picked = []
    for index in indices:
        rows = corner_rows(math.isqrt(index.shape[0] - 1)) + (0,)
        rows = jnp.concatenate([index[r : r + 1] for r in rows])
        picked.append(jnp.pad(rows, ((0, 8 - len(rows)), (0, lanes - index.shape[1])), constant_values=-1))
    return picked


def expand_bias(table, indices, grids, heads, seq):
    lanes = round_up(seq, 128)
    return pl.pallas_call(
        functools.partial(expand_kernel, grids),
        out_shape=jax.ShapeDtypeStruct((2, heads, seq, lanes), jnp.float32),
        scratch_shapes=[pltpu.VMEM((2, heads, ROW_SLOTS, lanes), jnp.float32)] * 2,
        compiler_params=pltpu.CompilerParams(vmem_limit_bytes=BIG),
        name="expand_bias",
    )(table, *pad_index(indices, lanes))


def collect_kernel(grids, index_g, index_l, sums_ref, grad_ref, rows_g, rows_l):
    grad_ref[...] = collect(
        grids, (sums_ref.at[0], sums_ref.at[1]), (index_g, index_l), (rows_g, rows_l), grad_ref.shape
    )


def collect_bias(sums, indices, grids, table_rows):
    _, heads, _, lanes = sums.shape
    return pl.pallas_call(
        functools.partial(collect_kernel, grids),
        out_shape=jax.ShapeDtypeStruct((heads, table_rows), jnp.float32),
        scratch_shapes=[pltpu.VMEM((2, heads, ROW_SLOTS, lanes), jnp.float32)] * 2,
        compiler_params=pltpu.CompilerParams(vmem_limit_bytes=BIG),
        name="collect_bias",
    )(*pad_index(indices, lanes), sums)


def head_lanes(shape, width):
    return lax.broadcasted_iota(jnp.int32, shape, 1) < width


def stack_heads(pair, width):
    first = head_lanes(pair.shape, width)
    zero = jnp.zeros_like(pair)
    return jnp.concatenate([jnp.where(first, pair, zero), jnp.where(first, zero, pair)], axis=0)


def merge_heads(stacked, width):
    rows = stacked.shape[0] // 2
    top, low = stacked[:rows], stacked[rows:]
    return jnp.where(head_lanes(top.shape, width), top, low)


def attend_kernel(
    glob, heads, x_ref, wqkv_ref, wproj_ref, vec_ref, bias_ref,
    normed_ref, qkv_ref, probs_ref, mixed_ref, attn_ref, resid_ref,
):
    seq, features = x_ref.shape
    width = features // heads
    vec = lambda k: vec_ref[pl.ds(k, 1), :]
    inputs = as_float(x_ref[...])
    unit, _ = unit_rows(inputs)
    normed = (unit * vec(V_LN1G) + vec(V_LN1B)).astype(jnp.bfloat16)
    normed_ref[...] = normed
    qkv_ref[:, pl.ds(0, features)] = (dot(normed, wqkv_ref[:, pl.ds(0, features)]) + vec(V_QB)).astype(jnp.bfloat16)
    qkv_ref[:, pl.ds(features, features)] = dot(normed, wqkv_ref[:, pl.ds(features, features)]).astype(jnp.bfloat16)
    qkv_ref[:, pl.ds(2 * features, features)] = (
        dot(normed, wqkv_ref[:, pl.ds(2 * features, features)]) + vec(V_VB)
    ).astype(jnp.bfloat16)

    for pair in range(heads // 2):
        at = 2 * width * pair
        queries = stack_heads(qkv_ref[:, pl.ds(at, 2 * width)], width)
        keys = qkv_ref[:, pl.ds(features + at, 2 * width)]
        values = qkv_ref[:, pl.ds(2 * features + at, 2 * width)]
        bias = bias_ref[0, pl.ds(2 * pair, 2), :, pl.ds(0, seq)].reshape(2 * seq, seq)
        scores = dot_nt(queries, keys) * (width**-0.5) + bias
        weights = jnp.exp(scores - jnp.max(scores, axis=-1, keepdims=True))
        probs = (weights * (1.0 / jnp.sum(weights, axis=-1, keepdims=True))).astype(jnp.bfloat16)
        probs_ref[0, pair] = probs
        mixed_ref[:, pl.ds(at, 2 * width)] = merge_heads(dot(probs, values), width).astype(jnp.bfloat16)

    attn = dot(mixed_ref[...], wproj_ref[...]) + vec(V_PB)
    attn_ref[...] = attn.astype(jnp.bfloat16)
    resid_ref[...] = inputs + vec(V_G1) * attn


def attend_forward(x, wqkv, wproj, vectors, bias, packs, glob, heads):
    rows, features = x.shape
    seq = rows // packs
    whole = lambda shape: pl.BlockSpec(shape, lambda p: (0,) * len(shape), pipeline_mode=pl.Buffered(1))
    by_rows = lambda cols: pl.BlockSpec((seq, cols), lambda p: (p, 0))
    return pl.pallas_call(
        functools.partial(attend_kernel, glob, heads),
        grid=(packs,),
        out_shape=[
            jax.ShapeDtypeStruct((rows, features), jnp.bfloat16),
            jax.ShapeDtypeStruct((rows, 3 * features), jnp.bfloat16),
            jax.ShapeDtypeStruct((packs, heads // 2, 2 * seq, seq), jnp.bfloat16),
            jax.ShapeDtypeStruct((rows, features), jnp.bfloat16),
            jax.ShapeDtypeStruct((rows, features), jnp.bfloat16),
            jax.ShapeDtypeStruct((rows, features), jnp.float32),
        ],
        in_specs=[
            by_rows(features),
            whole(wqkv.shape),
            whole(wproj.shape),
            whole(vectors.shape),
            pl.BlockSpec((1,) + bias.shape[1:], lambda p: (jnp.where(p < glob, 0, 1), 0, 0, 0)),
        ],
        out_specs=[
            by_rows(features),
            by_rows(3 * features),
            pl.BlockSpec((1, heads // 2, 2 * seq, seq), lambda p: (p, 0, 0, 0)),
            by_rows(features),
            by_rows(features),
            by_rows(features),
        ],
        compiler_params=pltpu.CompilerParams(vmem_limit_bytes=BIG),
        name="attend_forward",
    )(x, wqkv, wproj, vectors, bias)


def attend_back_kernel(
    packs, glob, heads, chunk, x_ref, normed_ref, qkv_ref, probs_ref, mixed_ref, attn_ref, gres_ref, wqkv_ref, wproj_ref, vec_ref,
    gx_ref, gwqkv_ref, gwproj_ref, bsum_ref, small_ref, gqb_ref,
    normed_all, mixed_all, gattn_all, gqkv_all,
):
    step = pl.program_id(0)
    seq, features = x_ref.shape
    width = features // heads
    vec = lambda k: vec_ref[pl.ds(k, 1), :]
    rows = packs * seq

    @pl.when(step == 0)
    def _():
        small_ref[...] = jnp.zeros_like(small_ref)
        gqb_ref[...] = jnp.zeros_like(gqb_ref)

    @pl.when((step == 0) | (step == glob))
    def _():
        bsum_ref[...] = jnp.zeros_like(bsum_ref)

    @pl.when(step < packs)
    def _():
        part = pl.ds(pl.multiple_of(step * seq, seq), seq)
        gres = gres_ref[...]
        gattn = (vec(V_G1) * gres).astype(jnp.bfloat16)
        gattn_all[part, :] = gattn
        mixed_all[part, :] = mixed_ref[...]
        normed_all[part, :] = normed_ref[...]
        small_ref[pl.ds(2, 1), :] += column_sum(as_float(gattn))
        small_ref[pl.ds(3, 1), :] += column_sum(gres * as_float(attn_ref[...]))
        gmixed = dot_nt(gattn, wproj_ref[...]).astype(jnp.bfloat16)
        scale = width**-0.5
        for pair in range(heads // 2):
            at = 2 * width * pair
            queries = stack_heads(qkv_ref[:, pl.ds(at, 2 * width)], width)
            keys = qkv_ref[:, pl.ds(features + at, 2 * width)]
            values = qkv_ref[:, pl.ds(2 * features + at, 2 * width)]
            grads = stack_heads(gmixed[:, at : at + 2 * width], width)
            mixed = as_float(mixed_ref[:, pl.ds(at, 2 * width)])
            probs = probs_ref[0, pair]
            twice = jnp.concatenate([mixed, mixed], axis=0)
            inner = jnp.sum(as_float(grads) * twice, axis=-1, keepdims=True)
            gscores = as_float(probs) * (dot_nt(grads, values) - inner)
            bsum_ref[0, pl.ds(2 * pair, 2), :, pl.ds(0, seq)] += gscores.reshape(2, seq, seq)
            low = gscores.astype(jnp.bfloat16)
            gqkv_all[part, pl.ds(at, 2 * width)] = (merge_heads(dot(low, keys), width) * scale).astype(jnp.bfloat16)
            gqkv_all[part, pl.ds(features + at, 2 * width)] = (dot_tn(low, queries) * scale).astype(jnp.bfloat16)
            gqkv_all[part, pl.ds(2 * features + at, 2 * width)] = dot_tn(probs, grads).astype(jnp.bfloat16)
        gqkv = gqkv_all[part, :]
        gqb_ref[...] += column_sum(as_float(gqkv))
        gnorm = dot_nt(gqkv, wqkv_ref[...])
        unit, spread = unit_rows(as_float(x_ref[...]))
        small_ref[pl.ds(0, 1), :] += column_sum(gnorm * unit)
        small_ref[pl.ds(1, 1), :] += column_sum(gnorm)
        gx_ref[...] = (gres + unit_back(gnorm * vec(V_LN1G), unit, spread)).astype(gx_ref.dtype)

    @pl.when(step >= packs)
    def _():
        j = step - packs
        wide = 3 * features // chunk

        @pl.when(j < wide)
        def _():
            gwqkv_ref[...] = dot_tn(normed_all[...], gqkv_all[:, pl.ds(pl.multiple_of(j * chunk, chunk), chunk)]).astype(gwqkv_ref.dtype)

        @pl.when(j >= wide)
        def _():
            gwproj_ref[...] = dot_tn(mixed_all[...], gattn_all[:, pl.ds(pl.multiple_of((j - wide) * chunk, chunk), chunk)]).astype(gwproj_ref.dtype)


def attend_backward(x, normed, qkv, probs, mixed, attn, gres, wqkv, wproj, vectors, packs, glob, heads, out_dtype, grad_dtype, lanes):
    rows, features = x.shape
    seq = rows // packs
    chunk = 256
    wide, narrow = 3 * features // chunk, features // chunk
    whole = lambda shape: pl.BlockSpec(shape, lambda s: (0,) * len(shape), pipeline_mode=pl.Buffered(1))
    pack = lambda s: jnp.minimum(s, packs - 1)
    by_rows = lambda cols: pl.BlockSpec((seq, cols), lambda s: (pack(s), 0))
    return pl.pallas_call(
        functools.partial(attend_back_kernel, packs, glob, heads, chunk),
        grid=(packs + wide + narrow,),
        out_shape=[
            jax.ShapeDtypeStruct((rows, features), out_dtype),
            jax.ShapeDtypeStruct((features, 3 * features), grad_dtype),
            jax.ShapeDtypeStruct((features, features), grad_dtype),
            jax.ShapeDtypeStruct((2, heads, seq, lanes), jnp.float32),
            jax.ShapeDtypeStruct((8, features), jnp.float32),
            jax.ShapeDtypeStruct((1, 3 * features), jnp.float32),
        ],
        in_specs=[
            by_rows(features),
            by_rows(features),
            by_rows(3 * features),
            pl.BlockSpec((1, heads // 2, 2 * seq, seq), lambda s: (pack(s), 0, 0, 0)),
            by_rows(features),
            by_rows(features),
            by_rows(features),
            whole(wqkv.shape),
            whole(wproj.shape),
            whole(vectors.shape),
        ],
        out_specs=[
            by_rows(features),
            pl.BlockSpec((features, chunk), lambda s: (0, jnp.clip(s - packs, 0, wide - 1))),
            pl.BlockSpec((features, chunk), lambda s: (0, jnp.clip(s - packs - wide, 0, narrow - 1))),
            pl.BlockSpec((1, heads, seq, lanes), lambda s: (jnp.where(s < glob, 0, 1), 0, 0, 0)),
            whole((8, features)),
            whole((1, 3 * features)),
        ],
        scratch_shapes=[
            pltpu.VMEM((rows, features), jnp.bfloat16),
            pltpu.VMEM((rows, features), jnp.bfloat16),
            pltpu.VMEM((rows, features), jnp.bfloat16),
            pltpu.VMEM((rows, 3 * features), jnp.bfloat16),
        ],
        compiler_params=pltpu.CompilerParams(vmem_limit_bytes=BIG),
        name="attend_backward",
    )(x, normed, qkv, probs, mixed, attn, gres, wqkv, wproj, vectors)


MESH = pl.DeviceIdType.MESH
LINE = 4
GRID = (LINE, 2, 2, 2)
EVERY = slice(None)


def place():
    me = lax.axis_index("fsdp")
    return (me // 8, (me // 4) % 2, (me // 2) % 2, me % 2)


def device_at(z, y, x, c):
    return (((z * 2 + y) * 2 + x) * 2 + c,)


def along(z, k):
    return (z + k) % LINE


def greet():
    z, y, x, c = place()
    barrier = pltpu.get_barrier_semaphore()
    peers = [device_at(z, y, x, 1 - c), device_at(z, y, 1 - x, c), device_at(z, 1 - y, x, c)]
    peers += [device_at(along(z, k), y, x, c) for k in range(1, LINE)]
    for peer in peers:
        pl.semaphore_signal(barrier, inc=1, device_id=peer, device_id_type=MESH)
    pl.semaphore_wait(barrier, len(peers))


def remote(src, dst, send, recv, peer):
    return pltpu.make_async_remote_copy(
        src_ref=src, dst_ref=dst, send_sem=send, recv_sem=recv, device_id=peer, device_id_type=MESH
    )


class Gather:
    SEMS = 24

    def __init__(self, own, full, send, recv):
        self.own, self.full, self.send, self.recv = own, full, send, recv
        self.z, self.y, self.x, self.c = place()
        self.cols = full.shape[-1] // 2

    def half(self, ref, part, half):
        cols = (EVERY, pl.ds(half * self.cols, self.cols))
        return ref.at[part + cols]

    def line_copy(self, k, source=None):
        z, y, x, c = self.z, self.y, self.x, self.c
        held = z if source is None else source
        peer = device_at(along(z, k), y, x, c)
        return remote(self.own, self.full.at[held, y, x, c], self.send.at[k - 1], self.recv.at[k - 1], peer)

    def over(self, half, near):
        z, y, x, c = self.z, self.y, self.x, self.c
        return device_at(z, y, 1 - x, c) if (half == 0) == near else device_at(z, 1 - y, x, c)

    def first(self, half):
        z, y, x, c = self.z, self.y, self.x, self.c
        k = 3 + half
        return remote(
            self.half(self.own, (), half), self.half(self.full, (z, y, x, c), half), self.send.at[k], self.recv.at[k],
            self.over(half, True),
        )

    def hop(self, half, k, near):
        z, y, x, c = self.z, self.y, self.x, self.c
        held = along(z, LINE - k) if k else z
        if near:
            part, sem = (held, y, x, c), 7 + 3 * half + k - 1
        else:
            part = (held, y, EVERY, c) if half == 0 else (held, EVERY, x, c)
            sem = 13 + 3 * half + k - 1 if k else 5 + half
        ref = self.half(self.full, part, half)
        return remote(ref, ref, self.send.at[sem], self.recv.at[sem], self.over(half, near))

    def pair(self, k):
        z, y, x, c = self.z, self.y, self.x, self.c
        part, half = (
            ((EVERY, y, x, c), None),
            ((EVERY, y, 1 - x, c), 0),
            ((EVERY, 1 - y, x, c), 1),
            ((EVERY, 1 - y, EVERY, c), 0),
            ((EVERY, EVERY, 1 - x, c), 1),
        )[k]
        ref = self.full.at[part] if half is None else self.half(self.full, part, half)
        return remote(ref, ref, self.send.at[19 + k], self.recv.at[19 + k], device_at(z, y, x, 1 - c))

    def mine(self):
        return pltpu.make_async_copy(self.own, self.full.at[self.z, self.y, self.x, self.c], self.recv.at[self.SEMS])

    def stage(self, name):
        away = range(1, LINE)
        if name == "a":
            for k in away:
                self.line_copy(k).start()
            for half in range(2):
                self.first(half).start()
            self.mine().start()
        elif name == "n":
            self.mine().wait()
            for half in range(2):
                self.first(half).wait_recv()
                self.hop(half, 0, False).start()
        elif name == "z":
            for k in away:
                self.line_copy(k, along(self.z, LINE - k)).wait_recv()
                for half in range(2):
                    self.hop(half, k, True).start()
            self.pair(0).start()
        elif name == "f":
            for k in away:
                for half in range(2):
                    self.hop(half, k, True).wait_recv()
                    self.hop(half, k, False).start()
            self.pair(1).start()
            self.pair(2).start()
        elif name == "q":
            for half in range(2):
                for k in range(LINE):
                    self.hop(half, k, False).wait_recv()
                self.pair(3 + half).start()
        else:
            for k in range(5):
                self.pair(k).wait_recv()

    def drain(self):
        away = range(1, LINE)
        for k in away:
            self.line_copy(k).wait_send()
        for half in range(2):
            self.first(half).wait_send()
            self.hop(half, 0, False).wait_send()
            for k in away:
                self.hop(half, k, True).wait_send()
                self.hop(half, k, False).wait_send()
        for k in range(5):
            self.pair(k).wait_send()


class Scatter:
    STAGES = 5
    SEMS = 9

    def __init__(self, terms, own, bufs, send, recv, finish):
        self.terms, self.loaded = terms, own
        self.pairbuf, self.buf1a, self.buf1b, self.buf2a, self.buf2b, self.line = bufs
        self.send, self.recv, self.finish = send, recv, finish
        self.z, self.y, self.x, self.c = place()
        self.cols = terms.shape[-1] // 2

    BUFS = 6

    @staticmethod
    def scratch(shape, dtype):
        rows, cols = shape
        half = cols // 2
        return [
            pltpu.VMEM((LINE, 2, 2, rows, cols), dtype),
            pltpu.VMEM((LINE, 2, rows, half), dtype),
            pltpu.VMEM((LINE, 2, rows, half), dtype),
            pltpu.VMEM((LINE, rows, half), dtype),
            pltpu.VMEM((LINE, rows, half), dtype),
            pltpu.VMEM((LINE - 1, rows, cols), dtype),
        ]

    def at(self, i, j, k, half=None):
        cols = () if half is None else (EVERY, pl.ds(half * self.cols, self.cols))
        if self.loaded is None:
            return self.terms.at[(i, j, k, self.c) + cols]
        return self.loaded.at[(i, j, k) + cols]

    def load(self):
        return pltpu.make_async_copy(self.terms.at[EVERY, EVERY, EVERY, self.c], self.loaded, self.send.at[8])

    def copy(self, name):
        z, y, x, c = self.z, self.y, self.x, self.c
        over_x, over_y = device_at(z, y, 1 - x, c), device_at(z, 1 - y, x, c)
        k, src, dst, peer = {
            "pair": lambda: (0, self.terms.at[EVERY, EVERY, EVERY, 1 - c], self.pairbuf, device_at(z, y, x, 1 - c)),
            "1a": lambda: (1, self.at(EVERY, 1 - y, EVERY, 0), self.buf1a, over_y),
            "1b": lambda: (2, self.at(EVERY, EVERY, 1 - x, 1), self.buf1b, over_x),
            "2a": lambda: (3, self.at(EVERY, y, 1 - x, 0), self.buf2a, over_x),
            "2b": lambda: (4, self.at(EVERY, 1 - y, x, 1), self.buf2b, over_y),
        }[name]()
        return remote(src, dst, self.send.at[k], self.recv.at[k], peer)

    def line_copy(self, k):
        z, y, x, c = self.z, self.y, self.x, self.c
        target = along(z, k)
        return remote(
            self.at(target, y, x), self.line.at[k - 1], self.send.at[4 + k], self.recv.at[4 + k], device_at(target, y, x, c)
        )

    def add(self, ref, term):
        ref[...] = ref[...] + term

    def stage(self, s):
        z, y, x = self.z, self.y, self.x
        if s == 0:
            self.copy("pair").start()
            if self.loaded is not None:
                self.load().start()
        elif s == 1:
            if self.loaded is not None:
                self.load().wait()
            self.copy("pair").wait_recv()

            @pl.loop(0, LINE)
            def _(i):
                for j in range(2):
                    for k in range(2):
                        self.add(self.at(i, j, k), self.pairbuf[i, j, k])

            self.copy("1a").start()
            self.copy("1b").start()
        elif s == 2:
            self.copy("1a").wait_recv()
            self.copy("1b").wait_recv()

            @pl.loop(0, LINE)
            def _(i):
                for k in range(2):
                    self.add(self.at(i, y, k, 0), self.buf1a[i, k])
                    self.add(self.at(i, k, x, 1), self.buf1b[i, k])

            self.copy("2a").start()
            self.copy("2b").start()
        elif s == 3:
            self.copy("2a").wait_recv()
            self.copy("2b").wait_recv()

            @pl.loop(0, LINE)
            def _(i):
                self.add(self.at(i, y, x, 0), self.buf2a[i])
                self.add(self.at(i, y, x, 1), self.buf2b[i])

            for k in range(1, LINE):
                self.line_copy(k).start()
        else:
            total = as_float(self.at(z, y, x)[...])
            for k in range(1, LINE):
                self.line_copy(k).wait_recv()
                total = total + as_float(self.line[k - 1])
            self.finish(total)

    def drain(self):
        for name in ("pair", "1a", "1b", "2a", "2b"):
            self.copy(name).wait_send()
        for k in range(1, LINE):
            self.line_copy(k).wait_send()


SMALL = (16, 256)


def back_kernel(
    shape, plan, x_ref, normed_ref, q_ref, k_ref, v_ref, probs_ref, mixed_ref, attn_ref, gres_ref, wqkv_ref, wproj_ref, vec_ref,
    two_ref, hidden_ref, early_ref, raw_g, raw_l, gfc1_ref, gfc2_ref,
    gxg_ref, gxl_ref, sqkv_ref, sproj_ref, sfc1_ref, sfc2_ref, ssmall_ref,
    gqkv, gmixed, bsum, vecs, tsum, corner, index_g, index_l, *scratch,
):
    packs, glob, heads, groups, blocks, grids = shape
    step = pl.program_id(0)
    rows, features = normed_ref.shape
    seq = rows // packs
    width = features // heads
    lanes = features // groups
    scale = width**-0.5
    vec = lambda k: vec_ref[pl.ds(k, 1), :]
    size = rows // blocks
    last = 1 + packs * groups + 1 + blocks

    send, recv = scratch[-2:]
    scratch = scratch[:-2]
    big = SPLIT + 1
    owns = list(scratch[:big]) + [None] * (groups + 2)
    terms = scratch[big : big + groups + 2]
    bufs = scratch[big + groups + 2 :]

    def put_group(g):
        def finish(value):
            for i in range(3):
                sqkv_ref[:, pl.ds(i * features + g * lanes, lanes)] = value[:, i * lanes : (i + 1) * lanes]

        return finish

    tall = gfc2_ref.shape[4] // SPLIT
    sources, ends = [], []
    for k in range(SPLIT):
        sources.append(gfc2_ref.at[EVERY, EVERY, EVERY, EVERY, pl.ds(k * tall, tall)])
        ends.append(put(sfc2_ref.at[pl.ds(k * tall, tall)]))
    sources.append(gfc1_ref)
    done = early_ref.shape[1]
    ends.append(put(sfc1_ref.at[EVERY, pl.ds(done, gfc1_ref.shape[5])]))
    sources += list(terms)
    ends += [put(sproj_ref)] + [put_group(g) for g in range(groups)] + [put(ssmall_ref)]
    flows = [
        Scatter(sources[t], owns[t], bufs[Scatter.BUFS * t : Scatter.BUFS * (t + 1)], send.at[t], recv.at[t], ends[t]) for t in range(len(ends))
    ]

    def slot(k):
        for t, s in plan.get(k, ()):
            flows[t].stage(s)

    @pl.when(step == 0)
    def _():
        greet()
        slot(0)
        sfc1_ref[:, pl.ds(0, done)] = early_ref[...]
        zero = jnp.zeros((1, features), jnp.float32)
        vecs[...] = jnp.zeros_like(vecs)

        def block(i, sums):
            part = pl.ds(pl.multiple_of(i * size, size), size)
            gres = gres_ref[part, :]
            gattn = (vec(V_G1) * gres).astype(jnp.bfloat16)
            gqkv[part, pl.ds(0, features)] = gattn
            gmixed[part, :] = dot_nt(gattn, wproj_ref[...]).astype(jnp.bfloat16)
            return (sums[0] + column_sum(as_float(gattn)), sums[1] + column_sum(gres * as_float(attn_ref[part, :])))

        sums = lax.fori_loop(0, blocks, block, (zero, zero))
        vecs[pl.ds(V_PB, 1), :] = sums[0]
        vecs[pl.ds(V_G1, 1), :] = sums[1]
        bsum[...] = jnp.zeros_like(bsum)
        fill_terms(terms[0], dot_tn(mixed_ref[...], gqkv[:, pl.ds(0, features)]))

    @pl.when((step >= 1) & (step <= packs * groups))
    def _():
        pack = (step - 1) % packs
        group = (step - 1) // packs
        part = pl.ds(pl.multiple_of(pack * seq, seq), seq)
        kind = jnp.where(pack < glob, 0, 1)
        for pair in range(heads // 2 // groups):
            at = 2 * width * pair
            wide = pl.ds(pl.multiple_of(group * lanes + at, 2 * width), 2 * width)
            queries = stack_heads(q_ref[:, pl.ds(at, 2 * width)], width)
            keys = k_ref[:, pl.ds(at, 2 * width)]
            values = v_ref[:, pl.ds(at, 2 * width)]
            grads = stack_heads(gmixed[part, wide], width)
            mixed = as_float(mixed_ref[part, wide])
            probs = probs_ref[0, pair]
            twice = jnp.concatenate([mixed, mixed], axis=0)
            inner = jnp.sum(as_float(grads) * twice, axis=-1, keepdims=True)
            gscores = as_float(probs) * (dot_nt(grads, values) - inner)
            head = group * (heads // groups) + 2 * pair
            bsum[kind, pl.ds(head, 2), :, pl.ds(0, seq)] += gscores.reshape(2, seq, seq)
            low = gscores.astype(jnp.bfloat16)
            gq = (merge_heads(dot(low, keys), width) * scale).astype(jnp.bfloat16)
            gk = (dot_tn(low, queries) * scale).astype(jnp.bfloat16)
            gv = dot_tn(probs, grads).astype(jnp.bfloat16)
            for i, piece in enumerate((gq, gk, gv)):
                at_lane = pl.multiple_of(group * lanes + at + i * features, 2 * width)
                gqkv[part, pl.ds(at_lane, 2 * width)] = piece

    for g in range(groups):
        @pl.when(step == packs * (g + 1))
        def _():
            pieces = [dot_tn(normed_ref[...], gqkv[:, pl.ds(i * features + g * lanes, lanes)]) for i in range(3)]
            fill_terms(terms[1 + g], jnp.concatenate(pieces, axis=1))

    @pl.when(step == packs * groups + 1)
    def _():
        pick_rows(raw_g, index_g)
        pick_rows(raw_l, index_l)
        tsum[...] = collect(
            grids, (bsum.at[0], bsum.at[1]), (index_g, index_l), (corner, corner), tsum.shape
        )

    @pl.when(step >= packs * groups + 2)
    def _():
        i = step - packs * groups - 2
        part = pl.ds(pl.multiple_of(i * size, size), size)
        low = gqkv[part, :]
        gnorm = dot_nt(low, wqkv_ref[...])
        unit, spread = unit_rows(as_float(x_ref[...]))
        vecs[pl.ds(V_LN1G, 1), :] += column_sum(gnorm * unit)
        vecs[pl.ds(V_LN1B, 1), :] += column_sum(gnorm)
        total = column_sum(as_float(low))
        vecs[pl.ds(V_QB, 1), :] += total[:, :features]
        vecs[pl.ds(V_VB, 1), :] += total[:, 2 * features :]
        value = gres_ref[part, :] + unit_back(gnorm * vec(V_LN1G), unit, spread)
        per_block = packs // blocks
        glob_len, loc_len, per_pack, slot = grids[0][1], grids[1][1], grids[1][2], grids[1][3]

        @pl.when(i < glob // per_block)
        def _():
            for n in range(per_block):
                gxg_ref[n] = value[n * seq : n * seq + glob_len].astype(gxg_ref.dtype)

        @pl.when(i >= glob // per_block)
        def _():
            for n in range(per_block):
                for k in range(per_pack):
                    start = n * seq + k * slot
                    gxl_ref[n * per_pack + k] = value[start : start + loc_len].astype(gxl_ref.dtype)

    @pl.when(step == last - 1)
    def _():
        for k, row in ((V_LN2G, 0), (V_LN2B, 1), (V_FB, 2), (V_G2, 3)):
            vecs[pl.ds(k, 1), :] = two_ref[pl.ds(row, 1), :]
        ref = terms[-1]
        ref[...] = jnp.zeros_like(ref)
        devices = LINE * 8
        count, wide, table = features // devices, hidden_ref.shape[1] // devices, tsum.shape[1] // devices
        for d in range(devices):
            block = ref.at[d // 8, d // 4 % 2, d // 2 % 2, d % 2]
            block[:, pl.ds(0, count)] = vecs[:, pl.ds(d * count, count)]
            block[pl.ds(10, 1), pl.ds(0, wide)] = hidden_ref[:, pl.ds(d * wide, wide)]
            block[pl.ds(0, heads), pl.ds(128, table)] = tsum[:, pl.ds(d * table, table)]

    for k in sorted(plan):
        if k:
            @pl.when(step == k)
            def _():
                slot(k)

    @pl.when(step == last - 1)
    def _():
        for flow in flows:
            flow.drain()


BACK_PLAN = {
    0: ((0, 0), (1, 0),),
    1: ((0, 1),),
    4: ((2, 0),),
    5: ((1, 1),),
    7: ((3, 0), (4, 0), (2, 1),),
    11: ((0, 2),),
    12: ((1, 2),),
    13: ((5, 0), (2, 2),),
    16: ((0, 3), (5, 1),),
    18: ((6, 0), (4, 1), (1, 3), (3, 1),),
    19: ((4, 2), (2, 3), (5, 2), (6, 1),),
    20: ((3, 2),),
    21: ((4, 3),),
    22: (
        (7, 0), (1, 4), (5, 3), (6, 2), (7, 1), (4, 4), (2, 4), (3, 3),
        (5, 4), (6, 3), (7, 2), (0, 4), (7, 3), (6, 4), (3, 4), (7, 4),
    ),
}
SPLIT = 2


def attend_back(
    x, normed, qkv, probs, mixed, attn, gres, wqkv, wproj, vectors, two, hidden, early, indices, gfc1, gfc2, packs, glob, heads,
    grids, table_rows, out_dtype, lanes,
):
    rows, features = x.shape
    seq = rows // packs
    groups, blocks = 3, 3
    per_block = packs // blocks
    cols = features // groups
    steps = 1 + packs * groups + 1 + blocks
    first_block = packs * groups + 2
    whole = lambda shape: pl.BlockSpec(shape, lambda s: (0,) * len(shape), pipeline_mode=pl.Buffered(1))
    at = lambda s: jnp.clip(s - 1, 0, packs * groups - 1)
    part = lambda i: pl.BlockSpec((seq, cols), lambda s: (at(s) % packs, i * groups + at(s) // packs))
    any_ref = pl.BlockSpec(memory_space=pl.ANY)
    by_block = pl.BlockSpec((rows // blocks, features), lambda s: (jnp.clip(s - first_block, 0, blocks - 1), 0))
    shard = lambda t: t.shape[4:]
    joined = (early.shape[0], early.shape[1] + shard(gfc1)[1])
    term_shapes = [(features // 32, features)] + [(features // 32, 3 * cols)] * groups
    tall = (shard(gfc2)[0] // SPLIT, shard(gfc2)[1])
    flow_shapes = [(tall, gfc2.dtype)] * SPLIT + [(shard(gfc1), gfc1.dtype)]
    scratch = [
        pltpu.VMEM((rows, 3 * features), jnp.bfloat16),
        pltpu.VMEM((rows, features), jnp.bfloat16),
        pltpu.VMEM((2, heads, seq, lanes), jnp.float32),
        pltpu.VMEM((16, features), jnp.float32),
        pltpu.VMEM((heads, table_rows), jnp.float32),
        pltpu.VMEM((2, heads, ROW_SLOTS, lanes), jnp.float32),
        pltpu.VMEM((8, lanes), jnp.int32),
        pltpu.VMEM((8, lanes), jnp.int32),
    ]
    scratch += [pltpu.VMEM((LINE, 2, 2) + s, d) for s, d in flow_shapes]
    flow_shapes += [(s, jnp.bfloat16) for s in term_shapes] + [(SMALL, jnp.float32)]
    scratch += [pltpu.VMEM(GRID + s, jnp.bfloat16) for s in term_shapes] + [pltpu.VMEM(GRID + SMALL, jnp.float32)]
    for s, d in flow_shapes:
        scratch += Scatter.scratch(s, d)
    scratch += [pltpu.SemaphoreType.DMA((len(flow_shapes), Scatter.SEMS))] * 2
    return pl.pallas_call(
        functools.partial(
            back_kernel, (packs, glob, heads, groups, blocks, grids), BACK_PLAN
        ),
        grid=(steps,),
        out_shape=[
            jax.ShapeDtypeStruct((glob, grids[0][1], features), out_dtype),
            jax.ShapeDtypeStruct(((packs - glob) * grids[1][2], grids[1][1], features), out_dtype),
            jax.ShapeDtypeStruct((features // 32, 3 * features), jnp.float32),
            jax.ShapeDtypeStruct((features // 32, features), jnp.float32),
            jax.ShapeDtypeStruct(joined, jnp.float32),
            jax.ShapeDtypeStruct(shard(gfc2), jnp.float32),
            jax.ShapeDtypeStruct(SMALL, jnp.float32),
        ],
        in_specs=[
            by_block,
            whole((rows, features)),
            part(0), part(1), part(2),
            pl.BlockSpec((1, heads // 2 // groups, 2 * seq, seq), lambda s: (at(s) % packs, at(s) // packs, 0, 0)),
            whole((rows, features)),
            whole((rows, features)),
            whole((rows, features)),
            whole(wqkv.shape),
            whole(wproj.shape),
            whole(vectors.shape),
            whole(two.shape),
            whole(hidden.shape),
            whole(early.shape),
            whole(indices[0].shape),
            whole(indices[1].shape),
            any_ref,
            any_ref,
        ],
        out_specs=[
            pl.BlockSpec(
                (per_block, grids[0][1], features),
                lambda s: (jnp.clip(s - first_block, 0, glob // per_block - 1), 0, 0),
            ),
            pl.BlockSpec(
                (per_block * grids[1][2], grids[1][1], features),
                lambda s: (jnp.maximum(s - first_block - glob // per_block, 0), 0, 0),
            ),
            whole((features // 32, 3 * features)),
            whole((features // 32, features)),
            whole(joined),
            whole(shard(gfc2)),
            whole(SMALL),
        ],
        scratch_shapes=scratch,
        compiler_params=pltpu.CompilerParams(vmem_limit_bytes=BIG, collective_id=1, has_side_effects=True),
        name="attend_back",
    )(x, normed, qkv, qkv, qkv, probs, mixed, attn, gres, wqkv, wproj, vectors, two, hidden, early, *indices, gfc1, gfc2)


GATHER_HEAD = (
    (0, "a"), (2, "a"), (1, "a"), (4, "a"), (0, "n"), (6, "a"), (0, "z"), (5, "a"), (1, "n"), (2, "n"), (0, "f"),
    (4, "n"), (6, "n"), (2, "z"), (5, "n"), (0, "q"), (3, "a"), (1, "z"), (0, "e"), (3, "n"), "unpack", (2, "f"),
    (1, "f"), "expand global", (6, "z"), (2, "q"), "expand local", (1, "q"), (4, "z"), (5, "z"), (2, "e"), (6, "f"),
    (1, "e"),
)
GATHER_LATER = {
    1: ((3, "z"), (4, "f")),
    2: ((6, "q"), (5, "f")),
    4: ((3, "f"), (4, "q")),
    5: ((4, "e"), (5, "q")),
    7: ((3, "q"), (6, "e"), (5, "e"), (3, "e")),
}


def pick_rows(index_ref, rows_ref):
    length = index_ref.shape[0]
    rows_ref[...] = jnp.full(rows_ref.shape, -1, jnp.int32)
    for k, row in enumerate(corner_rows(math.isqrt(length - 1)) + (0,)):
        rows_ref[pl.ds(k, 1), pl.ds(0, length)] = index_ref[pl.ds(row, 1), :]


def front_kernel(
    shape, xg_ref, xl_ref, vecs_ref, shift_ref, table_ref, oqkv_ref, oproj_ref, ofc1_ref, ofc2_ref, raw_g, raw_l,
    x_ref, normed_ref, qkv_ref, probs_ref, mixed_ref, attn_ref, resid_ref, vec_ref, hidden_ref,
    fqkv_ref, fproj_ref, ffc1_ref, ffc2_ref,
    table, bias, rows_g, rows_l, padded, wqkv, wproj, small_ref, small_full, index_g, index_l, load, send, recv,
):
    packs, glob, heads, grids = shape
    step = pl.program_id(0)
    seq, features = x_ref.shape
    width = features // heads
    devices = LINE * 8
    vec = lambda k: vec_ref[pl.ds(k, 1), :]
    wide, tall = ofc1_ref.shape[1] // 2, ofc2_ref.shape[0] // 2
    ends = [(small_ref, small_full), (oqkv_ref, fqkv_ref), (oproj_ref, fproj_ref)]
    lead = (EVERY,) * 4
    for k in range(2):
        cols = (EVERY, pl.ds(k * wide, wide))
        ends.append((ofc1_ref.at[cols], ffc1_ref.at[lead + cols]))
    for k in range(2):
        lines = (pl.ds(k * tall, tall),)
        ends.append((ofc2_ref.at[lines], ffc2_ref.at[lead + lines]))
    flows = [Gather(o, f, send.at[t], recv.at[t]) for t, (o, f) in enumerate(ends)]

    def each_shard(act):
        @pl.loop(0, devices)
        def _(d):
            for k, (ref, held) in enumerate(((fqkv_ref, wqkv), (fproj_ref, wproj))):
                count = held.shape[0] // devices
                part = held.at[pl.ds(pl.multiple_of(d * count, 8), count)]
                act(pltpu.make_async_copy(ref.at[d // 8, d // 4 % 2, d // 2 % 2, d % 2], part, load.at[k, d]))

    @pl.when(step == 0)
    def _():
        greet()
        small_ref[...] = jnp.zeros_like(small_ref)
        small_ref[pl.ds(0, vecs_ref.shape[0]), pl.ds(0, vecs_ref.shape[1])] = as_float(vecs_ref[...])
        small_ref[pl.ds(10, 1), pl.ds(0, shift_ref.shape[1])] = as_float(shift_ref[...])
        small_ref[pl.ds(0, heads), pl.ds(128, table_ref.shape[1])] = as_float(table_ref[...])
        pick_rows(raw_g, index_g)
        pick_rows(raw_l, index_l)
        table[...] = jnp.zeros_like(table)
        for item in GATHER_HEAD:
            if item == "unpack":
                count, wide = features // devices, hidden_ref.shape[1] // devices
                lines = table.shape[1] // devices
                for d in range(devices):
                    block = small_full.at[d // 8, d // 4 % 2, d // 2 % 2, d % 2]
                    vec_ref[:, pl.ds(d * count, count)] = block[:, pl.ds(0, count)]
                    hidden_ref[:, pl.ds(d * wide, wide)] = block[pl.ds(10, 1), pl.ds(0, wide)]
                    table[pl.ds(0, heads), pl.ds(d * lines, lines)] = block[pl.ds(0, heads), pl.ds(128, lines)]
            elif item == "expand global":
                expand(grids[:1], table, (index_g,), (bias.at[0],), (rows_g,))
            elif item == "expand local":
                expand(grids[1:], table, (index_l,), (bias.at[1],), (rows_l,))
            else:
                flows[item[0]].stage(item[1])
        each_shard(lambda copy: copy.start())
        each_shard(lambda copy: copy.wait())

    @pl.when((step >= 1) & (step <= packs))
    def _():
        padded[...] = jnp.zeros_like(padded)

        @pl.when(step <= glob)
        def _():
            padded[pl.ds(0, xg_ref.shape[1]), :] = as_float(xg_ref[0])

        @pl.when(step > glob)
        def _():
            for k in range(xl_ref.shape[0]):
                padded[pl.ds(k * grids[1][3], xl_ref.shape[1]), :] = as_float(xl_ref[k])

        inputs = padded[...]
        x_ref[...] = inputs.astype(jnp.bfloat16)
        unit, _ = unit_rows(inputs)
        normed = (unit * vec(V_LN1G) + vec(V_LN1B)).astype(jnp.bfloat16)
        normed_ref[...] = normed
        qkv_ref[:, pl.ds(0, features)] = (dot(normed, wqkv[:, pl.ds(0, features)]) + vec(V_QB)).astype(jnp.bfloat16)
        qkv_ref[:, pl.ds(features, features)] = dot(normed, wqkv[:, pl.ds(features, features)]).astype(jnp.bfloat16)
        qkv_ref[:, pl.ds(2 * features, features)] = (
            dot(normed, wqkv[:, pl.ds(2 * features, features)]) + vec(V_VB)
        ).astype(jnp.bfloat16)
        kind = jnp.where(step <= glob, 0, 1)
        for pair in range(heads // 2):
            at = 2 * width * pair
            queries = stack_heads(qkv_ref[:, pl.ds(at, 2 * width)], width)
            keys = qkv_ref[:, pl.ds(features + at, 2 * width)]
            values = qkv_ref[:, pl.ds(2 * features + at, 2 * width)]
            part = bias[kind, pl.ds(2 * pair, 2), :, pl.ds(0, seq)].reshape(2 * seq, seq)
            scores = dot_nt(queries, keys) * (width**-0.5) + part
            weights = jnp.exp(scores - jnp.max(scores, axis=-1, keepdims=True))
            probs = (weights * (1.0 / jnp.sum(weights, axis=-1, keepdims=True))).astype(jnp.bfloat16)
            probs_ref[0, pair] = probs
            mixed_ref[:, pl.ds(at, 2 * width)] = merge_heads(dot(probs, values), width).astype(jnp.bfloat16)

        attn = dot(mixed_ref[...], wproj[...]) + vec(V_PB)
        attn_ref[...] = attn.astype(jnp.bfloat16)
        resid_ref[...] = inputs + vec(V_G1) * attn

    for k, items in GATHER_LATER.items():
        @pl.when(step == k)
        def _():
            for t, s in items:
                flows[t].stage(s)

    @pl.when(step == packs + 1)
    def _():
        for flow in flows:
            flow.drain()


def attend_front(xg, xl, smalls, shards, indices, packs, heads, grids, seq, table_rows):
    glob, glob_len, features = xg.shape
    loc, loc_len, _ = xl.shape
    per_pack = loc // (packs - glob)
    rows, lanes = packs * seq, round_up(seq, 128)
    hidden = shards[2].shape[1]
    whole = lambda shape: pl.BlockSpec(shape, lambda s: (0,) * len(shape), pipeline_mode=pl.Buffered(1))
    at = lambda s: jnp.clip(s - 1, 0, packs - 1)
    by_rows = lambda cols: pl.BlockSpec((seq, cols), lambda s: (at(s), 0))
    any_ref = pl.BlockSpec(memory_space=pl.ANY)
    owns = list(smalls) + list(shards)
    return pl.pallas_call(
        functools.partial(front_kernel, (packs, glob, heads, grids)),
        grid=(packs + 2,),
        out_shape=[
            jax.ShapeDtypeStruct((rows, features), jnp.bfloat16),
            jax.ShapeDtypeStruct((rows, features), jnp.bfloat16),
            jax.ShapeDtypeStruct((rows, 3 * features), jnp.bfloat16),
            jax.ShapeDtypeStruct((packs, heads // 2, 2 * seq, seq), jnp.bfloat16),
            jax.ShapeDtypeStruct((rows, features), jnp.bfloat16),
            jax.ShapeDtypeStruct((rows, features), jnp.bfloat16),
            jax.ShapeDtypeStruct((rows, features), jnp.float32),
            jax.ShapeDtypeStruct((16, features), jnp.float32),
            jax.ShapeDtypeStruct((1, hidden), jnp.float32),
        ]
        + [jax.ShapeDtypeStruct(GRID + s.shape, s.dtype) for s in shards],
        in_specs=[
            pl.BlockSpec((1, glob_len, features), lambda s: (jnp.minimum(at(s), glob - 1), 0, 0)),
            pl.BlockSpec((per_pack, loc_len, features), lambda s: (jnp.maximum(at(s) - glob, 0), 0, 0)),
        ]
        + [whole(o.shape) for o in owns]
        + [whole(i.shape) for i in indices],
        out_specs=[
            by_rows(features),
            by_rows(features),
            by_rows(3 * features),
            pl.BlockSpec((1, heads // 2, 2 * seq, seq), lambda s: (at(s), 0, 0, 0)),
            by_rows(features),
            by_rows(features),
            by_rows(features),
            whole((16, features)),
            whole((1, hidden)),
        ]
        + [any_ref] * 4,
        scratch_shapes=[
            pltpu.VMEM((16, table_rows), jnp.float32),
            pltpu.VMEM((2, heads, seq, lanes), jnp.float32),
            pltpu.VMEM((2, heads, ROW_SLOTS, lanes), jnp.float32),
            pltpu.VMEM((2, heads, ROW_SLOTS, lanes), jnp.float32),
            pltpu.VMEM((seq, features), jnp.float32),
            pltpu.VMEM((features, 3 * features), jnp.bfloat16),
            pltpu.VMEM((features, features), jnp.bfloat16),
            pltpu.VMEM(SMALL, jnp.float32),
            pltpu.VMEM(GRID + SMALL, jnp.float32),
            pltpu.VMEM((8, lanes), jnp.int32),
            pltpu.VMEM((8, lanes), jnp.int32),
            pltpu.SemaphoreType.DMA((2, LINE * 8)),
            pltpu.SemaphoreType.DMA((len(shards) + 3, Gather.SEMS + 1)),
            pltpu.SemaphoreType.DMA((len(shards) + 3, Gather.SEMS + 1)),
        ],
        compiler_params=pltpu.CompilerParams(vmem_limit_bytes=BIG, collective_id=0, has_side_effects=True),
        name="attend_front",
    )(xg, xl, *owns, *indices)


def gather_params(vectors, hidden_shift, table, weights):
    whole = lambda v: lax.all_gather(v, "fsdp", axis=0, tiled=True)
    return ([as_float(whole(v)) for v in vectors], as_float(whole(hidden_shift)), as_float(whole(table)), [whole(w) for w in weights])


def scatter_grads(vectors, hidden_shift, table, weights):
    share = lambda v: lax.psum_scatter(as_float(v), "fsdp", scatter_dimension=0, tiled=True)
    return ([share(v) for v in vectors], share(hidden_shift), share(table), [share(w) for w in weights])


def slot_rows(values, slot, seq):
    crops, length, features = values.shape
    per_pack = seq // slot
    values = jnp.pad(values, ((0, 0), (0, slot - length), (0, 0)))
    values = values.reshape(crops // per_pack, per_pack * slot, features)
    return jnp.pad(values, ((0, 0), (0, seq - per_pack * slot), (0, 0)))


def crop_rows(packed, slot, crops, length):
    packs, seq, features = packed.shape
    per_pack = seq // slot
    return packed[:, : per_pack * slot].reshape(crops, slot, features)[:, :length]


def per_device(
    x_global, x_local, cot_global, cot_local, global_count, local_count, index_global, index_local,
    ln1_gain, ln1_bias, qkv_weight, q_bias, v_bias, proj_weight, proj_bias, gamma1, bias_table,
    ln2_gain, ln2_bias, fc1_weight, fc1_bias, fc2_weight, fc2_bias, gamma2,
):
    glob, glob_len, features = x_global.shape
    loc, loc_len = x_local.shape[:2]
    heads = bias_table.shape[1]
    seq = round_up(glob_len, 16)
    slot = round_up(loc_len, 8)
    per_pack = seq // slot
    packs = glob + loc // per_pack
    devices = lax.axis_size("fsdp")
    vector_args = [ln1_gain, ln1_bias, q_bias, v_bias, proj_bias, gamma1, ln2_gain, ln2_bias, fc2_bias, gamma2]
    weights = [qkv_weight, proj_weight, fc1_weight, fc2_weight]
    table_rows = bias_table.shape[0] * devices
    indices = (index_global, index_local)
    sides = (math.isqrt(glob_len - 1), math.isqrt(loc_len - 1))
    grids = ((sides[0], glob_len, 1, seq), (sides[1], loc_len, per_pack, slot))

    rows_of = lambda g, l: jnp.concatenate([slot_rows(g, seq, seq), slot_rows(l, slot, seq)]).reshape(-1, features)
    if devices == 32:
        x, normed, qkv, probs, mixed, attn, resid, vectors, hidden_row, *full = attend_front(
            x_global, x_local, (jnp.stack(vector_args), fc1_bias[None], bias_table.T), weights, indices, packs, heads, grids, seq,
            table_rows,
        )
        qkv_full, proj_full, fc1_full, fc2_full = [f.reshape(devices * f.shape[4], f.shape[5]) for f in full]
        lanes = round_up(seq, 128)
    else:
        small_full, hidden_full, table_full, (qkv_full, proj_full, fc1_full, fc2_full) = gather_params(
            vector_args, fc1_bias, bias_table, weights
        )
        vectors = jnp.pad(jnp.stack(small_full), ((0, 6), (0, 0)))
        hidden_row = hidden_full[None]
        table = jnp.pad(table_full.T, ((0, round_up(heads, 16) - heads), (0, 0))).astype(jnp.bfloat16)
        x = rows_of(x_global, x_local)
        bias = expand_bias(table, indices, grids, heads, seq)
        lanes = bias.shape[-1]
        normed, qkv, probs, mixed, attn, resid = attend_forward(
            x, qkv_full, proj_full, vectors, bias, packs, glob, heads
        )
    out_global, out_local, gres, gfc1, gfc2, gfc1_shift, small_two, *early = mlp_both(
        global_count, local_count, resid, cot_global, cot_local, vectors, fc1_full, hidden_row, fc2_full, seq, slot,
        x_global.dtype, jnp.bfloat16, 2 if devices == 32 else 0,
    )
    if devices == 32:
        shaped = lambda g: g.reshape(GRID + (g.shape[0] // devices, g.shape[1]))
        gx_global, gx_local, *shares, small = attend_back(
            x, normed, qkv, probs, mixed, attn, gres, qkv_full, proj_full, vectors, small_two, gfc1_shift, early[0], indices,
            shaped(gfc1), shaped(gfc2), packs, glob, heads, grids, table_rows, x_global.dtype, lanes,
        )
        sums = [small[k, : features // devices] for k in range(10)]
        hidden_sum = small[10, : fc1_bias.shape[0]]
        table_sum = small[:heads, 128 : 128 + table_rows // devices].T
    else:
        gx, gqkv, gproj, bias_sums, small_one, gqkv_shift = attend_backward(
            x, normed, qkv, probs, mixed, attn, gres, qkv_full, proj_full, vectors, packs, glob, heads,
            x_global.dtype, jnp.bfloat16, lanes,
        )
        gx = gx.reshape(packs, seq, features)
        gx_global, gx_local = crop_rows(gx[:glob], seq, glob, glob_len), crop_rows(gx[glob:], slot, loc, loc_len)
        gtable = collect_bias(bias_sums, indices, grids, table_rows).T
        vector_grads = [
            small_one[0], small_one[1], gqkv_shift[0, :features], gqkv_shift[0, 2 * features :], small_one[2],
            small_one[3], small_two[0], small_two[1], small_two[2], small_two[3],
        ]
        sums, hidden_sum, table_sum, shares = scatter_grads(
            vector_grads, gfc1_shift[0], gtable, [gqkv, gproj, gfc1, gfc2]
        )
    return (
        out_global, out_local, gx_global, gx_local,
        sums[0], sums[1], shares[0], sums[2], sums[3], shares[1], sums[4], sums[5], table_sum,
        sums[6], sums[7], shares[2], hidden_sum, shares[3], sums[8], sums[9],
    )


def solution(mesh):
    placed = (
        P("fsdp", None, None),
        P("fsdp", None, None),
        P("fsdp", None, None),
        P("fsdp", None, None),
        P("fsdp"),
        P("fsdp"),
        P(),
        P(),
        P("fsdp"),
        P("fsdp"),
        P("fsdp", None),
        P("fsdp"),
        P("fsdp"),
        P("fsdp", None),
        P("fsdp"),
        P("fsdp"),
        P("fsdp", None),
        P("fsdp"),
        P("fsdp"),
        P("fsdp", None),
        P("fsdp"),
        P("fsdp", None),
        P("fsdp"),
        P("fsdp"),
    )
    return jax.shard_map(
        per_device,
        mesh=mesh,
        in_specs=placed,
        out_specs=(
            P("fsdp", None, None),
            P("fsdp", None, None),
            P("fsdp", None, None),
            P("fsdp", None, None),
            P("fsdp"),
            P("fsdp"),
            P("fsdp", None),
            P("fsdp"),
            P("fsdp"),
            P("fsdp", None),
            P("fsdp"),
            P("fsdp"),
            P("fsdp", None),
            P("fsdp"),
            P("fsdp"),
            P("fsdp", None),
            P("fsdp"),
            P("fsdp", None),
            P("fsdp"),
            P("fsdp"),
        ),
        check_vma=False,
    )
```
